32 devices in a mesh: blk: 8 (over y, x, core), mp: 4 (over z).
Axes of the slice: x: 2, y: 2, z: 4, core: 2. Of those that a mesh axis runs over, the one named last changes fastest.
Arguments:
- streams: bfloat16 [8192, 4, 2048], P('blk', None, 'mp'), may hold values from -36 to 36
- proj_master: float32 [2048, 4, 2048], P(('blk', 'mp')), may hold values from -3 to 3
- hc_proj: float32 [2048, 6], P('mp'), may hold values from -0.125 to 0.125
- hc_static: float32 [4, 6], replicated, may hold values from -2 to 2
- segment_ids: int32 [8192], P('blk'), may hold values from 0 to 31, as said below
- block_mask: int32 [16], P('blk'), may hold values from 0 to 1, as said below
Outputs:
- new_streams: bfloat16 [8192, 4, 2048], P('blk', None, 'mp')
The draws below stay inside these ranges and needn't reach their ends.
Inputs may be any that keep to these rules, and one draw needn't show every extreme that they name: `segment_ids`: never falls along the tokens; every prompt has 1 to 511 tokens, one of them exactly 511; each block of 512 tokens holds the start of two prompts. `block_mask`: entry b is 1 exactly where the first token of block b belongs to the prompt of the last token of block b - 1; entry 0 is 0.
All inputs are finite; a program needn't handle non-finite values.
Results may differ from the reference program's by a relative error of at most 0.0023.
Values may be sent and summed in bfloat16 or wider, within the bound.
No kernel may reach another device: no remote copies, remote signals or barrier semaphores. Data moves between devices by JAX's collectives and lax.ppermute only.
A program may use at most 128 MiB of HBM per device.

```python
import jax
import jax.numpy as jnp
from jax import lax

D = 2048
HEADS = 16
HEAD_DIM = 128
STREAMS = 4
TOK_DEV = 1024
BLOCK = 512
TOKENS = 8192


def doc_layout(key):
    seeded = jax.random.fold_in(key, 11)
    key_one, key_two, key_three = jax.random.split(seeded, 3)
    half_block = BLOCK // 2
    block_count = TOKENS // BLOCK
    first_device = TOK_DEV // BLOCK
    carried = jax.random.randint(key_one, (block_count,), 0, 2)
    carried = carried.at[first_device].set(1)
    first_start = jax.random.randint(key_two, (block_count,), 1, half_block) * carried
    first_start = first_start.at[first_device].set(half_block - 1)
    first_start = first_start.at[0].set(0)
    second_start = jax.random.randint(key_three, (block_count,), 0, half_block)
    second_start = second_start.at[0].set(half_block - 1)
    second_start = second_start.at[first_device - 1].set(0)
    block_base = jnp.arange(block_count, dtype=jnp.int32) * BLOCK
    starts = jnp.stack([block_base + first_start, block_base + half_block + second_start], axis=1).reshape(-1)
    marker = jnp.zeros((TOKENS,), jnp.int32).at[starts].add(1)
    segments = (jnp.cumsum(marker) - 1).astype(jnp.int32)
    mask_values = (first_start > 0).astype(jnp.int32)
    return (segments, mask_values)


def draw_segment_ids(key, part):
    return doc_layout(key)[0]


def draw_block_mask(key, part):
    return doc_layout(key)[1]


def draw_streams(key, part):
    key_one, key_two, key_three = jax.random.split(jax.random.fold_in(key, 3), 3)
    row_scale = jnp.exp(jax.random.uniform(key_two, (TOKENS, STREAMS, 1), jnp.float32, jnp.log(0.5), jnp.log(2.0)))
    base = jnp.clip(jax.random.normal(key_one, (TOKENS, STREAMS, D), jnp.float32), -4.0, 4.0)
    column_scale = jnp.exp(jax.random.uniform(key_three, (D,), jnp.float32, jnp.log(0.3), jnp.log(3.0)))
    return (base * row_scale * column_scale[None, None, :]).astype(jnp.bfloat16)


def draw_proj_master(key, part):
    key_one = jax.random.fold_in(jax.random.fold_in(key, 5), 0)
    base = jnp.clip(jax.random.normal(key_one, (D, 4, D), jnp.float32), -4.0, 4.0) * D ** (-0.5)
    return base


def levels(own_key, dims, shards, low, high):
    level, own = 1.0, jax.random.fold_in(own_key, 6)
    for axis_at, shards_of in shards:
        steps = jnp.exp(jax.random.uniform(jax.random.fold_in(own, axis_at), (shards_of,), jnp.float32, low / len(shards), high / len(shards)))
        level = level * jnp.repeat(steps, dims[axis_at] // shards_of).reshape([-1 if axis == axis_at else 1 for axis in range(len(dims))])
    return level


def scatter_about(stream_key, shape, width, reach, cuts=(), held_as=jnp.bfloat16):
    values = jax.random.normal(stream_key, shape, jnp.float32) * width
    if len(cuts) > 0:
        values = levels(stream_key, shape, cuts, -0.22, 0.18) * values
    return jnp.clip(values, min=-reach, max=reach).astype(held_as)


def setup_inputs(seed: int = 0) -> dict:
    streams_of = jax.random.split(jax.random.key(seed), 7)
    return {
        "streams": draw_streams(jax.random.fold_in(streams_of[6], 71), 0),
        "proj_master": draw_proj_master(jax.random.fold_in(streams_of[6], 71), 0),
        "hc_proj": scatter_about(streams_of[2], (D, 6), D ** -0.5, 0.125, ((0, 4),), jnp.float32),
        "hc_static": scatter_about(streams_of[3], (STREAMS, 6), 0.5, 2.0, (), jnp.float32),
        "segment_ids": draw_segment_ids(jax.random.fold_in(streams_of[6], 71), 0),
        "block_mask": draw_block_mask(jax.random.fold_in(streams_of[6], 71), 0),
    }


def layer_norm(values):
    center = lax.optimization_barrier(jnp.mean(values, axis=-1, keepdims=True))
    centered = values - center
    spread = lax.optimization_barrier(jnp.mean(centered * centered, axis=-1, keepdims=True))
    return centered * lax.rsqrt(spread + 1e-05)

def rotate(values, positions):
    half_dim = values.shape[-1] // 2
    inverse = 10000.0 ** (-(jnp.arange(half_dim, dtype=jnp.float32) * 2.0 / values.shape[-1]))
    angles = positions.astype(jnp.float32)[:, None] * inverse[None, :]
    cosine = jnp.cos(angles)[:, None, :]
    sine = jnp.sin(angles)[:, None, :]
    first_half = values[..., :half_dim]
    second_half = values[..., half_dim:]
    return jnp.concatenate([first_half * cosine - second_half * sine, second_half * cosine + first_half * sine], axis=-1)

def reference(streams, proj_master, hc_proj, hc_static, segment_ids, block_mask):
    highest = lax.Precision.HIGHEST
    block_count = TOKENS // BLOCK
    stream_blocks = streams.reshape(block_count, BLOCK, STREAMS, D)

    def stream_input(block_values):
        stream_values = block_values.astype(jnp.float32)
        hnorm = layer_norm(stream_values)
        dynamic = jnp.tanh(jnp.einsum('tkd,dj->tkj', hnorm, hc_proj, precision=highest))
        coefficients = hc_static[None] + dynamic
        mixed = jnp.einsum('tk,tkd->td', coefficients[..., 0], stream_values, precision=highest)
        return (layer_norm(mixed).astype(jnp.bfloat16), coefficients)
    normed, coefficients = lax.map(stream_input, stream_blocks)
    normed = normed.reshape(TOKENS, D)
    projections = proj_master.astype(jnp.bfloat16).reshape(D, 4 * D)
    qkv = jnp.dot(normed, projections[:, :3 * D], preferred_element_type=jnp.float32)
    token_index = jnp.arange(TOKENS, dtype=jnp.int32)
    opening = jnp.concatenate([jnp.ones((1,), dtype=bool), segment_ids[1:] != segment_ids[:-1]])
    doc_start = lax.cummax(jnp.where(opening, token_index, 0))
    positions = (token_index - doc_start).astype(jnp.int32)
    queries = rotate(qkv[:, :D].reshape(TOKENS, HEADS, HEAD_DIM), positions).astype(jnp.bfloat16)
    keys_rot = rotate(qkv[:, D:2 * D].reshape(TOKENS, HEADS, HEAD_DIM), positions).astype(jnp.bfloat16)
    values_v = qkv[:, 2 * D:].reshape(TOKENS, HEADS, HEAD_DIM).astype(jnp.bfloat16)
    keys_pad = jnp.concatenate([jnp.zeros((BLOCK, HEADS, HEAD_DIM), jnp.bfloat16), keys_rot])
    values_pad = jnp.concatenate([jnp.zeros((BLOCK, HEADS, HEAD_DIM), jnp.bfloat16), values_v])
    segments_pad = jnp.concatenate([jnp.full((BLOCK,), -1, jnp.int32), segment_ids])
    scale = 1.0 / HEAD_DIM ** 0.5

    def attend(block):
        offset = (block * BLOCK).astype(jnp.int32)
        query_rows = lax.dynamic_slice_in_dim(queries, offset, BLOCK, 0)
        key_rows = lax.dynamic_slice_in_dim(keys_pad, offset, 2 * BLOCK, 0)
        value_rows = lax.dynamic_slice_in_dim(values_pad, offset, 2 * BLOCK, 0)
        query_segments = lax.dynamic_slice_in_dim(segment_ids, offset, BLOCK, 0)
        key_segments = lax.dynamic_slice_in_dim(segments_pad, offset, 2 * BLOCK, 0)
        scores = jnp.einsum('qhc,khc->hqk', query_rows.astype(jnp.float32), key_rows.astype(jnp.float32), precision=highest) * scale
        key_slot = jnp.arange(2 * BLOCK, dtype=jnp.int32)[None, :]
        query_slot = jnp.arange(BLOCK, dtype=jnp.int32)[:, None]
        current = (key_slot >= BLOCK) & (key_slot - BLOCK <= query_slot)
        earlier = (key_slot < BLOCK) & (block_mask[block] == 1)
        allowed = (query_segments[:, None] == key_segments[None, :]) & (current | earlier)
        masked = jnp.where(allowed[None], scores, -1e+30)
        row_max = lax.optimization_barrier(jnp.max(masked, axis=-1, keepdims=True))
        weights_exp = jnp.where(allowed[None], jnp.exp(masked - row_max), 0.0)
        row_total = lax.optimization_barrier(jnp.sum(weights_exp, axis=-1))
        rounded = weights_exp.astype(jnp.bfloat16)
        result = jnp.einsum('hqk,khc->qhc', rounded.astype(jnp.float32), value_rows.astype(jnp.float32), precision=highest)
        result = result / jnp.transpose(row_total)[:, :, None]
        return result.astype(jnp.bfloat16).reshape(BLOCK, D)
    attended = lax.map(attend, jnp.arange(block_count, dtype=jnp.int32)).reshape(TOKENS, D)
    update = jnp.dot(attended, jnp.transpose(projections[:, 3 * D:]), preferred_element_type=jnp.float32)

    def stream_output(pieces):
        block_values, block_coefficients, block_update = pieces
        stream_values = block_values.astype(jnp.float32)
        kept = jnp.einsum('tkj,tkd->tjd', block_coefficients[..., 1:1 + STREAMS], stream_values, precision=highest)
        added = block_coefficients[..., 1 + STREAMS][..., None] * block_update[:, None, :]
        return (kept + added).astype(jnp.bfloat16)
    result_blocks = lax.map(stream_output, (stream_blocks, coefficients, update.reshape(block_count, BLOCK, D)))
    return result_blocks.reshape(TOKENS, STREAMS, D)
```

```python
import functools

import jax
import jax.numpy as jnp
from jax import lax
from jax.experimental import pallas as pl
from jax.experimental.pallas import tpu as pltpu
from jax.sharding import PartitionSpec as P

D = 2048
HEAD_DIM = 128
BLOCK = 512
CHUNK = 256
SUB = 64
STREAMS = 4
EPS = 1e-05
BF = jnp.bfloat16
F32 = jnp.float32


def passed_along(value, axis, steps):
    count = lax.axis_size(axis)
    first, last = (max(0, -steps), min(count, count - steps))
    return lax.ppermute(value, axis, [(source, source + steps) for source in range(first, last)])


def from_others(value, axis):
    count = lax.axis_size(axis)
    return [
        lax.ppermute(value, axis, [(source, (source + step) % count) for source in range(count)])
        for step in range(1, count)
    ]


def cost(flops, nbytes, transcendentals=0):
    return pl.CostEstimate(flops=flops, bytes_accessed=nbytes, transcendentals=transcendentals)


def params(limit=40):
    return pltpu.CompilerParams(vmem_limit_bytes=limit << 20)


def split(value, parts):
    out = []
    for _ in range(parts):
        part = value.astype(BF)
        out.append(part)
        value = value - part.astype(F32)
    return out


def contract(a, b, a_dim, b_dim):
    return lax.dot_general(a, b, (((a_dim,), (b_dim,)), ((), ())), preferred_element_type=F32)


def iotas(rows, cols):
    return (
        lax.broadcasted_iota(jnp.int32, (rows, cols), 0),
        lax.broadcasted_iota(jnp.int32, (rows, cols), 1),
    )


def regroup_kernel(master_ref, qkv_ref, out_ref):
    width = out_ref.shape[-1]
    for slot in range(4):
        part = master_ref[:, slot, :].astype(BF)
        if slot < 3:
            qkv_ref[0, :, slot * width : (slot + 1) * width] = part
        else:
            out_ref[0] = part


def regroup(master, servers):
    rows, _, total = master.shape
    width = total // servers
    return pl.pallas_call(
        regroup_kernel,
        grid=(servers,),
        in_specs=[pl.BlockSpec((rows, 4, width), lambda i: (0, 0, i))],
        out_specs=[
            pl.BlockSpec((1, rows, 3 * width), lambda i: (i, 0, 0)),
            pl.BlockSpec((1, rows, width), lambda i: (i, 0, 0)),
        ],
        out_shape=[
            jax.ShapeDtypeStruct((servers, rows, 3 * width), BF),
            jax.ShapeDtypeStruct((servers, rows, width), BF),
        ],
        cost_estimate=cost(0, rows * total * 24),
        name="regroup",
    )(master)


def stats_kernel(x_ref, proj_ref, first_ref, second_ref):
    tokens, _, width = x_ref.shape
    proj = proj_ref[...]
    pieces = jnp.concatenate(split(proj, 3), axis=0)
    column = jnp.sum(proj, axis=1, keepdims=True)
    row, col = iotas(4 * SUB, 4 * SUB)
    same = (row >> 2) == (col >> 2)
    ring = jnp.where(same, (row - col) & 3, -1)
    for at in range(tokens // SUB):
        lanes = slice(at * 4 * SUB, (at + 1) * 4 * SUB)
        v = x_ref[at * SUB : (at + 1) * SUB].reshape(4 * SUB, width)
        sums = contract(pieces, v, 1, 1)
        sums = sums[0:8] + sums[8:16] + sums[16:24]
        gram = contract(v, v, 1, 1)
        first_ref[0:1, lanes] = sums[0:1]
        first_ref[1:2, lanes] = sums[6:7]
        for shift in range(3):
            first_ref[2 + shift : 3 + shift, lanes] = jnp.sum(
                jnp.where(ring == shift, gram, 0.0), axis=0, keepdims=True
            )
        first_ref[5:6, lanes] = jnp.broadcast_to(column[0:1], (1, 4 * SUB))
        first_ref[6:8, lanes] = sums[1:3]
        second_ref[0:3, lanes] = sums[3:6]
        second_ref[3:8, lanes] = jnp.broadcast_to(column[1:6], (5, 4 * SUB))


def stats(x, proj, start, tokens, step=128):
    width = x.shape[-1]
    return pl.pallas_call(
        stats_kernel,
        grid=(tokens // step,),
        in_specs=[
            pl.BlockSpec((step, 4, width), lambda i: (start // step + i, 0, 0)),
            pl.BlockSpec((8, width), lambda i: (0, 0)),
        ],
        out_specs=[pl.BlockSpec((8, 4 * step), lambda i: (0, i))] * 2,
        out_shape=[jax.ShapeDtypeStruct((8, 4 * tokens), F32)] * 2,
        cost_estimate=cost(tokens * 4 * width * 600, tokens * 8 * width),
        compiler_params=params(),
        name="stats",
    )(x, proj)


def by_stream(static_ref, column, stream):
    value = jnp.full(stream.shape, static_ref[0, column], F32)
    for k in range(1, 4):
        value = jnp.where(stream == k, static_ref[k, column], value)
    return value


def centre(first):
    mean = first[1:2] * (1.0 / D)
    spread = first[2:3] * (1.0 / D) - mean * mean
    return mean, lax.rsqrt(spread + EPS)


def mix_kernel(static_ref, x_ref, own_ref, a_ref, b_ref, c_ref, sums_ref, normed_ref):
    tokens, _, width = x_ref.shape
    lanes_total = 4 * tokens
    first = (own_ref[...] + a_ref[...]) + (b_ref[...] + c_ref[...])
    sums_ref[...] = first
    mean, inverse = centre(first)
    stream = lax.broadcasted_iota(jnp.int32, (1, lanes_total), 1) & 3
    mix = by_stream(static_ref, 0, stream) + jnp.tanh(
        inverse * (first[0:1] - mean * first[5:6])
    )
    one = jnp.where(stream < 3, pltpu.roll(mix, lanes_total - 1, 1), pltpu.roll(mix, 3, 1))
    two = jnp.where(stream < 2, pltpu.roll(mix, lanes_total - 2, 1), pltpu.roll(mix, 2, 1))
    linear = mix * first[1:2]
    square = mix * (mix * first[2:3] + 2.0 * one * first[3:4] + two * first[4:5])
    row, col = iotas(SUB, 4 * SUB)
    mine = row == (col >> 2)
    for at in range(tokens // SUB):
        lanes = slice(at * 4 * SUB, (at + 1) * 4 * SUB)
        v = x_ref[at * SUB : (at + 1) * SUB].reshape(4 * SUB, width)
        matrix = jnp.where(mine, mix[:, lanes], 0.0)
        mixed = contract(jnp.concatenate(split(matrix, 3), axis=0), v, 1, 0)
        mixed = mixed[0:SUB] + mixed[SUB : 2 * SUB] + mixed[2 * SUB : 3 * SUB]
        average = jnp.sum(jnp.where(mine, linear[:, lanes], 0.0), axis=1, keepdims=True) * (1.0 / D)
        power = jnp.sum(jnp.where(mine, square[:, lanes], 0.0), axis=1, keepdims=True) * (1.0 / D)
        scale = lax.rsqrt(jnp.maximum(power - average * average, 0.0) + EPS)
        normed_ref[at * SUB : (at + 1) * SUB, :] = ((mixed - average) * scale).astype(BF)


def mix(static, x, parts, start, tokens, offset, step=128):
    width = x.shape[-1]
    lane_block = pl.BlockSpec((8, 4 * step), lambda i: (0, offset // step + i))
    return pl.pallas_call(
        mix_kernel,
        grid=(tokens // step,),
        in_specs=[
            pl.BlockSpec(memory_space=pltpu.SMEM),
            pl.BlockSpec((step, 4, width), lambda i: (start // step + i, 0, 0)),
        ]
        + [lane_block] * 4,
        out_specs=[
            pl.BlockSpec((8, 4 * step), lambda i: (0, i)),
            pl.BlockSpec((step, width), lambda i: (i, 0)),
        ],
        out_shape=[
            jax.ShapeDtypeStruct((8, 4 * tokens), F32),
            jax.ShapeDtypeStruct((tokens, width), BF),
        ],
        cost_estimate=cost(tokens * 4 * width * 400, tokens * 10 * width),
        compiler_params=params(),
        name="mix",
    )(static, x, *parts)


def qkv_kernel(rows_ref, weight_ref, cosine_ref, sine_ref, out_ref):
    servers, _, width = rows_ref.shape
    total = contract(rows_ref[0], weight_ref[0:width, :], 1, 0)
    for server in range(1, servers):
        total += contract(rows_ref[server], weight_ref[server * width : (server + 1) * width, :], 1, 0)
    slot = pl.program_id(0)

    @pl.when(slot < 2)
    def _():
        cosine, sine = cosine_ref[...], sine_ref[...]
        for head in range(total.shape[1] // HEAD_DIM):
            part = total[:, head * HEAD_DIM : (head + 1) * HEAD_DIM]
            turned = part * cosine + pltpu.roll(part, HEAD_DIM // 2, 1) * sine
            out_ref[0, :, head * HEAD_DIM : (head + 1) * HEAD_DIM] = turned.astype(BF)

    @pl.when(slot == 2)
    def _():
        out_ref[0] = total.astype(BF)


def qkv_columns(rows, weight, cosine, sine, start):
    servers, tokens, width = rows.shape
    table = pl.BlockSpec((tokens, HEAD_DIM), lambda j: (start // tokens, 0))
    return pl.pallas_call(
        qkv_kernel,
        grid=(3,),
        in_specs=[
            pl.BlockSpec((servers, tokens, width), lambda j: (0, 0, 0)),
            pl.BlockSpec((D, width), lambda j: (0, j)),
            table,
            table,
        ],
        out_specs=pl.BlockSpec((1, tokens, width), lambda j: (j, 0, 0)),
        out_shape=jax.ShapeDtypeStruct((3, tokens, width), BF),
        cost_estimate=cost(2 * tokens * D * 3 * width, D * 6 * width + tokens * D * 5),
        compiler_params=params(),
        name="qkv",
    )(rows, weight, cosine, sine)


def attend_kernel(
    place_ref, q_ref, k0, k1, k2, v0, v1, v2, qseg_ref, kseg_ref, out_ref, sent_ref, own_ref
):
    tokens, width = q_ref.shape[1:]
    window = kseg_ref.shape[-1]
    place = place_ref[0]
    row, col = iotas(tokens, window)
    allowed = (qseg_ref[...] == kseg_ref[0]) & (col - (window - tokens) <= row)
    bias = jnp.where(allowed, 0.0, -1e30)
    factor = 1.4426950408889634 / HEAD_DIM**0.5
    heads = []
    for head in range(width // HEAD_DIM):
        lanes = slice(head * HEAD_DIM, (head + 1) * HEAD_DIM)
        query = q_ref[0, :, lanes]
        scores = jnp.concatenate(
            [contract(query, k[0, :, lanes], 1, 1) for k in (k0, k1, k2)], axis=1
        )
        scores = scores + bias
        weights = jnp.exp2((scores - jnp.max(scores, axis=1, keepdims=True)) * factor)
        total = jnp.sum(weights, axis=1, keepdims=True)
        values = jnp.concatenate([v[0, :, lanes] for v in (v0, v1, v2)], axis=0)
        heads.append((contract(weights.astype(BF), values, 1, 0) / total).astype(BF))
    attended = jnp.concatenate(heads, axis=1)
    for server in range(sent_ref.shape[0]):
        part = contract(attended, out_ref[server * width : (server + 1) * width, :], 1, 1)
        sent_ref[server] = jnp.where(place == server, 0.0, part).astype(BF)

        @pl.when(place == server)
        def _():
            own_ref[...] = part


def attend(place, query, window, qseg, kseg, weight, chunk):
    source, at = query
    width = source.shape[-1]
    servers = D // width
    block = (1, CHUNK, width)
    keys = [pl.BlockSpec(block, lambda i, s=slot, r=where: (s, r, 0)) for _, slot, where in window]
    values = [
        pl.BlockSpec(block, lambda i, s=slot + 1, r=where: (s, r, 0)) for _, slot, where in window
    ]
    arrays = [array for array, _, _ in window]
    reach = kseg.shape[-1]
    return pl.pallas_call(
        attend_kernel,
        grid=(1,),
        in_specs=[pl.BlockSpec(memory_space=pltpu.SMEM), pl.BlockSpec(block, lambda i: (0, at, 0))]
        + keys
        + values
        + [
            pl.BlockSpec((CHUNK, 1), lambda i: (chunk, 0)),
            pl.BlockSpec((1, 1, reach), lambda i: (chunk, 0, 0)),
            pl.BlockSpec((D, width), lambda i: (0, 0)),
        ],
        out_specs=[
            pl.BlockSpec((servers, CHUNK, width), lambda i: (0, 0, 0)),
            pl.BlockSpec((CHUNK, width), lambda i: (0, 0)),
        ],
        out_shape=[
            jax.ShapeDtypeStruct((servers, CHUNK, width), BF),
            jax.ShapeDtypeStruct((CHUNK, width), F32),
        ],
        cost_estimate=cost(
            4 * CHUNK * reach * width + 2 * CHUNK * D * width,
            D * width * 2 + CHUNK * width * 24,
            CHUNK * reach * 4,
        ),
        compiler_params=params(),
        name="attend",
    )(place, source, *arrays, *arrays, qseg, kseg, weight)


def final_kernel(
    static_ref, x_ref, first_ref, own2_ref, a_ref, b_ref, c_ref, other_ref, own_ref, *rest
):
    new_ref = rest[-1]
    tokens, _, width = x_ref.shape
    first = first_ref[...]
    second = (own2_ref[...] + a_ref[...]) + (b_ref[...] + c_ref[...])
    mean, inverse = centre(first)
    stream = lax.broadcasted_iota(jnp.int32, (1, 4 * tokens), 1) & 3

    def coefficient(column, projected):
        dynamic = jnp.tanh(inverse * (projected - mean * second[2 + column : 3 + column]))
        return by_stream(static_ref, column, stream) + dynamic

    projected = [first[6:7], first[7:8], second[0:1], second[1:2], second[2:3]]
    columns = [coefficient(1 + j, projected[j]) for j in range(5)]
    residual = jnp.concatenate(columns[:4] + columns[:4], axis=0)
    row, col = iotas(4 * SUB, 4 * SUB)
    same = (row >> 2) == (col >> 2)
    row, col = iotas(SUB, 4 * SUB)
    mine = row == (col >> 2)
    for at in range(tokens // SUB):
        lanes = slice(at * 4 * SUB, (at + 1) * 4 * SUB)
        rows = slice(at * SUB, (at + 1) * SUB)
        v = x_ref[rows].reshape(4 * SUB, width)
        matrix = jnp.where(same, jnp.tile(residual[:, lanes], (SUB // 2, 1)), 0.0)
        high, low = split(matrix, 2)
        new = contract(high, v, 1, 0) + contract(low, v, 1, 0)
        update = other_ref[rows, :].astype(F32) + own_ref[rows, :]
        update_high, update_low = split(update, 2)
        spread_high, spread_low = split(jnp.where(mine, columns[4][:, lanes], 0.0), 2)
        new += contract(
            jnp.concatenate([spread_high, spread_high, spread_low], axis=0),
            jnp.concatenate([update_high, update_low, update_high], axis=0),
            0,
            0,
        )
        new_ref[rows] = new.astype(BF).reshape(SUB, 4, width)


def final(static, x, first, first_at, second, second_at, others, own, start, previous, step=128):
    tokens, width = own.shape
    lane_block = pl.BlockSpec((8, 4 * step), lambda i: (0, second_at // step + i))
    stream_block = pl.BlockSpec((step, 4, width), lambda i: (start // step + i, 0, 0))
    specs = [
        pl.BlockSpec(memory_space=pltpu.SMEM),
        stream_block,
        pl.BlockSpec((8, 4 * step), lambda i: (0, first_at // step + i)),
    ]
    specs += [lane_block] * 4
    specs += [pl.BlockSpec((step, width), lambda i: (i, 0))] * 2
    args = [static, x, first, *second, others, own]
    aliases = {}
    if previous is not None:
        specs.append(pl.BlockSpec(memory_space=pl.ANY))
        aliases = {len(args): 0}
        args.append(previous)
    return pl.pallas_call(
        final_kernel,
        grid=(tokens // step,),
        in_specs=specs,
        out_specs=stream_block,
        out_shape=jax.ShapeDtypeStruct(x.shape, BF),
        input_output_aliases=aliases,
        cost_estimate=cost(tokens * 4 * width * 1200, tokens * 22 * width),
        compiler_params=params(),
        name="final",
    )(*args)


def body(streams, proj_master, hc_proj, hc_static, segment_ids, block_mask):
    tokens_local, _, width = streams.shape
    group_size = lax.axis_size("mp")
    place = lax.axis_index("mp").astype(jnp.int32).reshape(1)

    proj_rows = jnp.concatenate(
        [hc_proj.T, jnp.ones((1, width), F32), jnp.zeros((1, width), F32)], axis=0
    )
    first_late, second_late = stats(streams, proj_rows, BLOCK, BLOCK)
    late = [first_late] + from_others(first_late, "mp")
    qkv_part, out_part = regroup(proj_master, group_size)
    first_early, second_early = stats(streams, proj_rows, 0, BLOCK)
    early = [first_early] + from_others(first_early, "mp")

    def served(part):
        exchanged = lax.all_to_all(part, "mp", split_axis=0, concat_axis=0, tiled=True)
        return lax.all_gather(exchanged.reshape(-1, part.shape[-1]), "blk", axis=0, tiled=True)

    qkv_weight = served(qkv_part)
    out_weight = served(out_part)

    def gathered(normed):
        rows = lax.all_gather(normed, "mp", axis=0, tiled=True)
        return rows.reshape(group_size, normed.shape[0], width)

    sums_late, normed_late = mix(hc_static, streams, late, BLOCK, BLOCK, 0)
    rows_late = gathered(normed_late)
    sums_0, normed_0 = mix(hc_static, streams, early, 0, CHUNK, 0)
    rows_0 = gathered(normed_0)
    sums_1, normed_1 = mix(hc_static, streams, early, CHUNK, CHUNK, CHUNK)
    rows_1 = gathered(normed_1)
    second_late = [second_late] + from_others(second_late, "mp")
    second_early = [second_early] + from_others(second_early, "mp")

    halo = passed_along(segment_ids[-BLOCK:], "blk", 1)
    halo = jnp.where(lax.axis_index("blk") == 0, -1, halo)
    extended = jnp.concatenate([halo, segment_ids])
    key_at = jnp.arange(tokens_local + BLOCK, dtype=jnp.int32)[None, :]
    query_at = jnp.arange(tokens_local, dtype=jnp.int32)[:, None] + BLOCK
    earlier = (extended[None, :] == segment_ids[:, None]) & (key_at < query_at)
    positions = jnp.sum(earlier.astype(jnp.int32), axis=1)
    half = HEAD_DIM // 2
    inverse = 10000.0 ** (-(jnp.arange(half, dtype=F32) * 2.0 / HEAD_DIM))
    angles = positions.astype(F32)[:, None] * inverse[None, :]
    cosine, sine = jnp.cos(angles), jnp.sin(angles)
    cosine = jnp.concatenate([cosine, cosine], axis=1)
    sine = jnp.concatenate([-sine, sine], axis=1)
    windows = []
    for block in range(tokens_local // BLOCK):
        before = extended[block * BLOCK : (block + 1) * BLOCK]
        before = jnp.where(block_mask[block] == 1, before, -1)
        seen = jnp.concatenate([before, segment_ids[block * BLOCK : (block + 1) * BLOCK]])
        for chunk in range(BLOCK // CHUNK):
            windows.append(seen[chunk * CHUNK : chunk * CHUNK + BLOCK + CHUNK])
    key_segments = jnp.stack(windows)[:, None, :]
    query_segments = segment_ids[:, None]

    qkv_late = qkv_columns(rows_late, qkv_weight, cosine, sine, BLOCK)
    halo_rows = passed_along(qkv_late[1:3], "blk", 1)
    qkv_0 = qkv_columns(rows_0, qkv_weight, cosine, sine, 0)
    qkv_1 = qkv_columns(rows_1, qkv_weight, cosine, sine, CHUNK)

    chunks = [(halo_rows, 0, 0), (halo_rows, 0, 1), (qkv_0, 1, 0), (qkv_1, 1, 0)]
    chunks += [(qkv_late, 1, 0), (qkv_late, 1, 1)]
    order = [
        (0, (sums_0, 0), (second_early, 0)),
        (1, (sums_1, 0), (second_early, CHUNK)),
        (2, (sums_late, 0), (second_late, 0)),
        (3, (sums_late, CHUNK), (second_late, CHUNK)),
    ]
    result = None
    for chunk, (first, first_at), (second, second_at) in order:
        source, _, at = chunks[chunk + 2]
        sent, own = attend(
            place,
            (source, at),
            chunks[chunk : chunk + 3],
            query_segments,
            key_segments,
            out_weight,
            chunk,
        )
        others = lax.psum_scatter(
            sent.reshape(group_size * CHUNK, width), "mp", scatter_dimension=0, tiled=True
        )
        result = final(
            hc_static,
            streams,
            first,
            first_at,
            second,
            second_at,
            others,
            own,
            chunk * CHUNK,
            result,
        )
    return result


def solution(mesh):
    in_specs = (
        P("blk", None, "mp"),
        P(("blk", "mp"), None, None),
        P("mp", None),
        P(),
        P("blk"),
        P("blk"),
    )
    out_specs = P("blk", None, "mp")
    return jax.shard_map(body, mesh=mesh, in_specs=in_specs, out_specs=out_specs, check_vma=False)
```

```python
import functools

import jax
import jax.numpy as jnp
from jax import lax
from jax.experimental import pallas as pl
from jax.experimental.pallas import tpu as pltpu
from jax.sharding import PartitionSpec as P

D = 2048
HEAD_DIM = 128
BLOCK = 512
CHUNK = 256
SUB = 64
STREAMS = 4
EPS = 1e-05
BF = jnp.bfloat16
F32 = jnp.float32


def passed_along(value, axis, steps):
    count = lax.axis_size(axis)
    first, last = (max(0, -steps), min(count, count - steps))
    return lax.ppermute(value, axis, [(source, source + steps) for source in range(first, last)])


def from_others(value, axis):
    count = lax.axis_size(axis)
    return [
        lax.ppermute(value, axis, [(source, (source + step) % count) for source in range(count)])
        for step in range(1, count)
    ]


def cost(flops, nbytes, transcendentals=0):
    return pl.CostEstimate(flops=flops, bytes_accessed=nbytes, transcendentals=transcendentals)


def params(limit=60):
    return pltpu.CompilerParams(vmem_limit_bytes=limit << 20)


def split(value, parts):
    out = []
    for _ in range(parts):
        part = value.astype(BF)
        out.append(part)
        value = value - part.astype(F32)
    return out


def contract(a, b, a_dim, b_dim):
    return lax.dot_general(a, b, (((a_dim,), (b_dim,)), ((), ())), preferred_element_type=F32)


def iotas(rows, cols):
    return (
        lax.broadcasted_iota(jnp.int32, (rows, cols), 0),
        lax.broadcasted_iota(jnp.int32, (rows, cols), 1),
    )


def regroup_kernel(place_ref, master_ref, *parts):
    servers = len(parts)
    width = master_ref.shape[-1] // servers
    for step, part_ref in enumerate(parts):
        server = (place_ref[0] + step) % servers
        own = pl.ds(pl.multiple_of(server * width, width), width)
        pair = pl.ds(pl.multiple_of((server // 2) * 2 * width, 2 * width), 2 * width)
        for slot in range(3):
            part_ref[:, slot * width : (slot + 1) * width] = master_ref[:, slot, own].astype(BF)
        part_ref[:, 3 * width :] = master_ref[:, 3, pair].astype(BF)


def regroup(place, master, servers):
    rows, _, total = master.shape
    columns = 5 * total // servers
    return pl.pallas_call(
        regroup_kernel,
        in_specs=[pl.BlockSpec(memory_space=pltpu.SMEM), pl.BlockSpec(memory_space=pltpu.VMEM)],
        out_specs=[pl.BlockSpec(memory_space=pltpu.VMEM)] * servers,
        out_shape=[jax.ShapeDtypeStruct((rows, columns), BF)] * servers,
        cost_estimate=cost(0, rows * total * 26),
        compiler_params=params(),
        name="regroup",
    )(place, master)


def assemble_kernel(place_ref, *refs):
    out_ref = refs[-1]
    parts = refs[:-1]
    rows = parts[0].shape[0]
    for step, part_ref in enumerate(parts):
        source = (place_ref[0] + len(parts) - step) % len(parts)
        out_ref[pl.ds(pl.multiple_of(source * rows, rows), rows), :] = part_ref[...]


def assemble(place, parts):
    rows, columns = parts[0].shape
    return pl.pallas_call(
        assemble_kernel,
        in_specs=[pl.BlockSpec(memory_space=pltpu.SMEM)]
        + [pl.BlockSpec(memory_space=pltpu.VMEM)] * len(parts),
        out_specs=pl.BlockSpec(memory_space=pltpu.VMEM),
        out_shape=jax.ShapeDtypeStruct((rows * len(parts), columns), BF),
        cost_estimate=cost(0, rows * columns * len(parts) * 4),
        compiler_params=params(),
        name="assemble",
    )(place, *parts)


def swapped(value, axis, mask):
    count = lax.axis_size(axis)
    return lax.ppermute(value, axis, [(source, source ^ mask) for source in range(count)])


def weight_pieces(part):
    count = lax.axis_size("blk")
    if count & (count - 1) or part.shape[0] % HEAD_DIM or count > 8:
        return [lax.all_gather(part, "blk", axis=0, tiled=True)]
    pieces = {0: part}
    for mask in range(2, count, 2):
        pieces[mask] = swapped(part, "blk", mask)
    for mask in range(0, count, 2):
        pieces[mask + 1] = swapped(pieces[mask], "blk", 1)
    return [pieces[mask] for mask in range(count)]


def stats_kernel(x_ref, proj_ref, first_ref, second_ref):
    tokens, _, width = x_ref.shape
    proj = proj_ref[...]
    pieces = jnp.concatenate(split(proj, 3), axis=0)
    column = jnp.sum(proj, axis=1, keepdims=True)
    row, col = iotas(4 * SUB, 4 * SUB)
    same = (row >> 2) == (col >> 2)
    ring = jnp.where(same, (row - col) & 3, -1)
    for at in range(tokens // SUB):
        lanes = slice(at * 4 * SUB, (at + 1) * 4 * SUB)
        v = x_ref[at * SUB : (at + 1) * SUB].reshape(4 * SUB, width)
        sums = contract(pieces, v, 1, 1)
        sums = sums[0:8] + sums[8:16] + sums[16:24]
        gram = contract(v, v, 1, 1)
        first_ref[0:1, lanes] = sums[0:1]
        first_ref[1:2, lanes] = sums[6:7]
        for shift in range(3):
            first_ref[2 + shift : 3 + shift, lanes] = jnp.sum(
                jnp.where(ring == shift, gram, 0.0), axis=0, keepdims=True
            )
        first_ref[5:6, lanes] = jnp.broadcast_to(column[0:1], (1, 4 * SUB))
        first_ref[6:8, lanes] = sums[1:3]
        second_ref[0:3, lanes] = sums[3:6]
        second_ref[3:8, lanes] = jnp.broadcast_to(column[1:6], (5, 4 * SUB))


def stats(x, proj, start, tokens, step=128):
    width = x.shape[-1]
    return pl.pallas_call(
        stats_kernel,
        grid=(tokens // step,),
        in_specs=[
            pl.BlockSpec((step, 4, width), lambda i: (start // step + i, 0, 0)),
            pl.BlockSpec((8, width), lambda i: (0, 0)),
        ],
        out_specs=[pl.BlockSpec((8, 4 * step), lambda i: (0, i))] * 2,
        out_shape=[jax.ShapeDtypeStruct((8, 4 * tokens), F32)] * 2,
        cost_estimate=cost(tokens * 4 * width * 600, tokens * 8 * width),
        compiler_params=params(),
        name="stats",
    )(x, proj)


def by_stream(static_ref, column, stream):
    value = jnp.full(stream.shape, static_ref[0, column], F32)
    for k in range(1, 4):
        value = jnp.where(stream == k, static_ref[k, column], value)
    return value


def centre(first):
    mean = first[1:2] * (1.0 / D)
    spread = first[2:3] * (1.0 / D) - mean * mean
    return mean, lax.rsqrt(spread + EPS)


def mix_kernel(static_ref, x_ref, own_ref, a_ref, b_ref, c_ref, sums_ref, normed_ref):
    tokens, _, width = x_ref.shape
    lanes_total = 4 * tokens
    first = (own_ref[...] + a_ref[...]) + (b_ref[...] + c_ref[...])
    sums_ref[...] = first
    mean, inverse = centre(first)
    stream = lax.broadcasted_iota(jnp.int32, (1, lanes_total), 1) & 3
    mix = by_stream(static_ref, 0, stream) + jnp.tanh(
        inverse * (first[0:1] - mean * first[5:6])
    )
    one = jnp.where(stream < 3, pltpu.roll(mix, lanes_total - 1, 1), pltpu.roll(mix, 3, 1))
    two = jnp.where(stream < 2, pltpu.roll(mix, lanes_total - 2, 1), pltpu.roll(mix, 2, 1))
    linear = mix * first[1:2]
    square = mix * (mix * first[2:3] + 2.0 * one * first[3:4] + two * first[4:5])
    row, col = iotas(SUB, 4 * SUB)
    mine = row == (col >> 2)
    for at in range(tokens // SUB):
        lanes = slice(at * 4 * SUB, (at + 1) * 4 * SUB)
        v = x_ref[at * SUB : (at + 1) * SUB].reshape(4 * SUB, width)
        matrix = jnp.where(mine, mix[:, lanes], 0.0)
        mixed = contract(jnp.concatenate(split(matrix, 3), axis=0), v, 1, 0)
        mixed = mixed[0:SUB] + mixed[SUB : 2 * SUB] + mixed[2 * SUB : 3 * SUB]
        average = jnp.sum(jnp.where(mine, linear[:, lanes], 0.0), axis=1, keepdims=True) * (1.0 / D)
        power = jnp.sum(jnp.where(mine, square[:, lanes], 0.0), axis=1, keepdims=True) * (1.0 / D)
        scale = lax.rsqrt(jnp.maximum(power - average * average, 0.0) + EPS)
        normed_ref[at * SUB : (at + 1) * SUB, :] = ((mixed - average) * scale).astype(BF)


def mix(static, x, parts, start, tokens, offset, step=128):
    width = x.shape[-1]
    lane_block = pl.BlockSpec((8, 4 * step), lambda i: (0, offset // step + i))
    return pl.pallas_call(
        mix_kernel,
        grid=(tokens // step,),
        in_specs=[
            pl.BlockSpec(memory_space=pltpu.SMEM),
            pl.BlockSpec((step, 4, width), lambda i: (start // step + i, 0, 0)),
        ]
        + [lane_block] * 4,
        out_specs=[
            pl.BlockSpec((8, 4 * step), lambda i: (0, i)),
            pl.BlockSpec((step, width), lambda i: (i, 0)),
        ],
        out_shape=[
            jax.ShapeDtypeStruct((8, 4 * tokens), F32),
            jax.ShapeDtypeStruct((tokens, width), BF),
        ],
        cost_estimate=cost(tokens * 4 * width * 400, tokens * 10 * width),
        compiler_params=params(),
        name="mix",
    )(static, x, *parts)


def qkv_kernel(ring_ref, rows_ref, cosine_ref, sine_ref, *refs):
    out_ref = refs[-1]
    pieces = refs[:-1]
    servers, _, width = rows_ref.shape
    depth = pieces[0].shape[0]
    if len(pieces) == 1:
        left = [rows_ref[server] for server in range(servers)]
    else:
        left = []
        for piece in range(len(pieces)):
            source = ring_ref[0] ^ piece
            inside = pl.multiple_of((source % (width // depth)) * depth, depth)
            left.append(rows_ref[source // (width // depth), :, pl.ds(inside, depth)])
    left = jnp.concatenate(left, axis=1)
    right = jnp.concatenate([piece[...] for piece in pieces], axis=0)
    total = contract(left, right, 1, 0)
    slot = pl.program_id(0)

    @pl.when(slot < 2)
    def _():
        cosine, sine = cosine_ref[...], sine_ref[...]
        for head in range(total.shape[1] // HEAD_DIM):
            part = total[:, head * HEAD_DIM : (head + 1) * HEAD_DIM]
            turned = part * cosine + pltpu.roll(part, HEAD_DIM // 2, 1) * sine
            out_ref[0, :, head * HEAD_DIM : (head + 1) * HEAD_DIM] = turned.astype(BF)

    @pl.when(slot == 2)
    def _():
        out_ref[0] = total.astype(BF)


def qkv_columns(ring, rows, pieces, cosine, sine, start):
    servers, tokens, width = rows.shape
    table = pl.BlockSpec((tokens, HEAD_DIM), lambda j: (start // tokens, 0))
    return pl.pallas_call(
        qkv_kernel,
        grid=(3,),
        in_specs=[
            pl.BlockSpec(memory_space=pltpu.SMEM),
            pl.BlockSpec((servers, tokens, width), lambda j: (0, 0, 0)),
            table,
            table,
        ]
        + [pl.BlockSpec((pieces[0].shape[0], width), lambda j: (0, j))] * len(pieces),
        out_specs=pl.BlockSpec((1, tokens, width), lambda j: (j, 0, 0)),
        out_shape=jax.ShapeDtypeStruct((3, tokens, width), BF),
        cost_estimate=cost(2 * tokens * D * 3 * width, D * 6 * width + tokens * D * 5),
        compiler_params=params(),
        name="qkv",
    )(ring, rows, cosine, sine, *pieces)


def attend_kernel(q_ref, k0, k1, k2, v0, v1, v2, qseg_ref, kseg_ref, attended_ref):
    tokens, width = q_ref.shape[1:]
    window = kseg_ref.shape[-1]
    row, col = iotas(tokens, window)
    allowed = (qseg_ref[...] == kseg_ref[0]) & (col - (window - tokens) <= row)
    bias = jnp.where(allowed, 0.0, -1e30)
    factor = 1.4426950408889634 / HEAD_DIM**0.5
    for head in range(width // HEAD_DIM):
        lanes = slice(head * HEAD_DIM, (head + 1) * HEAD_DIM)
        query = q_ref[0, :, lanes]
        scores = jnp.concatenate(
            [contract(query, k[0, :, lanes], 1, 1) for k in (k0, k1, k2)], axis=1
        )
        scores = scores + bias
        weights = jnp.exp2((scores - jnp.max(scores, axis=1, keepdims=True)) * factor)
        total = jnp.sum(weights, axis=1, keepdims=True)
        values = jnp.concatenate([v[0, :, lanes] for v in (v0, v1, v2)], axis=0)
        attended_ref[:, lanes] = (contract(weights.astype(BF), values, 1, 0) / total).astype(BF)


def attend(query, window, qseg, kseg, chunk):
    source, at = query
    width = source.shape[-1]
    block = (1, CHUNK, width)
    keys = [pl.BlockSpec(block, lambda i, s=slot, r=where: (s, r, 0)) for _, slot, where in window]
    values = [
        pl.BlockSpec(block, lambda i, s=slot + 1, r=where: (s, r, 0)) for _, slot, where in window
    ]
    arrays = [array for array, _, _ in window]
    reach = kseg.shape[-1]
    return pl.pallas_call(
        attend_kernel,
        grid=(1,),
        in_specs=[pl.BlockSpec(block, lambda i: (0, at, 0))]
        + keys
        + values
        + [
            pl.BlockSpec((CHUNK, 1), lambda i: (chunk, 0)),
            pl.BlockSpec((1, 1, reach), lambda i: (chunk, 0, 0)),
        ],
        out_specs=pl.BlockSpec((CHUNK, width), lambda i: (0, 0)),
        out_shape=jax.ShapeDtypeStruct((CHUNK, width), BF),
        cost_estimate=cost(4 * CHUNK * reach * width, CHUNK * width * 16, CHUNK * reach * 4),
        compiler_params=params(),
        name="attend",
    )(source, *arrays, *arrays, qseg, kseg)


def project_kernel(place_ref, ring_ref, own_ref, other_ref, *refs):
    pieces = refs[:-4]
    kept_ref, inner_ref, outer_ref, sums = refs[-4:]
    servers, _, width = sums.shape
    place = place_ref[0]
    even = place % 2 == 0
    own, other = own_ref[...], other_ref[...]
    both = jnp.concatenate([jnp.where(even, own, other), jnp.where(even, other, own)], axis=1)
    depth = pieces[0].shape[0]
    if len(pieces) == 1:
        for server in range(servers):
            rows = pieces[0][server * width : (server + 1) * width, :]
            sums[server] = contract(both, rows, 1, 1)
    else:
        for piece in range(len(pieces)):
            target = ring_ref[0] ^ piece
            inside = pl.multiple_of((target % (width // depth)) * depth, depth)
            sums[target // (width // depth), :, pl.ds(inside, depth)] = contract(
                both, pieces[piece][...], 1, 1
            )
    kept_ref[...] = sums[place]
    low = place < 2
    inner_ref[...] = sums[jnp.where(low, 2, 1)].astype(BF)
    outer_ref[...] = sums[jnp.where(low, 3, 0)].astype(BF)


def project(place, ring, own, other, pieces, servers):
    tokens, width = own.shape
    rows, columns = pieces[0].shape
    pair = 2 * width
    tail = pl.BlockSpec((pl.Element(rows), pl.Element(pair)), lambda i: (0, columns - pair))
    full = pl.BlockSpec((tokens, width), lambda i: (0, 0))
    return pl.pallas_call(
        project_kernel,
        grid=(1,),
        in_specs=[pl.BlockSpec(memory_space=pltpu.SMEM)] * 2 + [full] * 2 + [tail] * len(pieces),
        out_specs=[full] * 3,
        out_shape=[
            jax.ShapeDtypeStruct((tokens, width), F32),
            jax.ShapeDtypeStruct((tokens, width), BF),
            jax.ShapeDtypeStruct((tokens, width), BF),
        ],
        scratch_shapes=[pltpu.VMEM((servers, tokens, width), F32)],
        cost_estimate=cost(2 * tokens * D * pair, D * pair * 2 + tokens * width * 12),
        compiler_params=params(),
        name="project",
    )(place, ring, own, other, *pieces)


def final_kernel(
    static_ref, x_ref, first_ref, own2_ref, a_ref, b_ref, c_ref, own_ref, inner_ref, outer_ref, *rest
):
    new_ref = rest[-1]
    tokens, _, width = x_ref.shape
    first = first_ref[...]
    second = (own2_ref[...] + a_ref[...]) + (b_ref[...] + c_ref[...])
    mean, inverse = centre(first)
    stream = lax.broadcasted_iota(jnp.int32, (1, 4 * tokens), 1) & 3

    def coefficient(column, projected):
        dynamic = jnp.tanh(inverse * (projected - mean * second[2 + column : 3 + column]))
        return by_stream(static_ref, column, stream) + dynamic

    projected = [first[6:7], first[7:8], second[0:1], second[1:2], second[2:3]]
    columns = [coefficient(1 + j, projected[j]) for j in range(5)]
    residual = jnp.concatenate(columns[:4] + columns[:4], axis=0)
    row, col = iotas(4 * SUB, 4 * SUB)
    same = (row >> 2) == (col >> 2)
    row, col = iotas(SUB, 4 * SUB)
    mine = row == (col >> 2)
    for at in range(tokens // SUB):
        lanes = slice(at * 4 * SUB, (at + 1) * 4 * SUB)
        rows = slice(at * SUB, (at + 1) * SUB)
        v = x_ref[rows].reshape(4 * SUB, width)
        matrix = jnp.where(same, jnp.tile(residual[:, lanes], (SUB // 2, 1)), 0.0)
        high, low = split(matrix, 2)
        new = contract(high, v, 1, 0) + contract(low, v, 1, 0)
        sent = inner_ref[rows, :].astype(F32) + outer_ref[rows, :].astype(F32)
        update = own_ref[rows, :] + sent
        update_high, update_low = split(update, 2)
        spread_high, spread_low = split(jnp.where(mine, columns[4][:, lanes], 0.0), 2)
        new += contract(
            jnp.concatenate([spread_high, spread_high, spread_low], axis=0),
            jnp.concatenate([update_high, update_low, update_high], axis=0),
            0,
            0,
        )
        new_ref[rows] = new.astype(BF).reshape(SUB, 4, width)


def final(static, x, first, first_at, second, second_at, updates, start, previous, step=128):
    tokens, width = updates[0].shape
    lane_block = pl.BlockSpec((8, 4 * step), lambda i: (0, second_at // step + i))
    stream_block = pl.BlockSpec((step, 4, width), lambda i: (start // step + i, 0, 0))
    specs = [
        pl.BlockSpec(memory_space=pltpu.SMEM),
        stream_block,
        pl.BlockSpec((8, 4 * step), lambda i: (0, first_at // step + i)),
    ]
    specs += [lane_block] * 4
    specs += [pl.BlockSpec((step, width), lambda i: (i, 0))] * 3
    args = [static, x, first, *second, *updates]
    aliases = {}
    if previous is not None:
        specs.append(pl.BlockSpec(memory_space=pl.ANY))
        aliases = {len(args): 0}
        args.append(previous)
    return pl.pallas_call(
        final_kernel,
        grid=(tokens // step,),
        in_specs=specs,
        out_specs=stream_block,
        out_shape=jax.ShapeDtypeStruct(x.shape, BF),
        input_output_aliases=aliases,
        cost_estimate=cost(tokens * 4 * width * 1200, tokens * 22 * width),
        compiler_params=params(),
        name="final",
    )(*args)


def body(streams, proj_master, hc_proj, hc_static, segment_ids, block_mask):
    tokens_local, _, width = streams.shape
    group_size = lax.axis_size("mp")
    place = lax.axis_index("mp").astype(jnp.int32).reshape(1)
    ring = lax.axis_index("blk").astype(jnp.int32).reshape(1)

    proj_rows = jnp.concatenate(
        [hc_proj.T, jnp.ones((1, width), F32), jnp.zeros((1, width), F32)], axis=0
    )
    first_late, second_late = stats(streams, proj_rows, BLOCK, BLOCK)
    late = [first_late] + from_others(first_late, "mp")
    parts = list(regroup(place, proj_master, group_size))
    first_early, second_early = stats(streams, proj_rows, 0, BLOCK)
    early = [first_early] + from_others(first_early, "mp")

    for step in range(1, group_size):
        parts[step] = lax.ppermute(
            parts[step], "mp", [(at, (at + step) % group_size) for at in range(group_size)]
        )
    pieces = weight_pieces(assemble(place, parts))

    def gathered(normed):
        rows = lax.all_gather(normed, "mp", axis=0, tiled=True)
        return rows.reshape(group_size, normed.shape[0], width)

    sums_late, normed_late = mix(hc_static, streams, late, BLOCK, BLOCK, 0)
    rows_late = gathered(normed_late)
    sums_early, normed_early = mix(hc_static, streams, early, 0, BLOCK, 0)
    rows_early = gathered(normed_early)
    second_late = [second_late] + from_others(second_late, "mp")
    second_early = [second_early] + from_others(second_early, "mp")

    halo = passed_along(segment_ids[-BLOCK:], "blk", 1)
    halo = jnp.where(lax.axis_index("blk") == 0, -1, halo)
    extended = jnp.concatenate([halo, segment_ids])
    key_at = jnp.arange(tokens_local + BLOCK, dtype=jnp.int32)[None, :]
    query_at = jnp.arange(tokens_local, dtype=jnp.int32)[:, None] + BLOCK
    earlier = (extended[None, :] == segment_ids[:, None]) & (key_at < query_at)
    positions = jnp.sum(earlier.astype(jnp.int32), axis=1)
    half = HEAD_DIM // 2
    inverse = 10000.0 ** (-(jnp.arange(half, dtype=F32) * 2.0 / HEAD_DIM))
    angles = positions.astype(F32)[:, None] * inverse[None, :]
    cosine, sine = jnp.cos(angles), jnp.sin(angles)
    cosine = jnp.concatenate([cosine, cosine], axis=1)
    sine = jnp.concatenate([-sine, sine], axis=1)
    windows = []
    for block in range(tokens_local // BLOCK):
        before = extended[block * BLOCK : (block + 1) * BLOCK]
        before = jnp.where(block_mask[block] == 1, before, -1)
        seen = jnp.concatenate([before, segment_ids[block * BLOCK : (block + 1) * BLOCK]])
        for chunk in range(BLOCK // CHUNK):
            windows.append(seen[chunk * CHUNK : chunk * CHUNK + BLOCK + CHUNK])
    key_segments = jnp.stack(windows)[:, None, :]
    query_segments = segment_ids[:, None]

    qkv_late = qkv_columns(ring, rows_late, pieces, cosine, sine, BLOCK)
    halo_rows = passed_along(qkv_late[1:3], "blk", 1)
    qkv_early = qkv_columns(ring, rows_early, pieces, cosine, sine, 0)

    chunks = [(halo_rows, 0, 0), (halo_rows, 0, 1), (qkv_early, 1, 0), (qkv_early, 1, 1)]
    chunks += [(qkv_late, 1, 0), (qkv_late, 1, 1)]
    order = [
        (2, sums_late, second_late, 0),
        (3, sums_late, second_late, CHUNK),
        (0, sums_early, second_early, 0),
        (1, sums_early, second_early, CHUNK),
    ]
    result = None
    for chunk, first, second, lanes_at in order:
        source, _, at = chunks[chunk + 2]
        window = chunks[chunk : chunk + 3]
        own = attend((source, at), window, query_segments, key_segments, chunk)
        kept, inner, outer = project(place, ring, own, swapped(own, "mp", 1), pieces, group_size)
        inner = lax.ppermute(inner, "mp", [(1, 2), (2, 1)])
        outer = lax.ppermute(outer, "mp", [(1, 3), (2, 0)])
        result = final(
            hc_static,
            streams,
            first,
            lanes_at,
            second,
            lanes_at,
            [kept, inner, outer],
            chunk * CHUNK,
            result,
        )
    return result


def solution(mesh):
    in_specs = (
        P("blk", None, "mp"),
        P(("blk", "mp"), None, None),
        P("mp", None),
        P(),
        P("blk"),
        P("blk"),
    )
    out_specs = P("blk", None, "mp")
    return jax.shard_map(body, mesh=mesh, in_specs=in_specs, out_specs=out_specs, check_vma=False)
```

```python
import functools

import jax
import jax.numpy as jnp
from jax import lax
from jax.experimental import pallas as pl
from jax.experimental.pallas import tpu as pltpu
from jax.sharding import PartitionSpec as P

D = 2048
HEAD_DIM = 128
BLOCK = 512
CHUNK = 256
SUB = 64
STREAMS = 4
EPS = 1e-05
BF = jnp.bfloat16
F32 = jnp.float32


def passed_along(value, axis, steps):
    count = lax.axis_size(axis)
    first, last = (max(0, -steps), min(count, count - steps))
    return lax.ppermute(value, axis, [(source, source + steps) for source in range(first, last)])


def from_others(value, axis):
    count = lax.axis_size(axis)
    return [
        lax.ppermute(value, axis, [(source, (source + step) % count) for source in range(count)])
        for step in range(1, count)
    ]


def cost(flops, nbytes, transcendentals=0):
    return pl.CostEstimate(flops=flops, bytes_accessed=nbytes, transcendentals=transcendentals)


def params(limit=60):
    return pltpu.CompilerParams(vmem_limit_bytes=limit << 20)


def split(value, parts):
    out = []
    for _ in range(parts):
        part = value.astype(BF)
        out.append(part)
        value = value - part.astype(F32)
    return out


def contract(a, b, a_dim, b_dim):
    return lax.dot_general(a, b, (((a_dim,), (b_dim,)), ((), ())), preferred_element_type=F32)


def iotas(rows, cols):
    return (
        lax.broadcasted_iota(jnp.int32, (rows, cols), 0),
        lax.broadcasted_iota(jnp.int32, (rows, cols), 1),
    )


def regroup_kernel(place_ref, master_ref, *parts):
    servers = len(parts)
    width = master_ref.shape[-1] // servers
    for step, part_ref in enumerate(parts):
        server = (place_ref[0] + step) % servers
        own = pl.ds(pl.multiple_of(server * width, width), width)
        pair = pl.ds(pl.multiple_of((server // 2) * 2 * width, 2 * width), 2 * width)
        for slot in range(3):
            part_ref[:, slot * width : (slot + 1) * width] = master_ref[:, slot, own].astype(BF)
        part_ref[:, 3 * width :] = master_ref[:, 3, pair].astype(BF)


def regroup(place, master, servers):
    rows, _, total = master.shape
    columns = 5 * total // servers
    return pl.pallas_call(
        regroup_kernel,
        in_specs=[pl.BlockSpec(memory_space=pltpu.SMEM), pl.BlockSpec(memory_space=pltpu.VMEM)],
        out_specs=[pl.BlockSpec(memory_space=pltpu.VMEM)] * servers,
        out_shape=[jax.ShapeDtypeStruct((rows, columns), BF)] * servers,
        cost_estimate=cost(0, rows * total * 26),
        compiler_params=params(),
        name="regroup",
    )(place, master)


def assemble_kernel(place_ref, *refs):
    out_ref = refs[-1]
    parts = refs[:-1]
    rows = parts[0].shape[0]
    for step, part_ref in enumerate(parts):
        source = (place_ref[0] + len(parts) - step) % len(parts)
        out_ref[pl.ds(pl.multiple_of(source * rows, rows), rows), :] = part_ref[...]


def assemble(place, parts):
    rows, columns = parts[0].shape
    return pl.pallas_call(
        assemble_kernel,
        in_specs=[pl.BlockSpec(memory_space=pltpu.SMEM)]
        + [pl.BlockSpec(memory_space=pltpu.VMEM)] * len(parts),
        out_specs=pl.BlockSpec(memory_space=pltpu.VMEM),
        out_shape=jax.ShapeDtypeStruct((rows * len(parts), columns), BF),
        cost_estimate=cost(0, rows * columns * len(parts) * 4),
        compiler_params=params(),
        name="assemble",
    )(place, *parts)


def swapped(value, axis, mask):
    count = lax.axis_size(axis)
    return lax.ppermute(value, axis, [(source, source ^ mask) for source in range(count)])


def weight_pieces(part):
    count = lax.axis_size("blk")
    if count & (count - 1) or part.shape[0] % HEAD_DIM or count > 8:
        return [lax.all_gather(part, "blk", axis=0, tiled=True)]
    pieces = {0: part}
    for mask in range(2, count, 2):
        pieces[mask] = swapped(part, "blk", mask)
    for mask in range(0, count, 2):
        pieces[mask + 1] = swapped(pieces[mask], "blk", 1)
    return [pieces[mask] for mask in range(count)]


def stats_kernel(x_ref, proj_ref, first_ref, second_ref):
    tokens, _, width = x_ref.shape
    proj = proj_ref[...]
    pieces = jnp.concatenate(split(proj, 3), axis=0)
    column = jnp.sum(proj, axis=1, keepdims=True)
    row, col = iotas(4 * SUB, 4 * SUB)
    same = (row >> 2) == (col >> 2)
    ring = jnp.where(same, (row - col) & 3, -1)
    for at in range(tokens // SUB):
        lanes = slice(at * 4 * SUB, (at + 1) * 4 * SUB)
        v = x_ref[at * SUB : (at + 1) * SUB].reshape(4 * SUB, width)
        sums = contract(pieces, v, 1, 1)
        sums = sums[0:8] + sums[8:16] + sums[16:24]
        gram = contract(v, v, 1, 1)
        first_ref[0:1, lanes] = sums[0:1]
        first_ref[1:2, lanes] = sums[6:7]
        for shift in range(3):
            first_ref[2 + shift : 3 + shift, lanes] = jnp.sum(
                jnp.where(ring == shift, gram, 0.0), axis=0, keepdims=True
            )
        first_ref[5:6, lanes] = jnp.broadcast_to(column[0:1], (1, 4 * SUB))
        first_ref[6:8, lanes] = sums[1:3]
        second_ref[0:3, lanes] = sums[3:6]
        second_ref[3:8, lanes] = jnp.broadcast_to(column[1:6], (5, 4 * SUB))


def stats(x, proj, start, tokens, step=128):
    width = x.shape[-1]
    return pl.pallas_call(
        stats_kernel,
        grid=(tokens // step,),
        in_specs=[
            pl.BlockSpec((step, 4, width), lambda i: (start // step + i, 0, 0)),
            pl.BlockSpec((8, width), lambda i: (0, 0)),
        ],
        out_specs=[pl.BlockSpec((8, 4 * step), lambda i: (0, i))] * 2,
        out_shape=[jax.ShapeDtypeStruct((8, 4 * tokens), F32)] * 2,
        cost_estimate=cost(tokens * 4 * width * 600, tokens * 8 * width),
        compiler_params=params(),
        name="stats",
    )(x, proj)


def by_stream(static_ref, column, stream):
    value = jnp.full(stream.shape, static_ref[0, column], F32)
    for k in range(1, 4):
        value = jnp.where(stream == k, static_ref[k, column], value)
    return value


def centre(first):
    mean = first[1:2] * (1.0 / D)
    spread = first[2:3] * (1.0 / D) - mean * mean
    return mean, lax.rsqrt(spread + EPS)


def mix_kernel(static_ref, x_ref, own_ref, a_ref, b_ref, c_ref, sums_ref, normed_ref):
    tokens, _, width = x_ref.shape
    lanes_total = 4 * tokens
    first = (own_ref[...] + a_ref[...]) + (b_ref[...] + c_ref[...])
    sums_ref[...] = first
    mean, inverse = centre(first)
    stream = lax.broadcasted_iota(jnp.int32, (1, lanes_total), 1) & 3
    mix = by_stream(static_ref, 0, stream) + jnp.tanh(
        inverse * (first[0:1] - mean * first[5:6])
    )
    one = jnp.where(stream < 3, pltpu.roll(mix, lanes_total - 1, 1), pltpu.roll(mix, 3, 1))
    two = jnp.where(stream < 2, pltpu.roll(mix, lanes_total - 2, 1), pltpu.roll(mix, 2, 1))
    linear = mix * first[1:2]
    square = mix * (mix * first[2:3] + 2.0 * one * first[3:4] + two * first[4:5])
    row, col = iotas(SUB, 4 * SUB)
    mine = row == (col >> 2)
    for at in range(tokens // SUB):
        lanes = slice(at * 4 * SUB, (at + 1) * 4 * SUB)
        v = x_ref[at * SUB : (at + 1) * SUB].reshape(4 * SUB, width)
        matrix = jnp.where(mine, mix[:, lanes], 0.0)
        mixed = contract(jnp.concatenate(split(matrix, 3), axis=0), v, 1, 0)
        mixed = mixed[0:SUB] + mixed[SUB : 2 * SUB] + mixed[2 * SUB : 3 * SUB]
        average = jnp.sum(jnp.where(mine, linear[:, lanes], 0.0), axis=1, keepdims=True) * (1.0 / D)
        power = jnp.sum(jnp.where(mine, square[:, lanes], 0.0), axis=1, keepdims=True) * (1.0 / D)
        scale = lax.rsqrt(jnp.maximum(power - average * average, 0.0) + EPS)
        normed_ref[at * SUB : (at + 1) * SUB, :] = ((mixed - average) * scale).astype(BF)


def mix(static, x, parts, start, tokens, offset, step=128):
    width = x.shape[-1]
    lane_block = pl.BlockSpec((8, 4 * step), lambda i: (0, offset // step + i))
    return pl.pallas_call(
        mix_kernel,
        grid=(tokens // step,),
        in_specs=[
            pl.BlockSpec(memory_space=pltpu.SMEM),
            pl.BlockSpec((step, 4, width), lambda i: (start // step + i, 0, 0)),
        ]
        + [lane_block] * 4,
        out_specs=[
            pl.BlockSpec((8, 4 * step), lambda i: (0, i)),
            pl.BlockSpec((step, width), lambda i: (i, 0)),
        ],
        out_shape=[
            jax.ShapeDtypeStruct((8, 4 * tokens), F32),
            jax.ShapeDtypeStruct((tokens, width), BF),
        ],
        cost_estimate=cost(tokens * 4 * width * 400, tokens * 10 * width),
        compiler_params=params(),
        name="mix",
    )(static, x, *parts)


def qkv_kernel(ring_ref, rows_ref, cosine_ref, sine_ref, *refs):
    out_ref = refs[-1]
    pieces = refs[:-1]
    servers, _, width = rows_ref.shape
    depth = pieces[0].shape[0]
    if len(pieces) == 1:
        left = [rows_ref[server] for server in range(servers)]
    else:
        left = []
        for piece in range(len(pieces)):
            source = ring_ref[0] ^ piece
            inside = pl.multiple_of((source % (width // depth)) * depth, depth)
            left.append(rows_ref[source // (width // depth), :, pl.ds(inside, depth)])
    left = jnp.concatenate(left, axis=1)
    right = jnp.concatenate([piece[...] for piece in pieces], axis=0)
    total = contract(left, right, 1, 0)
    slot = pl.program_id(0)

    @pl.when(slot < 2)
    def _():
        cosine, sine = cosine_ref[...], sine_ref[...]
        for head in range(total.shape[1] // HEAD_DIM):
            part = total[:, head * HEAD_DIM : (head + 1) * HEAD_DIM]
            turned = part * cosine + pltpu.roll(part, HEAD_DIM // 2, 1) * sine
            out_ref[0, :, head * HEAD_DIM : (head + 1) * HEAD_DIM] = turned.astype(BF)

    @pl.when(slot == 2)
    def _():
        out_ref[0] = total.astype(BF)


def qkv_columns(ring, rows, pieces, cosine, sine, start):
    servers, tokens, width = rows.shape
    table = pl.BlockSpec((tokens, HEAD_DIM), lambda j: (start // tokens, 0))
    return pl.pallas_call(
        qkv_kernel,
        grid=(3,),
        in_specs=[
            pl.BlockSpec(memory_space=pltpu.SMEM),
            pl.BlockSpec((servers, tokens, width), lambda j: (0, 0, 0)),
            table,
            table,
        ]
        + [pl.BlockSpec((pieces[0].shape[0], width), lambda j: (0, j))] * len(pieces),
        out_specs=pl.BlockSpec((1, tokens, width), lambda j: (j, 0, 0)),
        out_shape=jax.ShapeDtypeStruct((3, tokens, width), BF),
        cost_estimate=cost(2 * tokens * D * 3 * width, D * 6 * width + tokens * D * 5),
        compiler_params=params(),
        name="qkv",
    )(ring, rows, cosine, sine, *pieces)


def attend_kernel(q_ref, k0, k1, k2, v0, v1, v2, qseg_ref, kseg_ref, attended_ref):
    tokens, width = q_ref.shape[1:]
    window = kseg_ref.shape[-1]
    row, col = iotas(tokens, window)
    allowed = (qseg_ref[...] == kseg_ref[0]) & (col - (window - tokens) <= row)
    bias = jnp.where(allowed, 0.0, -1e30)
    factor = 1.4426950408889634 / HEAD_DIM**0.5
    for head in range(width // HEAD_DIM):
        lanes = slice(head * HEAD_DIM, (head + 1) * HEAD_DIM)
        query = q_ref[0, :, lanes]
        scores = jnp.concatenate(
            [contract(query, k[0, :, lanes], 1, 1) for k in (k0, k1, k2)], axis=1
        )
        scores = scores + bias
        weights = jnp.exp2((scores - jnp.max(scores, axis=1, keepdims=True)) * factor)
        total = jnp.sum(weights, axis=1, keepdims=True)
        values = jnp.concatenate([v[0, :, lanes] for v in (v0, v1, v2)], axis=0)
        attended_ref[:, lanes] = (contract(weights.astype(BF), values, 1, 0) / total).astype(BF)


def attend(query, window, qseg, kseg, chunk):
    source, at = query
    width = source.shape[-1]
    block = (1, CHUNK, width)
    keys = [pl.BlockSpec(block, lambda i, s=slot, r=where: (s, r, 0)) for _, slot, where in window]
    values = [
        pl.BlockSpec(block, lambda i, s=slot + 1, r=where: (s, r, 0)) for _, slot, where in window
    ]
    arrays = [array for array, _, _ in window]
    reach = kseg.shape[-1]
    return pl.pallas_call(
        attend_kernel,
        grid=(1,),
        in_specs=[pl.BlockSpec(block, lambda i: (0, at, 0))]
        + keys
        + values
        + [
            pl.BlockSpec((CHUNK, 1), lambda i: (chunk, 0)),
            pl.BlockSpec((1, 1, reach), lambda i: (chunk, 0, 0)),
        ],
        out_specs=pl.BlockSpec((CHUNK, width), lambda i: (0, 0)),
        out_shape=jax.ShapeDtypeStruct((CHUNK, width), BF),
        cost_estimate=cost(4 * CHUNK * reach * width, CHUNK * width * 16, CHUNK * reach * 4),
        compiler_params=params(),
        name="attend",
    )(source, *arrays, *arrays, qseg, kseg)


def project_kernel(place_ref, ring_ref, own_ref, other_ref, *refs):
    pieces = refs[:-6]
    kept_ref, inner_ref, outer_ref, sums, held, arrived = refs[-6:]
    servers, _, width = sums.shape
    depth, pair = held.shape[1:]
    copies = []
    for at, piece in enumerate(pieces):
        start = piece.shape[1] - pair
        copies.append(
            pltpu.make_async_copy(piece.at[:, start : start + pair], held.at[at], arrived.at[at])
        )
        copies[-1].start()
    place = place_ref[0]
    even = place % 2 == 0
    own, other = own_ref[...], other_ref[...]
    both = jnp.concatenate([jnp.where(even, own, other), jnp.where(even, other, own)], axis=1)
    for at, copy in enumerate(copies):
        copy.wait()
        if len(pieces) == 1:
            for server in range(servers):
                rows = held[0, server * width : (server + 1) * width, :]
                sums[server] = contract(both, rows, 1, 1)
        else:
            target = ring_ref[0] ^ at
            inside = pl.multiple_of((target % (width // depth)) * depth, depth)
            sums[target // (width // depth), :, pl.ds(inside, depth)] = contract(
                both, held[at], 1, 1
            )
    kept_ref[...] = sums[place]
    low = place < 2
    inner_ref[...] = sums[jnp.where(low, 2, 1)].astype(BF)
    outer_ref[...] = sums[jnp.where(low, 3, 0)].astype(BF)


def project(place, ring, own, other, pieces, servers):
    tokens, width = own.shape
    rows = pieces[0].shape[0]
    pair = 2 * width
    full = pl.BlockSpec(memory_space=pltpu.VMEM)
    return pl.pallas_call(
        project_kernel,
        in_specs=[pl.BlockSpec(memory_space=pltpu.SMEM)] * 2
        + [full] * 2
        + [pl.BlockSpec(memory_space=pl.ANY)] * len(pieces),
        out_specs=[full] * 3,
        out_shape=[
            jax.ShapeDtypeStruct((tokens, width), F32),
            jax.ShapeDtypeStruct((tokens, width), BF),
            jax.ShapeDtypeStruct((tokens, width), BF),
        ],
        scratch_shapes=[
            pltpu.VMEM((servers, tokens, width), F32),
            pltpu.VMEM((len(pieces), rows, pair), BF),
            pltpu.SemaphoreType.DMA((len(pieces),)),
        ],
        cost_estimate=cost(2 * tokens * D * pair, D * pair * 2 + tokens * width * 12),
        compiler_params=params(),
        name="project",
    )(place, ring, own, other, *pieces)


def final_kernel(
    static_ref, x_ref, first_ref, own2_ref, a_ref, b_ref, c_ref, own_ref, inner_ref, outer_ref, *rest
):
    new_ref = rest[-1]
    tokens, _, width = x_ref.shape
    first = first_ref[...]
    second = (own2_ref[...] + a_ref[...]) + (b_ref[...] + c_ref[...])
    mean, inverse = centre(first)
    stream = lax.broadcasted_iota(jnp.int32, (1, 4 * tokens), 1) & 3

    def coefficient(column, projected):
        dynamic = jnp.tanh(inverse * (projected - mean * second[2 + column : 3 + column]))
        return by_stream(static_ref, column, stream) + dynamic

    projected = [first[6:7], first[7:8], second[0:1], second[1:2], second[2:3]]
    columns = [coefficient(1 + j, projected[j]) for j in range(5)]
    residual = jnp.concatenate(columns[:4] + columns[:4], axis=0)
    row, col = iotas(4 * SUB, 4 * SUB)
    same = (row >> 2) == (col >> 2)
    row, col = iotas(SUB, 4 * SUB)
    mine = row == (col >> 2)
    for at in range(tokens // SUB):
        lanes = slice(at * 4 * SUB, (at + 1) * 4 * SUB)
        rows = slice(at * SUB, (at + 1) * SUB)
        v = x_ref[rows].reshape(4 * SUB, width)
        matrix = jnp.where(same, jnp.tile(residual[:, lanes], (SUB // 2, 1)), 0.0)
        high, low = split(matrix, 2)
        new = contract(high, v, 1, 0) + contract(low, v, 1, 0)
        sent = inner_ref[rows, :].astype(F32) + outer_ref[rows, :].astype(F32)
        update = own_ref[rows, :] + sent
        update_high, update_low = split(update, 2)
        spread_high, spread_low = split(jnp.where(mine, columns[4][:, lanes], 0.0), 2)
        new += contract(
            jnp.concatenate([spread_high, spread_high, spread_low], axis=0),
            jnp.concatenate([update_high, update_low, update_high], axis=0),
            0,
            0,
        )
        new_ref[rows] = new.astype(BF).reshape(SUB, 4, width)


def final(static, x, first, first_at, second, second_at, updates, start, previous, step=128):
    tokens, width = updates[0].shape
    lane_block = pl.BlockSpec((8, 4 * step), lambda i: (0, second_at // step + i))
    stream_block = pl.BlockSpec((step, 4, width), lambda i: (start // step + i, 0, 0))
    specs = [
        pl.BlockSpec(memory_space=pltpu.SMEM),
        stream_block,
        pl.BlockSpec((8, 4 * step), lambda i: (0, first_at // step + i)),
    ]
    specs += [lane_block] * 4
    specs += [pl.BlockSpec((step, width), lambda i: (i, 0))] * 3
    args = [static, x, first, *second, *updates]
    aliases = {}
    if previous is not None:
        specs.append(pl.BlockSpec(memory_space=pl.ANY))
        aliases = {len(args): 0}
        args.append(previous)
    return pl.pallas_call(
        final_kernel,
        grid=(tokens // step,),
        in_specs=specs,
        out_specs=stream_block,
        out_shape=jax.ShapeDtypeStruct(x.shape, BF),
        input_output_aliases=aliases,
        cost_estimate=cost(tokens * 4 * width * 1200, tokens * 22 * width),
        compiler_params=params(),
        name="final",
    )(*args)


def body(streams, proj_master, hc_proj, hc_static, segment_ids, block_mask):
    tokens_local, _, width = streams.shape
    group_size = lax.axis_size("mp")
    place = lax.axis_index("mp").astype(jnp.int32).reshape(1)
    ring = lax.axis_index("blk").astype(jnp.int32).reshape(1)

    proj_rows = jnp.concatenate(
        [hc_proj.T, jnp.ones((1, width), F32), jnp.zeros((1, width), F32)], axis=0
    )
    first_late, second_late = stats(streams, proj_rows, BLOCK, BLOCK)
    late = from_others(first_late, "mp")
    parts = list(regroup(place, proj_master, group_size))
    first_early, second_early = stats(streams, proj_rows, 0, BLOCK)
    late, parts, first_early = lax.optimization_barrier((late, parts, first_early))
    early = from_others(first_early, "mp")
    for step in range(1, group_size):
        parts[step] = lax.ppermute(
            parts[step], "mp", [(at, (at + step) % group_size) for at in range(group_size)]
        )

    def gathered(normed):
        rows = lax.all_gather(normed, "mp", axis=0, tiled=True)
        return rows.reshape(group_size, normed.shape[0], width)

    sums_late, normed_late = mix(hc_static, streams, [first_late] + late, BLOCK, BLOCK, 0)
    rows_late = gathered(normed_late)
    sums_early, normed_early = mix(hc_static, streams, [first_early] + early, 0, BLOCK, 0)

    parts, normed_early = lax.optimization_barrier((parts, normed_early))
    rows_early = gathered(normed_early)
    pieces = weight_pieces(assemble(place, parts))
    second_late = [second_late] + from_others(second_late, "mp")
    second_early = [second_early] + from_others(second_early, "mp")
    rows_late, second_late, second_early = lax.optimization_barrier(
        (rows_late, second_late, second_early)
    )

    halo = passed_along(segment_ids[-BLOCK:], "blk", 1)
    halo = jnp.where(lax.axis_index("blk") == 0, -1, halo)
    extended = jnp.concatenate([halo, segment_ids])
    key_at = jnp.arange(tokens_local + BLOCK, dtype=jnp.int32)[None, :]
    query_at = jnp.arange(tokens_local, dtype=jnp.int32)[:, None] + BLOCK
    earlier = (extended[None, :] == segment_ids[:, None]) & (key_at < query_at)
    positions = jnp.sum(earlier.astype(jnp.int32), axis=1)
    half = HEAD_DIM // 2
    inverse = 10000.0 ** (-(jnp.arange(half, dtype=F32) * 2.0 / HEAD_DIM))
    angles = positions.astype(F32)[:, None] * inverse[None, :]
    cosine, sine = jnp.cos(angles), jnp.sin(angles)
    cosine = jnp.concatenate([cosine, cosine], axis=1)
    sine = jnp.concatenate([-sine, sine], axis=1)
    windows = []
    for block in range(tokens_local // BLOCK):
        before = extended[block * BLOCK : (block + 1) * BLOCK]
        before = jnp.where(block_mask[block] == 1, before, -1)
        seen = jnp.concatenate([before, segment_ids[block * BLOCK : (block + 1) * BLOCK]])
        for chunk in range(BLOCK // CHUNK):
            windows.append(seen[chunk * CHUNK : chunk * CHUNK + BLOCK + CHUNK])
    key_segments = jnp.stack(windows)[:, None, :]
    query_segments = segment_ids[:, None]

    qkv_late = qkv_columns(ring, rows_late, pieces, cosine, sine, BLOCK)
    halo_rows = passed_along(qkv_late[1:3], "blk", 1)
    qkv_early = qkv_columns(ring, rows_early, pieces, cosine, sine, 0)

    chunks = [(halo_rows, 0, 0), (halo_rows, 0, 1), (qkv_early, 1, 0), (qkv_early, 1, 1)]
    chunks += [(qkv_late, 1, 0), (qkv_late, 1, 1)]
    order = [
        (2, sums_late, second_late, 0),
        (3, sums_late, second_late, CHUNK),
        (0, sums_early, second_early, 0),
        (1, sums_early, second_early, CHUNK),
    ]
    result = None
    for chunk, first, second, lanes_at in order:
        source, _, at = chunks[chunk + 2]
        window = chunks[chunk : chunk + 3]
        own = attend((source, at), window, query_segments, key_segments, chunk)
        kept, inner, outer = project(place, ring, own, swapped(own, "mp", 1), pieces, group_size)
        inner = lax.ppermute(inner, "mp", [(1, 2), (2, 1)])
        outer = lax.ppermute(outer, "mp", [(1, 3), (2, 0)])
        result = final(
            hc_static,
            streams,
            first,
            lanes_at,
            second,
            lanes_at,
            [kept, inner, outer],
            chunk * CHUNK,
            result,
        )
    return result


def solution(mesh):
    in_specs = (
        P("blk", None, "mp"),
        P(("blk", "mp"), None, None),
        P("mp", None),
        P(),
        P("blk"),
        P("blk"),
    )
    out_specs = P("blk", None, "mp")
    return jax.shard_map(body, mesh=mesh, in_specs=in_specs, out_specs=out_specs, check_vma=False)
```

```python
import functools

import jax
import jax.numpy as jnp
from jax import lax
from jax.experimental import pallas as pl
from jax.experimental.pallas import tpu as pltpu
from jax.sharding import PartitionSpec as P

D = 2048
HEAD_DIM = 128
BLOCK = 512
CHUNK = 256
SUB = 64
STEP = 128
STREAMS = 4
EPS = 1e-05
BF = jnp.bfloat16
F32 = jnp.float32


def passed_along(value, axis, steps):
    count = lax.axis_size(axis)
    first, last = (max(0, -steps), min(count, count - steps))
    return lax.ppermute(value, axis, [(source, source + steps) for source in range(first, last)])


def from_others(value, axis):
    count = lax.axis_size(axis)
    return [
        lax.ppermute(value, axis, [(source, (source + step) % count) for source in range(count)])
        for step in range(1, count)
    ]


def cost(flops, nbytes, transcendentals=0):
    return pl.CostEstimate(flops=flops, bytes_accessed=nbytes, transcendentals=transcendentals)


def params(limit=60):
    return pltpu.CompilerParams(vmem_limit_bytes=limit << 20)


def split(value, parts):
    out = []
    for _ in range(parts):
        part = value.astype(BF)
        out.append(part)
        value = value - part.astype(F32)
    return out


def contract(a, b, a_dim, b_dim):
    return lax.dot_general(a, b, (((a_dim,), (b_dim,)), ((), ())), preferred_element_type=F32)


def iotas(rows, cols):
    return (
        lax.broadcasted_iota(jnp.int32, (rows, cols), 0),
        lax.broadcasted_iota(jnp.int32, (rows, cols), 1),
    )


def regroup_kernel(place_ref, master_ref, *parts):
    servers = len(parts) // 2
    width = master_ref.shape[-1] // servers
    for step in range(servers):
        server = (place_ref[0] + step) % servers
        own = pl.ds(pl.multiple_of(server * width, width), width)
        pair = pl.ds(pl.multiple_of((server // 2) * 2 * width, 2 * width), 2 * width)
        for slot in range(3):
            parts[step][:, slot * width : (slot + 1) * width] = master_ref[:, slot, own].astype(BF)
        parts[servers + step][...] = master_ref[:, 3, pair].astype(BF)


def regroup(place, master, servers):
    rows, _, total = master.shape
    width = total // servers
    parts = pl.pallas_call(
        regroup_kernel,
        in_specs=[pl.BlockSpec(memory_space=pltpu.SMEM), pl.BlockSpec(memory_space=pltpu.VMEM)],
        out_specs=[pl.BlockSpec(memory_space=pltpu.VMEM)] * (2 * servers),
        out_shape=[jax.ShapeDtypeStruct((rows, 3 * width), BF)] * servers
        + [jax.ShapeDtypeStruct((rows, 2 * width), BF)] * servers,
        cost_estimate=cost(0, rows * total * 26),
        compiler_params=params(),
        name="regroup",
    )(place, master)
    return list(parts[:servers]), list(parts[servers:])


def assemble_kernel(place_ref, *refs):
    out_ref = refs[-1]
    parts = refs[:-1]
    rows = parts[0].shape[0]
    for step, part_ref in enumerate(parts):
        source = (place_ref[0] + len(parts) - step) % len(parts)
        out_ref[pl.ds(pl.multiple_of(source * rows, rows), rows), :] = part_ref[...]


def assemble(place, parts):
    rows, columns = parts[0].shape
    return pl.pallas_call(
        assemble_kernel,
        in_specs=[pl.BlockSpec(memory_space=pltpu.SMEM)]
        + [pl.BlockSpec(memory_space=pltpu.VMEM)] * len(parts),
        out_specs=pl.BlockSpec(memory_space=pltpu.VMEM),
        out_shape=jax.ShapeDtypeStruct((rows * len(parts), columns), BF),
        cost_estimate=cost(0, rows * columns * len(parts) * 4),
        compiler_params=params(),
        name="assemble",
    )(place, *parts)


def swapped(value, axis, mask):
    count = lax.axis_size(axis)
    return lax.ppermute(value, axis, [(source, source ^ mask) for source in range(count)])


def weight_pieces(part):
    count = lax.axis_size("blk")
    if count & (count - 1) or part.shape[0] % HEAD_DIM or count > 8:
        return [lax.all_gather(part, "blk", axis=0, tiled=True)]
    pieces = {0: part}
    for mask in range(2, count, 2):
        pieces[mask] = swapped(part, "blk", mask)
    for mask in range(0, count, 2):
        pieces[mask + 1] = swapped(pieces[mask], "blk", 1)
    return [pieces[mask] for mask in range(count)]


def stats_kernel(x_ref, proj_ref, out_ref):
    block, _, width = x_ref.shape
    tokens = block * pl.num_programs(0)
    base = pl.program_id(0) * (block // STEP)
    proj = proj_ref[...]
    pieces = jnp.concatenate(split(proj, 3), axis=0)
    out_ref[:, out_ref.shape[1] - 128 :] = jnp.broadcast_to(jnp.sum(proj, axis=1, keepdims=True), (8, 128))
    row, col = iotas(4 * SUB, 4 * SUB)
    same = (row >> 2) == (col >> 2)
    ring = jnp.where(same, (row - col) & 3, -1)

    @pl.loop(0, block // STEP)
    def _(local):
        step = base + local
        folded = []
        for half in range(STEP // SUB):
            lanes = pl.ds(pl.multiple_of(step * 4 * STEP, 4 * STEP) + half * 4 * SUB, 4 * SUB)
            v = x_ref[pl.ds(local * STEP + half * SUB, SUB)].reshape(4 * SUB, width)
            sums = contract(pieces, v, 1, 1)
            sums = sums[0:8] + sums[8:16] + sums[16:24]
            gram = contract(v, v, 1, 1)
            out_ref[0:1, lanes] = sums[0:1]
            out_ref[1:2, lanes] = sums[6:7]
            for shift in range(3):
                out_ref[2 + shift : 3 + shift, lanes] = jnp.sum(
                    jnp.where(ring == shift, gram, 0.0), axis=0, keepdims=True
                )
            out_ref[5:8, lanes] = sums[1:4]
            folded.append(sums[4:6])
        folded = jnp.concatenate(folded, axis=1)
        lanes = pl.ds(pl.multiple_of(4 * tokens + step * STEP, STEP), STEP)
        for part in range(4):
            for which in range(2):
                out_ref[4 * which + part : 4 * which + part + 1, lanes] = folded[
                    which : which + 1, part * STEP : (part + 1) * STEP
                ]


def stats(x, proj):
    tokens, _, width = x.shape
    lanes = 5 * tokens + 128
    return pl.pallas_call(
        stats_kernel,
        grid=(tokens // (2 * STEP),),
        in_specs=[
            pl.BlockSpec((2 * STEP, 4, width), lambda i: (i, 0, 0)),
            pl.BlockSpec((8, width), lambda i: (0, 0)),
        ],
        out_specs=pl.BlockSpec((8, lanes), lambda i: (0, 0)),
        out_shape=jax.ShapeDtypeStruct((8, lanes), F32),
        cost_estimate=cost(tokens * 4 * width * 600, tokens * 8 * width),
        compiler_params=params(),
        name="stats",
    )(x, proj)


def by_stream(static_ref, column, stream):
    value = jnp.full(stream.shape, static_ref[0, column], F32)
    for k in range(1, 4):
        value = jnp.where(stream == k, static_ref[k, column], value)
    return value


def centre(first):
    mean = first[1:2] * (1.0 / D)
    spread = first[2:3] * (1.0 / D) - mean * mean
    return mean, lax.rsqrt(spread + EPS)


def mix_kernel(offset, static_ref, x_ref, own_ref, a_ref, b_ref, c_ref, sums_ref, normed_ref):
    tokens, _, width = x_ref.shape
    sums_ref[...] = (own_ref[...] + a_ref[...]) + (b_ref[...] + c_ref[...])
    last = sums_ref.shape[1] - 128
    column = sums_ref[0:1, last : last + 1]
    stream = lax.broadcasted_iota(jnp.int32, (1, 4 * STEP), 1) & 3
    static = by_stream(static_ref, 0, stream)
    row, col = iotas(SUB, 4 * SUB)
    mine = row == (col >> 2)

    @pl.loop(0, tokens // STEP)
    def _(step):
        at = pl.multiple_of(4 * offset + step * 4 * STEP, 4 * STEP)
        first = sums_ref[:, pl.ds(at, 4 * STEP)]
        mean, inverse = centre(first)
        mix = static + jnp.tanh(inverse * (first[0:1] - mean * column))
        one = jnp.where(stream < 3, pltpu.roll(mix, 4 * STEP - 1, 1), pltpu.roll(mix, 3, 1))
        two = jnp.where(stream < 2, pltpu.roll(mix, 4 * STEP - 2, 1), pltpu.roll(mix, 2, 1))
        linear = mix * first[1:2]
        square = mix * (mix * first[2:3] + 2.0 * one * first[3:4] + two * first[4:5])
        for half in range(STEP // SUB):
            lanes = slice(half * 4 * SUB, (half + 1) * 4 * SUB)
            rows = pl.ds(step * STEP + half * SUB, SUB)
            v = x_ref[rows].reshape(4 * SUB, width)
            matrix = jnp.where(mine, mix[:, lanes], 0.0)
            mixed = contract(jnp.concatenate(split(matrix, 3), axis=0), v, 1, 0)
            mixed = mixed[0:SUB] + mixed[SUB : 2 * SUB] + mixed[2 * SUB : 3 * SUB]
            average = jnp.sum(jnp.where(mine, linear[:, lanes], 0.0), axis=1, keepdims=True)
            power = jnp.sum(jnp.where(mine, square[:, lanes], 0.0), axis=1, keepdims=True)
            average, power = average * (1.0 / D), power * (1.0 / D)
            scale = lax.rsqrt(jnp.maximum(power - average * average, 0.0) + EPS)
            normed_ref[rows, :] = ((mixed - average) * scale).astype(BF)


def mix(static, x, parts, start, tokens):
    width = x.shape[-1]
    lanes = parts[0].shape[1]
    whole = pl.BlockSpec((8, lanes), lambda i: (0, 0))
    return pl.pallas_call(
        functools.partial(mix_kernel, start),
        grid=(1,),
        in_specs=[
            pl.BlockSpec(memory_space=pltpu.SMEM),
            pl.BlockSpec((tokens, 4, width), lambda i: (start // tokens, 0, 0)),
        ]
        + [whole] * 4,
        out_specs=[whole, pl.BlockSpec((tokens, width), lambda i: (0, 0))],
        out_shape=[
            jax.ShapeDtypeStruct((8, lanes), F32),
            jax.ShapeDtypeStruct((tokens, width), BF),
        ],
        cost_estimate=cost(tokens * 4 * width * 400, tokens * 10 * width),
        compiler_params=params(),
        name="mix",
    )(static, x, *parts)


def qkv_kernel(ring_ref, rows_ref, cosine_ref, sine_ref, *refs):
    out_ref = refs[-1]
    pieces = refs[:-1]
    servers, _, width = rows_ref.shape
    depth = pieces[0].shape[0]
    if len(pieces) == 1:
        left = [rows_ref[server] for server in range(servers)]
    else:
        left = []
        for piece in range(len(pieces)):
            source = ring_ref[0] ^ piece
            inside = pl.multiple_of((source % (width // depth)) * depth, depth)
            left.append(rows_ref[source // (width // depth), :, pl.ds(inside, depth)])
    left = jnp.concatenate(left, axis=1)
    right = jnp.concatenate([piece[...] for piece in pieces], axis=0)
    total = contract(left, right, 1, 0)
    slot = pl.program_id(0)

    @pl.when(slot < 2)
    def _():
        cosine, sine = cosine_ref[...], sine_ref[...]
        for head in range(total.shape[1] // HEAD_DIM):
            part = total[:, head * HEAD_DIM : (head + 1) * HEAD_DIM]
            turned = part * cosine + pltpu.roll(part, HEAD_DIM // 2, 1) * sine
            out_ref[0, :, head * HEAD_DIM : (head + 1) * HEAD_DIM] = turned.astype(BF)

    @pl.when(slot == 2)
    def _():
        out_ref[0] = total.astype(BF)


def qkv_columns(ring, rows, pieces, cosine, sine, start):
    servers, tokens, width = rows.shape
    table = pl.BlockSpec((tokens, HEAD_DIM), lambda j: (start // tokens, 0))
    return pl.pallas_call(
        qkv_kernel,
        grid=(3,),
        in_specs=[
            pl.BlockSpec(memory_space=pltpu.SMEM),
            pl.BlockSpec((servers, tokens, width), lambda j: (0, 0, 0)),
            table,
            table,
        ]
        + [pl.BlockSpec((pieces[0].shape[0], width), lambda j: (0, j))] * len(pieces),
        out_specs=pl.BlockSpec((1, tokens, width), lambda j: (j, 0, 0)),
        out_shape=jax.ShapeDtypeStruct((3, tokens, width), BF),
        cost_estimate=cost(2 * tokens * D * 3 * width, D * 6 * width + tokens * D * 5),
        compiler_params=params(),
        name="qkv",
    )(ring, rows, cosine, sine, *pieces)


def attend_kernel(q_ref, k0, k1, k2, v0, v1, v2, qseg_ref, kseg_ref, attended_ref):
    tokens, width = q_ref.shape[1:]
    window = kseg_ref.shape[-1]
    row, col = iotas(tokens, window)
    allowed = (qseg_ref[...] == kseg_ref[0]) & (col - (window - tokens) <= row)
    bias = jnp.where(allowed, 0.0, -1e30)
    factor = 1.4426950408889634 / HEAD_DIM**0.5
    for head in range(width // HEAD_DIM):
        lanes = slice(head * HEAD_DIM, (head + 1) * HEAD_DIM)
        query = q_ref[0, :, lanes]
        scores = jnp.concatenate(
            [contract(query, k[0, :, lanes], 1, 1) for k in (k0, k1, k2)], axis=1
        )
        scores = scores + bias
        weights = jnp.exp2((scores - jnp.max(scores, axis=1, keepdims=True)) * factor)
        total = jnp.sum(weights, axis=1, keepdims=True)
        values = jnp.concatenate([v[0, :, lanes] for v in (v0, v1, v2)], axis=0)
        attended_ref[:, lanes] = (contract(weights.astype(BF), values, 1, 0) / total).astype(BF)


def attend(query, window, qseg, kseg, chunk):
    source, at = query
    width = source.shape[-1]
    block = (1, CHUNK, width)
    keys = [pl.BlockSpec(block, lambda i, s=slot, r=where: (s, r, 0)) for _, slot, where in window]
    values = [
        pl.BlockSpec(block, lambda i, s=slot + 1, r=where: (s, r, 0)) for _, slot, where in window
    ]
    arrays = [array for array, _, _ in window]
    reach = kseg.shape[-1]
    return pl.pallas_call(
        attend_kernel,
        grid=(1,),
        in_specs=[pl.BlockSpec(block, lambda i: (0, at, 0))]
        + keys
        + values
        + [
            pl.BlockSpec((CHUNK, 1), lambda i: (chunk, 0)),
            pl.BlockSpec((1, 1, reach), lambda i: (chunk, 0, 0)),
        ],
        out_specs=pl.BlockSpec((CHUNK, width), lambda i: (0, 0)),
        out_shape=jax.ShapeDtypeStruct((CHUNK, width), BF),
        cost_estimate=cost(4 * CHUNK * reach * width, CHUNK * width * 16, CHUNK * reach * 4),
        compiler_params=params(),
        name="attend",
    )(source, *arrays, *arrays, qseg, kseg)


def project_kernel(place_ref, ring_ref, own_ref, other_ref, *refs):
    pieces = refs[:-4]
    kept_ref, inner_ref, outer_ref, sums = refs[-4:]
    servers, _, width = sums.shape
    place = place_ref[0]
    even = place % 2 == 0
    own, other = own_ref[...], other_ref[...]
    both = jnp.concatenate([jnp.where(even, own, other), jnp.where(even, other, own)], axis=1)
    depth = pieces[0].shape[0]
    if len(pieces) == 1:
        for server in range(servers):
            rows = pieces[0][server * width : (server + 1) * width, :]
            sums[server] = contract(both, rows, 1, 1)
    else:
        for piece in range(len(pieces)):
            target = ring_ref[0] ^ piece
            inside = pl.multiple_of((target % (width // depth)) * depth, depth)
            sums[target // (width // depth), :, pl.ds(inside, depth)] = contract(
                both, pieces[piece][...], 1, 1
            )
    kept_ref[...] = sums[place]
    low = place < 2
    inner_ref[...] = sums[jnp.where(low, 2, 1)].astype(BF)
    outer_ref[...] = sums[jnp.where(low, 3, 0)].astype(BF)


def project(place, ring, own, other, pieces, servers):
    tokens, width = own.shape
    rows, pair = pieces[0].shape
    tail = pl.BlockSpec((rows, pair), lambda i: (0, 0))
    full = pl.BlockSpec((tokens, width), lambda i: (0, 0))
    return pl.pallas_call(
        project_kernel,
        grid=(1,),
        in_specs=[pl.BlockSpec(memory_space=pltpu.SMEM)] * 2 + [full] * 2 + [tail] * len(pieces),
        out_specs=[full] * 3,
        out_shape=[
            jax.ShapeDtypeStruct((tokens, width), F32),
            jax.ShapeDtypeStruct((tokens, width), BF),
            jax.ShapeDtypeStruct((tokens, width), BF),
        ],
        scratch_shapes=[pltpu.VMEM((servers, tokens, width), F32)],
        cost_estimate=cost(2 * tokens * D * pair, D * pair * 2 + tokens * width * 12),
        compiler_params=params(),
        name="project",
    )(place, ring, own, other, *pieces)


def final_kernel(
    static_ref, x_ref, first_ref, folded_ref, column_ref, own_ref, inner_ref, outer_ref, *rest
):
    new_ref = rest[-1]
    tokens, _, width = x_ref.shape
    first = first_ref[...]
    mean, inverse = centre(first)
    stream = lax.broadcasted_iota(jnp.int32, (1, 4 * tokens), 1) & 3

    def coefficient(column, projected):
        dynamic = jnp.tanh(inverse * (projected - mean * column_ref[column : column + 1, 0:1]))
        return by_stream(static_ref, column, stream) + dynamic

    def unfolded(which):
        return jnp.concatenate(
            [folded_ref[4 * which + part : 4 * which + part + 1] for part in range(4)], axis=1
        )

    projected = [first[5:6], first[6:7], first[7:8], unfolded(0), unfolded(1)]
    columns = [coefficient(1 + j, projected[j]) for j in range(5)]
    residual = jnp.concatenate(columns[:4] + columns[:4], axis=0)
    row, col = iotas(4 * SUB, 4 * SUB)
    same = (row >> 2) == (col >> 2)
    row, col = iotas(SUB, 4 * SUB)
    mine = row == (col >> 2)
    for at in range(tokens // SUB):
        lanes = slice(at * 4 * SUB, (at + 1) * 4 * SUB)
        rows = slice(at * SUB, (at + 1) * SUB)
        v = x_ref[rows].reshape(4 * SUB, width)
        matrix = jnp.where(same, jnp.tile(residual[:, lanes], (SUB // 2, 1)), 0.0)
        high, low = split(matrix, 2)
        new = contract(high, v, 1, 0) + contract(low, v, 1, 0)
        sent = inner_ref[rows, :].astype(F32) + outer_ref[rows, :].astype(F32)
        update_high, update_low = split(own_ref[rows, :] + sent, 2)
        spread_high, spread_low = split(jnp.where(mine, columns[4][:, lanes], 0.0), 2)
        new += contract(
            jnp.concatenate([spread_high, spread_high, spread_low], axis=0),
            jnp.concatenate([update_high, update_low, update_high], axis=0),
            0,
            0,
        )
        new_ref[rows] = new.astype(BF).reshape(SUB, 4, width)


def final(static, x, sums, updates, start, previous):
    tokens, width = updates[0].shape
    group = (sums.shape[1] - 128) // 5
    stream_block = pl.BlockSpec((STEP, 4, width), lambda i: (start // STEP + i, 0, 0))
    specs = [
        pl.BlockSpec(memory_space=pltpu.SMEM),
        stream_block,
        pl.BlockSpec((8, 4 * STEP), lambda i: (0, start // STEP + i)),
        pl.BlockSpec((8, STEP), lambda i: (0, 4 * group // STEP + start // STEP + i)),
        pl.BlockSpec((8, 128), lambda i: (0, 5 * group // 128)),
    ]
    specs += [pl.BlockSpec((STEP, width), lambda i: (i, 0))] * 3
    args = [static, x, sums, sums, sums, *updates]
    aliases = {}
    if previous is not None:
        specs.append(pl.BlockSpec(memory_space=pl.ANY))
        aliases = {len(args): 0}
        args.append(previous)
    return pl.pallas_call(
        final_kernel,
        grid=(tokens // STEP,),
        in_specs=specs,
        out_specs=stream_block,
        out_shape=jax.ShapeDtypeStruct(x.shape, BF),
        input_output_aliases=aliases,
        cost_estimate=cost(tokens * 4 * width * 1200, tokens * 22 * width),
        compiler_params=params(),
        name="final",
    )(*args)


def body(streams, proj_master, hc_proj, hc_static, segment_ids, block_mask):
    tokens_local, _, width = streams.shape
    group_size = lax.axis_size("mp")
    place = lax.axis_index("mp").astype(jnp.int32).reshape(1)
    ring = lax.axis_index("blk").astype(jnp.int32).reshape(1)

    proj_rows = jnp.concatenate(
        [hc_proj.T, jnp.ones((1, width), F32), jnp.zeros((1, width), F32)], axis=0
    )
    own = stats(streams, proj_rows)
    qkv_parts, out_parts = regroup(place, proj_master, group_size)
    sums, qkv_parts = lax.optimization_barrier(([own] + from_others(own, "mp"), qkv_parts))

    def gathered(normed):
        rows = lax.all_gather(normed, "mp", axis=0, tiled=True)
        return rows.reshape(group_size, normed.shape[0], width)

    sums_late, normed_late = mix(hc_static, streams, sums, BLOCK, BLOCK)
    rows_late = gathered(normed_late)
    _, normed_early = mix(hc_static, streams, sums, 0, BLOCK)
    rows_early = gathered(normed_early)

    def served(parts):
        for step in range(1, group_size):
            parts[step] = lax.ppermute(
                parts[step], "mp", [(at, (at + step) % group_size) for at in range(group_size)]
            )
        return assemble(place, parts)

    qkv_part = served(qkv_parts)
    qkv_part, out_parts, normed_early = lax.optimization_barrier((qkv_part, out_parts, normed_early))
    qkv_pieces = weight_pieces(qkv_part)
    out_pieces = weight_pieces(served(out_parts))

    halo = passed_along(segment_ids[-BLOCK:], "blk", 1)
    halo = jnp.where(lax.axis_index("blk") == 0, -1, halo)
    extended = jnp.concatenate([halo, segment_ids])
    key_at = jnp.arange(tokens_local + BLOCK, dtype=jnp.int32)[None, :]
    query_at = jnp.arange(tokens_local, dtype=jnp.int32)[:, None] + BLOCK
    earlier = (extended[None, :] == segment_ids[:, None]) & (key_at < query_at)
    positions = jnp.sum(earlier.astype(jnp.int32), axis=1)
    half = HEAD_DIM // 2
    inverse = 10000.0 ** (-(jnp.arange(half, dtype=F32) * 2.0 / HEAD_DIM))
    angles = positions.astype(F32)[:, None] * inverse[None, :]
    cosine, sine = jnp.cos(angles), jnp.sin(angles)
    cosine = jnp.concatenate([cosine, cosine], axis=1)
    sine = jnp.concatenate([-sine, sine], axis=1)
    windows = []
    for block in range(tokens_local // BLOCK):
        before = extended[block * BLOCK : (block + 1) * BLOCK]
        before = jnp.where(block_mask[block] == 1, before, -1)
        seen = jnp.concatenate([before, segment_ids[block * BLOCK : (block + 1) * BLOCK]])
        for chunk in range(BLOCK // CHUNK):
            windows.append(seen[chunk * CHUNK : chunk * CHUNK + BLOCK + CHUNK])
    key_segments = jnp.stack(windows)[:, None, :]
    query_segments = segment_ids[:, None]

    qkv_late = qkv_columns(ring, rows_late, qkv_pieces, cosine, sine, BLOCK)
    halo_rows = passed_along(qkv_late[1:3], "blk", 1)
    qkv_early = qkv_columns(ring, rows_early, qkv_pieces, cosine, sine, 0)

    chunks = [(halo_rows, 0, 0), (halo_rows, 0, 1), (qkv_early, 1, 0), (qkv_early, 1, 1)]
    chunks += [(qkv_late, 1, 0), (qkv_late, 1, 1)]
    result = None
    for chunk in (2, 3, 0, 1):
        source, _, at = chunks[chunk + 2]
        window = chunks[chunk : chunk + 3]
        attended = attend((source, at), window, query_segments, key_segments, chunk)
        other = swapped(attended, "mp", 1)
        kept, inner, outer = project(place, ring, attended, other, out_pieces, group_size)
        inner = lax.ppermute(inner, "mp", [(1, 2), (2, 1)])
        outer = lax.ppermute(outer, "mp", [(1, 3), (2, 0)])
        updates = [kept, inner, outer]
        result = final(hc_static, streams, sums_late, updates, chunk * CHUNK, result)
    return result


def solution(mesh):
    in_specs = (
        P("blk", None, "mp"),
        P(("blk", "mp"), None, None),
        P("mp", None),
        P(),
        P("blk"),
        P("blk"),
    )
    out_specs = P("blk", None, "mp")
    return jax.shard_map(body, mesh=mesh, in_specs=in_specs, out_specs=out_specs, check_vma=False)
```

```python
import functools

import jax
import jax.numpy as jnp
from jax import lax
from jax.experimental import pallas as pl
from jax.experimental.pallas import tpu as pltpu
from jax.sharding import PartitionSpec as P

D = 2048
HEAD_DIM = 128
BLOCK = 512
CHUNK = 256
SUB = 64
STEP = 128
STREAMS = 4
EPS = 1e-05
BF = jnp.bfloat16
F32 = jnp.float32


def passed_along(value, axis, steps):
    count = lax.axis_size(axis)
    first, last = (max(0, -steps), min(count, count - steps))
    return lax.ppermute(value, axis, [(source, source + steps) for source in range(first, last)])


def from_others(value, axis):
    count = lax.axis_size(axis)
    return [
        lax.ppermute(value, axis, [(source, (source + step) % count) for source in range(count)])
        for step in range(1, count)
    ]


def cost(flops, nbytes, transcendentals=0):
    return pl.CostEstimate(flops=flops, bytes_accessed=nbytes, transcendentals=transcendentals)


def params(limit=60):
    return pltpu.CompilerParams(vmem_limit_bytes=limit << 20)


def split(value, parts):
    out = []
    for _ in range(parts):
        part = value.astype(BF)
        out.append(part)
        value = value - part.astype(F32)
    return out


def contract(a, b, a_dim, b_dim):
    return lax.dot_general(a, b, (((a_dim,), (b_dim,)), ((), ())), preferred_element_type=F32)


def iotas(rows, cols):
    return (
        lax.broadcasted_iota(jnp.int32, (rows, cols), 0),
        lax.broadcasted_iota(jnp.int32, (rows, cols), 1),
    )


def regroup_kernel(place_ref, master_ref, *parts):
    servers = len(parts)
    width = master_ref.shape[-1] // servers
    for step, part_ref in enumerate(parts):
        server = (place_ref[0] + step) % servers
        own = pl.ds(pl.multiple_of(server * width, width), width)
        pair = pl.ds(pl.multiple_of((server // 2) * 2 * width, 2 * width), 2 * width)
        for slot in range(3):
            part_ref[:, slot * width : (slot + 1) * width] = master_ref[:, slot, own].astype(BF)
        part_ref[:, 3 * width :] = master_ref[:, 3, pair].astype(BF)


def regroup(place, master, servers):
    rows, _, total = master.shape
    columns = 5 * total // servers
    return pl.pallas_call(
        regroup_kernel,
        in_specs=[pl.BlockSpec(memory_space=pltpu.SMEM), pl.BlockSpec(memory_space=pltpu.VMEM)],
        out_specs=[pl.BlockSpec(memory_space=pltpu.VMEM)] * servers,
        out_shape=[jax.ShapeDtypeStruct((rows, columns), BF)] * servers,
        cost_estimate=cost(0, rows * total * 26),
        compiler_params=params(),
        name="regroup",
    )(place, master)


def assemble_kernel(place_ref, *refs):
    qkv_ref, out_ref = refs[-2:]
    parts = refs[:-2]
    rows = parts[0].shape[0]
    cut = qkv_ref.shape[1]
    for step, part_ref in enumerate(parts):
        source = (place_ref[0] + len(parts) - step) % len(parts)
        at = pl.ds(pl.multiple_of(source * rows, rows), rows)
        qkv_ref[at, :] = part_ref[:, :cut]
        out_ref[at, :] = part_ref[:, cut:]


def assemble(place, parts):
    rows, columns = parts[0].shape
    rows *= len(parts)
    return pl.pallas_call(
        assemble_kernel,
        in_specs=[pl.BlockSpec(memory_space=pltpu.SMEM)]
        + [pl.BlockSpec(memory_space=pltpu.VMEM)] * len(parts),
        out_specs=[pl.BlockSpec(memory_space=pltpu.VMEM)] * 2,
        out_shape=[
            jax.ShapeDtypeStruct((rows, columns // 5 * 3), BF),
            jax.ShapeDtypeStruct((rows, columns // 5 * 2), BF),
        ],
        cost_estimate=cost(0, rows * columns * 4),
        compiler_params=params(),
        name="assemble",
    )(place, *parts)


def swapped(value, axis, mask):
    count = lax.axis_size(axis)
    return lax.ppermute(value, axis, [(source, source ^ mask) for source in range(count)])


def weight_pieces(part):
    count = lax.axis_size("blk")
    if count & (count - 1) or part.shape[0] % HEAD_DIM or count > 8:
        return [lax.all_gather(part, "blk", axis=0, tiled=True)]
    pieces = {0: part}
    for mask in range(2, count, 2):
        pieces[mask] = swapped(part, "blk", mask)
    for mask in range(0, count, 2):
        pieces[mask + 1] = swapped(pieces[mask], "blk", 1)
    return [pieces[mask] for mask in range(count)]


def stats_kernel(x_ref, proj_ref, out_ref):
    block, _, width = x_ref.shape
    tokens = block * pl.num_programs(0)
    base = pl.program_id(0) * (block // STEP)
    proj = proj_ref[...]
    pieces = jnp.concatenate(split(proj, 3), axis=0)
    out_ref[:, out_ref.shape[1] - 128 :] = jnp.broadcast_to(jnp.sum(proj, axis=1, keepdims=True), (8, 128))
    row, col = iotas(4 * SUB, 4 * SUB)
    same = (row >> 2) == (col >> 2)
    ring = jnp.where(same, (row - col) & 3, -1)

    @pl.loop(0, block // STEP)
    def _(local):
        step = base + local
        folded = []
        for half in range(STEP // SUB):
            lanes = pl.ds(pl.multiple_of(step * 4 * STEP, 4 * STEP) + half * 4 * SUB, 4 * SUB)
            v = x_ref[pl.ds(local * STEP + half * SUB, SUB)].reshape(4 * SUB, width)
            sums = contract(pieces, v, 1, 1)
            sums = sums[0:8] + sums[8:16] + sums[16:24]
            gram = contract(v, v, 1, 1)
            out_ref[0:1, lanes] = sums[0:1]
            out_ref[1:2, lanes] = sums[6:7]
            for shift in range(3):
                out_ref[2 + shift : 3 + shift, lanes] = jnp.sum(
                    jnp.where(ring == shift, gram, 0.0), axis=0, keepdims=True
                )
            out_ref[5:8, lanes] = sums[1:4]
            folded.append(sums[4:6])
        folded = jnp.concatenate(folded, axis=1)
        lanes = pl.ds(pl.multiple_of(4 * tokens + step * STEP, STEP), STEP)
        for part in range(4):
            for which in range(2):
                out_ref[4 * which + part : 4 * which + part + 1, lanes] = folded[
                    which : which + 1, part * STEP : (part + 1) * STEP
                ]


def stats(x, proj):
    tokens, _, width = x.shape
    lanes = 5 * tokens + 128
    return pl.pallas_call(
        stats_kernel,
        grid=(tokens // (2 * STEP),),
        in_specs=[
            pl.BlockSpec((2 * STEP, 4, width), lambda i: (i, 0, 0)),
            pl.BlockSpec((8, width), lambda i: (0, 0)),
        ],
        out_specs=pl.BlockSpec((8, lanes), lambda i: (0, 0)),
        out_shape=jax.ShapeDtypeStruct((8, lanes), F32),
        cost_estimate=cost(tokens * 4 * width * 600, tokens * 8 * width),
        compiler_params=params(),
        name="stats",
    )(x, proj)


def by_stream(static_ref, column, stream):
    value = jnp.full(stream.shape, static_ref[0, column], F32)
    for k in range(1, 4):
        value = jnp.where(stream == k, static_ref[k, column], value)
    return value


def centre(first):
    mean = first[1:2] * (1.0 / D)
    spread = first[2:3] * (1.0 / D) - mean * mean
    return mean, lax.rsqrt(spread + EPS)


def mix_kernel(offset, static_ref, x_ref, own_ref, a_ref, b_ref, c_ref, sums_ref, normed_ref):
    tokens, _, width = x_ref.shape

    @pl.when(pl.program_id(0) == 0)
    def _():
        sums_ref[...] = (own_ref[...] + a_ref[...]) + (b_ref[...] + c_ref[...])

    base = 4 * (offset + pl.program_id(0) * tokens)
    last = sums_ref.shape[1] - 128
    column = sums_ref[0:1, last : last + 1]
    stream = lax.broadcasted_iota(jnp.int32, (1, 4 * STEP), 1) & 3
    static = by_stream(static_ref, 0, stream)
    row, col = iotas(SUB, 4 * SUB)
    mine = row == (col >> 2)

    @pl.loop(0, tokens // STEP)
    def _(step):
        at = pl.multiple_of(base + step * 4 * STEP, 4 * STEP)
        first = sums_ref[:, pl.ds(at, 4 * STEP)]
        mean, inverse = centre(first)
        mix = static + jnp.tanh(inverse * (first[0:1] - mean * column))
        one = jnp.where(stream < 3, pltpu.roll(mix, 4 * STEP - 1, 1), pltpu.roll(mix, 3, 1))
        two = jnp.where(stream < 2, pltpu.roll(mix, 4 * STEP - 2, 1), pltpu.roll(mix, 2, 1))
        linear = mix * first[1:2]
        square = mix * (mix * first[2:3] + 2.0 * one * first[3:4] + two * first[4:5])
        for half in range(STEP // SUB):
            lanes = slice(half * 4 * SUB, (half + 1) * 4 * SUB)
            rows = pl.ds(step * STEP + half * SUB, SUB)
            v = x_ref[rows].reshape(4 * SUB, width)
            matrix = jnp.where(mine, mix[:, lanes], 0.0)
            mixed = contract(jnp.concatenate(split(matrix, 3), axis=0), v, 1, 0)
            mixed = mixed[0:SUB] + mixed[SUB : 2 * SUB] + mixed[2 * SUB : 3 * SUB]
            average = jnp.sum(jnp.where(mine, linear[:, lanes], 0.0), axis=1, keepdims=True)
            power = jnp.sum(jnp.where(mine, square[:, lanes], 0.0), axis=1, keepdims=True)
            average, power = average * (1.0 / D), power * (1.0 / D)
            scale = lax.rsqrt(jnp.maximum(power - average * average, 0.0) + EPS)
            normed_ref[rows, :] = ((mixed - average) * scale).astype(BF)


def mix(static, x, parts, start, tokens):
    width = x.shape[-1]
    lanes = parts[0].shape[1]
    whole = pl.BlockSpec((8, lanes), lambda i: (0, 0))
    return pl.pallas_call(
        functools.partial(mix_kernel, start),
        grid=(tokens // CHUNK,),
        in_specs=[
            pl.BlockSpec(memory_space=pltpu.SMEM),
            pl.BlockSpec((CHUNK, 4, width), lambda i: (start // CHUNK + i, 0, 0)),
        ]
        + [whole] * 4,
        out_specs=[whole, pl.BlockSpec((CHUNK, width), lambda i: (i, 0))],
        out_shape=[
            jax.ShapeDtypeStruct((8, lanes), F32),
            jax.ShapeDtypeStruct((tokens, width), BF),
        ],
        cost_estimate=cost(tokens * 4 * width * 400, tokens * 10 * width),
        compiler_params=params(),
        name="mix",
    )(static, x, *parts)


def qkv_kernel(ring_ref, rows_ref, cosine_ref, sine_ref, *refs):
    out_ref = refs[-1]
    pieces = refs[:-1]
    servers, _, width = rows_ref.shape
    depth = pieces[0].shape[0]
    if len(pieces) == 1:
        left = [rows_ref[server] for server in range(servers)]
    else:
        left = []
        for piece in range(len(pieces)):
            source = ring_ref[0] ^ piece
            inside = pl.multiple_of((source % (width // depth)) * depth, depth)
            left.append(rows_ref[source // (width // depth), :, pl.ds(inside, depth)])
    left = jnp.concatenate(left, axis=1)
    right = jnp.concatenate([piece[...] for piece in pieces], axis=0)
    total = contract(left, right, 1, 0)
    slot = pl.program_id(0)

    @pl.when(slot < 2)
    def _():
        cosine, sine = cosine_ref[...], sine_ref[...]
        for head in range(total.shape[1] // HEAD_DIM):
            part = total[:, head * HEAD_DIM : (head + 1) * HEAD_DIM]
            turned = part * cosine + pltpu.roll(part, HEAD_DIM // 2, 1) * sine
            out_ref[0, :, head * HEAD_DIM : (head + 1) * HEAD_DIM] = turned.astype(BF)

    @pl.when(slot == 2)
    def _():
        out_ref[0] = total.astype(BF)


def qkv_columns(ring, rows, pieces, cosine, sine):
    servers, tokens, width = rows.shape
    table = pl.BlockSpec((tokens, HEAD_DIM), lambda j: (0, 0))
    return pl.pallas_call(
        qkv_kernel,
        grid=(3,),
        in_specs=[
            pl.BlockSpec(memory_space=pltpu.SMEM),
            pl.BlockSpec((servers, tokens, width), lambda j: (0, 0, 0)),
            table,
            table,
        ]
        + [pl.BlockSpec((pieces[0].shape[0], width), lambda j: (0, j))] * len(pieces),
        out_specs=pl.BlockSpec((1, tokens, width), lambda j: (j, 0, 0)),
        out_shape=jax.ShapeDtypeStruct((3, tokens, width), BF),
        cost_estimate=cost(2 * tokens * D * 3 * width, D * 6 * width + tokens * D * 5),
        compiler_params=params(),
        name="qkv",
    )(ring, rows, cosine, sine, *pieces)


def attend_kernel(q_ref, k0, k1, k2, v0, v1, v2, qseg_ref, kseg_ref, attended_ref):
    tokens, width = q_ref.shape[1:]
    window = kseg_ref.shape[-1]
    row, col = iotas(tokens, window)
    allowed = (qseg_ref[...] == kseg_ref[0]) & (col - (window - tokens) <= row)
    bias = jnp.where(allowed, 0.0, -1e30)
    factor = 1.4426950408889634 / HEAD_DIM**0.5
    for head in range(width // HEAD_DIM):
        lanes = slice(head * HEAD_DIM, (head + 1) * HEAD_DIM)
        query = q_ref[0, :, lanes]
        scores = jnp.concatenate(
            [contract(query, k[0, :, lanes], 1, 1) for k in (k0, k1, k2)], axis=1
        )
        scores = scores + bias
        weights = jnp.exp2((scores - jnp.max(scores, axis=1, keepdims=True)) * factor)
        total = jnp.sum(weights, axis=1, keepdims=True)
        values = jnp.concatenate([v[0, :, lanes] for v in (v0, v1, v2)], axis=0)
        attended_ref[:, lanes] = (contract(weights.astype(BF), values, 1, 0) / total).astype(BF)


def attend(query, window, qseg, kseg, chunk):
    source, at = query
    width = source.shape[-1]
    block = (1, CHUNK, width)
    keys = [pl.BlockSpec(block, lambda i, s=slot, r=where: (s, r, 0)) for _, slot, where in window]
    values = [
        pl.BlockSpec(block, lambda i, s=slot + 1, r=where: (s, r, 0)) for _, slot, where in window
    ]
    arrays = [array for array, _, _ in window]
    reach = kseg.shape[-1]
    return pl.pallas_call(
        attend_kernel,
        grid=(1,),
        in_specs=[pl.BlockSpec(block, lambda i: (0, at, 0))]
        + keys
        + values
        + [
            pl.BlockSpec((CHUNK, 1), lambda i: (chunk, 0)),
            pl.BlockSpec((1, 1, reach), lambda i: (chunk, 0, 0)),
        ],
        out_specs=pl.BlockSpec((CHUNK, width), lambda i: (0, 0)),
        out_shape=jax.ShapeDtypeStruct((CHUNK, width), BF),
        cost_estimate=cost(4 * CHUNK * reach * width, CHUNK * width * 16, CHUNK * reach * 4),
        compiler_params=params(),
        name="attend",
    )(source, *arrays, *arrays, qseg, kseg)


def project_kernel(place_ref, ring_ref, own_ref, other_ref, *refs):
    pieces = refs[:-4]
    kept_ref, inner_ref, outer_ref, sums = refs[-4:]
    servers, _, width = sums.shape
    place = place_ref[0]
    even = place % 2 == 0
    own, other = own_ref[...], other_ref[...]
    both = jnp.concatenate([jnp.where(even, own, other), jnp.where(even, other, own)], axis=1)
    depth = pieces[0].shape[0]
    if len(pieces) == 1:
        for server in range(servers):
            rows = pieces[0][server * width : (server + 1) * width, :]
            sums[server] = contract(both, rows, 1, 1)
    else:
        for piece in range(len(pieces)):
            target = ring_ref[0] ^ piece
            inside = pl.multiple_of((target % (width // depth)) * depth, depth)
            sums[target // (width // depth), :, pl.ds(inside, depth)] = contract(
                both, pieces[piece][...], 1, 1
            )
    kept_ref[...] = sums[place]
    low = place < 2
    inner_ref[...] = sums[jnp.where(low, 2, 1)].astype(BF)
    outer_ref[...] = sums[jnp.where(low, 3, 0)].astype(BF)


def project(place, ring, own, other, pieces, servers):
    tokens, width = own.shape
    rows, pair = pieces[0].shape
    tail = pl.BlockSpec((rows, pair), lambda i: (0, 0))
    full = pl.BlockSpec((tokens, width), lambda i: (0, 0))
    return pl.pallas_call(
        project_kernel,
        grid=(1,),
        in_specs=[pl.BlockSpec(memory_space=pltpu.SMEM)] * 2 + [full] * 2 + [tail] * len(pieces),
        out_specs=[full] * 3,
        out_shape=[
            jax.ShapeDtypeStruct((tokens, width), F32),
            jax.ShapeDtypeStruct((tokens, width), BF),
            jax.ShapeDtypeStruct((tokens, width), BF),
        ],
        scratch_shapes=[pltpu.VMEM((servers, tokens, width), F32)],
        cost_estimate=cost(2 * tokens * D * pair, D * pair * 2 + tokens * width * 12),
        compiler_params=params(),
        name="project",
    )(place, ring, own, other, *pieces)


def final_kernel(
    static_ref, x_ref, first_ref, folded_ref, column_ref, own_ref, inner_ref, outer_ref, *rest
):
    new_ref = rest[-1]
    tokens, _, width = x_ref.shape
    first = first_ref[...]
    mean, inverse = centre(first)
    stream = lax.broadcasted_iota(jnp.int32, (1, 4 * tokens), 1) & 3

    def coefficient(column, projected):
        dynamic = jnp.tanh(inverse * (projected - mean * column_ref[column : column + 1, 0:1]))
        return by_stream(static_ref, column, stream) + dynamic

    def unfolded(which):
        return jnp.concatenate(
            [folded_ref[4 * which + part : 4 * which + part + 1] for part in range(4)], axis=1
        )

    projected = [first[5:6], first[6:7], first[7:8], unfolded(0), unfolded(1)]
    columns = [coefficient(1 + j, projected[j]) for j in range(5)]
    residual = jnp.concatenate(columns[:4] + columns[:4], axis=0)
    row, col = iotas(4 * SUB, 4 * SUB)
    same = (row >> 2) == (col >> 2)
    row, col = iotas(SUB, 4 * SUB)
    mine = row == (col >> 2)
    for at in range(tokens // SUB):
        lanes = slice(at * 4 * SUB, (at + 1) * 4 * SUB)
        rows = slice(at * SUB, (at + 1) * SUB)
        v = x_ref[rows].reshape(4 * SUB, width)
        matrix = jnp.where(same, jnp.tile(residual[:, lanes], (SUB // 2, 1)), 0.0)
        high, low = split(matrix, 2)
        new = contract(high, v, 1, 0) + contract(low, v, 1, 0)
        sent = inner_ref[rows, :].astype(F32) + outer_ref[rows, :].astype(F32)
        update_high, update_low = split(own_ref[rows, :] + sent, 2)
        spread_high, spread_low = split(jnp.where(mine, columns[4][:, lanes], 0.0), 2)
        new += contract(
            jnp.concatenate([spread_high, spread_high, spread_low], axis=0),
            jnp.concatenate([update_high, update_low, update_high], axis=0),
            0,
            0,
        )
        new_ref[rows] = new.astype(BF).reshape(SUB, 4, width)


def final(static, x, sums, updates, start, previous):
    tokens, width = updates[0].shape
    group = (sums.shape[1] - 128) // 5
    stream_block = pl.BlockSpec((STEP, 4, width), lambda i: (start // STEP + i, 0, 0))
    specs = [
        pl.BlockSpec(memory_space=pltpu.SMEM),
        stream_block,
        pl.BlockSpec((8, 4 * STEP), lambda i: (0, start // STEP + i)),
        pl.BlockSpec((8, STEP), lambda i: (0, 4 * group // STEP + start // STEP + i)),
        pl.BlockSpec((8, 128), lambda i: (0, 5 * group // 128)),
    ]
    specs += [pl.BlockSpec((STEP, width), lambda i: (i, 0))] * 3
    args = [static, x, sums, sums, sums, *updates]
    aliases = {}
    if previous is not None:
        specs.append(pl.BlockSpec(memory_space=pl.ANY))
        aliases = {len(args): 0}
        args.append(previous)
    return pl.pallas_call(
        final_kernel,
        grid=(tokens // STEP,),
        in_specs=specs,
        out_specs=stream_block,
        out_shape=jax.ShapeDtypeStruct(x.shape, BF),
        input_output_aliases=aliases,
        cost_estimate=cost(tokens * 4 * width * 1200, tokens * 22 * width),
        compiler_params=params(),
        name="final",
    )(*args)


def body(streams, proj_master, hc_proj, hc_static, segment_ids, block_mask):
    tokens_local, _, width = streams.shape
    group_size = lax.axis_size("mp")
    place = lax.axis_index("mp").astype(jnp.int32).reshape(1)
    ring = lax.axis_index("blk").astype(jnp.int32).reshape(1)

    proj_rows = jnp.concatenate(
        [hc_proj.T, jnp.ones((1, width), F32), jnp.zeros((1, width), F32)], axis=0
    )
    own = stats(streams, proj_rows)
    parts = list(regroup(place, proj_master, group_size))
    sums, parts = lax.optimization_barrier(([own] + from_others(own, "mp"), parts))

    def gathered(normed):
        rows = lax.all_gather(normed, "mp", axis=0, tiled=True)
        return rows.reshape(group_size, normed.shape[0], width)

    sums_all, normed_late = mix(hc_static, streams, sums, CHUNK, tokens_local - CHUNK)
    rows_late = gathered(normed_late)
    _, normed_first = mix(hc_static, streams, sums, 0, CHUNK)
    rows_first = gathered(normed_first)

    for step in range(1, group_size):
        parts[step] = lax.ppermute(
            parts[step], "mp", [(at, (at + step) % group_size) for at in range(group_size)]
        )
    qkv_part, out_part = assemble(place, parts)
    qkv_pieces = weight_pieces(qkv_part)
    out_part, qkv_pieces = lax.optimization_barrier((out_part, qkv_pieces))
    out_pieces = weight_pieces(out_part)

    halo = passed_along(segment_ids[-BLOCK:], "blk", 1)
    halo = jnp.where(lax.axis_index("blk") == 0, -1, halo)
    extended = jnp.concatenate([halo, segment_ids])
    key_at = jnp.arange(tokens_local + BLOCK, dtype=jnp.int32)[None, :]
    query_at = jnp.arange(tokens_local, dtype=jnp.int32)[:, None] + BLOCK
    earlier = (extended[None, :] == segment_ids[:, None]) & (key_at < query_at)
    positions = jnp.sum(earlier.astype(jnp.int32), axis=1)
    half = HEAD_DIM // 2
    inverse = 10000.0 ** (-(jnp.arange(half, dtype=F32) * 2.0 / HEAD_DIM))
    angles = positions.astype(F32)[:, None] * inverse[None, :]
    cosine, sine = jnp.cos(angles), jnp.sin(angles)
    cosine = jnp.concatenate([cosine, cosine], axis=1)
    sine = jnp.concatenate([-sine, sine], axis=1)
    windows = []
    for block in range(tokens_local // BLOCK):
        before = extended[block * BLOCK : (block + 1) * BLOCK]
        before = jnp.where(block_mask[block] == 1, before, -1)
        seen = jnp.concatenate([before, segment_ids[block * BLOCK : (block + 1) * BLOCK]])
        for chunk in range(BLOCK // CHUNK):
            windows.append(seen[chunk * CHUNK : chunk * CHUNK + BLOCK + CHUNK])
    key_segments = jnp.stack(windows)[:, None, :]
    query_segments = segment_ids[:, None]

    qkv_late = qkv_columns(ring, rows_late, qkv_pieces, cosine[CHUNK:], sine[CHUNK:])
    halo_rows = passed_along(qkv_late[1:3, -BLOCK:], "blk", 1)

    last = tokens_local // CHUNK - 1
    late_chunks = [(qkv_late, 1, at) for at in range(last)]

    def attended_chunk(chunk, window):
        source, _, at = window[-1]
        return attend((source, at), window, query_segments, key_segments, chunk)

    def projected(own):
        other = swapped(own, "mp", 1)
        return project(place, ring, own, other, out_pieces, group_size)

    parts = {last: projected(attended_chunk(last, late_chunks[-3:]))}
    rows_first, parts[last] = lax.optimization_barrier((rows_first, parts[last]))
    qkv_first = qkv_columns(ring, rows_first, qkv_pieces, cosine[:CHUNK], sine[:CHUNK])
    chunks = [(halo_rows, 0, 0), (halo_rows, 0, 1), (qkv_first, 1, 0)] + late_chunks
    for chunk in reversed(range(last)):
        parts[chunk] = projected(attended_chunk(chunk, chunks[chunk : chunk + 3]))

    result = None
    for chunk in reversed(range(last + 1)):
        kept, inner, outer = parts[chunk]
        inner = lax.ppermute(inner, "mp", [(1, 2), (2, 1)])
        outer = lax.ppermute(outer, "mp", [(1, 3), (2, 0)])
        updates = [kept, inner, outer]
        result = final(hc_static, streams, sums_all, updates, chunk * CHUNK, result)
    return result


def solution(mesh):
    in_specs = (
        P("blk", None, "mp"),
        P(("blk", "mp"), None, None),
        P("mp", None),
        P(),
        P("blk"),
        P("blk"),
    )
    out_specs = P("blk", None, "mp")
    return jax.shard_map(body, mesh=mesh, in_specs=in_specs, out_specs=out_specs, check_vma=False)
```

```python
import functools

import jax
import jax.numpy as jnp
from jax import lax
from jax.experimental import pallas as pl
from jax.experimental.pallas import tpu as pltpu
from jax.sharding import PartitionSpec as P

D = 2048
HEAD_DIM = 128
BLOCK = 512
CHUNK = 256
SUB = 64
STEP = 128
STREAMS = 4
EPS = 1e-05
BF = jnp.bfloat16
F32 = jnp.float32


def passed_along(value, axis, steps):
    count = lax.axis_size(axis)
    first, last = (max(0, -steps), min(count, count - steps))
    return lax.ppermute(value, axis, [(source, source + steps) for source in range(first, last)])


def from_others(value, axis):
    count = lax.axis_size(axis)
    return [
        lax.ppermute(value, axis, [(source, (source + step) % count) for source in range(count)])
        for step in range(1, count)
    ]


def cost(flops, nbytes, transcendentals=0):
    return pl.CostEstimate(flops=flops, bytes_accessed=nbytes, transcendentals=transcendentals)


def params(limit=60):
    return pltpu.CompilerParams(vmem_limit_bytes=limit << 20)


def split(value, parts):
    out = []
    for _ in range(parts):
        part = value.astype(BF)
        out.append(part)
        value = value - part.astype(F32)
    return out


def contract(a, b, a_dim, b_dim):
    return lax.dot_general(a, b, (((a_dim,), (b_dim,)), ((), ())), preferred_element_type=F32)


def iotas(rows, cols):
    return (
        lax.broadcasted_iota(jnp.int32, (rows, cols), 0),
        lax.broadcasted_iota(jnp.int32, (rows, cols), 1),
    )


def regroup_kernel(place_ref, master_ref, *parts):
    servers = len(parts)
    width = master_ref.shape[-1] // servers
    for step, part_ref in enumerate(parts):
        server = (place_ref[0] + step) % servers
        own = pl.ds(pl.multiple_of(server * width, width), width)
        pair = pl.ds(pl.multiple_of((server // 2) * 2 * width, 2 * width), 2 * width)
        for slot in range(3):
            part_ref[:, slot * width : (slot + 1) * width] = master_ref[:, slot, own].astype(BF)
        part_ref[:, 3 * width :] = master_ref[:, 3, pair].astype(BF)


def regroup(place, master, servers):
    rows, _, total = master.shape
    columns = 5 * total // servers
    return pl.pallas_call(
        regroup_kernel,
        in_specs=[pl.BlockSpec(memory_space=pltpu.SMEM), pl.BlockSpec(memory_space=pltpu.VMEM)],
        out_specs=[pl.BlockSpec(memory_space=pltpu.VMEM)] * servers,
        out_shape=[jax.ShapeDtypeStruct((rows, columns), BF)] * servers,
        cost_estimate=cost(0, rows * total * 26),
        compiler_params=params(),
        name="regroup",
    )(place, master)


def assemble_kernel(place_ref, *refs):
    qkv_ref, out_ref = refs[-2:]
    parts = refs[:-2]
    rows = parts[0].shape[0]
    cut = qkv_ref.shape[1]
    for step, part_ref in enumerate(parts):
        source = (place_ref[0] + len(parts) - step) % len(parts)
        at = pl.ds(pl.multiple_of(source * rows, rows), rows)
        qkv_ref[at, :] = part_ref[:, :cut]
        out_ref[at, :] = part_ref[:, cut:]


def assemble(place, parts):
    rows, columns = parts[0].shape
    rows *= len(parts)
    return pl.pallas_call(
        assemble_kernel,
        in_specs=[pl.BlockSpec(memory_space=pltpu.SMEM)]
        + [pl.BlockSpec(memory_space=pltpu.VMEM)] * len(parts),
        out_specs=[pl.BlockSpec(memory_space=pltpu.VMEM)] * 2,
        out_shape=[
            jax.ShapeDtypeStruct((rows, columns // 5 * 3), BF),
            jax.ShapeDtypeStruct((rows, columns // 5 * 2), BF),
        ],
        cost_estimate=cost(0, rows * columns * 4),
        compiler_params=params(),
        name="assemble",
    )(place, *parts)


def swapped(value, axis, mask):
    count = lax.axis_size(axis)
    return lax.ppermute(value, axis, [(source, source ^ mask) for source in range(count)])


def weight_pieces(part):
    count = lax.axis_size("blk")
    if count & (count - 1) or part.shape[0] % HEAD_DIM or count > 8:
        return [lax.all_gather(part, "blk", axis=0, tiled=True)]
    pieces = {0: part}
    for mask in range(2, count, 2):
        pieces[mask] = swapped(part, "blk", mask)
    for mask in range(0, count, 2):
        pieces[mask + 1] = swapped(pieces[mask], "blk", 1)
    return [pieces[mask] for mask in range(count)]


def stats_kernel(x_ref, proj_ref, out_ref):
    block, _, width = x_ref.shape
    tokens = block * pl.num_programs(0)
    base = pl.program_id(0) * (block // STEP)
    proj = proj_ref[...]
    pieces = jnp.concatenate(split(proj, 3), axis=0)
    out_ref[:, out_ref.shape[1] - 128 :] = jnp.broadcast_to(jnp.sum(proj, axis=1, keepdims=True), (8, 128))
    row, col = iotas(4 * SUB, 4 * SUB)
    same = (row >> 2) == (col >> 2)
    ring = jnp.where(same, (row - col) & 3, -1)

    @pl.loop(0, block // STEP)
    def _(local):
        step = base + local
        folded = []
        for half in range(STEP // SUB):
            lanes = pl.ds(pl.multiple_of(step * 4 * STEP, 4 * STEP) + half * 4 * SUB, 4 * SUB)
            v = x_ref[pl.ds(local * STEP + half * SUB, SUB)].reshape(4 * SUB, width)
            sums = contract(pieces, v, 1, 1)
            sums = sums[0:8] + sums[8:16] + sums[16:24]
            gram = contract(v, v, 1, 1)
            out_ref[0:1, lanes] = sums[0:1]
            out_ref[1:2, lanes] = sums[6:7]
            for shift in range(3):
                out_ref[2 + shift : 3 + shift, lanes] = jnp.sum(
                    jnp.where(ring == shift, gram, 0.0), axis=0, keepdims=True
                )
            out_ref[5:8, lanes] = sums[1:4]
            folded.append(sums[4:6])
        folded = jnp.concatenate(folded, axis=1)
        lanes = pl.ds(pl.multiple_of(4 * tokens + step * STEP, STEP), STEP)
        for part in range(4):
            for which in range(2):
                out_ref[4 * which + part : 4 * which + part + 1, lanes] = folded[
                    which : which + 1, part * STEP : (part + 1) * STEP
                ]


def stats(x, proj):
    tokens, _, width = x.shape
    lanes = 5 * tokens + 128
    return pl.pallas_call(
        stats_kernel,
        grid=(tokens // (2 * STEP),),
        in_specs=[
            pl.BlockSpec((2 * STEP, 4, width), lambda i: (i, 0, 0)),
            pl.BlockSpec((8, width), lambda i: (0, 0)),
        ],
        out_specs=pl.BlockSpec((8, lanes), lambda i: (0, 0)),
        out_shape=jax.ShapeDtypeStruct((8, lanes), F32),
        cost_estimate=cost(tokens * 4 * width * 600, tokens * 8 * width),
        compiler_params=params(),
        name="stats",
    )(x, proj)


def by_stream(static_ref, column, stream):
    value = jnp.full(stream.shape, static_ref[0, column], F32)
    for k in range(1, 4):
        value = jnp.where(stream == k, static_ref[k, column], value)
    return value


def centre(first):
    mean = first[1:2] * (1.0 / D)
    spread = first[2:3] * (1.0 / D) - mean * mean
    return mean, lax.rsqrt(spread + EPS)


def mix_kernel(offset, static_ref, x_ref, own_ref, a_ref, b_ref, c_ref, sums_ref, normed_ref):
    tokens, _, width = x_ref.shape

    @pl.when(pl.program_id(0) == 0)
    def _():
        sums_ref[...] = (own_ref[...] + a_ref[...]) + (b_ref[...] + c_ref[...])

    base = 4 * (offset + pl.program_id(0) * tokens)
    last = sums_ref.shape[1] - 128
    column = sums_ref[0:1, last : last + 1]
    stream = lax.broadcasted_iota(jnp.int32, (1, 4 * STEP), 1) & 3
    static = by_stream(static_ref, 0, stream)
    row, col = iotas(SUB, 4 * SUB)
    mine = row == (col >> 2)

    @pl.loop(0, tokens // STEP)
    def _(step):
        at = pl.multiple_of(base + step * 4 * STEP, 4 * STEP)
        first = sums_ref[:, pl.ds(at, 4 * STEP)]
        mean, inverse = centre(first)
        mix = static + jnp.tanh(inverse * (first[0:1] - mean * column))
        one = jnp.where(stream < 3, pltpu.roll(mix, 4 * STEP - 1, 1), pltpu.roll(mix, 3, 1))
        two = jnp.where(stream < 2, pltpu.roll(mix, 4 * STEP - 2, 1), pltpu.roll(mix, 2, 1))
        linear = mix * first[1:2]
        square = mix * (mix * first[2:3] + 2.0 * one * first[3:4] + two * first[4:5])
        for half in range(STEP // SUB):
            lanes = slice(half * 4 * SUB, (half + 1) * 4 * SUB)
            rows = pl.ds(step * STEP + half * SUB, SUB)
            v = x_ref[rows].reshape(4 * SUB, width)
            matrix = jnp.where(mine, mix[:, lanes], 0.0)
            mixed = contract(jnp.concatenate(split(matrix, 3), axis=0), v, 1, 0)
            mixed = mixed[0:SUB] + mixed[SUB : 2 * SUB] + mixed[2 * SUB : 3 * SUB]
            average = jnp.sum(jnp.where(mine, linear[:, lanes], 0.0), axis=1, keepdims=True)
            power = jnp.sum(jnp.where(mine, square[:, lanes], 0.0), axis=1, keepdims=True)
            average, power = average * (1.0 / D), power * (1.0 / D)
            scale = lax.rsqrt(jnp.maximum(power - average * average, 0.0) + EPS)
            normed_ref[rows, :] = ((mixed - average) * scale).astype(BF)


def mix(static, x, parts, start, tokens):
    width = x.shape[-1]
    lanes = parts[0].shape[1]
    whole = pl.BlockSpec((8, lanes), lambda i: (0, 0))
    return pl.pallas_call(
        functools.partial(mix_kernel, start),
        grid=(tokens // CHUNK,),
        in_specs=[
            pl.BlockSpec(memory_space=pltpu.SMEM),
            pl.BlockSpec((CHUNK, 4, width), lambda i: (start // CHUNK + i, 0, 0)),
        ]
        + [whole] * 4,
        out_specs=[whole, pl.BlockSpec((CHUNK, width), lambda i: (i, 0))],
        out_shape=[
            jax.ShapeDtypeStruct((8, lanes), F32),
            jax.ShapeDtypeStruct((tokens, width), BF),
        ],
        cost_estimate=cost(tokens * 4 * width * 400, tokens * 10 * width),
        compiler_params=params(),
        name="mix",
    )(static, x, *parts)


def qkv_kernel(ring_ref, rows_ref, cosine_ref, sine_ref, *refs):
    out_ref = refs[-1]
    pieces = refs[:-1]
    servers, _, width = rows_ref.shape
    depth = pieces[0].shape[0]
    if len(pieces) == 1:
        left = [rows_ref[server] for server in range(servers)]
    else:
        left = []
        for piece in range(len(pieces)):
            source = ring_ref[0] ^ piece
            inside = pl.multiple_of((source % (width // depth)) * depth, depth)
            left.append(rows_ref[source // (width // depth), :, pl.ds(inside, depth)])
    left = jnp.concatenate(left, axis=1)
    right = jnp.concatenate([piece[...] for piece in pieces], axis=0)
    total = contract(left, right, 1, 0)
    slot = pl.program_id(0)

    @pl.when(slot < 2)
    def _():
        cosine, sine = cosine_ref[...], sine_ref[...]
        for head in range(total.shape[1] // HEAD_DIM):
            part = total[:, head * HEAD_DIM : (head + 1) * HEAD_DIM]
            turned = part * cosine + pltpu.roll(part, HEAD_DIM // 2, 1) * sine
            out_ref[0, :, head * HEAD_DIM : (head + 1) * HEAD_DIM] = turned.astype(BF)

    @pl.when(slot == 2)
    def _():
        out_ref[0] = total.astype(BF)


def qkv_columns(ring, rows, pieces, cosine, sine):
    servers, tokens, width = rows.shape
    table = pl.BlockSpec((tokens, HEAD_DIM), lambda j: (0, 0))
    return pl.pallas_call(
        qkv_kernel,
        grid=(3,),
        in_specs=[
            pl.BlockSpec(memory_space=pltpu.SMEM),
            pl.BlockSpec((servers, tokens, width), lambda j: (0, 0, 0)),
            table,
            table,
        ]
        + [pl.BlockSpec((pieces[0].shape[0], width), lambda j: (0, j))] * len(pieces),
        out_specs=pl.BlockSpec((1, tokens, width), lambda j: (j, 0, 0)),
        out_shape=jax.ShapeDtypeStruct((3, tokens, width), BF),
        cost_estimate=cost(2 * tokens * D * 3 * width, D * 6 * width + tokens * D * 5),
        compiler_params=params(),
        name="qkv",
    )(ring, rows, cosine, sine, *pieces)


def attend_kernel(q_ref, k0, k1, k2, v0, v1, v2, qseg_ref, kseg_ref, attended_ref):
    tokens, width = q_ref.shape[1:]
    window = kseg_ref.shape[-1]
    row, col = iotas(tokens, window)
    allowed = (qseg_ref[...] == kseg_ref[0]) & (col - (window - tokens) <= row)
    bias = jnp.where(allowed, 0.0, -1e30)
    factor = 1.4426950408889634 / HEAD_DIM**0.5
    for head in range(width // HEAD_DIM):
        lanes = slice(head * HEAD_DIM, (head + 1) * HEAD_DIM)
        query = q_ref[0, :, lanes]
        scores = jnp.concatenate(
            [contract(query, k[0, :, lanes], 1, 1) for k in (k0, k1, k2)], axis=1
        )
        scores = scores + bias
        weights = jnp.exp2((scores - jnp.max(scores, axis=1, keepdims=True)) * factor)
        total = jnp.sum(weights, axis=1, keepdims=True)
        values = jnp.concatenate([v[0, :, lanes] for v in (v0, v1, v2)], axis=0)
        attended_ref[:, lanes] = (contract(weights.astype(BF), values, 1, 0) / total).astype(BF)


def attend(query, window, qseg, kseg, chunk):
    source, at = query
    width = source.shape[-1]
    block = (1, CHUNK, width)
    keys = [pl.BlockSpec(block, lambda i, s=slot, r=where: (s, r, 0)) for _, slot, where in window]
    values = [
        pl.BlockSpec(block, lambda i, s=slot + 1, r=where: (s, r, 0)) for _, slot, where in window
    ]
    arrays = [array for array, _, _ in window]
    reach = kseg.shape[-1]
    return pl.pallas_call(
        attend_kernel,
        grid=(1,),
        in_specs=[pl.BlockSpec(block, lambda i: (0, at, 0))]
        + keys
        + values
        + [
            pl.BlockSpec((CHUNK, 1), lambda i: (chunk, 0)),
            pl.BlockSpec((1, 1, reach), lambda i: (chunk, 0, 0)),
        ],
        out_specs=pl.BlockSpec((CHUNK, width), lambda i: (0, 0)),
        out_shape=jax.ShapeDtypeStruct((CHUNK, width), BF),
        cost_estimate=cost(4 * CHUNK * reach * width, CHUNK * width * 16, CHUNK * reach * 4),
        compiler_params=params(),
        name="attend",
    )(source, *arrays, *arrays, qseg, kseg)


def project_kernel(place_ref, ring_ref, own_ref, other_ref, *refs):
    pieces = refs[:-4]
    kept_ref, inner_ref, outer_ref, sums = refs[-4:]
    servers, _, width = sums.shape
    place = place_ref[0]
    even = place % 2 == 0
    own, other = own_ref[...], other_ref[...]
    both = jnp.concatenate([jnp.where(even, own, other), jnp.where(even, other, own)], axis=1)
    depth = pieces[0].shape[0]
    if len(pieces) == 1:
        for server in range(servers):
            rows = pieces[0][server * width : (server + 1) * width, :]
            sums[server] = contract(both, rows, 1, 1)
    else:
        for piece in range(len(pieces)):
            target = ring_ref[0] ^ piece
            inside = pl.multiple_of((target % (width // depth)) * depth, depth)
            sums[target // (width // depth), :, pl.ds(inside, depth)] = contract(
                both, pieces[piece][...], 1, 1
            )
    kept_ref[...] = sums[place]
    low = place < 2
    inner_ref[...] = sums[jnp.where(low, 2, 1)].astype(BF)
    outer_ref[...] = sums[jnp.where(low, 3, 0)].astype(BF)


def project(place, ring, own, other, pieces, servers):
    tokens, width = own.shape
    rows, pair = pieces[0].shape
    tail = pl.BlockSpec((rows, pair), lambda i: (0, 0))
    full = pl.BlockSpec((tokens, width), lambda i: (0, 0))
    return pl.pallas_call(
        project_kernel,
        grid=(1,),
        in_specs=[pl.BlockSpec(memory_space=pltpu.SMEM)] * 2 + [full] * 2 + [tail] * len(pieces),
        out_specs=[full] * 3,
        out_shape=[
            jax.ShapeDtypeStruct((tokens, width), F32),
            jax.ShapeDtypeStruct((tokens, width), BF),
            jax.ShapeDtypeStruct((tokens, width), BF),
        ],
        scratch_shapes=[pltpu.VMEM((servers, tokens, width), F32)],
        cost_estimate=cost(2 * tokens * D * pair, D * pair * 2 + tokens * width * 12),
        compiler_params=params(),
        name="project",
    )(place, ring, own, other, *pieces)


def final_kernel(
    static_ref, x_ref, first_ref, folded_ref, column_ref, own_ref, inner_ref, outer_ref, *rest
):
    new_ref = rest[-1]
    tokens, _, width = x_ref.shape
    first = first_ref[...]
    mean, inverse = centre(first)
    stream = lax.broadcasted_iota(jnp.int32, (1, 4 * tokens), 1) & 3

    def coefficient(column, projected):
        dynamic = jnp.tanh(inverse * (projected - mean * column_ref[column : column + 1, 0:1]))
        return by_stream(static_ref, column, stream) + dynamic

    def unfolded(which):
        return jnp.concatenate(
            [folded_ref[4 * which + part : 4 * which + part + 1] for part in range(4)], axis=1
        )

    projected = [first[5:6], first[6:7], first[7:8], unfolded(0), unfolded(1)]
    columns = [coefficient(1 + j, projected[j]) for j in range(5)]
    residual = jnp.concatenate(columns[:4] + columns[:4], axis=0)
    row, col = iotas(4 * SUB, 4 * SUB)
    same = (row >> 2) == (col >> 2)
    row, col = iotas(SUB, 4 * SUB)
    mine = row == (col >> 2)
    for at in range(tokens // SUB):
        lanes = slice(at * 4 * SUB, (at + 1) * 4 * SUB)
        rows = slice(at * SUB, (at + 1) * SUB)
        v = x_ref[rows].reshape(4 * SUB, width)
        matrix = jnp.where(same, jnp.tile(residual[:, lanes], (SUB // 2, 1)), 0.0)
        high, low = split(matrix, 2)
        new = contract(high, v, 1, 0) + contract(low, v, 1, 0)
        sent = inner_ref[rows, :].astype(F32) + outer_ref[rows, :].astype(F32)
        update_high, update_low = split(own_ref[rows, :] + sent, 2)
        spread_high, spread_low = split(jnp.where(mine, columns[4][:, lanes], 0.0), 2)
        new += contract(
            jnp.concatenate([spread_high, spread_high, spread_low], axis=0),
            jnp.concatenate([update_high, update_low, update_high], axis=0),
            0,
            0,
        )
        new_ref[rows] = new.astype(BF).reshape(SUB, 4, width)


def final(static, x, sums, updates, start, previous):
    tokens, width = updates[0].shape
    group = (sums.shape[1] - 128) // 5
    stream_block = pl.BlockSpec((STEP, 4, width), lambda i: (start // STEP + i, 0, 0))
    specs = [
        pl.BlockSpec(memory_space=pltpu.SMEM),
        stream_block,
        pl.BlockSpec((8, 4 * STEP), lambda i: (0, start // STEP + i)),
        pl.BlockSpec((8, STEP), lambda i: (0, 4 * group // STEP + start // STEP + i)),
        pl.BlockSpec((8, 128), lambda i: (0, 5 * group // 128)),
    ]
    specs += [pl.BlockSpec((STEP, width), lambda i: (i, 0))] * 3
    args = [static, x, sums, sums, sums, *updates]
    aliases = {}
    if previous is not None:
        specs.append(pl.BlockSpec(memory_space=pl.ANY))
        aliases = {len(args): 0}
        args.append(previous)
    return pl.pallas_call(
        final_kernel,
        grid=(tokens // STEP,),
        in_specs=specs,
        out_specs=stream_block,
        out_shape=jax.ShapeDtypeStruct(x.shape, BF),
        input_output_aliases=aliases,
        cost_estimate=cost(tokens * 4 * width * 1200, tokens * 22 * width),
        compiler_params=params(),
        name="final",
    )(*args)


def body(streams, proj_master, hc_proj, hc_static, segment_ids, block_mask):
    tokens_local, _, width = streams.shape
    group_size = lax.axis_size("mp")
    place = lax.axis_index("mp").astype(jnp.int32).reshape(1)
    ring = lax.axis_index("blk").astype(jnp.int32).reshape(1)

    proj_rows = jnp.concatenate(
        [hc_proj.T, jnp.ones((1, width), F32), jnp.zeros((1, width), F32)], axis=0
    )
    own = stats(streams, proj_rows)
    parts = list(regroup(place, proj_master, group_size))
    sums, parts = lax.optimization_barrier(([own] + from_others(own, "mp"), parts))

    def gathered(normed):
        rows = lax.all_gather(normed, "mp", axis=0, tiled=True)
        return rows.reshape(group_size, normed.shape[0], width)

    for step in range(1, group_size):
        parts[step] = lax.ppermute(
            parts[step], "mp", [(at, (at + step) % group_size) for at in range(group_size)]
        )
    sums_all, normed_late = mix(hc_static, streams, sums, CHUNK, tokens_local - CHUNK)
    _, normed_first = mix(hc_static, streams, sums, 0, CHUNK)
    parts[1], normed_late, normed_first = lax.optimization_barrier(
        (parts[1], normed_late, normed_first)
    )
    rows_late = gathered(normed_late)
    rows_first = gathered(normed_first)

    qkv_part, out_part = assemble(place, parts)
    qkv_pieces = weight_pieces(qkv_part)
    out_part, qkv_pieces = lax.optimization_barrier((out_part, qkv_pieces))
    out_pieces = weight_pieces(out_part)

    halo = passed_along(segment_ids[-BLOCK:], "blk", 1)
    halo = jnp.where(lax.axis_index("blk") == 0, -1, halo)
    extended = jnp.concatenate([halo, segment_ids])
    key_at = jnp.arange(tokens_local + BLOCK, dtype=jnp.int32)[None, :]
    query_at = jnp.arange(tokens_local, dtype=jnp.int32)[:, None] + BLOCK
    earlier = (extended[None, :] == segment_ids[:, None]) & (key_at < query_at)
    positions = jnp.sum(earlier.astype(jnp.int32), axis=1)
    half = HEAD_DIM // 2
    inverse = 10000.0 ** (-(jnp.arange(half, dtype=F32) * 2.0 / HEAD_DIM))
    angles = positions.astype(F32)[:, None] * inverse[None, :]
    cosine, sine = jnp.cos(angles), jnp.sin(angles)
    cosine = jnp.concatenate([cosine, cosine], axis=1)
    sine = jnp.concatenate([-sine, sine], axis=1)
    windows = []
    for block in range(tokens_local // BLOCK):
        before = extended[block * BLOCK : (block + 1) * BLOCK]
        before = jnp.where(block_mask[block] == 1, before, -1)
        seen = jnp.concatenate([before, segment_ids[block * BLOCK : (block + 1) * BLOCK]])
        for chunk in range(BLOCK // CHUNK):
            windows.append(seen[chunk * CHUNK : chunk * CHUNK + BLOCK + CHUNK])
    key_segments = jnp.stack(windows)[:, None, :]
    query_segments = segment_ids[:, None]

    qkv_late = qkv_columns(ring, rows_late, qkv_pieces, cosine[CHUNK:], sine[CHUNK:])
    halo_rows = passed_along(qkv_late[1:3, -BLOCK:], "blk", 1)

    last = tokens_local // CHUNK - 1
    late_chunks = [(qkv_late, 1, at) for at in range(last)]

    def attended_chunk(chunk, window):
        source, _, at = window[-1]
        return attend((source, at), window, query_segments, key_segments, chunk)

    def projected(own):
        other = swapped(own, "mp", 1)
        return project(place, ring, own, other, out_pieces, group_size)

    parts = {last: projected(attended_chunk(last, late_chunks[-3:]))}
    rows_first, parts[last] = lax.optimization_barrier((rows_first, parts[last]))
    qkv_first = qkv_columns(ring, rows_first, qkv_pieces, cosine[:CHUNK], sine[:CHUNK])
    chunks = [(halo_rows, 0, 0), (halo_rows, 0, 1), (qkv_first, 1, 0)] + late_chunks
    for chunk in reversed(range(last)):
        parts[chunk] = projected(attended_chunk(chunk, chunks[chunk : chunk + 3]))

    result = None
    for chunk in reversed(range(last + 1)):
        kept, inner, outer = parts[chunk]
        inner = lax.ppermute(inner, "mp", [(1, 2), (2, 1)])
        outer = lax.ppermute(outer, "mp", [(1, 3), (2, 0)])
        updates = [kept, inner, outer]
        result = final(hc_static, streams, sums_all, updates, chunk * CHUNK, result)
    return result


def solution(mesh):
    in_specs = (
        P("blk", None, "mp"),
        P(("blk", "mp"), None, None),
        P("mp", None),
        P(),
        P("blk"),
        P("blk"),
    )
    out_specs = P("blk", None, "mp")
    return jax.shard_map(body, mesh=mesh, in_specs=in_specs, out_specs=out_specs, check_vma=False)
```

```python
import functools

import jax
import jax.numpy as jnp
from jax import lax
from jax.experimental import pallas as pl
from jax.experimental.pallas import tpu as pltpu
from jax.sharding import PartitionSpec as P

D = 2048
HEAD_DIM = 128
BLOCK = 512
CHUNK = 256
SUB = 64
STEP = 128
STREAMS = 4
EPS = 1e-05
BF = jnp.bfloat16
F32 = jnp.float32


def passed_along(value, axis, steps):
    count = lax.axis_size(axis)
    first, last = (max(0, -steps), min(count, count - steps))
    return lax.ppermute(value, axis, [(source, source + steps) for source in range(first, last)])


def from_others(value, axis):
    count = lax.axis_size(axis)
    return [
        lax.ppermute(value, axis, [(source, (source + step) % count) for source in range(count)])
        for step in range(1, count)
    ]


def cost(flops, nbytes, transcendentals=0):
    return pl.CostEstimate(flops=flops, bytes_accessed=nbytes, transcendentals=transcendentals)


def params(limit=60):
    return pltpu.CompilerParams(vmem_limit_bytes=limit << 20)


def split(value, parts):
    out = []
    for _ in range(parts):
        part = value.astype(BF)
        out.append(part)
        value = value - part.astype(F32)
    return out


def contract(a, b, a_dim, b_dim):
    return lax.dot_general(a, b, (((a_dim,), (b_dim,)), ((), ())), preferred_element_type=F32)


def iotas(rows, cols):
    return (
        lax.broadcasted_iota(jnp.int32, (rows, cols), 0),
        lax.broadcasted_iota(jnp.int32, (rows, cols), 1),
    )


def regroup_kernel(place_ref, master_ref, *parts):
    servers = len(parts)
    width = master_ref.shape[-1] // servers
    for step, part_ref in enumerate(parts):
        server = (place_ref[0] + step) % servers
        own = pl.ds(pl.multiple_of(server * width, width), width)
        pair = pl.ds(pl.multiple_of((server // 2) * 2 * width, 2 * width), 2 * width)
        for slot in range(3):
            part_ref[:, slot * width : (slot + 1) * width] = master_ref[:, slot, own].astype(BF)
        part_ref[:, 3 * width :] = master_ref[:, 3, pair].astype(BF)


def regroup(place, master, servers):
    rows, _, total = master.shape
    columns = 5 * total // servers
    return pl.pallas_call(
        regroup_kernel,
        in_specs=[pl.BlockSpec(memory_space=pltpu.SMEM), pl.BlockSpec(memory_space=pltpu.VMEM)],
        out_specs=[pl.BlockSpec(memory_space=pltpu.VMEM)] * servers,
        out_shape=[jax.ShapeDtypeStruct((rows, columns), BF)] * servers,
        cost_estimate=cost(0, rows * total * 26),
        compiler_params=params(),
        name="regroup",
    )(place, master)


def assemble_kernel(place_ref, *refs):
    out_ref = refs[-1]
    parts = refs[:-1]
    rows = parts[0].shape[0]
    for step, part_ref in enumerate(parts):
        source = (place_ref[0] + len(parts) - step) % len(parts)
        out_ref[pl.ds(pl.multiple_of(source * rows, rows), rows), :] = part_ref[...]


def assemble(place, parts):
    rows, columns = parts[0].shape
    return pl.pallas_call(
        assemble_kernel,
        in_specs=[pl.BlockSpec(memory_space=pltpu.SMEM)]
        + [pl.BlockSpec(memory_space=pltpu.VMEM)] * len(parts),
        out_specs=pl.BlockSpec(memory_space=pltpu.VMEM),
        out_shape=jax.ShapeDtypeStruct((rows * len(parts), columns), BF),
        cost_estimate=cost(0, rows * columns * len(parts) * 4),
        compiler_params=params(),
        name="assemble",
    )(place, *parts)


def swapped(value, axis, mask):
    count = lax.axis_size(axis)
    return lax.ppermute(value, axis, [(source, source ^ mask) for source in range(count)])


def weight_pieces(part):
    count = lax.axis_size("blk")
    if count & (count - 1) or part.shape[0] % HEAD_DIM or count > 8:
        return [lax.all_gather(part, "blk", axis=0, tiled=True)]
    pieces = {0: part}
    for mask in range(2, count, 2):
        pieces[mask] = swapped(part, "blk", mask)
    for mask in range(0, count, 2):
        pieces[mask + 1] = swapped(pieces[mask], "blk", 1)
    return [pieces[mask] for mask in range(count)]


def stats_kernel(x_ref, proj_ref, out_ref):
    block, _, width = x_ref.shape
    tokens = block * pl.num_programs(0)
    base = pl.program_id(0) * (block // STEP)
    proj = proj_ref[...]
    pieces = jnp.concatenate(split(proj, 3), axis=0)
    out_ref[:, out_ref.shape[1] - 128 :] = jnp.broadcast_to(jnp.sum(proj, axis=1, keepdims=True), (8, 128))
    row, col = iotas(4 * SUB, 4 * SUB)
    same = (row >> 2) == (col >> 2)
    ring = jnp.where(same, (row - col) & 3, -1)

    @pl.loop(0, block // STEP)
    def _(local):
        step = base + local
        folded = []
        for half in range(STEP // SUB):
            lanes = pl.ds(pl.multiple_of(step * 4 * STEP, 4 * STEP) + half * 4 * SUB, 4 * SUB)
            v = x_ref[pl.ds(local * STEP + half * SUB, SUB)].reshape(4 * SUB, width)
            sums = contract(pieces, v, 1, 1)
            sums = sums[0:8] + sums[8:16] + sums[16:24]
            gram = contract(v, v, 1, 1)
            out_ref[0:1, lanes] = sums[0:1]
            out_ref[1:2, lanes] = sums[6:7]
            for shift in range(3):
                out_ref[2 + shift : 3 + shift, lanes] = jnp.sum(
                    jnp.where(ring == shift, gram, 0.0), axis=0, keepdims=True
                )
            out_ref[5:8, lanes] = sums[1:4]
            folded.append(sums[4:6])
        folded = jnp.concatenate(folded, axis=1)
        lanes = pl.ds(pl.multiple_of(4 * tokens + step * STEP, STEP), STEP)
        for part in range(4):
            for which in range(2):
                out_ref[4 * which + part : 4 * which + part + 1, lanes] = folded[
                    which : which + 1, part * STEP : (part + 1) * STEP
                ]


def stats(x, proj):
    tokens, _, width = x.shape
    lanes = 5 * tokens + 128
    return pl.pallas_call(
        stats_kernel,
        grid=(tokens // (2 * STEP),),
        in_specs=[
            pl.BlockSpec((2 * STEP, 4, width), lambda i: (i, 0, 0)),
            pl.BlockSpec((8, width), lambda i: (0, 0)),
        ],
        out_specs=pl.BlockSpec((8, lanes), lambda i: (0, 0)),
        out_shape=jax.ShapeDtypeStruct((8, lanes), F32),
        cost_estimate=cost(tokens * 4 * width * 600, tokens * 8 * width),
        compiler_params=params(),
        name="stats",
    )(x, proj)


def by_stream(static_ref, column, stream):
    value = jnp.full(stream.shape, static_ref[0, column], F32)
    for k in range(1, 4):
        value = jnp.where(stream == k, static_ref[k, column], value)
    return value


def centre(first):
    mean = first[1:2] * (1.0 / D)
    spread = first[2:3] * (1.0 / D) - mean * mean
    return mean, lax.rsqrt(spread + EPS)


def mix_kernel(offset, static_ref, x_ref, own_ref, a_ref, b_ref, c_ref, sums_ref, normed_ref):
    tokens, _, width = x_ref.shape

    @pl.when(pl.program_id(0) == 0)
    def _():
        sums_ref[...] = (own_ref[...] + a_ref[...]) + (b_ref[...] + c_ref[...])

    base = 4 * (offset + pl.program_id(0) * tokens)
    last = sums_ref.shape[1] - 128
    column = sums_ref[0:1, last : last + 1]
    stream = lax.broadcasted_iota(jnp.int32, (1, 4 * STEP), 1) & 3
    static = by_stream(static_ref, 0, stream)
    row, col = iotas(SUB, 4 * SUB)
    mine = row == (col >> 2)

    @pl.loop(0, tokens // STEP)
    def _(step):
        at = pl.multiple_of(base + step * 4 * STEP, 4 * STEP)
        first = sums_ref[:, pl.ds(at, 4 * STEP)]
        mean, inverse = centre(first)
        mix = static + jnp.tanh(inverse * (first[0:1] - mean * column))
        one = jnp.where(stream < 3, pltpu.roll(mix, 4 * STEP - 1, 1), pltpu.roll(mix, 3, 1))
        two = jnp.where(stream < 2, pltpu.roll(mix, 4 * STEP - 2, 1), pltpu.roll(mix, 2, 1))
        linear = mix * first[1:2]
        square = mix * (mix * first[2:3] + 2.0 * one * first[3:4] + two * first[4:5])
        for half in range(STEP // SUB):
            lanes = slice(half * 4 * SUB, (half + 1) * 4 * SUB)
            rows = pl.ds(step * STEP + half * SUB, SUB)
            v = x_ref[rows].reshape(4 * SUB, width)
            matrix = jnp.where(mine, mix[:, lanes], 0.0)
            mixed = contract(jnp.concatenate(split(matrix, 3), axis=0), v, 1, 0)
            mixed = mixed[0:SUB] + mixed[SUB : 2 * SUB] + mixed[2 * SUB : 3 * SUB]
            average = jnp.sum(jnp.where(mine, linear[:, lanes], 0.0), axis=1, keepdims=True)
            power = jnp.sum(jnp.where(mine, square[:, lanes], 0.0), axis=1, keepdims=True)
            average, power = average * (1.0 / D), power * (1.0 / D)
            scale = lax.rsqrt(jnp.maximum(power - average * average, 0.0) + EPS)
            normed_ref[rows, :] = ((mixed - average) * scale).astype(BF)


def mix(static, x, parts, start, tokens):
    width = x.shape[-1]
    lanes = parts[0].shape[1]
    whole = pl.BlockSpec((8, lanes), lambda i: (0, 0))
    return pl.pallas_call(
        functools.partial(mix_kernel, start),
        grid=(tokens // CHUNK,),
        in_specs=[
            pl.BlockSpec(memory_space=pltpu.SMEM),
            pl.BlockSpec((CHUNK, 4, width), lambda i: (start // CHUNK + i, 0, 0)),
        ]
        + [whole] * 4,
        out_specs=[whole, pl.BlockSpec((CHUNK, width), lambda i: (i, 0))],
        out_shape=[
            jax.ShapeDtypeStruct((8, lanes), F32),
            jax.ShapeDtypeStruct((tokens, width), BF),
        ],
        cost_estimate=cost(tokens * 4 * width * 400, tokens * 10 * width),
        compiler_params=params(),
        name="mix",
    )(static, x, *parts)


def qkv_kernel(ring_ref, rows_ref, cosine_ref, sine_ref, *refs):
    out_ref, halo_ref = refs[-2:]
    pieces = refs[:-2]
    servers, _, width = rows_ref.shape
    depth = pieces[0].shape[0]
    if len(pieces) == 1:
        left = [rows_ref[server] for server in range(servers)]
    else:
        left = []
        for piece in range(len(pieces)):
            source = ring_ref[0] ^ piece
            inside = pl.multiple_of((source % (width // depth)) * depth, depth)
            left.append(rows_ref[source // (width // depth), :, pl.ds(inside, depth)])
    left = jnp.concatenate(left, axis=1)
    right = jnp.concatenate([piece[...] for piece in pieces], axis=0)
    total = contract(left, right, 1, 0)
    slot = pl.program_id(0)

    @pl.when(slot < 2)
    def _():
        cosine, sine = cosine_ref[...], sine_ref[...]
        for head in range(total.shape[1] // HEAD_DIM):
            part = total[:, head * HEAD_DIM : (head + 1) * HEAD_DIM]
            turned = part * cosine + pltpu.roll(part, HEAD_DIM // 2, 1) * sine
            out_ref[0, :, head * HEAD_DIM : (head + 1) * HEAD_DIM] = turned.astype(BF)

    @pl.when(slot == 2)
    def _():
        out_ref[0] = total.astype(BF)

    halo_ref[0] = out_ref[0, -BLOCK:, :]


def qkv_columns(ring, rows, pieces, cosine, sine):
    servers, tokens, width = rows.shape
    table = pl.BlockSpec((tokens, HEAD_DIM), lambda j: (0, 0))
    return pl.pallas_call(
        qkv_kernel,
        grid=(3,),
        in_specs=[
            pl.BlockSpec(memory_space=pltpu.SMEM),
            pl.BlockSpec((servers, tokens, width), lambda j: (0, 0, 0)),
            table,
            table,
        ]
        + [pl.BlockSpec((pieces[0].shape[0], width), lambda j: (0, j))] * len(pieces),
        out_specs=[
            pl.BlockSpec((1, tokens, width), lambda j: (j, 0, 0)),
            pl.BlockSpec((1, BLOCK, width), lambda j: (jnp.maximum(j - 1, 0), 0, 0)),
        ],
        out_shape=[
            jax.ShapeDtypeStruct((3, tokens, width), BF),
            jax.ShapeDtypeStruct((2, BLOCK, width), BF),
        ],
        cost_estimate=cost(2 * tokens * D * 3 * width, D * 6 * width + tokens * D * 5),
        compiler_params=params(),
        name="qkv",
    )(ring, rows, cosine, sine, *pieces)


def attend_kernel(q_ref, k0, k1, k2, v0, v1, v2, qseg_ref, kseg_ref, attended_ref):
    tokens, width = q_ref.shape[1:]
    window = kseg_ref.shape[-1]
    row, col = iotas(tokens, window)
    allowed = (qseg_ref[...] == kseg_ref[0]) & (col - (window - tokens) <= row)
    bias = jnp.where(allowed, 0.0, -1e30)
    factor = 1.4426950408889634 / HEAD_DIM**0.5
    for head in range(width // HEAD_DIM):
        lanes = slice(head * HEAD_DIM, (head + 1) * HEAD_DIM)
        query = q_ref[0, :, lanes]
        scores = jnp.concatenate(
            [contract(query, k[0, :, lanes], 1, 1) for k in (k0, k1, k2)], axis=1
        )
        scores = scores + bias
        weights = jnp.exp2((scores - jnp.max(scores, axis=1, keepdims=True)) * factor)
        total = jnp.sum(weights, axis=1, keepdims=True)
        values = jnp.concatenate([v[0, :, lanes] for v in (v0, v1, v2)], axis=0)
        attended_ref[:, lanes] = (contract(weights.astype(BF), values, 1, 0) / total).astype(BF)


def attend(query, window, qseg, kseg, chunk):
    source, at = query
    width = source.shape[-1]
    block = (1, CHUNK, width)
    keys = [pl.BlockSpec(block, lambda i, s=slot, r=where: (s, r, 0)) for _, slot, where in window]
    values = [
        pl.BlockSpec(block, lambda i, s=slot + 1, r=where: (s, r, 0)) for _, slot, where in window
    ]
    arrays = [array for array, _, _ in window]
    reach = kseg.shape[-1]
    return pl.pallas_call(
        attend_kernel,
        grid=(1,),
        in_specs=[pl.BlockSpec(block, lambda i: (0, at, 0))]
        + keys
        + values
        + [
            pl.BlockSpec((CHUNK, 1), lambda i: (chunk, 0)),
            pl.BlockSpec((1, 1, reach), lambda i: (chunk, 0, 0)),
        ],
        out_specs=pl.BlockSpec((CHUNK, width), lambda i: (0, 0)),
        out_shape=jax.ShapeDtypeStruct((CHUNK, width), BF),
        cost_estimate=cost(4 * CHUNK * reach * width, CHUNK * width * 16, CHUNK * reach * 4),
        compiler_params=params(),
        name="attend",
    )(source, *arrays, *arrays, qseg, kseg)


def project_kernel(place_ref, ring_ref, own_ref, other_ref, *refs):
    pieces = refs[:-4]
    kept_ref, inner_ref, outer_ref, sums = refs[-4:]
    servers, _, width = sums.shape
    place = place_ref[0]
    even = place % 2 == 0
    own, other = own_ref[...], other_ref[...]
    both = jnp.concatenate([jnp.where(even, own, other), jnp.where(even, other, own)], axis=1)
    depth = pieces[0].shape[0]
    if len(pieces) == 1:
        for server in range(servers):
            rows = pieces[0][server * width : (server + 1) * width, :]
            sums[server] = contract(both, rows, 1, 1)
    else:
        for piece in range(len(pieces)):
            target = ring_ref[0] ^ piece
            inside = pl.multiple_of((target % (width // depth)) * depth, depth)
            sums[target // (width // depth), :, pl.ds(inside, depth)] = contract(
                both, pieces[piece][...], 1, 1
            )
    kept_ref[...] = sums[place]
    low = place < 2
    inner_ref[...] = sums[jnp.where(low, 2, 1)].astype(BF)
    outer_ref[...] = sums[jnp.where(low, 3, 0)].astype(BF)


def project(place, ring, own, other, pieces, servers):
    tokens, width = own.shape
    rows, columns = pieces[0].shape
    pair = 2 * width
    tail = pl.BlockSpec((pl.Element(rows), pl.Element(pair)), lambda i: (0, columns - pair))
    full = pl.BlockSpec((tokens, width), lambda i: (0, 0))
    return pl.pallas_call(
        project_kernel,
        grid=(1,),
        in_specs=[pl.BlockSpec(memory_space=pltpu.SMEM)] * 2 + [full] * 2 + [tail] * len(pieces),
        out_specs=[full] * 3,
        out_shape=[
            jax.ShapeDtypeStruct((tokens, width), F32),
            jax.ShapeDtypeStruct((tokens, width), BF),
            jax.ShapeDtypeStruct((tokens, width), BF),
        ],
        scratch_shapes=[pltpu.VMEM((servers, tokens, width), F32)],
        cost_estimate=cost(2 * tokens * D * pair, D * pair * 2 + tokens * width * 12),
        compiler_params=params(),
        name="project",
    )(place, ring, own, other, *pieces)


def final_kernel(
    static_ref, x_ref, first_ref, folded_ref, column_ref, own_ref, inner_ref, outer_ref, *rest
):
    new_ref = rest[-1]
    tokens, _, width = x_ref.shape
    first = first_ref[...]
    mean, inverse = centre(first)
    stream = lax.broadcasted_iota(jnp.int32, (1, 4 * tokens), 1) & 3

    def coefficient(column, projected):
        dynamic = jnp.tanh(inverse * (projected - mean * column_ref[column : column + 1, 0:1]))
        return by_stream(static_ref, column, stream) + dynamic

    def unfolded(which):
        return jnp.concatenate(
            [folded_ref[4 * which + part : 4 * which + part + 1] for part in range(4)], axis=1
        )

    projected = [first[5:6], first[6:7], first[7:8], unfolded(0), unfolded(1)]
    columns = [coefficient(1 + j, projected[j]) for j in range(5)]
    residual = jnp.concatenate(columns[:4] + columns[:4], axis=0)
    row, col = iotas(4 * SUB, 4 * SUB)
    same = (row >> 2) == (col >> 2)
    row, col = iotas(SUB, 4 * SUB)
    mine = row == (col >> 2)
    for at in range(tokens // SUB):
        lanes = slice(at * 4 * SUB, (at + 1) * 4 * SUB)
        rows = slice(at * SUB, (at + 1) * SUB)
        v = x_ref[rows].reshape(4 * SUB, width)
        matrix = jnp.where(same, jnp.tile(residual[:, lanes], (SUB // 2, 1)), 0.0)
        high, low = split(matrix, 2)
        new = contract(high, v, 1, 0) + contract(low, v, 1, 0)
        sent = inner_ref[rows, :].astype(F32) + outer_ref[rows, :].astype(F32)
        update_high, update_low = split(own_ref[rows, :] + sent, 2)
        spread_high, spread_low = split(jnp.where(mine, columns[4][:, lanes], 0.0), 2)
        new += contract(
            jnp.concatenate([spread_high, spread_high, spread_low], axis=0),
            jnp.concatenate([update_high, update_low, update_high], axis=0),
            0,
            0,
        )
        new_ref[rows] = new.astype(BF).reshape(SUB, 4, width)


def final(static, x, sums, updates, start, previous):
    tokens, width = updates[0].shape
    group = (sums.shape[1] - 128) // 5
    stream_block = pl.BlockSpec((STEP, 4, width), lambda i: (start // STEP + i, 0, 0))
    specs = [
        pl.BlockSpec(memory_space=pltpu.SMEM),
        stream_block,
        pl.BlockSpec((8, 4 * STEP), lambda i: (0, start // STEP + i)),
        pl.BlockSpec((8, STEP), lambda i: (0, 4 * group // STEP + start // STEP + i)),
        pl.BlockSpec((8, 128), lambda i: (0, 5 * group // 128)),
    ]
    specs += [pl.BlockSpec((STEP, width), lambda i: (i, 0))] * 3
    args = [static, x, sums, sums, sums, *updates]
    aliases = {}
    if previous is not None:
        specs.append(pl.BlockSpec(memory_space=pl.ANY))
        aliases = {len(args): 0}
        args.append(previous)
    return pl.pallas_call(
        final_kernel,
        grid=(tokens // STEP,),
        in_specs=specs,
        out_specs=stream_block,
        out_shape=jax.ShapeDtypeStruct(x.shape, BF),
        input_output_aliases=aliases,
        cost_estimate=cost(tokens * 4 * width * 1200, tokens * 22 * width),
        compiler_params=params(),
        name="final",
    )(*args)


def body(streams, proj_master, hc_proj, hc_static, segment_ids, block_mask):
    tokens_local, _, width = streams.shape
    group_size = lax.axis_size("mp")
    place = lax.axis_index("mp").astype(jnp.int32).reshape(1)
    ring = lax.axis_index("blk").astype(jnp.int32).reshape(1)

    proj_rows = jnp.concatenate(
        [hc_proj.T, jnp.ones((1, width), F32), jnp.zeros((1, width), F32)], axis=0
    )
    own = stats(streams, proj_rows)
    parts = list(regroup(place, proj_master, group_size))
    sums, parts = lax.optimization_barrier(([own] + from_others(own, "mp"), parts))

    def gathered(normed):
        rows = lax.all_gather(normed, "mp", axis=0, tiled=True)
        return rows.reshape(group_size, normed.shape[0], width)

    for step in range(1, group_size):
        parts[step] = lax.ppermute(
            parts[step], "mp", [(at, (at + step) % group_size) for at in range(group_size)]
        )
    sums_all, normed = mix(hc_static, streams, sums, 0, tokens_local)
    parts, normed = lax.optimization_barrier((parts, normed))
    rows = gathered(normed)

    pieces = weight_pieces(assemble(place, parts))
    rows, pieces = lax.optimization_barrier((rows, pieces))

    halo = passed_along(segment_ids[-BLOCK:], "blk", 1)
    halo = jnp.where(lax.axis_index("blk") == 0, -1, halo)
    extended = jnp.concatenate([halo, segment_ids])
    key_at = jnp.arange(tokens_local + BLOCK, dtype=jnp.int32)[None, :]
    query_at = jnp.arange(tokens_local, dtype=jnp.int32)[:, None] + BLOCK
    earlier = (extended[None, :] == segment_ids[:, None]) & (key_at < query_at)
    positions = jnp.sum(earlier.astype(jnp.int32), axis=1)
    half = HEAD_DIM // 2
    inverse = 10000.0 ** (-(jnp.arange(half, dtype=F32) * 2.0 / HEAD_DIM))
    angles = positions.astype(F32)[:, None] * inverse[None, :]
    cosine, sine = jnp.cos(angles), jnp.sin(angles)
    cosine = jnp.concatenate([cosine, cosine], axis=1)
    sine = jnp.concatenate([-sine, sine], axis=1)
    windows = []
    for block in range(tokens_local // BLOCK):
        before = extended[block * BLOCK : (block + 1) * BLOCK]
        before = jnp.where(block_mask[block] == 1, before, -1)
        seen = jnp.concatenate([before, segment_ids[block * BLOCK : (block + 1) * BLOCK]])
        for chunk in range(BLOCK // CHUNK):
            windows.append(seen[chunk * CHUNK : chunk * CHUNK + BLOCK + CHUNK])
    key_segments = jnp.stack(windows)[:, None, :]
    query_segments = segment_ids[:, None]

    qkv, halo_rows = qkv_columns(ring, rows, pieces, cosine, sine)
    halo_rows = passed_along(halo_rows, "blk", 1)

    def projected(own):
        other = swapped(own, "mp", 1)
        return project(place, ring, own, other, pieces, group_size)

    last = tokens_local // CHUNK - 1
    chunks = [(halo_rows, 0, 0), (halo_rows, 0, 1)] + [(qkv, 1, at) for at in range(last + 1)]
    parts = {}
    for chunk in reversed(range(last + 1)):
        window = chunks[chunk : chunk + 3]
        own = attend((qkv, chunk), window, query_segments, key_segments, chunk)
        parts[chunk] = projected(own)

    result = None
    for chunk in reversed(range(last + 1)):
        kept, inner, outer = parts[chunk]
        inner = lax.ppermute(inner, "mp", [(1, 2), (2, 1)])
        outer = lax.ppermute(outer, "mp", [(1, 3), (2, 0)])
        updates = [kept, inner, outer]
        result = final(hc_static, streams, sums_all, updates, chunk * CHUNK, result)
    return result


def solution(mesh):
    in_specs = (
        P("blk", None, "mp"),
        P(("blk", "mp"), None, None),
        P("mp", None),
        P(),
        P("blk"),
        P("blk"),
    )
    out_specs = P("blk", None, "mp")
    return jax.shard_map(body, mesh=mesh, in_specs=in_specs, out_specs=out_specs, check_vma=False)
```

```python
import functools

import jax
import jax.numpy as jnp
from jax import lax
from jax.experimental import pallas as pl
from jax.experimental.pallas import tpu as pltpu
from jax.sharding import PartitionSpec as P

D = 2048
HEAD_DIM = 128
BLOCK = 512
CHUNK = 256
SUB = 64
STEP = 128
STREAMS = 4
EPS = 1e-05
BF = jnp.bfloat16
F32 = jnp.float32


def passed_along(value, axis, steps):
    count = lax.axis_size(axis)
    first, last = (max(0, -steps), min(count, count - steps))
    return lax.ppermute(value, axis, [(source, source + steps) for source in range(first, last)])


def from_others(value, axis):
    count = lax.axis_size(axis)
    return [
        lax.ppermute(value, axis, [(source, (source + step) % count) for source in range(count)])
        for step in range(1, count)
    ]


def cost(flops, nbytes, transcendentals=0):
    return pl.CostEstimate(flops=flops, bytes_accessed=nbytes, transcendentals=transcendentals)


def params(limit=60):
    return pltpu.CompilerParams(vmem_limit_bytes=limit << 20)


def split(value, parts):
    out = []
    for _ in range(parts):
        part = value.astype(BF)
        out.append(part)
        value = value - part.astype(F32)
    return out


def contract(a, b, a_dim, b_dim):
    return lax.dot_general(a, b, (((a_dim,), (b_dim,)), ((), ())), preferred_element_type=F32)


def iotas(rows, cols):
    return (
        lax.broadcasted_iota(jnp.int32, (rows, cols), 0),
        lax.broadcasted_iota(jnp.int32, (rows, cols), 1),
    )


def regroup_kernel(place_ref, master_ref, *parts):
    servers = len(parts)
    width = master_ref.shape[-1] // servers
    for step, part_ref in enumerate(parts):
        server = (place_ref[0] + step) % servers
        own = pl.ds(pl.multiple_of(server * width, width), width)
        pair = pl.ds(pl.multiple_of((server // 2) * 2 * width, 2 * width), 2 * width)
        for slot in range(3):
            part_ref[:, slot * width : (slot + 1) * width] = master_ref[:, slot, own].astype(BF)
        part_ref[:, 3 * width :] = master_ref[:, 3, pair].astype(BF)


def regroup(place, master, servers):
    rows, _, total = master.shape
    columns = 5 * total // servers
    return pl.pallas_call(
        regroup_kernel,
        in_specs=[pl.BlockSpec(memory_space=pltpu.SMEM), pl.BlockSpec(memory_space=pltpu.VMEM)],
        out_specs=[pl.BlockSpec(memory_space=pltpu.VMEM)] * servers,
        out_shape=[jax.ShapeDtypeStruct((rows, columns), BF)] * servers,
        cost_estimate=cost(0, rows * total * 26),
        compiler_params=params(),
        name="regroup",
    )(place, master)


def assemble_kernel(place_ref, *refs):
    out_ref = refs[-1]
    parts = refs[:-1]
    rows = parts[0].shape[0]
    for step, part_ref in enumerate(parts):
        source = (place_ref[0] + len(parts) - step) % len(parts)
        out_ref[pl.ds(pl.multiple_of(source * rows, rows), rows), :] = part_ref[...]


def assemble(place, parts):
    rows, columns = parts[0].shape
    return pl.pallas_call(
        assemble_kernel,
        in_specs=[pl.BlockSpec(memory_space=pltpu.SMEM)]
        + [pl.BlockSpec(memory_space=pltpu.VMEM)] * len(parts),
        out_specs=pl.BlockSpec(memory_space=pltpu.VMEM),
        out_shape=jax.ShapeDtypeStruct((rows * len(parts), columns), BF),
        cost_estimate=cost(0, rows * columns * len(parts) * 4),
        compiler_params=params(),
        name="assemble",
    )(place, *parts)


def swapped(value, axis, mask):
    count = lax.axis_size(axis)
    return lax.ppermute(value, axis, [(source, source ^ mask) for source in range(count)])


def weight_pieces(part, beside):
    count = lax.axis_size("blk")
    if count & (count - 1) or part.shape[0] % HEAD_DIM or count > 8:
        return [lax.all_gather(part, "blk", axis=0, tiled=True)], beside
    even = [part] + [swapped(part, "blk", mask) for mask in range(2, count, 2)]
    even, beside = lax.optimization_barrier((even, beside))
    pieces = []
    for piece in even:
        pieces += [piece, swapped(piece, "blk", 1)]
    return pieces, beside


def stats_kernel(x_ref, proj_ref, first_ref, second_ref):
    block, _, width = x_ref.shape
    tokens = block * pl.num_programs(0)
    base = pl.program_id(0) * (block // STEP)
    proj = proj_ref[...]
    pieces = jnp.concatenate(split(proj, 3), axis=0)
    column = jnp.broadcast_to(jnp.sum(proj, axis=1, keepdims=True), (8, 128))
    first_ref[:, 5 * tokens :] = column[0:4]
    second_ref[:, 5 * tokens : 5 * tokens + 128] = column[1:5]
    second_ref[:, 5 * tokens + 128 :] = column[5:6] + jnp.zeros((4, 128), F32)
    row, col = iotas(4 * SUB, 4 * SUB)
    same = (row >> 2) == (col >> 2)
    ring = jnp.where(same, (row - col) & 3, -1)

    @pl.loop(0, block // STEP)
    def _(local):
        step = base + local
        folded = []
        for half in range(STEP // SUB):
            lanes = pl.ds(pl.multiple_of(step * 4 * STEP, 4 * STEP) + half * 4 * SUB, 4 * SUB)
            v = x_ref[pl.ds(local * STEP + half * SUB, SUB)].reshape(4 * SUB, width)
            sums = contract(pieces, v, 1, 1)
            sums = sums[0:8] + sums[8:16] + sums[16:24]
            gram = contract(v, v, 1, 1)
            gram = [
                jnp.sum(jnp.where(ring == shift, gram, 0.0), axis=0, keepdims=True)
                for shift in range(3)
            ]
            first_ref[0:1, lanes] = sums[0:1]
            first_ref[1:2, lanes] = sums[6:7]
            first_ref[2:3, lanes] = gram[0]
            first_ref[3:4, lanes] = gram[1]
            second_ref[:, lanes] = sums[1:5]
            folded.append(jnp.concatenate([gram[2], sums[5:6]], axis=0))
        folded = jnp.concatenate(folded, axis=1)
        lanes = pl.ds(pl.multiple_of(4 * tokens + step * STEP, STEP), STEP)
        for part in range(4):
            piece = folded[:, part * STEP : (part + 1) * STEP]
            first_ref[part : part + 1, lanes] = piece[0:1]
            second_ref[part : part + 1, lanes] = piece[1:2]


def stats(x, proj):
    tokens, _, width = x.shape
    lanes = [5 * tokens + 128, 5 * tokens + 256]
    return pl.pallas_call(
        stats_kernel,
        grid=(tokens // (2 * STEP),),
        in_specs=[
            pl.BlockSpec((2 * STEP, 4, width), lambda i: (i, 0, 0)),
            pl.BlockSpec((8, width), lambda i: (0, 0)),
        ],
        out_specs=[pl.BlockSpec((4, count), lambda i: (0, 0)) for count in lanes],
        out_shape=[jax.ShapeDtypeStruct((4, count), F32) for count in lanes],
        cost_estimate=cost(tokens * 4 * width * 600, tokens * 8 * width),
        compiler_params=params(),
        name="stats",
    )(x, proj)


def unfolded(block):
    return jnp.concatenate([block[part : part + 1] for part in range(4)], axis=1)


def by_stream(static_ref, column, stream):
    value = jnp.full(stream.shape, static_ref[0, column], F32)
    for k in range(1, 4):
        value = jnp.where(stream == k, static_ref[k, column], value)
    return value


def centre(first):
    mean = first[1:2] * (1.0 / D)
    spread = first[2:3] * (1.0 / D) - mean * mean
    return mean, lax.rsqrt(spread + EPS)


def mix_kernel(offset, static_ref, x_ref, own_ref, a_ref, b_ref, c_ref, sums_ref, normed_ref):
    tokens, _, width = x_ref.shape

    @pl.when(pl.program_id(0) == 0)
    def _():
        sums_ref[...] = (own_ref[...] + a_ref[...]) + (b_ref[...] + c_ref[...])

    base = 4 * (offset + pl.program_id(0) * tokens)
    last = sums_ref.shape[1] - 128
    column = sums_ref[0:1, last : last + 1]
    stream = lax.broadcasted_iota(jnp.int32, (1, 4 * STEP), 1) & 3
    static = by_stream(static_ref, 0, stream)
    row, col = iotas(SUB, 4 * SUB)
    mine = row == (col >> 2)

    @pl.loop(0, tokens // STEP)
    def _(step):
        at = pl.multiple_of(base + step * 4 * STEP, 4 * STEP)
        first = sums_ref[:, pl.ds(at, 4 * STEP)]
        folded = pl.multiple_of(4 * (last // 5) + base // 4 + step * STEP, STEP)
        cross = unfolded(sums_ref[:, pl.ds(folded, STEP)])
        mean, inverse = centre(first)
        mix = static + jnp.tanh(inverse * (first[0:1] - mean * column))
        one = jnp.where(stream < 3, pltpu.roll(mix, 4 * STEP - 1, 1), pltpu.roll(mix, 3, 1))
        two = jnp.where(stream < 2, pltpu.roll(mix, 4 * STEP - 2, 1), pltpu.roll(mix, 2, 1))
        linear = mix * first[1:2]
        square = mix * (mix * first[2:3] + 2.0 * one * first[3:4] + two * cross)
        for half in range(STEP // SUB):
            lanes = slice(half * 4 * SUB, (half + 1) * 4 * SUB)
            rows = pl.ds(step * STEP + half * SUB, SUB)
            v = x_ref[rows].reshape(4 * SUB, width)
            matrix = jnp.where(mine, mix[:, lanes], 0.0)
            mixed = contract(jnp.concatenate(split(matrix, 3), axis=0), v, 1, 0)
            mixed = mixed[0:SUB] + mixed[SUB : 2 * SUB] + mixed[2 * SUB : 3 * SUB]
            average = jnp.sum(jnp.where(mine, linear[:, lanes], 0.0), axis=1, keepdims=True)
            power = jnp.sum(jnp.where(mine, square[:, lanes], 0.0), axis=1, keepdims=True)
            average, power = average * (1.0 / D), power * (1.0 / D)
            scale = lax.rsqrt(jnp.maximum(power - average * average, 0.0) + EPS)
            normed_ref[rows, :] = ((mixed - average) * scale).astype(BF)


def mix(static, x, parts, start, tokens):
    width = x.shape[-1]
    lanes = parts[0].shape[1]
    whole = pl.BlockSpec((4, lanes), lambda i: (0, 0))
    return pl.pallas_call(
        functools.partial(mix_kernel, start),
        grid=(tokens // CHUNK,),
        in_specs=[
            pl.BlockSpec(memory_space=pltpu.SMEM),
            pl.BlockSpec((CHUNK, 4, width), lambda i: (start // CHUNK + i, 0, 0)),
        ]
        + [whole] * 4,
        out_specs=[whole, pl.BlockSpec((CHUNK, width), lambda i: (i, 0))],
        out_shape=[
            jax.ShapeDtypeStruct((4, lanes), F32),
            jax.ShapeDtypeStruct((tokens, width), BF),
        ],
        cost_estimate=cost(tokens * 4 * width * 400, tokens * 10 * width),
        compiler_params=params(),
        name="mix",
    )(static, x, *parts)


def qkv_kernel(ring_ref, rows_ref, cosine_ref, sine_ref, *refs):
    out_ref, halo_ref, left_ref = refs[-3:]
    pieces = refs[:-3]
    servers, _, width = rows_ref.shape
    depth = pieces[0].shape[0]
    slot = pl.program_id(0)

    @pl.when(slot == 0)
    def _():
        if len(pieces) == 1:
            for server in range(servers):
                left_ref[:, server * width : (server + 1) * width] = rows_ref[server]
        else:
            for piece in range(len(pieces)):
                source = ring_ref[0] ^ piece
                inside = pl.multiple_of((source % (width // depth)) * depth, depth)
                left_ref[:, piece * depth : (piece + 1) * depth] = rows_ref[
                    source // (width // depth), :, pl.ds(inside, depth)
                ]

    right = jnp.concatenate([piece[...] for piece in pieces], axis=0)
    total = contract(left_ref[...], right, 1, 0)

    @pl.when(slot < 2)
    def _():
        cosine, sine = cosine_ref[...], sine_ref[...]
        for head in range(total.shape[1] // HEAD_DIM):
            part = total[:, head * HEAD_DIM : (head + 1) * HEAD_DIM]
            turned = part * cosine + pltpu.roll(part, HEAD_DIM // 2, 1) * sine
            out_ref[0, :, head * HEAD_DIM : (head + 1) * HEAD_DIM] = turned.astype(BF)

    @pl.when(slot == 2)
    def _():
        out_ref[0] = total.astype(BF)

    halo_ref[0] = out_ref[0, -halo_ref.shape[1] :, :]


def qkv_columns(ring, rows, pieces, cosine, sine):
    servers, tokens, width = rows.shape
    kept = min(BLOCK, tokens)
    table = pl.BlockSpec((tokens, HEAD_DIM), lambda j: (0, 0))
    return pl.pallas_call(
        qkv_kernel,
        grid=(3,),
        in_specs=[
            pl.BlockSpec(memory_space=pltpu.SMEM),
            pl.BlockSpec((servers, tokens, width), lambda j: (0, 0, 0)),
            table,
            table,
        ]
        + [pl.BlockSpec((pieces[0].shape[0], width), lambda j: (0, j))] * len(pieces),
        out_specs=[
            pl.BlockSpec((1, tokens, width), lambda j: (j, 0, 0)),
            pl.BlockSpec((1, kept, width), lambda j: (jnp.maximum(j - 1, 0), 0, 0)),
        ],
        out_shape=[
            jax.ShapeDtypeStruct((3, tokens, width), BF),
            jax.ShapeDtypeStruct((2, kept, width), BF),
        ],
        scratch_shapes=[pltpu.VMEM((tokens, D), BF)],
        cost_estimate=cost(2 * tokens * D * 3 * width, D * 6 * width + tokens * D * 5),
        compiler_params=params(),
        name="qkv",
    )(ring, rows, cosine, sine, *pieces)


def attend_kernel(q_ref, k0, k1, k2, v0, v1, v2, qseg_ref, kseg_ref, attended_ref):
    tokens, width = q_ref.shape[1:]
    window = kseg_ref.shape[-1]
    row, col = iotas(tokens, window)
    allowed = (qseg_ref[...] == kseg_ref[0]) & (col - (window - tokens) <= row)
    bias = jnp.where(allowed, 0.0, -1e30)
    factor = 1.4426950408889634 / HEAD_DIM**0.5
    for head in range(width // HEAD_DIM):
        lanes = slice(head * HEAD_DIM, (head + 1) * HEAD_DIM)
        query = q_ref[0, :, lanes]
        scores = jnp.concatenate(
            [contract(query, k[0, :, lanes], 1, 1) for k in (k0, k1, k2)], axis=1
        )
        scores = scores + bias
        weights = jnp.exp2((scores - jnp.max(scores, axis=1, keepdims=True)) * factor)
        total = jnp.sum(weights, axis=1, keepdims=True)
        values = jnp.concatenate([v[0, :, lanes] for v in (v0, v1, v2)], axis=0)
        attended_ref[:, lanes] = (contract(weights.astype(BF), values, 1, 0) / total).astype(BF)


def attend(query, window, qseg, kseg, chunk):
    source, at = query
    width = source.shape[-1]
    block = (1, CHUNK, width)
    keys = [pl.BlockSpec(block, lambda i, s=slot, r=where: (s, r, 0)) for _, slot, where in window]
    values = [
        pl.BlockSpec(block, lambda i, s=slot + 1, r=where: (s, r, 0)) for _, slot, where in window
    ]
    arrays = [array for array, _, _ in window]
    reach = kseg.shape[-1]
    return pl.pallas_call(
        attend_kernel,
        grid=(1,),
        in_specs=[pl.BlockSpec(block, lambda i: (0, at, 0))]
        + keys
        + values
        + [
            pl.BlockSpec((CHUNK, 1), lambda i: (chunk, 0)),
            pl.BlockSpec((1, 1, reach), lambda i: (chunk, 0, 0)),
        ],
        out_specs=pl.BlockSpec((CHUNK, width), lambda i: (0, 0)),
        out_shape=jax.ShapeDtypeStruct((CHUNK, width), BF),
        cost_estimate=cost(4 * CHUNK * reach * width, CHUNK * width * 16, CHUNK * reach * 4),
        compiler_params=params(),
        name="attend",
    )(source, *arrays, *arrays, qseg, kseg)


def project_kernel(place_ref, ring_ref, own_ref, other_ref, *refs):
    pieces = refs[:-4]
    kept_ref, inner_ref, outer_ref, sums = refs[-4:]
    servers, _, width = sums.shape
    place = place_ref[0]
    even = place % 2 == 0
    own, other = own_ref[...], other_ref[...]
    both = jnp.concatenate([jnp.where(even, own, other), jnp.where(even, other, own)], axis=1)
    depth = pieces[0].shape[0]
    if len(pieces) == 1:
        for server in range(servers):
            rows = pieces[0][server * width : (server + 1) * width, :]
            sums[server] = contract(both, rows, 1, 1)
    else:
        for piece in range(len(pieces)):
            target = ring_ref[0] ^ piece
            inside = pl.multiple_of((target % (width // depth)) * depth, depth)
            sums[target // (width // depth), :, pl.ds(inside, depth)] = contract(
                both, pieces[piece][...], 1, 1
            )
    kept_ref[...] = sums[place]
    low = place < 2
    inner_ref[...] = sums[jnp.where(low, 2, 1)].astype(BF)
    outer_ref[...] = sums[jnp.where(low, 3, 0)].astype(BF)


def project(place, ring, own, other, pieces, servers):
    tokens, width = own.shape
    rows, columns = pieces[0].shape
    pair = 2 * width
    tail = pl.BlockSpec((pl.Element(rows), pl.Element(pair)), lambda i: (0, columns - pair))
    full = pl.BlockSpec((tokens, width), lambda i: (0, 0))
    return pl.pallas_call(
        project_kernel,
        grid=(1,),
        in_specs=[pl.BlockSpec(memory_space=pltpu.SMEM)] * 2 + [full] * 2 + [tail] * len(pieces),
        out_specs=[full] * 3,
        out_shape=[
            jax.ShapeDtypeStruct((tokens, width), F32),
            jax.ShapeDtypeStruct((tokens, width), BF),
            jax.ShapeDtypeStruct((tokens, width), BF),
        ],
        scratch_shapes=[pltpu.VMEM((servers, tokens, width), F32)],
        cost_estimate=cost(2 * tokens * D * pair, D * pair * 2 + tokens * width * 12),
        compiler_params=params(),
        name="project",
    )(place, ring, own, other, *pieces)


def final_kernel(static_ref, x_ref, first_ref, *refs):
    second = [refs[3 * at][...] for at in range(4)]
    folded = [refs[3 * at + 1][...] for at in range(4)]
    column = [refs[3 * at + 2][...] for at in range(4)]
    second, folded, column = [(a + b) + (c + d) for a, b, c, d in (second, folded, column)]
    own_ref, inner_ref, outer_ref = refs[12:15]
    new_ref = refs[-1]
    tokens, _, width = x_ref.shape
    mean, inverse = centre(first_ref[...])
    stream = lax.broadcasted_iota(jnp.int32, (1, 4 * tokens), 1) & 3
    projected = [second[at : at + 1] for at in range(4)] + [unfolded(folded)]
    totals = [column[at : at + 1, 0:1] for at in range(4)] + [column[0:1, 128:129]]
    columns = [
        by_stream(static_ref, 1 + at, stream)
        + jnp.tanh(inverse * (projected[at] - mean * totals[at]))
        for at in range(5)
    ]
    residual = jnp.concatenate(columns[:4] + columns[:4], axis=0)
    row, col = iotas(4 * SUB, 4 * SUB)
    same = (row >> 2) == (col >> 2)
    row, col = iotas(SUB, 4 * SUB)
    mine = row == (col >> 2)
    for at in range(tokens // SUB):
        lanes = slice(at * 4 * SUB, (at + 1) * 4 * SUB)
        rows = slice(at * SUB, (at + 1) * SUB)
        v = x_ref[rows].reshape(4 * SUB, width)
        matrix = jnp.where(same, jnp.tile(residual[:, lanes], (SUB // 2, 1)), 0.0)
        high, low = split(matrix, 2)
        new = contract(high, v, 1, 0) + contract(low, v, 1, 0)
        sent = inner_ref[rows, :].astype(F32) + outer_ref[rows, :].astype(F32)
        update_high, update_low = split(own_ref[rows, :] + sent, 2)
        spread_high, spread_low = split(jnp.where(mine, columns[4][:, lanes], 0.0), 2)
        new += contract(
            jnp.concatenate([spread_high, spread_high, spread_low], axis=0),
            jnp.concatenate([update_high, update_low, update_high], axis=0),
            0,
            0,
        )
        new_ref[rows] = new.astype(BF).reshape(SUB, 4, width)


def final(static, x, sums, second, updates, start, previous):
    tokens, width = updates[0].shape
    group = x.shape[0]
    stream_block = pl.BlockSpec((STEP, 4, width), lambda i: (start // STEP + i, 0, 0))
    specs = [
        pl.BlockSpec(memory_space=pltpu.SMEM),
        stream_block,
        pl.BlockSpec((4, 4 * STEP), lambda i: (0, start // STEP + i)),
    ]
    specs += [
        pl.BlockSpec((4, 4 * STEP), lambda i: (0, start // STEP + i)),
        pl.BlockSpec((4, STEP), lambda i: (0, 4 * group // STEP + start // STEP + i)),
        pl.BlockSpec((4, 256), lambda i: (0, 5 * group // 256)),
    ] * 4
    seconds = [array for array in second for _ in range(3)]
    specs += [pl.BlockSpec((STEP, width), lambda i: (i, 0))] * 3
    args = [static, x, sums, *seconds, *updates]
    aliases = {}
    if previous is not None:
        specs.append(pl.BlockSpec(memory_space=pl.ANY))
        aliases = {len(args): 0}
        args.append(previous)
    return pl.pallas_call(
        final_kernel,
        grid=(tokens // STEP,),
        in_specs=specs,
        out_specs=stream_block,
        out_shape=jax.ShapeDtypeStruct(x.shape, BF),
        input_output_aliases=aliases,
        cost_estimate=cost(tokens * 4 * width * 1200, tokens * 22 * width),
        compiler_params=params(),
        name="final",
    )(*args)


def body(streams, proj_master, hc_proj, hc_static, segment_ids, block_mask):
    tokens_local, _, width = streams.shape
    group_size = lax.axis_size("mp")
    place = lax.axis_index("mp").astype(jnp.int32).reshape(1)
    ring = lax.axis_index("blk").astype(jnp.int32).reshape(1)

    proj_rows = jnp.concatenate(
        [hc_proj.T, jnp.ones((1, width), F32), jnp.zeros((1, width), F32)], axis=0
    )
    first, second = stats(streams, proj_rows)
    parts = list(regroup(place, proj_master, group_size))
    halo = passed_along(segment_ids[-BLOCK:], "blk", 1)
    sums = [first] + from_others(first, "mp")
    sums, parts, halo = lax.optimization_barrier((sums, parts, halo))
    for step in range(1, group_size):
        parts[step] = lax.ppermute(
            parts[step], "mp", [(at, (at + step) % group_size) for at in range(group_size)]
        )

    sums_all, normed_late = mix(hc_static, streams, sums, CHUNK, tokens_local - CHUNK)
    _, normed_first = mix(hc_static, streams, sums, 0, CHUNK)
    parts, normed_late, normed_first = lax.optimization_barrier((parts, normed_late, normed_first))
    rows_late = lax.all_gather(normed_late, "mp", axis=0, tiled=True)
    rows_late = rows_late.reshape(group_size, tokens_local - CHUNK, width)
    others = from_others(normed_first, "mp")
    pieces, others = weight_pieces(assemble(place, parts), others)
    rows_first = assemble(place, [normed_first] + others)
    rows_first = rows_first.reshape(group_size, CHUNK, width)
    second, pieces = lax.optimization_barrier((second, pieces))
    second = [second] + from_others(second, "mp")

    halo = jnp.where(lax.axis_index("blk") == 0, -1, halo)
    extended = jnp.concatenate([halo, segment_ids])
    key_at = jnp.arange(tokens_local + BLOCK, dtype=jnp.int32)[None, :]
    query_at = jnp.arange(tokens_local, dtype=jnp.int32)[:, None] + BLOCK
    earlier = (extended[None, :] == segment_ids[:, None]) & (key_at < query_at)
    positions = jnp.sum(earlier.astype(jnp.int32), axis=1)
    half = HEAD_DIM // 2
    inverse = 10000.0 ** (-(jnp.arange(half, dtype=F32) * 2.0 / HEAD_DIM))
    angles = positions.astype(F32)[:, None] * inverse[None, :]
    cosine, sine = jnp.cos(angles), jnp.sin(angles)
    cosine = jnp.concatenate([cosine, cosine], axis=1)
    sine = jnp.concatenate([-sine, sine], axis=1)
    windows = []
    for block in range(tokens_local // BLOCK):
        before = extended[block * BLOCK : (block + 1) * BLOCK]
        before = jnp.where(block_mask[block] == 1, before, -1)
        seen = jnp.concatenate([before, segment_ids[block * BLOCK : (block + 1) * BLOCK]])
        for chunk in range(BLOCK // CHUNK):
            windows.append(seen[chunk * CHUNK : chunk * CHUNK + BLOCK + CHUNK])
    key_segments = jnp.stack(windows)[:, None, :]
    query_segments = segment_ids[:, None]

    qkv_first, _ = qkv_columns(ring, rows_first, pieces, cosine[:CHUNK], sine[:CHUNK])
    rows_late, qkv_first, second = lax.optimization_barrier((rows_late, qkv_first, second))
    qkv_late, halo_rows = qkv_columns(ring, rows_late, pieces, cosine[CHUNK:], sine[CHUNK:])
    halo_rows = passed_along(halo_rows, "blk", 1)

    def projected(own):
        other = swapped(own, "mp", 1)
        return project(place, ring, own, other, pieces, group_size)

    last = tokens_local // CHUNK - 1
    chunks = [(halo_rows, 0, 0), (halo_rows, 0, 1), (qkv_first, 1, 0)]
    chunks += [(qkv_late, 1, at) for at in range(last)]
    parts = {}
    for chunk in reversed(range(last + 1)):
        window = chunks[chunk : chunk + 3]
        source, _, at = window[-1]
        own = attend((source, at), window, query_segments, key_segments, chunk)
        parts[chunk] = projected(own)

    result = None
    for chunk in reversed(range(last + 1)):
        kept, inner, outer = parts[chunk]
        inner = lax.ppermute(inner, "mp", [(1, 2), (2, 1)])
        outer = lax.ppermute(outer, "mp", [(1, 3), (2, 0)])
        updates = [kept, inner, outer]
        result = final(hc_static, streams, sums_all, second, updates, chunk * CHUNK, result)
    return result


def solution(mesh):
    in_specs = (
        P("blk", None, "mp"),
        P(("blk", "mp"), None, None),
        P("mp", None),
        P(),
        P("blk"),
        P("blk"),
    )
    out_specs = P("blk", None, "mp")
    return jax.shard_map(body, mesh=mesh, in_specs=in_specs, out_specs=out_specs, check_vma=False)
```

```python
import functools

import jax
import jax.numpy as jnp
from jax import lax
from jax.experimental import pallas as pl
from jax.experimental.pallas import tpu as pltpu
from jax.sharding import PartitionSpec as P

D = 2048
HEAD_DIM = 128
BLOCK = 512
CHUNK = 256
SUB = 64
STEP = 128
STREAMS = 4
EPS = 1e-05
BF = jnp.bfloat16
F32 = jnp.float32


def passed_along(value, axis, steps):
    count = lax.axis_size(axis)
    first, last = (max(0, -steps), min(count, count - steps))
    return lax.ppermute(value, axis, [(source, source + steps) for source in range(first, last)])


def from_others(value, axis):
    count = lax.axis_size(axis)
    return [
        lax.ppermute(value, axis, [(source, (source + step) % count) for source in range(count)])
        for step in range(1, count)
    ]


def cost(flops, nbytes, transcendentals=0):
    return pl.CostEstimate(flops=flops, bytes_accessed=nbytes, transcendentals=transcendentals)


def params(limit=60):
    return pltpu.CompilerParams(vmem_limit_bytes=limit << 20)


def split(value, parts):
    out = []
    for _ in range(parts):
        part = value.astype(BF)
        out.append(part)
        value = value - part.astype(F32)
    return out


def contract(a, b, a_dim, b_dim):
    return lax.dot_general(a, b, (((a_dim,), (b_dim,)), ((), ())), preferred_element_type=F32)


def iotas(rows, cols):
    return (
        lax.broadcasted_iota(jnp.int32, (rows, cols), 0),
        lax.broadcasted_iota(jnp.int32, (rows, cols), 1),
    )


def regroup_kernel(place_ref, master_ref, *parts):
    servers = len(parts)
    width = master_ref.shape[-1] // servers
    for step, part_ref in enumerate(parts):
        server = (place_ref[0] + step) % servers
        own = pl.ds(pl.multiple_of(server * width, width), width)
        pair = pl.ds(pl.multiple_of((server // 2) * 2 * width, 2 * width), 2 * width)
        for slot in range(3):
            part_ref[:, slot * width : (slot + 1) * width] = master_ref[:, slot, own].astype(BF)
        part_ref[:, 3 * width :] = master_ref[:, 3, pair].astype(BF)


def regroup(place, master, servers):
    rows, _, total = master.shape
    columns = 5 * total // servers
    return pl.pallas_call(
        regroup_kernel,
        in_specs=[pl.BlockSpec(memory_space=pltpu.SMEM), pl.BlockSpec(memory_space=pltpu.VMEM)],
        out_specs=[pl.BlockSpec(memory_space=pltpu.VMEM)] * servers,
        out_shape=[jax.ShapeDtypeStruct((rows, columns), BF)] * servers,
        cost_estimate=cost(0, rows * total * 26),
        compiler_params=params(),
        name="regroup",
    )(place, master)


def assemble_kernel(place_ref, *refs):
    out_ref = refs[-1]
    parts = refs[:-1]
    rows = parts[0].shape[0]
    for step, part_ref in enumerate(parts):
        source = (place_ref[0] + len(parts) - step) % len(parts)
        out_ref[pl.ds(pl.multiple_of(source * rows, rows), rows), :] = part_ref[...]


def assemble(place, parts):
    rows, columns = parts[0].shape
    return pl.pallas_call(
        assemble_kernel,
        in_specs=[pl.BlockSpec(memory_space=pltpu.SMEM)]
        + [pl.BlockSpec(memory_space=pltpu.VMEM)] * len(parts),
        out_specs=pl.BlockSpec(memory_space=pltpu.VMEM),
        out_shape=jax.ShapeDtypeStruct((rows * len(parts), columns), BF),
        cost_estimate=cost(0, rows * columns * len(parts) * 4),
        compiler_params=params(),
        name="assemble",
    )(place, *parts)


def swapped(value, axis, mask):
    count = lax.axis_size(axis)
    return lax.ppermute(value, axis, [(source, source ^ mask) for source in range(count)])


def weight_pieces(part):
    count = lax.axis_size("blk")
    if count & (count - 1) or part.shape[0] % HEAD_DIM or count > 8:
        return [lax.all_gather(part, "blk", axis=0, tiled=True)]
    pieces = {0: part}
    for mask in range(2, count, 2):
        pieces[mask] = swapped(part, "blk", mask)
    for mask in range(0, count, 2):
        pieces[mask + 1] = swapped(pieces[mask], "blk", 1)
    return [pieces[mask] for mask in range(count)]


def stats_kernel(x_ref, proj_ref, first_ref, second_ref):
    block, _, width = x_ref.shape
    tokens = block * pl.num_programs(0)
    base = pl.program_id(0) * (block // STEP)
    proj = proj_ref[...]
    pieces = jnp.concatenate(split(proj, 3), axis=0)
    column = jnp.broadcast_to(jnp.sum(proj, axis=1, keepdims=True), (8, 128))
    first_ref[:, 5 * tokens :] = column[0:4]
    second_ref[:, 5 * tokens : 5 * tokens + 128] = column[1:5]
    second_ref[:, 5 * tokens + 128 :] = column[5:6] + jnp.zeros((4, 128), F32)
    row, col = iotas(4 * SUB, 4 * SUB)
    same = (row >> 2) == (col >> 2)
    ring = jnp.where(same, (row - col) & 3, -1)

    @pl.loop(0, block // STEP)
    def _(local):
        step = base + local
        folded = []
        for half in range(STEP // SUB):
            lanes = pl.ds(pl.multiple_of(step * 4 * STEP, 4 * STEP) + half * 4 * SUB, 4 * SUB)
            v = x_ref[pl.ds(local * STEP + half * SUB, SUB)].reshape(4 * SUB, width)
            sums = contract(pieces, v, 1, 1)
            sums = sums[0:8] + sums[8:16] + sums[16:24]
            gram = contract(v, v, 1, 1)
            gram = [
                jnp.sum(jnp.where(ring == shift, gram, 0.0), axis=0, keepdims=True)
                for shift in range(3)
            ]
            first_ref[0:1, lanes] = sums[0:1]
            first_ref[1:2, lanes] = sums[6:7]
            first_ref[2:3, lanes] = gram[0]
            first_ref[3:4, lanes] = gram[1]
            second_ref[:, lanes] = sums[1:5]
            folded.append(jnp.concatenate([gram[2], sums[5:6]], axis=0))
        folded = jnp.concatenate(folded, axis=1)
        lanes = pl.ds(pl.multiple_of(4 * tokens + step * STEP, STEP), STEP)
        for part in range(4):
            piece = folded[:, part * STEP : (part + 1) * STEP]
            first_ref[part : part + 1, lanes] = piece[0:1]
            second_ref[part : part + 1, lanes] = piece[1:2]


def stats(x, proj):
    tokens, _, width = x.shape
    lanes = [5 * tokens + 128, 5 * tokens + 256]
    return pl.pallas_call(
        stats_kernel,
        grid=(tokens // (2 * STEP),),
        in_specs=[
            pl.BlockSpec((2 * STEP, 4, width), lambda i: (i, 0, 0)),
            pl.BlockSpec((8, width), lambda i: (0, 0)),
        ],
        out_specs=[pl.BlockSpec((4, count), lambda i: (0, 0)) for count in lanes],
        out_shape=[jax.ShapeDtypeStruct((4, count), F32) for count in lanes],
        cost_estimate=cost(tokens * 4 * width * 600, tokens * 8 * width),
        compiler_params=params(),
        name="stats",
    )(x, proj)


def unfolded(block):
    return jnp.concatenate([block[part : part + 1] for part in range(4)], axis=1)


def by_stream(static_ref, column, stream):
    value = jnp.full(stream.shape, static_ref[0, column], F32)
    for k in range(1, 4):
        value = jnp.where(stream == k, static_ref[k, column], value)
    return value


def centre(first):
    mean = first[1:2] * (1.0 / D)
    spread = first[2:3] * (1.0 / D) - mean * mean
    return mean, lax.rsqrt(spread + EPS)


def mix_kernel(offset, static_ref, x_ref, own_ref, a_ref, b_ref, c_ref, sums_ref, normed_ref):
    tokens, _, width = x_ref.shape

    @pl.when(pl.program_id(0) == 0)
    def _():
        sums_ref[...] = (own_ref[...] + a_ref[...]) + (b_ref[...] + c_ref[...])

    base = 4 * (offset + pl.program_id(0) * tokens)
    last = sums_ref.shape[1] - 128
    column = sums_ref[0:1, last : last + 1]
    stream = lax.broadcasted_iota(jnp.int32, (1, 4 * STEP), 1) & 3
    static = by_stream(static_ref, 0, stream)
    row, col = iotas(SUB, 4 * SUB)
    mine = row == (col >> 2)

    @pl.loop(0, tokens // STEP)
    def _(step):
        at = pl.multiple_of(base + step * 4 * STEP, 4 * STEP)
        first = sums_ref[:, pl.ds(at, 4 * STEP)]
        folded = pl.multiple_of(4 * (last // 5) + base // 4 + step * STEP, STEP)
        cross = unfolded(sums_ref[:, pl.ds(folded, STEP)])
        mean, inverse = centre(first)
        mix = static + jnp.tanh(inverse * (first[0:1] - mean * column))
        one = jnp.where(stream < 3, pltpu.roll(mix, 4 * STEP - 1, 1), pltpu.roll(mix, 3, 1))
        two = jnp.where(stream < 2, pltpu.roll(mix, 4 * STEP - 2, 1), pltpu.roll(mix, 2, 1))
        linear = mix * first[1:2]
        square = mix * (mix * first[2:3] + 2.0 * one * first[3:4] + two * cross)
        for half in range(STEP // SUB):
            lanes = slice(half * 4 * SUB, (half + 1) * 4 * SUB)
            rows = pl.ds(step * STEP + half * SUB, SUB)
            v = x_ref[rows].reshape(4 * SUB, width)
            matrix = jnp.where(mine, mix[:, lanes], 0.0)
            mixed = contract(jnp.concatenate(split(matrix, 3), axis=0), v, 1, 0)
            mixed = mixed[0:SUB] + mixed[SUB : 2 * SUB] + mixed[2 * SUB : 3 * SUB]
            average = jnp.sum(jnp.where(mine, linear[:, lanes], 0.0), axis=1, keepdims=True)
            power = jnp.sum(jnp.where(mine, square[:, lanes], 0.0), axis=1, keepdims=True)
            average, power = average * (1.0 / D), power * (1.0 / D)
            scale = lax.rsqrt(jnp.maximum(power - average * average, 0.0) + EPS)
            normed_ref[rows, :] = ((mixed - average) * scale).astype(BF)


def mix(static, x, parts, start, tokens):
    width = x.shape[-1]
    lanes = parts[0].shape[1]
    whole = pl.BlockSpec((4, lanes), lambda i: (0, 0))
    return pl.pallas_call(
        functools.partial(mix_kernel, start),
        grid=(tokens // CHUNK,),
        in_specs=[
            pl.BlockSpec(memory_space=pltpu.SMEM),
            pl.BlockSpec((CHUNK, 4, width), lambda i: (start // CHUNK + i, 0, 0)),
        ]
        + [whole] * 4,
        out_specs=[whole, pl.BlockSpec((CHUNK, width), lambda i: (i, 0))],
        out_shape=[
            jax.ShapeDtypeStruct((4, lanes), F32),
            jax.ShapeDtypeStruct((tokens, width), BF),
        ],
        cost_estimate=cost(tokens * 4 * width * 400, tokens * 10 * width),
        compiler_params=params(),
        name="mix",
    )(static, x, *parts)


def qkv_kernel(ring_ref, rows_ref, cosine_ref, sine_ref, *refs):
    out_ref, halo_ref = refs[-2:]
    pieces = refs[:-2]
    servers, _, width = rows_ref.shape
    depth = pieces[0].shape[0]
    if len(pieces) == 1:
        left = [rows_ref[server] for server in range(servers)]
    else:
        left = []
        for piece in range(len(pieces)):
            source = ring_ref[0] ^ piece
            inside = pl.multiple_of((source % (width // depth)) * depth, depth)
            left.append(rows_ref[source // (width // depth), :, pl.ds(inside, depth)])
    left = jnp.concatenate(left, axis=1)
    right = jnp.concatenate([piece[...] for piece in pieces], axis=0)
    total = contract(left, right, 1, 0)
    slot = pl.program_id(0)

    @pl.when(slot < 2)
    def _():
        cosine, sine = cosine_ref[...], sine_ref[...]
        for head in range(total.shape[1] // HEAD_DIM):
            part = total[:, head * HEAD_DIM : (head + 1) * HEAD_DIM]
            turned = part * cosine + pltpu.roll(part, HEAD_DIM // 2, 1) * sine
            out_ref[0, :, head * HEAD_DIM : (head + 1) * HEAD_DIM] = turned.astype(BF)

    @pl.when(slot == 2)
    def _():
        out_ref[0] = total.astype(BF)

    halo_ref[0] = out_ref[0, -BLOCK:, :]


def qkv_columns(ring, rows, pieces, cosine, sine):
    servers, tokens, width = rows.shape
    table = pl.BlockSpec((tokens, HEAD_DIM), lambda j: (0, 0))
    return pl.pallas_call(
        qkv_kernel,
        grid=(3,),
        in_specs=[
            pl.BlockSpec(memory_space=pltpu.SMEM),
            pl.BlockSpec((servers, tokens, width), lambda j: (0, 0, 0)),
            table,
            table,
        ]
        + [pl.BlockSpec((pieces[0].shape[0], width), lambda j: (0, j))] * len(pieces),
        out_specs=[
            pl.BlockSpec((1, tokens, width), lambda j: (j, 0, 0)),
            pl.BlockSpec((1, BLOCK, width), lambda j: (jnp.maximum(j - 1, 0), 0, 0)),
        ],
        out_shape=[
            jax.ShapeDtypeStruct((3, tokens, width), BF),
            jax.ShapeDtypeStruct((2, BLOCK, width), BF),
        ],
        cost_estimate=cost(2 * tokens * D * 3 * width, D * 6 * width + tokens * D * 5),
        compiler_params=params(),
        name="qkv",
    )(ring, rows, cosine, sine, *pieces)


def attend_kernel(q_ref, k0, k1, k2, v0, v1, v2, qseg_ref, kseg_ref, attended_ref):
    tokens, width = q_ref.shape[1:]
    window = kseg_ref.shape[-1]
    row, col = iotas(tokens, window)
    allowed = (qseg_ref[...] == kseg_ref[0]) & (col - (window - tokens) <= row)
    bias = jnp.where(allowed, 0.0, -1e30)
    factor = 1.4426950408889634 / HEAD_DIM**0.5
    for head in range(width // HEAD_DIM):
        lanes = slice(head * HEAD_DIM, (head + 1) * HEAD_DIM)
        query = q_ref[0, :, lanes]
        scores = jnp.concatenate(
            [contract(query, k[0, :, lanes], 1, 1) for k in (k0, k1, k2)], axis=1
        )
        scores = scores + bias
        weights = jnp.exp2((scores - jnp.max(scores, axis=1, keepdims=True)) * factor)
        total = jnp.sum(weights, axis=1, keepdims=True)
        values = jnp.concatenate([v[0, :, lanes] for v in (v0, v1, v2)], axis=0)
        attended_ref[:, lanes] = (contract(weights.astype(BF), values, 1, 0) / total).astype(BF)


def attend(query, window, qseg, kseg, chunk):
    source, at = query
    width = source.shape[-1]
    block = (1, CHUNK, width)
    keys = [pl.BlockSpec(block, lambda i, s=slot, r=where: (s, r, 0)) for _, slot, where in window]
    values = [
        pl.BlockSpec(block, lambda i, s=slot + 1, r=where: (s, r, 0)) for _, slot, where in window
    ]
    arrays = [array for array, _, _ in window]
    reach = kseg.shape[-1]
    return pl.pallas_call(
        attend_kernel,
        grid=(1,),
        in_specs=[pl.BlockSpec(block, lambda i: (0, at, 0))]
        + keys
        + values
        + [
            pl.BlockSpec((CHUNK, 1), lambda i: (chunk, 0)),
            pl.BlockSpec((1, 1, reach), lambda i: (chunk, 0, 0)),
        ],
        out_specs=pl.BlockSpec((CHUNK, width), lambda i: (0, 0)),
        out_shape=jax.ShapeDtypeStruct((CHUNK, width), BF),
        cost_estimate=cost(4 * CHUNK * reach * width, CHUNK * width * 16, CHUNK * reach * 4),
        compiler_params=params(),
        name="attend",
    )(source, *arrays, *arrays, qseg, kseg)


def project_kernel(place_ref, ring_ref, own_ref, other_ref, *refs):
    pieces = refs[:-4]
    kept_ref, inner_ref, outer_ref, sums = refs[-4:]
    servers, _, width = sums.shape
    place = place_ref[0]
    even = place % 2 == 0
    own, other = own_ref[...], other_ref[...]
    both = jnp.concatenate([jnp.where(even, own, other), jnp.where(even, other, own)], axis=1)
    depth = pieces[0].shape[0]
    if len(pieces) == 1:
        for server in range(servers):
            rows = pieces[0][server * width : (server + 1) * width, :]
            sums[server] = contract(both, rows, 1, 1)
    else:
        for piece in range(len(pieces)):
            target = ring_ref[0] ^ piece
            inside = pl.multiple_of((target % (width // depth)) * depth, depth)
            sums[target // (width // depth), :, pl.ds(inside, depth)] = contract(
                both, pieces[piece][...], 1, 1
            )
    kept_ref[...] = sums[place]
    low = place < 2
    inner_ref[...] = sums[jnp.where(low, 2, 1)].astype(BF)
    outer_ref[...] = sums[jnp.where(low, 3, 0)].astype(BF)


def project(place, ring, own, other, pieces, servers):
    tokens, width = own.shape
    rows, columns = pieces[0].shape
    pair = 2 * width
    tail = pl.BlockSpec((pl.Element(rows), pl.Element(pair)), lambda i: (0, columns - pair))
    full = pl.BlockSpec((tokens, width), lambda i: (0, 0))
    return pl.pallas_call(
        project_kernel,
        grid=(1,),
        in_specs=[pl.BlockSpec(memory_space=pltpu.SMEM)] * 2 + [full] * 2 + [tail] * len(pieces),
        out_specs=[full] * 3,
        out_shape=[
            jax.ShapeDtypeStruct((tokens, width), F32),
            jax.ShapeDtypeStruct((tokens, width), BF),
            jax.ShapeDtypeStruct((tokens, width), BF),
        ],
        scratch_shapes=[pltpu.VMEM((servers, tokens, width), F32)],
        cost_estimate=cost(2 * tokens * D * pair, D * pair * 2 + tokens * width * 12),
        compiler_params=params(),
        name="project",
    )(place, ring, own, other, *pieces)


def final_kernel(static_ref, x_ref, first_ref, *refs):
    second = [refs[3 * at][...] for at in range(4)]
    folded = [refs[3 * at + 1][...] for at in range(4)]
    column = [refs[3 * at + 2][...] for at in range(4)]
    second, folded, column = [(a + b) + (c + d) for a, b, c, d in (second, folded, column)]
    own_ref, inner_ref, outer_ref = refs[12:15]
    new_ref = refs[-1]
    tokens, _, width = x_ref.shape
    mean, inverse = centre(first_ref[...])
    stream = lax.broadcasted_iota(jnp.int32, (1, 4 * tokens), 1) & 3
    projected = [second[at : at + 1] for at in range(4)] + [unfolded(folded)]
    totals = [column[at : at + 1, 0:1] for at in range(4)] + [column[0:1, 128:129]]
    columns = [
        by_stream(static_ref, 1 + at, stream)
        + jnp.tanh(inverse * (projected[at] - mean * totals[at]))
        for at in range(5)
    ]
    residual = jnp.concatenate(columns[:4] + columns[:4], axis=0)
    row, col = iotas(4 * SUB, 4 * SUB)
    same = (row >> 2) == (col >> 2)
    row, col = iotas(SUB, 4 * SUB)
    mine = row == (col >> 2)
    for at in range(tokens // SUB):
        lanes = slice(at * 4 * SUB, (at + 1) * 4 * SUB)
        rows = slice(at * SUB, (at + 1) * SUB)
        v = x_ref[rows].reshape(4 * SUB, width)
        matrix = jnp.where(same, jnp.tile(residual[:, lanes], (SUB // 2, 1)), 0.0)
        high, low = split(matrix, 2)
        new = contract(high, v, 1, 0) + contract(low, v, 1, 0)
        sent = inner_ref[rows, :].astype(F32) + outer_ref[rows, :].astype(F32)
        update_high, update_low = split(own_ref[rows, :] + sent, 2)
        spread_high, spread_low = split(jnp.where(mine, columns[4][:, lanes], 0.0), 2)
        new += contract(
            jnp.concatenate([spread_high, spread_high, spread_low], axis=0),
            jnp.concatenate([update_high, update_low, update_high], axis=0),
            0,
            0,
        )
        new_ref[rows] = new.astype(BF).reshape(SUB, 4, width)


def final(static, x, sums, second, updates, start, previous):
    tokens, width = updates[0].shape
    group = x.shape[0]
    stream_block = pl.BlockSpec((STEP, 4, width), lambda i: (start // STEP + i, 0, 0))
    specs = [
        pl.BlockSpec(memory_space=pltpu.SMEM),
        stream_block,
        pl.BlockSpec((4, 4 * STEP), lambda i: (0, start // STEP + i)),
    ]
    specs += [
        pl.BlockSpec((4, 4 * STEP), lambda i: (0, start // STEP + i)),
        pl.BlockSpec((4, STEP), lambda i: (0, 4 * group // STEP + start // STEP + i)),
        pl.BlockSpec((4, 256), lambda i: (0, 5 * group // 256)),
    ] * 4
    seconds = [array for array in second for _ in range(3)]
    specs += [pl.BlockSpec((STEP, width), lambda i: (i, 0))] * 3
    args = [static, x, sums, *seconds, *updates]
    aliases = {}
    if previous is not None:
        specs.append(pl.BlockSpec(memory_space=pl.ANY))
        aliases = {len(args): 0}
        args.append(previous)
    return pl.pallas_call(
        final_kernel,
        grid=(tokens // STEP,),
        in_specs=specs,
        out_specs=stream_block,
        out_shape=jax.ShapeDtypeStruct(x.shape, BF),
        input_output_aliases=aliases,
        cost_estimate=cost(tokens * 4 * width * 1200, tokens * 22 * width),
        compiler_params=params(),
        name="final",
    )(*args)


def body(streams, proj_master, hc_proj, hc_static, segment_ids, block_mask):
    tokens_local, _, width = streams.shape
    group_size = lax.axis_size("mp")
    place = lax.axis_index("mp").astype(jnp.int32).reshape(1)
    ring = lax.axis_index("blk").astype(jnp.int32).reshape(1)

    proj_rows = jnp.concatenate(
        [hc_proj.T, jnp.ones((1, width), F32), jnp.zeros((1, width), F32)], axis=0
    )
    parts = list(regroup(place, proj_master, group_size))
    proj_rows, parts = lax.optimization_barrier((proj_rows, parts))
    for step in range(1, group_size):
        parts[step] = lax.ppermute(
            parts[step], "mp", [(at, (at + step) % group_size) for at in range(group_size)]
        )
    first, second = stats(streams, proj_rows)
    halo = passed_along(segment_ids[-BLOCK:], "blk", 1)

    sums = [first] + from_others(first, "mp")
    sums_all, normed = mix(hc_static, streams, sums, 0, tokens_local)
    parts, normed, halo = lax.optimization_barrier((parts, normed, halo))
    rows = lax.all_gather(normed, "mp", axis=0, tiled=True)
    rows = rows.reshape(group_size, tokens_local, width)

    pieces = weight_pieces(assemble(place, parts))
    second, pieces = lax.optimization_barrier((second, pieces))
    second = [second] + from_others(second, "mp")
    rows, pieces, second = lax.optimization_barrier((rows, pieces, second))

    halo = jnp.where(lax.axis_index("blk") == 0, -1, halo)
    extended = jnp.concatenate([halo, segment_ids])
    key_at = jnp.arange(tokens_local + BLOCK, dtype=jnp.int32)[None, :]
    query_at = jnp.arange(tokens_local, dtype=jnp.int32)[:, None] + BLOCK
    earlier = (extended[None, :] == segment_ids[:, None]) & (key_at < query_at)
    positions = jnp.sum(earlier.astype(jnp.int32), axis=1)
    half = HEAD_DIM // 2
    inverse = 10000.0 ** (-(jnp.arange(half, dtype=F32) * 2.0 / HEAD_DIM))
    angles = positions.astype(F32)[:, None] * inverse[None, :]
    cosine, sine = jnp.cos(angles), jnp.sin(angles)
    cosine = jnp.concatenate([cosine, cosine], axis=1)
    sine = jnp.concatenate([-sine, sine], axis=1)
    windows = []
    for block in range(tokens_local // BLOCK):
        before = extended[block * BLOCK : (block + 1) * BLOCK]
        before = jnp.where(block_mask[block] == 1, before, -1)
        seen = jnp.concatenate([before, segment_ids[block * BLOCK : (block + 1) * BLOCK]])
        for chunk in range(BLOCK // CHUNK):
            windows.append(seen[chunk * CHUNK : chunk * CHUNK + BLOCK + CHUNK])
    key_segments = jnp.stack(windows)[:, None, :]
    query_segments = segment_ids[:, None]

    qkv, halo_rows = qkv_columns(ring, rows, pieces, cosine, sine)
    halo_rows = passed_along(halo_rows, "blk", 1)

    def projected(own):
        other = swapped(own, "mp", 1)
        return project(place, ring, own, other, pieces, group_size)

    last = tokens_local // CHUNK - 1
    chunks = [(halo_rows, 0, 0), (halo_rows, 0, 1)] + [(qkv, 1, at) for at in range(last + 1)]
    parts = {}
    for chunk in reversed(range(last + 1)):
        window = chunks[chunk : chunk + 3]
        own = attend((qkv, chunk), window, query_segments, key_segments, chunk)
        parts[chunk] = projected(own)

    result = None
    for chunk in reversed(range(last + 1)):
        kept, inner, outer = parts[chunk]
        inner = lax.ppermute(inner, "mp", [(1, 2), (2, 1)])
        outer = lax.ppermute(outer, "mp", [(1, 3), (2, 0)])
        updates = [kept, inner, outer]
        result = final(hc_static, streams, sums_all, second, updates, chunk * CHUNK, result)
    return result


def solution(mesh):
    in_specs = (
        P("blk", None, "mp"),
        P(("blk", "mp"), None, None),
        P("mp", None),
        P(),
        P("blk"),
        P("blk"),
    )
    out_specs = P("blk", None, "mp")
    return jax.shard_map(body, mesh=mesh, in_specs=in_specs, out_specs=out_specs, check_vma=False)
```

```python
import functools

import jax
import jax.numpy as jnp
from jax import lax
from jax.experimental import pallas as pl
from jax.experimental.pallas import tpu as pltpu
from jax.sharding import PartitionSpec as P

D = 2048
HEAD_DIM = 128
BLOCK = 512
CHUNK = 256
SUB = 64
STEP = 128
STREAMS = 4
EPS = 1e-05
BF = jnp.bfloat16
F32 = jnp.float32


def passed_along(value, axis, steps):
    count = lax.axis_size(axis)
    first, last = (max(0, -steps), min(count, count - steps))
    return lax.ppermute(value, axis, [(source, source + steps) for source in range(first, last)])


def from_others(value, axis):
    count = lax.axis_size(axis)
    return [
        lax.ppermute(value, axis, [(source, (source + step) % count) for source in range(count)])
        for step in range(1, count)
    ]


def cost(flops, nbytes, transcendentals=0):
    return pl.CostEstimate(flops=flops, bytes_accessed=nbytes, transcendentals=transcendentals)


def params(limit=60):
    return pltpu.CompilerParams(vmem_limit_bytes=limit << 20)


def split(value, parts):
    out = []
    for _ in range(parts):
        part = value.astype(BF)
        out.append(part)
        value = value - part.astype(F32)
    return out


def contract(a, b, a_dim, b_dim):
    return lax.dot_general(a, b, (((a_dim,), (b_dim,)), ((), ())), preferred_element_type=F32)


def iotas(rows, cols):
    return (
        lax.broadcasted_iota(jnp.int32, (rows, cols), 0),
        lax.broadcasted_iota(jnp.int32, (rows, cols), 1),
    )


def regroup_kernel(place_ref, master_ref, *parts):
    servers = len(parts)
    width = master_ref.shape[-1] // servers
    for step, part_ref in enumerate(parts):
        server = (place_ref[0] + step) % servers
        own = pl.ds(pl.multiple_of(server * width, width), width)
        pair = pl.ds(pl.multiple_of((server // 2) * 2 * width, 2 * width), 2 * width)
        for slot in range(3):
            part_ref[:, slot * width : (slot + 1) * width] = master_ref[:, slot, own].astype(BF)
        part_ref[:, 3 * width :] = master_ref[:, 3, pair].astype(BF)


def regroup(place, master, servers):
    rows, _, total = master.shape
    columns = 5 * total // servers
    return pl.pallas_call(
        regroup_kernel,
        in_specs=[pl.BlockSpec(memory_space=pltpu.SMEM), pl.BlockSpec(memory_space=pltpu.VMEM)],
        out_specs=[pl.BlockSpec(memory_space=pltpu.VMEM)] * servers,
        out_shape=[jax.ShapeDtypeStruct((rows, columns), BF)] * servers,
        cost_estimate=cost(0, rows * total * 26),
        compiler_params=params(),
        name="regroup",
    )(place, master)


def assemble_kernel(place_ref, *refs):
    out_ref = refs[-1]
    parts = refs[:-1]
    rows = parts[0].shape[0]
    for step, part_ref in enumerate(parts):
        source = (place_ref[0] + len(parts) - step) % len(parts)
        out_ref[pl.ds(pl.multiple_of(source * rows, rows), rows), :] = part_ref[...]


def assemble(place, parts):
    rows, columns = parts[0].shape
    return pl.pallas_call(
        assemble_kernel,
        in_specs=[pl.BlockSpec(memory_space=pltpu.SMEM)]
        + [pl.BlockSpec(memory_space=pltpu.VMEM)] * len(parts),
        out_specs=pl.BlockSpec(memory_space=pltpu.VMEM),
        out_shape=jax.ShapeDtypeStruct((rows * len(parts), columns), BF),
        cost_estimate=cost(0, rows * columns * len(parts) * 4),
        compiler_params=params(),
        name="assemble",
    )(place, *parts)


def swapped(value, axis, mask):
    count = lax.axis_size(axis)
    return lax.ppermute(value, axis, [(source, source ^ mask) for source in range(count)])


def weight_pieces(part):
    count = lax.axis_size("blk")
    if count & (count - 1) or part.shape[0] % HEAD_DIM or count > 8:
        return [lax.all_gather(part, "blk", axis=0, tiled=True)]
    pieces = {0: part}
    for mask in range(2, count, 2):
        pieces[mask] = swapped(part, "blk", mask)
    for mask in range(0, count, 2):
        pieces[mask + 1] = swapped(pieces[mask], "blk", 1)
    return [pieces[mask] for mask in range(count)]


def stats_kernel(x_ref, proj_ref, out_ref):
    block, _, width = x_ref.shape
    tokens = block * pl.num_programs(0)
    base = pl.program_id(0) * (block // STEP)
    proj = proj_ref[...]
    pieces = jnp.concatenate(split(proj, 3), axis=0)
    out_ref[:, out_ref.shape[1] - 128 :] = jnp.broadcast_to(jnp.sum(proj, axis=1, keepdims=True), (8, 128))
    row, col = iotas(4 * SUB, 4 * SUB)
    same = (row >> 2) == (col >> 2)
    ring = jnp.where(same, (row - col) & 3, -1)

    @pl.loop(0, block // STEP)
    def _(local):
        step = base + local
        folded = []
        for half in range(STEP // SUB):
            lanes = pl.ds(pl.multiple_of(step * 4 * STEP, 4 * STEP) + half * 4 * SUB, 4 * SUB)
            v = x_ref[pl.ds(local * STEP + half * SUB, SUB)].reshape(4 * SUB, width)
            sums = contract(pieces, v, 1, 1)
            sums = sums[0:8] + sums[8:16] + sums[16:24]
            gram = contract(v, v, 1, 1)
            out_ref[0:1, lanes] = sums[0:1]
            out_ref[1:2, lanes] = sums[6:7]
            for shift in range(3):
                out_ref[2 + shift : 3 + shift, lanes] = jnp.sum(
                    jnp.where(ring == shift, gram, 0.0), axis=0, keepdims=True
                )
            out_ref[5:8, lanes] = sums[1:4]
            folded.append(sums[4:6])
        folded = jnp.concatenate(folded, axis=1)
        lanes = pl.ds(pl.multiple_of(4 * tokens + step * STEP, STEP), STEP)
        for part in range(4):
            for which in range(2):
                out_ref[4 * which + part : 4 * which + part + 1, lanes] = folded[
                    which : which + 1, part * STEP : (part + 1) * STEP
                ]


def stats(x, proj):
    tokens, _, width = x.shape
    lanes = 5 * tokens + 128
    return pl.pallas_call(
        stats_kernel,
        grid=(tokens // (2 * STEP),),
        in_specs=[
            pl.BlockSpec((2 * STEP, 4, width), lambda i: (i, 0, 0)),
            pl.BlockSpec((8, width), lambda i: (0, 0)),
        ],
        out_specs=pl.BlockSpec((8, lanes), lambda i: (0, 0)),
        out_shape=jax.ShapeDtypeStruct((8, lanes), F32),
        cost_estimate=cost(tokens * 4 * width * 600, tokens * 8 * width),
        compiler_params=params(),
        name="stats",
    )(x, proj)


def by_stream(static_ref, column, stream):
    value = jnp.full(stream.shape, static_ref[0, column], F32)
    for k in range(1, 4):
        value = jnp.where(stream == k, static_ref[k, column], value)
    return value


def centre(first):
    mean = first[1:2] * (1.0 / D)
    spread = first[2:3] * (1.0 / D) - mean * mean
    return mean, lax.rsqrt(spread + EPS)


def mix_kernel(offset, static_ref, x_ref, own_ref, a_ref, b_ref, c_ref, sums_ref, normed_ref):
    tokens, _, width = x_ref.shape

    @pl.when(pl.program_id(0) == 0)
    def _():
        sums_ref[...] = (own_ref[...] + a_ref[...]) + (b_ref[...] + c_ref[...])

    base = 4 * (offset + pl.program_id(0) * tokens)
    last = sums_ref.shape[1] - 128
    column = sums_ref[0:1, last : last + 1]
    stream = lax.broadcasted_iota(jnp.int32, (1, 4 * STEP), 1) & 3
    static = by_stream(static_ref, 0, stream)
    row, col = iotas(SUB, 4 * SUB)
    mine = row == (col >> 2)

    @pl.loop(0, tokens // STEP)
    def _(step):
        at = pl.multiple_of(base + step * 4 * STEP, 4 * STEP)
        first = sums_ref[:, pl.ds(at, 4 * STEP)]
        mean, inverse = centre(first)
        mix = static + jnp.tanh(inverse * (first[0:1] - mean * column))
        one = jnp.where(stream < 3, pltpu.roll(mix, 4 * STEP - 1, 1), pltpu.roll(mix, 3, 1))
        two = jnp.where(stream < 2, pltpu.roll(mix, 4 * STEP - 2, 1), pltpu.roll(mix, 2, 1))
        linear = mix * first[1:2]
        square = mix * (mix * first[2:3] + 2.0 * one * first[3:4] + two * first[4:5])
        for half in range(STEP // SUB):
            lanes = slice(half * 4 * SUB, (half + 1) * 4 * SUB)
            rows = pl.ds(step * STEP + half * SUB, SUB)
            v = x_ref[rows].reshape(4 * SUB, width)
            matrix = jnp.where(mine, mix[:, lanes], 0.0)
            mixed = contract(jnp.concatenate(split(matrix, 3), axis=0), v, 1, 0)
            mixed = mixed[0:SUB] + mixed[SUB : 2 * SUB] + mixed[2 * SUB : 3 * SUB]
            average = jnp.sum(jnp.where(mine, linear[:, lanes], 0.0), axis=1, keepdims=True)
            power = jnp.sum(jnp.where(mine, square[:, lanes], 0.0), axis=1, keepdims=True)
            average, power = average * (1.0 / D), power * (1.0 / D)
            scale = lax.rsqrt(jnp.maximum(power - average * average, 0.0) + EPS)
            normed_ref[rows, :] = ((mixed - average) * scale).astype(BF)


def mix(static, x, parts, start, tokens):
    width = x.shape[-1]
    lanes = parts[0].shape[1]
    whole = pl.BlockSpec((8, lanes), lambda i: (0, 0))
    return pl.pallas_call(
        functools.partial(mix_kernel, start),
        grid=(tokens // CHUNK,),
        in_specs=[
            pl.BlockSpec(memory_space=pltpu.SMEM),
            pl.BlockSpec((CHUNK, 4, width), lambda i: (start // CHUNK + i, 0, 0)),
        ]
        + [whole] * 4,
        out_specs=[whole, pl.BlockSpec((CHUNK, width), lambda i: (i, 0))],
        out_shape=[
            jax.ShapeDtypeStruct((8, lanes), F32),
            jax.ShapeDtypeStruct((tokens, width), BF),
        ],
        cost_estimate=cost(tokens * 4 * width * 400, tokens * 10 * width),
        compiler_params=params(),
        name="mix",
    )(static, x, *parts)


def qkv_kernel(ring_ref, rows_ref, cosine_ref, sine_ref, *refs):
    out_ref, halo_ref = refs[-2:]
    pieces = refs[:-2]
    servers, _, width = rows_ref.shape
    depth = pieces[0].shape[0]
    if len(pieces) == 1:
        left = [rows_ref[server] for server in range(servers)]
    else:
        left = []
        for piece in range(len(pieces)):
            source = ring_ref[0] ^ piece
            inside = pl.multiple_of((source % (width // depth)) * depth, depth)
            left.append(rows_ref[source // (width // depth), :, pl.ds(inside, depth)])
    left = jnp.concatenate(left, axis=1)
    right = jnp.concatenate([piece[...] for piece in pieces], axis=0)
    total = contract(left, right, 1, 0)
    slot = pl.program_id(0)

    @pl.when(slot < 2)
    def _():
        cosine, sine = cosine_ref[...], sine_ref[...]
        for head in range(total.shape[1] // HEAD_DIM):
            part = total[:, head * HEAD_DIM : (head + 1) * HEAD_DIM]
            turned = part * cosine + pltpu.roll(part, HEAD_DIM // 2, 1) * sine
            out_ref[0, :, head * HEAD_DIM : (head + 1) * HEAD_DIM] = turned.astype(BF)

    @pl.when(slot == 2)
    def _():
        out_ref[0] = total.astype(BF)

    halo_ref[0] = out_ref[0, -halo_ref.shape[1] :, :]


def qkv_columns(ring, rows, pieces, cosine, sine):
    servers, tokens, width = rows.shape
    kept = min(BLOCK, tokens)
    table = pl.BlockSpec((tokens, HEAD_DIM), lambda j: (0, 0))
    return pl.pallas_call(
        qkv_kernel,
        grid=(3,),
        in_specs=[
            pl.BlockSpec(memory_space=pltpu.SMEM),
            pl.BlockSpec((servers, tokens, width), lambda j: (0, 0, 0)),
            table,
            table,
        ]
        + [pl.BlockSpec((pieces[0].shape[0], width), lambda j: (0, j))] * len(pieces),
        out_specs=[
            pl.BlockSpec((1, tokens, width), lambda j: (j, 0, 0)),
            pl.BlockSpec((1, kept, width), lambda j: (jnp.maximum(j - 1, 0), 0, 0)),
        ],
        out_shape=[
            jax.ShapeDtypeStruct((3, tokens, width), BF),
            jax.ShapeDtypeStruct((2, kept, width), BF),
        ],
        cost_estimate=cost(2 * tokens * D * 3 * width, D * 6 * width + tokens * D * 5),
        compiler_params=params(),
        name="qkv",
    )(ring, rows, cosine, sine, *pieces)


def attend_kernel(q_ref, k0, k1, k2, v0, v1, v2, qseg_ref, kseg_ref, attended_ref):
    tokens, width = q_ref.shape[1:]
    window = kseg_ref.shape[-1]
    row, col = iotas(tokens, window)
    allowed = (qseg_ref[...] == kseg_ref[0]) & (col - (window - tokens) <= row)
    bias = jnp.where(allowed, 0.0, -1e30)
    factor = 1.4426950408889634 / HEAD_DIM**0.5
    for head in range(width // HEAD_DIM):
        lanes = slice(head * HEAD_DIM, (head + 1) * HEAD_DIM)
        query = q_ref[0, :, lanes]
        scores = jnp.concatenate(
            [contract(query, k[0, :, lanes], 1, 1) for k in (k0, k1, k2)], axis=1
        )
        scores = scores + bias
        weights = jnp.exp2((scores - jnp.max(scores, axis=1, keepdims=True)) * factor)
        total = jnp.sum(weights, axis=1, keepdims=True)
        values = jnp.concatenate([v[0, :, lanes] for v in (v0, v1, v2)], axis=0)
        attended_ref[:, lanes] = (contract(weights.astype(BF), values, 1, 0) / total).astype(BF)


def attend(query, window, qseg, kseg, chunk):
    source, at = query
    width = source.shape[-1]
    block = (1, CHUNK, width)
    keys = [pl.BlockSpec(block, lambda i, s=slot, r=where: (s, r, 0)) for _, slot, where in window]
    values = [
        pl.BlockSpec(block, lambda i, s=slot + 1, r=where: (s, r, 0)) for _, slot, where in window
    ]
    arrays = [array for array, _, _ in window]
    reach = kseg.shape[-1]
    return pl.pallas_call(
        attend_kernel,
        grid=(1,),
        in_specs=[pl.BlockSpec(block, lambda i: (0, at, 0))]
        + keys
        + values
        + [
            pl.BlockSpec((CHUNK, 1), lambda i: (chunk, 0)),
            pl.BlockSpec((1, 1, reach), lambda i: (chunk, 0, 0)),
        ],
        out_specs=pl.BlockSpec((CHUNK, width), lambda i: (0, 0)),
        out_shape=jax.ShapeDtypeStruct((CHUNK, width), BF),
        cost_estimate=cost(4 * CHUNK * reach * width, CHUNK * width * 16, CHUNK * reach * 4),
        compiler_params=params(),
        name="attend",
    )(source, *arrays, *arrays, qseg, kseg)


def project_kernel(place_ref, ring_ref, own_ref, other_ref, *refs):
    pieces = refs[:-4]
    kept_ref, inner_ref, outer_ref, sums = refs[-4:]
    servers, _, width = sums.shape
    place = place_ref[0]
    even = place % 2 == 0
    own, other = own_ref[...], other_ref[...]
    both = jnp.concatenate([jnp.where(even, own, other), jnp.where(even, other, own)], axis=1)
    depth = pieces[0].shape[0]
    if len(pieces) == 1:
        for server in range(servers):
            rows = pieces[0][server * width : (server + 1) * width, :]
            sums[server] = contract(both, rows, 1, 1)
    else:
        for piece in range(len(pieces)):
            target = ring_ref[0] ^ piece
            inside = pl.multiple_of((target % (width // depth)) * depth, depth)
            sums[target // (width // depth), :, pl.ds(inside, depth)] = contract(
                both, pieces[piece][...], 1, 1
            )
    kept_ref[...] = sums[place]
    low = place < 2
    inner_ref[...] = sums[jnp.where(low, 2, 1)].astype(BF)
    outer_ref[...] = sums[jnp.where(low, 3, 0)].astype(BF)


def project(place, ring, own, other, pieces, servers):
    tokens, width = own.shape
    rows, columns = pieces[0].shape
    pair = 2 * width
    tail = pl.BlockSpec((pl.Element(rows), pl.Element(pair)), lambda i: (0, columns - pair))
    full = pl.BlockSpec((tokens, width), lambda i: (0, 0))
    return pl.pallas_call(
        project_kernel,
        grid=(1,),
        in_specs=[pl.BlockSpec(memory_space=pltpu.SMEM)] * 2 + [full] * 2 + [tail] * len(pieces),
        out_specs=[full] * 3,
        out_shape=[
            jax.ShapeDtypeStruct((tokens, width), F32),
            jax.ShapeDtypeStruct((tokens, width), BF),
            jax.ShapeDtypeStruct((tokens, width), BF),
        ],
        scratch_shapes=[pltpu.VMEM((servers, tokens, width), F32)],
        cost_estimate=cost(2 * tokens * D * pair, D * pair * 2 + tokens * width * 12),
        compiler_params=params(),
        name="project",
    )(place, ring, own, other, *pieces)


def final_kernel(
    static_ref, x_ref, first_ref, folded_ref, column_ref, own_ref, inner_ref, outer_ref, *rest
):
    new_ref = rest[-1]
    tokens, _, width = x_ref.shape
    first = first_ref[...]
    mean, inverse = centre(first)
    stream = lax.broadcasted_iota(jnp.int32, (1, 4 * tokens), 1) & 3

    def coefficient(column, projected):
        dynamic = jnp.tanh(inverse * (projected - mean * column_ref[column : column + 1, 0:1]))
        return by_stream(static_ref, column, stream) + dynamic

    def unfolded(which):
        return jnp.concatenate(
            [folded_ref[4 * which + part : 4 * which + part + 1] for part in range(4)], axis=1
        )

    projected = [first[5:6], first[6:7], first[7:8], unfolded(0), unfolded(1)]
    columns = [coefficient(1 + j, projected[j]) for j in range(5)]
    residual = jnp.concatenate(columns[:4] + columns[:4], axis=0)
    row, col = iotas(4 * SUB, 4 * SUB)
    same = (row >> 2) == (col >> 2)
    row, col = iotas(SUB, 4 * SUB)
    mine = row == (col >> 2)
    for at in range(tokens // SUB):
        lanes = slice(at * 4 * SUB, (at + 1) * 4 * SUB)
        rows = slice(at * SUB, (at + 1) * SUB)
        v = x_ref[rows].reshape(4 * SUB, width)
        matrix = jnp.where(same, jnp.tile(residual[:, lanes], (SUB // 2, 1)), 0.0)
        high, low = split(matrix, 2)
        new = contract(high, v, 1, 0) + contract(low, v, 1, 0)
        sent = inner_ref[rows, :].astype(F32) + outer_ref[rows, :].astype(F32)
        update_high, update_low = split(own_ref[rows, :] + sent, 2)
        spread_high, spread_low = split(jnp.where(mine, columns[4][:, lanes], 0.0), 2)
        new += contract(
            jnp.concatenate([spread_high, spread_high, spread_low], axis=0),
            jnp.concatenate([update_high, update_low, update_high], axis=0),
            0,
            0,
        )
        new_ref[rows] = new.astype(BF).reshape(SUB, 4, width)


def final(static, x, sums, updates, start, previous):
    tokens, width = updates[0].shape
    group = (sums.shape[1] - 128) // 5
    stream_block = pl.BlockSpec((STEP, 4, width), lambda i: (start // STEP + i, 0, 0))
    specs = [
        pl.BlockSpec(memory_space=pltpu.SMEM),
        stream_block,
        pl.BlockSpec((8, 4 * STEP), lambda i: (0, start // STEP + i)),
        pl.BlockSpec((8, STEP), lambda i: (0, 4 * group // STEP + start // STEP + i)),
        pl.BlockSpec((8, 128), lambda i: (0, 5 * group // 128)),
    ]
    specs += [pl.BlockSpec((STEP, width), lambda i: (i, 0))] * 3
    args = [static, x, sums, sums, sums, *updates]
    aliases = {}
    if previous is not None:
        specs.append(pl.BlockSpec(memory_space=pl.ANY))
        aliases = {len(args): 0}
        args.append(previous)
    return pl.pallas_call(
        final_kernel,
        grid=(tokens // STEP,),
        in_specs=specs,
        out_specs=stream_block,
        out_shape=jax.ShapeDtypeStruct(x.shape, BF),
        input_output_aliases=aliases,
        cost_estimate=cost(tokens * 4 * width * 1200, tokens * 22 * width),
        compiler_params=params(),
        name="final",
    )(*args)


def body(streams, proj_master, hc_proj, hc_static, segment_ids, block_mask):
    tokens_local, _, width = streams.shape
    group_size = lax.axis_size("mp")
    place = lax.axis_index("mp").astype(jnp.int32).reshape(1)
    ring = lax.axis_index("blk").astype(jnp.int32).reshape(1)

    proj_rows = jnp.concatenate(
        [hc_proj.T, jnp.ones((1, width), F32), jnp.zeros((1, width), F32)], axis=0
    )
    own = stats(streams, proj_rows)
    parts = list(regroup(place, proj_master, group_size))
    sums, parts = lax.optimization_barrier(([own] + from_others(own, "mp"), parts))

    def gathered(normed):
        rows = lax.all_gather(normed, "mp", axis=0, tiled=True)
        return rows.reshape(group_size, normed.shape[0], width)

    for step in range(1, group_size):
        parts[step] = lax.ppermute(
            parts[step], "mp", [(at, (at + step) % group_size) for at in range(group_size)]
        )
    sums_all, normed_late = mix(hc_static, streams, sums, CHUNK, tokens_local - CHUNK)
    _, normed_first = mix(hc_static, streams, sums, 0, CHUNK)
    parts, normed_late, normed_first = lax.optimization_barrier((parts, normed_late, normed_first))
    rows_late = gathered(normed_late)
    rows_first = gathered(normed_first)

    pieces = weight_pieces(assemble(place, parts))
    rows_late, pieces = lax.optimization_barrier((rows_late, pieces))

    halo = passed_along(segment_ids[-BLOCK:], "blk", 1)
    halo = jnp.where(lax.axis_index("blk") == 0, -1, halo)
    extended = jnp.concatenate([halo, segment_ids])
    key_at = jnp.arange(tokens_local + BLOCK, dtype=jnp.int32)[None, :]
    query_at = jnp.arange(tokens_local, dtype=jnp.int32)[:, None] + BLOCK
    earlier = (extended[None, :] == segment_ids[:, None]) & (key_at < query_at)
    positions = jnp.sum(earlier.astype(jnp.int32), axis=1)
    half = HEAD_DIM // 2
    inverse = 10000.0 ** (-(jnp.arange(half, dtype=F32) * 2.0 / HEAD_DIM))
    angles = positions.astype(F32)[:, None] * inverse[None, :]
    cosine, sine = jnp.cos(angles), jnp.sin(angles)
    cosine = jnp.concatenate([cosine, cosine], axis=1)
    sine = jnp.concatenate([-sine, sine], axis=1)
    windows = []
    for block in range(tokens_local // BLOCK):
        before = extended[block * BLOCK : (block + 1) * BLOCK]
        before = jnp.where(block_mask[block] == 1, before, -1)
        seen = jnp.concatenate([before, segment_ids[block * BLOCK : (block + 1) * BLOCK]])
        for chunk in range(BLOCK // CHUNK):
            windows.append(seen[chunk * CHUNK : chunk * CHUNK + BLOCK + CHUNK])
    key_segments = jnp.stack(windows)[:, None, :]
    query_segments = segment_ids[:, None]

    qkv_late, halo_rows = qkv_columns(ring, rows_late, pieces, cosine[CHUNK:], sine[CHUNK:])
    halo_rows = passed_along(halo_rows, "blk", 1)

    def projected(own, other):
        return project(place, ring, own, other, pieces, group_size)

    last = tokens_local // CHUNK - 1
    late_chunks = [(qkv_late, 1, at) for at in range(last)]

    def attended(chunk, window):
        source, _, at = window[-1]
        return attend((source, at), window, query_segments, key_segments, chunk)

    own = attended(last, late_chunks[-3:])
    both = (own, swapped(own, "mp", 1))
    rows_first, both = lax.optimization_barrier((rows_first, both))
    parts = {last: projected(*both)}
    qkv_first, _ = qkv_columns(ring, rows_first, pieces, cosine[:CHUNK], sine[:CHUNK])
    chunks = [(halo_rows, 0, 0), (halo_rows, 0, 1), (qkv_first, 1, 0)] + late_chunks
    for chunk in reversed(range(last)):
        own = attended(chunk, chunks[chunk : chunk + 3])
        parts[chunk] = projected(own, swapped(own, "mp", 1))

    result = None
    for chunk in reversed(range(last + 1)):
        kept, inner, outer = parts[chunk]
        inner = lax.ppermute(inner, "mp", [(1, 2), (2, 1)])
        outer = lax.ppermute(outer, "mp", [(1, 3), (2, 0)])
        updates = [kept, inner, outer]
        result = final(hc_static, streams, sums_all, updates, chunk * CHUNK, result)
    return result


def solution(mesh):
    in_specs = (
        P("blk", None, "mp"),
        P(("blk", "mp"), None, None),
        P("mp", None),
        P(),
        P("blk"),
        P("blk"),
    )
    out_specs = P("blk", None, "mp")
    return jax.shard_map(body, mesh=mesh, in_specs=in_specs, out_specs=out_specs, check_vma=False)
```

```python
import functools

import jax
import jax.numpy as jnp
from jax import lax
from jax.experimental import pallas as pl
from jax.experimental.pallas import tpu as pltpu
from jax.sharding import PartitionSpec as P

D = 2048
HEAD_DIM = 128
BLOCK = 512
CHUNK = 256
SUB = 64
STEP = 128
STREAMS = 4
EPS = 1e-05
BF = jnp.bfloat16
F32 = jnp.float32


def passed_along(value, axis, steps):
    count = lax.axis_size(axis)
    first, last = (max(0, -steps), min(count, count - steps))
    return lax.ppermute(value, axis, [(source, source + steps) for source in range(first, last)])


def from_others(value, axis):
    count = lax.axis_size(axis)
    return [
        lax.ppermute(value, axis, [(source, (source + step) % count) for source in range(count)])
        for step in range(1, count)
    ]


def cost(flops, nbytes, transcendentals=0):
    return pl.CostEstimate(flops=flops, bytes_accessed=nbytes, transcendentals=transcendentals)


def params(limit=60):
    return pltpu.CompilerParams(vmem_limit_bytes=limit << 20)


def split(value, parts):
    out = []
    for _ in range(parts):
        part = value.astype(BF)
        out.append(part)
        value = value - part.astype(F32)
    return out


def contract(a, b, a_dim, b_dim):
    return lax.dot_general(a, b, (((a_dim,), (b_dim,)), ((), ())), preferred_element_type=F32)


def iotas(rows, cols):
    return (
        lax.broadcasted_iota(jnp.int32, (rows, cols), 0),
        lax.broadcasted_iota(jnp.int32, (rows, cols), 1),
    )


def regroup_kernel(place_ref, master_ref, *parts):
    servers = len(parts)
    width = master_ref.shape[-1] // servers
    for step, part_ref in enumerate(parts):
        server = (place_ref[0] + step) % servers
        own = pl.ds(pl.multiple_of(server * width, width), width)
        pair = pl.ds(pl.multiple_of((server // 2) * 2 * width, 2 * width), 2 * width)
        for slot in range(3):
            part_ref[:, slot * width : (slot + 1) * width] = master_ref[:, slot, own].astype(BF)
        part_ref[:, 3 * width :] = master_ref[:, 3, pair].astype(BF)


def regroup(place, master, servers):
    rows, _, total = master.shape
    columns = 5 * total // servers
    return pl.pallas_call(
        regroup_kernel,
        in_specs=[pl.BlockSpec(memory_space=pltpu.SMEM), pl.BlockSpec(memory_space=pltpu.VMEM)],
        out_specs=[pl.BlockSpec(memory_space=pltpu.VMEM)] * servers,
        out_shape=[jax.ShapeDtypeStruct((rows, columns), BF)] * servers,
        cost_estimate=cost(0, rows * total * 26),
        compiler_params=params(),
        name="regroup",
    )(place, master)


def assemble_kernel(place_ref, *refs):
    out_ref = refs[-1]
    parts = refs[:-1]
    rows = parts[0].shape[0]
    for step, part_ref in enumerate(parts):
        source = (place_ref[0] + len(parts) - step) % len(parts)
        out_ref[pl.ds(pl.multiple_of(source * rows, rows), rows), :] = part_ref[...]


def assemble(place, parts):
    rows, columns = parts[0].shape
    return pl.pallas_call(
        assemble_kernel,
        in_specs=[pl.BlockSpec(memory_space=pltpu.SMEM)]
        + [pl.BlockSpec(memory_space=pltpu.VMEM)] * len(parts),
        out_specs=pl.BlockSpec(memory_space=pltpu.VMEM),
        out_shape=jax.ShapeDtypeStruct((rows * len(parts), columns), BF),
        cost_estimate=cost(0, rows * columns * len(parts) * 4),
        compiler_params=params(),
        name="assemble",
    )(place, *parts)


def swapped(value, axis, mask):
    count = lax.axis_size(axis)
    return lax.ppermute(value, axis, [(source, source ^ mask) for source in range(count)])


def weight_pieces(part):
    count = lax.axis_size("blk")
    if count & (count - 1) or part.shape[0] % HEAD_DIM or count > 8:
        return [lax.all_gather(part, "blk", axis=0, tiled=True)]
    pieces = {0: part}
    for mask in range(2, count, 2):
        pieces[mask] = swapped(part, "blk", mask)
    for mask in range(0, count, 2):
        pieces[mask + 1] = swapped(pieces[mask], "blk", 1)
    return [pieces[mask] for mask in range(count)]


def stats_kernel(x_ref, proj_ref, out_ref):
    block, _, width = x_ref.shape
    tokens = block * pl.num_programs(0)
    base = pl.program_id(0) * (block // STEP)
    proj = proj_ref[...]
    pieces = jnp.concatenate(split(proj, 3), axis=0)
    out_ref[:, out_ref.shape[1] - 128 :] = jnp.broadcast_to(jnp.sum(proj, axis=1, keepdims=True), (8, 128))
    row, col = iotas(4 * SUB, 4 * SUB)
    same = (row >> 2) == (col >> 2)
    ring = jnp.where(same, (row - col) & 3, -1)

    @pl.loop(0, block // STEP)
    def _(local):
        step = base + local
        folded = []
        for half in range(STEP // SUB):
            lanes = pl.ds(pl.multiple_of(step * 4 * STEP, 4 * STEP) + half * 4 * SUB, 4 * SUB)
            v = x_ref[pl.ds(local * STEP + half * SUB, SUB)].reshape(4 * SUB, width)
            sums = contract(pieces, v, 1, 1)
            sums = sums[0:8] + sums[8:16] + sums[16:24]
            gram = contract(v, v, 1, 1)
            out_ref[0:1, lanes] = sums[0:1]
            out_ref[1:2, lanes] = sums[6:7]
            for shift in range(3):
                out_ref[2 + shift : 3 + shift, lanes] = jnp.sum(
                    jnp.where(ring == shift, gram, 0.0), axis=0, keepdims=True
                )
            out_ref[5:8, lanes] = sums[1:4]
            folded.append(sums[4:6])
        folded = jnp.concatenate(folded, axis=1)
        lanes = pl.ds(pl.multiple_of(4 * tokens + step * STEP, STEP), STEP)
        for part in range(4):
            for which in range(2):
                out_ref[4 * which + part : 4 * which + part + 1, lanes] = folded[
                    which : which + 1, part * STEP : (part + 1) * STEP
                ]


def stats(x, proj):
    tokens, _, width = x.shape
    lanes = 5 * tokens + 128
    return pl.pallas_call(
        stats_kernel,
        grid=(tokens // (2 * STEP),),
        in_specs=[
            pl.BlockSpec((2 * STEP, 4, width), lambda i: (i, 0, 0)),
            pl.BlockSpec((8, width), lambda i: (0, 0)),
        ],
        out_specs=pl.BlockSpec((8, lanes), lambda i: (0, 0)),
        out_shape=jax.ShapeDtypeStruct((8, lanes), F32),
        cost_estimate=cost(tokens * 4 * width * 600, tokens * 8 * width),
        compiler_params=params(),
        name="stats",
    )(x, proj)


def by_stream(static_ref, column, stream):
    value = jnp.full(stream.shape, static_ref[0, column], F32)
    for k in range(1, 4):
        value = jnp.where(stream == k, static_ref[k, column], value)
    return value


def centre(first):
    mean = first[1:2] * (1.0 / D)
    spread = first[2:3] * (1.0 / D) - mean * mean
    return mean, lax.rsqrt(spread + EPS)


def mix_kernel(offset, static_ref, x_ref, own_ref, a_ref, b_ref, c_ref, sums_ref, normed_ref):
    tokens, _, width = x_ref.shape

    @pl.when(pl.program_id(0) == 0)
    def _():
        sums_ref[...] = (own_ref[...] + a_ref[...]) + (b_ref[...] + c_ref[...])

    base = 4 * (offset + pl.program_id(0) * tokens)
    last = sums_ref.shape[1] - 128
    column = sums_ref[0:1, last : last + 1]
    stream = lax.broadcasted_iota(jnp.int32, (1, 4 * STEP), 1) & 3
    static = by_stream(static_ref, 0, stream)
    row, col = iotas(SUB, 4 * SUB)
    mine = row == (col >> 2)

    @pl.loop(0, tokens // STEP)
    def _(step):
        at = pl.multiple_of(base + step * 4 * STEP, 4 * STEP)
        first = sums_ref[:, pl.ds(at, 4 * STEP)]
        mean, inverse = centre(first)
        mix = static + jnp.tanh(inverse * (first[0:1] - mean * column))
        one = jnp.where(stream < 3, pltpu.roll(mix, 4 * STEP - 1, 1), pltpu.roll(mix, 3, 1))
        two = jnp.where(stream < 2, pltpu.roll(mix, 4 * STEP - 2, 1), pltpu.roll(mix, 2, 1))
        linear = mix * first[1:2]
        square = mix * (mix * first[2:3] + 2.0 * one * first[3:4] + two * first[4:5])
        for half in range(STEP // SUB):
            lanes = slice(half * 4 * SUB, (half + 1) * 4 * SUB)
            rows = pl.ds(step * STEP + half * SUB, SUB)
            v = x_ref[rows].reshape(4 * SUB, width)
            matrix = jnp.where(mine, mix[:, lanes], 0.0)
            mixed = contract(jnp.concatenate(split(matrix, 3), axis=0), v, 1, 0)
            mixed = mixed[0:SUB] + mixed[SUB : 2 * SUB] + mixed[2 * SUB : 3 * SUB]
            average = jnp.sum(jnp.where(mine, linear[:, lanes], 0.0), axis=1, keepdims=True)
            power = jnp.sum(jnp.where(mine, square[:, lanes], 0.0), axis=1, keepdims=True)
            average, power = average * (1.0 / D), power * (1.0 / D)
            scale = lax.rsqrt(jnp.maximum(power - average * average, 0.0) + EPS)
            normed_ref[rows, :] = ((mixed - average) * scale).astype(BF)


def mix(static, x, parts, start, tokens):
    width = x.shape[-1]
    lanes = parts[0].shape[1]
    whole = pl.BlockSpec((8, lanes), lambda i: (0, 0))
    return pl.pallas_call(
        functools.partial(mix_kernel, start),
        grid=(tokens // CHUNK,),
        in_specs=[
            pl.BlockSpec(memory_space=pltpu.SMEM),
            pl.BlockSpec((CHUNK, 4, width), lambda i: (start // CHUNK + i, 0, 0)),
        ]
        + [whole] * 4,
        out_specs=[whole, pl.BlockSpec((CHUNK, width), lambda i: (i, 0))],
        out_shape=[
            jax.ShapeDtypeStruct((8, lanes), F32),
            jax.ShapeDtypeStruct((tokens, width), BF),
        ],
        cost_estimate=cost(tokens * 4 * width * 400, tokens * 10 * width),
        compiler_params=params(),
        name="mix",
    )(static, x, *parts)


def qkv_kernel(ring_ref, rows_ref, cosine_ref, sine_ref, *refs):
    out_ref, halo_ref = refs[-2:]
    pieces = refs[:-2]
    servers, _, width = rows_ref.shape
    depth = pieces[0].shape[0]
    if len(pieces) == 1:
        left = [rows_ref[server] for server in range(servers)]
    else:
        left = []
        for piece in range(len(pieces)):
            source = ring_ref[0] ^ piece
            inside = pl.multiple_of((source % (width // depth)) * depth, depth)
            left.append(rows_ref[source // (width // depth), :, pl.ds(inside, depth)])
    left = jnp.concatenate(left, axis=1)
    right = jnp.concatenate([piece[...] for piece in pieces], axis=0)
    total = contract(left, right, 1, 0)
    slot = pl.program_id(0)

    @pl.when(slot < 2)
    def _():
        cosine, sine = cosine_ref[...], sine_ref[...]
        for head in range(total.shape[1] // HEAD_DIM):
            part = total[:, head * HEAD_DIM : (head + 1) * HEAD_DIM]
            turned = part * cosine + pltpu.roll(part, HEAD_DIM // 2, 1) * sine
            out_ref[0, :, head * HEAD_DIM : (head + 1) * HEAD_DIM] = turned.astype(BF)

    @pl.when(slot == 2)
    def _():
        out_ref[0] = total.astype(BF)

    halo_ref[0] = out_ref[0, -halo_ref.shape[1] :, :]


def qkv_columns(ring, rows, pieces, cosine, sine):
    servers, tokens, width = rows.shape
    kept = min(BLOCK, tokens)
    table = pl.BlockSpec((tokens, HEAD_DIM), lambda j: (0, 0))
    return pl.pallas_call(
        qkv_kernel,
        grid=(3,),
        in_specs=[
            pl.BlockSpec(memory_space=pltpu.SMEM),
            pl.BlockSpec((servers, tokens, width), lambda j: (0, 0, 0)),
            table,
            table,
        ]
        + [pl.BlockSpec((pieces[0].shape[0], width), lambda j: (0, j))] * len(pieces),
        out_specs=[
            pl.BlockSpec((1, tokens, width), lambda j: (j, 0, 0)),
            pl.BlockSpec((1, kept, width), lambda j: (jnp.maximum(j - 1, 0), 0, 0)),
        ],
        out_shape=[
            jax.ShapeDtypeStruct((3, tokens, width), BF),
            jax.ShapeDtypeStruct((2, kept, width), BF),
        ],
        cost_estimate=cost(2 * tokens * D * 3 * width, D * 6 * width + tokens * D * 5),
        compiler_params=params(),
        name="qkv",
    )(ring, rows, cosine, sine, *pieces)


def attend_step(q_ref, k0, k1, k2, v0, v1, v2, qseg_ref, kseg_ref, attended_ref):
    tokens, width = q_ref.shape[1:]
    window = kseg_ref.shape[-1]
    row, col = iotas(tokens, window)
    allowed = (qseg_ref[...] == kseg_ref[0]) & (col - (window - tokens) <= row)
    bias = jnp.where(allowed, 0.0, -1e30)
    factor = 1.4426950408889634 / HEAD_DIM**0.5
    for head in range(width // HEAD_DIM):
        lanes = slice(head * HEAD_DIM, (head + 1) * HEAD_DIM)
        query = q_ref[0, :, lanes]
        scores = jnp.concatenate(
            [contract(query, k[0, :, lanes], 1, 1) for k in (k0, k1, k2)], axis=1
        )
        scores = scores + bias
        weights = jnp.exp2((scores - jnp.max(scores, axis=1, keepdims=True)) * factor)
        total = jnp.sum(weights, axis=1, keepdims=True)
        values = jnp.concatenate([v[0, :, lanes] for v in (v0, v1, v2)], axis=0)
        attended_ref[:, lanes] = (contract(weights.astype(BF), values, 1, 0) / total).astype(BF)


def project_step(place_ref, ring_ref, own_ref, other_ref, pieces, kept_ref, inner_ref, outer_ref, sums):
    servers, _, width = sums.shape
    half = pl.program_id(0)
    place = place_ref[0]
    left = jnp.where(place % 2 == half, own_ref[...], other_ref[...])
    depth = pieces[0].shape[0]

    def add(server, lanes, rows):
        so_far = jnp.where(half == 0, 0.0, sums[server, :, lanes])
        sums[server, :, lanes] = so_far + contract(left, rows, 1, 1)

    if len(pieces) == 1:
        for server in range(servers):
            add(server, slice(None), pieces[0][server * width : (server + 1) * width, :])
    else:
        for at, piece in enumerate(pieces):
            target = ring_ref[0] ^ at
            inside = pl.multiple_of((target % (width // depth)) * depth, depth)
            add(target // (width // depth), pl.ds(inside, depth), piece[...])

    @pl.when(half == 1)
    def _():
        kept_ref[...] = sums[place]
        low = place < 2
        inner_ref[...] = sums[jnp.where(low, 2, 1)].astype(BF)
        outer_ref[...] = sums[jnp.where(low, 3, 0)].astype(BF)


def output_kernel(attends, projects, *refs):
    refs = list(refs)
    left = [refs.pop(0) for _ in range(9 if attends else 0)]
    right = [refs.pop(0) for _ in range(4 if projects else 0)]
    sums = refs.pop() if projects else None
    updates = [refs.pop() for _ in range(3 if projects else 0)][::-1]
    if attends:
        attended_ref = refs.pop()

        @pl.when(pl.program_id(0) == 0)
        def _():
            attend_step(*left, attended_ref)

    if projects:
        project_step(*right, refs, *updates, sums)


def output_step(attends, projects):
    specs, args, outs, shapes, scratch = [], [], [], [], []
    work = 0
    smem = pl.BlockSpec(memory_space=pltpu.SMEM)
    if attends:
        chunk, window, qseg, kseg = attends
        source, _, at = window[-1]
        width = source.shape[-1]
        block = (1, CHUNK, width)
        reach = kseg.shape[-1]
        specs.append(pl.BlockSpec(block, lambda i: (0, at, 0)))
        for which in range(2):
            specs += [
                pl.BlockSpec(block, lambda i, s=slot + which, r=where: (s, r, 0))
                for _, slot, where in window
            ]
        specs += [
            pl.BlockSpec((CHUNK, 1), lambda i: (chunk, 0)),
            pl.BlockSpec((1, 1, reach), lambda i: (chunk, 0, 0)),
        ]
        args += [source] + [array for array, _, _ in window] * 2 + [qseg, kseg]
        outs.append(pl.BlockSpec((CHUNK, width), lambda i: (0, 0)))
        shapes.append(jax.ShapeDtypeStruct((CHUNK, width), BF))
        work += 4 * CHUNK * reach * width
    if projects:
        place, ring, own, other, pieces, servers = projects
        tokens, width = own.shape
        rows, columns = pieces[0].shape
        full = pl.BlockSpec((tokens, width), lambda i: (0, 0))
        tail = pl.BlockSpec((rows, width), lambda i: (0, columns // width - 2 + i))
        specs += [smem] * 2 + [full] * 2 + [tail] * len(pieces)
        args += [place, ring, own, other, *pieces]
        outs += [full] * 3
        shapes += [jax.ShapeDtypeStruct((tokens, width), kind) for kind in (F32, BF, BF)]
        scratch.append(pltpu.VMEM((servers, tokens, width), F32))
        work += 4 * tokens * D * width
    return pl.pallas_call(
        functools.partial(output_kernel, bool(attends), bool(projects)),
        grid=(2 if projects else 1,),
        in_specs=specs,
        out_specs=outs,
        out_shape=shapes,
        scratch_shapes=scratch,
        cost_estimate=cost(work, work // 512),
        compiler_params=params(),
        name="output" if attends and projects else "attend" if attends else "project",
    )(*args)


def final_kernel(
    static_ref, x_ref, first_ref, folded_ref, column_ref, own_ref, inner_ref, outer_ref, *rest
):
    new_ref = rest[-1]
    tokens, _, width = x_ref.shape
    first = first_ref[...]
    mean, inverse = centre(first)
    stream = lax.broadcasted_iota(jnp.int32, (1, 4 * tokens), 1) & 3

    def coefficient(column, projected):
        dynamic = jnp.tanh(inverse * (projected - mean * column_ref[column : column + 1, 0:1]))
        return by_stream(static_ref, column, stream) + dynamic

    def unfolded(which):
        return jnp.concatenate(
            [folded_ref[4 * which + part : 4 * which + part + 1] for part in range(4)], axis=1
        )

    projected = [first[5:6], first[6:7], first[7:8], unfolded(0), unfolded(1)]
    columns = [coefficient(1 + j, projected[j]) for j in range(5)]
    residual = jnp.concatenate(columns[:4] + columns[:4], axis=0)
    row, col = iotas(4 * SUB, 4 * SUB)
    same = (row >> 2) == (col >> 2)
    row, col = iotas(SUB, 4 * SUB)
    mine = row == (col >> 2)
    for at in range(tokens // SUB):
        lanes = slice(at * 4 * SUB, (at + 1) * 4 * SUB)
        rows = slice(at * SUB, (at + 1) * SUB)
        v = x_ref[rows].reshape(4 * SUB, width)
        matrix = jnp.where(same, jnp.tile(residual[:, lanes], (SUB // 2, 1)), 0.0)
        high, low = split(matrix, 2)
        new = contract(high, v, 1, 0) + contract(low, v, 1, 0)
        sent = inner_ref[rows, :].astype(F32) + outer_ref[rows, :].astype(F32)
        update_high, update_low = split(own_ref[rows, :] + sent, 2)
        spread_high, spread_low = split(jnp.where(mine, columns[4][:, lanes], 0.0), 2)
        new += contract(
            jnp.concatenate([spread_high, spread_high, spread_low], axis=0),
            jnp.concatenate([update_high, update_low, update_high], axis=0),
            0,
            0,
        )
        new_ref[rows] = new.astype(BF).reshape(SUB, 4, width)


def final(static, x, sums, updates, start, previous):
    tokens, width = updates[0].shape
    group = (sums.shape[1] - 128) // 5
    stream_block = pl.BlockSpec((STEP, 4, width), lambda i: (start // STEP + i, 0, 0))
    specs = [
        pl.BlockSpec(memory_space=pltpu.SMEM),
        stream_block,
        pl.BlockSpec((8, 4 * STEP), lambda i: (0, start // STEP + i)),
        pl.BlockSpec((8, STEP), lambda i: (0, 4 * group // STEP + start // STEP + i)),
        pl.BlockSpec((8, 128), lambda i: (0, 5 * group // 128)),
    ]
    specs += [pl.BlockSpec((STEP, width), lambda i: (i, 0))] * 3
    args = [static, x, sums, sums, sums, *updates]
    aliases = {}
    if previous is not None:
        specs.append(pl.BlockSpec(memory_space=pl.ANY))
        aliases = {len(args): 0}
        args.append(previous)
    return pl.pallas_call(
        final_kernel,
        grid=(tokens // STEP,),
        in_specs=specs,
        out_specs=stream_block,
        out_shape=jax.ShapeDtypeStruct(x.shape, BF),
        input_output_aliases=aliases,
        cost_estimate=cost(tokens * 4 * width * 1200, tokens * 22 * width),
        compiler_params=params(),
        name="final",
    )(*args)


def body(streams, proj_master, hc_proj, hc_static, segment_ids, block_mask):
    tokens_local, _, width = streams.shape
    group_size = lax.axis_size("mp")
    place = lax.axis_index("mp").astype(jnp.int32).reshape(1)
    ring = lax.axis_index("blk").astype(jnp.int32).reshape(1)

    proj_rows = jnp.concatenate(
        [hc_proj.T, jnp.ones((1, width), F32), jnp.zeros((1, width), F32)], axis=0
    )
    own = stats(streams, proj_rows)
    parts = list(regroup(place, proj_master, group_size))
    sums, parts = lax.optimization_barrier(([own] + from_others(own, "mp"), parts))

    def gathered(normed):
        rows = lax.all_gather(normed, "mp", axis=0, tiled=True)
        return rows.reshape(group_size, normed.shape[0], width)

    for step in range(1, group_size):
        parts[step] = lax.ppermute(
            parts[step], "mp", [(at, (at + step) % group_size) for at in range(group_size)]
        )
    sums_all, normed_late = mix(hc_static, streams, sums, CHUNK, tokens_local - CHUNK)
    _, normed_first = mix(hc_static, streams, sums, 0, CHUNK)
    parts, normed_late, normed_first = lax.optimization_barrier((parts, normed_late, normed_first))
    rows_late = gathered(normed_late)
    rows_first = gathered(normed_first)

    pieces = weight_pieces(assemble(place, parts))
    rows_late, pieces = lax.optimization_barrier((rows_late, pieces))

    halo = passed_along(segment_ids[-BLOCK:], "blk", 1)
    halo = jnp.where(lax.axis_index("blk") == 0, -1, halo)
    extended = jnp.concatenate([halo, segment_ids])
    key_at = jnp.arange(tokens_local + BLOCK, dtype=jnp.int32)[None, :]
    query_at = jnp.arange(tokens_local, dtype=jnp.int32)[:, None] + BLOCK
    earlier = (extended[None, :] == segment_ids[:, None]) & (key_at < query_at)
    positions = jnp.sum(earlier.astype(jnp.int32), axis=1)
    half = HEAD_DIM // 2
    inverse = 10000.0 ** (-(jnp.arange(half, dtype=F32) * 2.0 / HEAD_DIM))
    angles = positions.astype(F32)[:, None] * inverse[None, :]
    cosine, sine = jnp.cos(angles), jnp.sin(angles)
    cosine = jnp.concatenate([cosine, cosine], axis=1)
    sine = jnp.concatenate([-sine, sine], axis=1)
    windows = []
    for block in range(tokens_local // BLOCK):
        before = extended[block * BLOCK : (block + 1) * BLOCK]
        before = jnp.where(block_mask[block] == 1, before, -1)
        seen = jnp.concatenate([before, segment_ids[block * BLOCK : (block + 1) * BLOCK]])
        for chunk in range(BLOCK // CHUNK):
            windows.append(seen[chunk * CHUNK : chunk * CHUNK + BLOCK + CHUNK])
    key_segments = jnp.stack(windows)[:, None, :]
    query_segments = segment_ids[:, None]

    qkv_late, halo_rows = qkv_columns(ring, rows_late, pieces, cosine[CHUNK:], sine[CHUNK:])
    halo_rows = passed_along(halo_rows, "blk", 1)

    last = tokens_local // CHUNK - 1
    late_chunks = [(qkv_late, 1, at) for at in range(last)]

    def attends(chunk, window):
        return (chunk, window, query_segments, key_segments)

    def projects(own):
        return (place, ring, own, swapped(own, "mp", 1), pieces, group_size)

    waiting = []
    (own,) = output_step(attends(last, late_chunks[-3:]), None)
    both = projects(own)
    rows_first, both = lax.optimization_barrier((rows_first, both[:4]))
    waiting.append((last, (*both, pieces, group_size)))
    qkv_first, _ = qkv_columns(ring, rows_first, pieces, cosine[:CHUNK], sine[:CHUNK])
    chunks = [(halo_rows, 0, 0), (halo_rows, 0, 1), (qkv_first, 1, 0)] + late_chunks
    parts = {}
    for chunk in reversed(range(last)):
        due = waiting.pop(0) if (last - chunk) % 2 else None
        step = output_step(attends(chunk, chunks[chunk : chunk + 3]), due and due[1])
        waiting.append((chunk, projects(step[0])))
        if due:
            parts[due[0]] = step[1:]
    for chunk, due in waiting:
        parts[chunk] = output_step(None, due)

    result = None
    for chunk in reversed(range(last + 1)):
        kept, inner, outer = parts[chunk]
        inner = lax.ppermute(inner, "mp", [(1, 2), (2, 1)])
        outer = lax.ppermute(outer, "mp", [(1, 3), (2, 0)])
        updates = [kept, inner, outer]
        result = final(hc_static, streams, sums_all, updates, chunk * CHUNK, result)
    return result


def solution(mesh):
    in_specs = (
        P("blk", None, "mp"),
        P(("blk", "mp"), None, None),
        P("mp", None),
        P(),
        P("blk"),
        P("blk"),
    )
    out_specs = P("blk", None, "mp")
    return jax.shard_map(body, mesh=mesh, in_specs=in_specs, out_specs=out_specs, check_vma=False)
```

```python
import functools

import jax
import jax.numpy as jnp
from jax import lax
from jax.experimental import pallas as pl
from jax.experimental.pallas import tpu as pltpu
from jax.sharding import PartitionSpec as P

D = 2048
HEAD_DIM = 128
BLOCK = 512
CHUNK = 256
SUB = 64
STEP = 128
STREAMS = 4
EPS = 1e-05
BF = jnp.bfloat16
F32 = jnp.float32


def passed_along(value, axis, steps):
    count = lax.axis_size(axis)
    first, last = (max(0, -steps), min(count, count - steps))
    return lax.ppermute(value, axis, [(source, source + steps) for source in range(first, last)])


def from_others(value, axis):
    count = lax.axis_size(axis)
    return [
        lax.ppermute(value, axis, [(source, (source + step) % count) for source in range(count)])
        for step in range(1, count)
    ]


def cost(flops, nbytes, transcendentals=0):
    return pl.CostEstimate(flops=flops, bytes_accessed=nbytes, transcendentals=transcendentals)


def params(limit=60):
    return pltpu.CompilerParams(vmem_limit_bytes=limit << 20)


def split(value, parts):
    out = []
    for _ in range(parts):
        part = value.astype(BF)
        out.append(part)
        value = value - part.astype(F32)
    return out


def contract(a, b, a_dim, b_dim):
    return lax.dot_general(a, b, (((a_dim,), (b_dim,)), ((), ())), preferred_element_type=F32)


def iotas(rows, cols):
    return (
        lax.broadcasted_iota(jnp.int32, (rows, cols), 0),
        lax.broadcasted_iota(jnp.int32, (rows, cols), 1),
    )


def regroup_kernel(place_ref, master_ref, *parts):
    servers = len(parts)
    width = master_ref.shape[-1] // servers
    for step, part_ref in enumerate(parts):
        server = (place_ref[0] + step) % servers
        own = pl.ds(pl.multiple_of(server * width, width), width)
        pair = pl.ds(pl.multiple_of((server // 2) * 2 * width, 2 * width), 2 * width)
        for slot in range(3):
            part_ref[:, slot * width : (slot + 1) * width] = master_ref[:, slot, own].astype(BF)
        part_ref[:, 3 * width :] = master_ref[:, 3, pair].astype(BF)


def regroup(place, master, servers):
    rows, _, total = master.shape
    columns = 5 * total // servers
    return pl.pallas_call(
        regroup_kernel,
        in_specs=[pl.BlockSpec(memory_space=pltpu.SMEM), pl.BlockSpec(memory_space=pltpu.VMEM)],
        out_specs=[pl.BlockSpec(memory_space=pltpu.VMEM)] * servers,
        out_shape=[jax.ShapeDtypeStruct((rows, columns), BF)] * servers,
        cost_estimate=cost(0, rows * total * 26),
        compiler_params=params(),
        name="regroup",
    )(place, master)


def assemble_kernel(place_ref, *refs):
    out_ref = refs[-1]
    parts = refs[:-1]
    rows = parts[0].shape[0]
    for step, part_ref in enumerate(parts):
        source = (place_ref[0] + len(parts) - step) % len(parts)
        out_ref[pl.ds(pl.multiple_of(source * rows, rows), rows), :] = part_ref[...]


def assemble(place, parts):
    rows, columns = parts[0].shape
    return pl.pallas_call(
        assemble_kernel,
        in_specs=[pl.BlockSpec(memory_space=pltpu.SMEM)]
        + [pl.BlockSpec(memory_space=pltpu.VMEM)] * len(parts),
        out_specs=pl.BlockSpec(memory_space=pltpu.VMEM),
        out_shape=jax.ShapeDtypeStruct((rows * len(parts), columns), BF),
        cost_estimate=cost(0, rows * columns * len(parts) * 4),
        compiler_params=params(),
        name="assemble",
    )(place, *parts)


def swapped(value, axis, mask):
    count = lax.axis_size(axis)
    return lax.ppermute(value, axis, [(source, source ^ mask) for source in range(count)])


def weight_pieces(part):
    count = lax.axis_size("blk")
    if count & (count - 1) or part.shape[0] % HEAD_DIM or count > 8:
        return [lax.all_gather(part, "blk", axis=0, tiled=True)]
    pieces = {0: part}
    for mask in range(2, count, 2):
        if mask & (mask - 1):
            low = mask & -mask
            cut = part.shape[0] // 2
            halves = [swapped(pieces[mask ^ low][:cut], "blk", low)]
            halves.append(swapped(pieces[low][cut:], "blk", mask ^ low))
            pieces[mask] = jnp.concatenate(halves, axis=0)
        else:
            pieces[mask] = swapped(part, "blk", mask)
    for mask in range(0, count, 2):
        pieces[mask + 1] = swapped(pieces[mask], "blk", 1)
    return [pieces[mask] for mask in range(count)]


def stats_kernel(x_ref, proj_ref, out_ref):
    block, _, width = x_ref.shape
    tokens = block * pl.num_programs(0)
    base = pl.program_id(0) * (block // STEP)
    proj = proj_ref[...]
    pieces = jnp.concatenate(split(proj, 3), axis=0)
    out_ref[:, out_ref.shape[1] - 128 :] = jnp.broadcast_to(jnp.sum(proj, axis=1, keepdims=True), (8, 128))
    row, col = iotas(4 * SUB, 4 * SUB)
    same = (row >> 2) == (col >> 2)
    ring = jnp.where(same, (row - col) & 3, -1)

    @pl.loop(0, block // STEP)
    def _(local):
        step = base + local
        folded = []
        for half in range(STEP // SUB):
            lanes = pl.ds(pl.multiple_of(step * 4 * STEP, 4 * STEP) + half * 4 * SUB, 4 * SUB)
            v = x_ref[pl.ds(local * STEP + half * SUB, SUB)].reshape(4 * SUB, width)
            sums = contract(pieces, v, 1, 1)
            sums = sums[0:8] + sums[8:16] + sums[16:24]
            gram = contract(v, v, 1, 1)
            out_ref[0:1, lanes] = sums[0:1]
            out_ref[1:2, lanes] = sums[6:7]
            for shift in range(3):
                out_ref[2 + shift : 3 + shift, lanes] = jnp.sum(
                    jnp.where(ring == shift, gram, 0.0), axis=0, keepdims=True
                )
            out_ref[5:8, lanes] = sums[1:4]
            folded.append(sums[4:6])
        folded = jnp.concatenate(folded, axis=1)
        lanes = pl.ds(pl.multiple_of(4 * tokens + step * STEP, STEP), STEP)
        for part in range(4):
            for which in range(2):
                out_ref[4 * which + part : 4 * which + part + 1, lanes] = folded[
                    which : which + 1, part * STEP : (part + 1) * STEP
                ]


def stats(x, proj):
    tokens, _, width = x.shape
    lanes = 5 * tokens + 128
    return pl.pallas_call(
        stats_kernel,
        grid=(tokens // (2 * STEP),),
        in_specs=[
            pl.BlockSpec((2 * STEP, 4, width), lambda i: (i, 0, 0)),
            pl.BlockSpec((8, width), lambda i: (0, 0)),
        ],
        out_specs=pl.BlockSpec((8, lanes), lambda i: (0, 0)),
        out_shape=jax.ShapeDtypeStruct((8, lanes), F32),
        cost_estimate=cost(tokens * 4 * width * 600, tokens * 8 * width),
        compiler_params=params(),
        name="stats",
    )(x, proj)


def by_stream(static_ref, column, stream):
    value = jnp.full(stream.shape, static_ref[0, column], F32)
    for k in range(1, 4):
        value = jnp.where(stream == k, static_ref[k, column], value)
    return value


def centre(first):
    mean = first[1:2] * (1.0 / D)
    spread = first[2:3] * (1.0 / D) - mean * mean
    return mean, lax.rsqrt(spread + EPS)


def mix_kernel(offset, static_ref, x_ref, own_ref, a_ref, b_ref, c_ref, sums_ref, normed_ref):
    tokens, _, width = x_ref.shape

    @pl.when(pl.program_id(0) == 0)
    def _():
        sums_ref[...] = (own_ref[...] + a_ref[...]) + (b_ref[...] + c_ref[...])

    base = 4 * (offset + pl.program_id(0) * tokens)
    last = sums_ref.shape[1] - 128
    column = sums_ref[0:1, last : last + 1]
    stream = lax.broadcasted_iota(jnp.int32, (1, 4 * STEP), 1) & 3
    static = by_stream(static_ref, 0, stream)
    row, col = iotas(SUB, 4 * SUB)
    mine = row == (col >> 2)

    @pl.loop(0, tokens // STEP)
    def _(step):
        at = pl.multiple_of(base + step * 4 * STEP, 4 * STEP)
        first = sums_ref[:, pl.ds(at, 4 * STEP)]
        mean, inverse = centre(first)
        mix = static + jnp.tanh(inverse * (first[0:1] - mean * column))
        one = jnp.where(stream < 3, pltpu.roll(mix, 4 * STEP - 1, 1), pltpu.roll(mix, 3, 1))
        two = jnp.where(stream < 2, pltpu.roll(mix, 4 * STEP - 2, 1), pltpu.roll(mix, 2, 1))
        linear = mix * first[1:2]
        square = mix * (mix * first[2:3] + 2.0 * one * first[3:4] + two * first[4:5])
        for half in range(STEP // SUB):
            lanes = slice(half * 4 * SUB, (half + 1) * 4 * SUB)
            rows = pl.ds(step * STEP + half * SUB, SUB)
            v = x_ref[rows].reshape(4 * SUB, width)
            matrix = jnp.where(mine, mix[:, lanes], 0.0)
            mixed = contract(jnp.concatenate(split(matrix, 3), axis=0), v, 1, 0)
            mixed = mixed[0:SUB] + mixed[SUB : 2 * SUB] + mixed[2 * SUB : 3 * SUB]
            average = jnp.sum(jnp.where(mine, linear[:, lanes], 0.0), axis=1, keepdims=True)
            power = jnp.sum(jnp.where(mine, square[:, lanes], 0.0), axis=1, keepdims=True)
            average, power = average * (1.0 / D), power * (1.0 / D)
            scale = lax.rsqrt(jnp.maximum(power - average * average, 0.0) + EPS)
            normed_ref[rows, :] = ((mixed - average) * scale).astype(BF)


def mix(static, x, parts, start, tokens):
    width = x.shape[-1]
    lanes = parts[0].shape[1]
    whole = pl.BlockSpec((8, lanes), lambda i: (0, 0))
    return pl.pallas_call(
        functools.partial(mix_kernel, start),
        grid=(tokens // CHUNK,),
        in_specs=[
            pl.BlockSpec(memory_space=pltpu.SMEM),
            pl.BlockSpec((CHUNK, 4, width), lambda i: (start // CHUNK + i, 0, 0)),
        ]
        + [whole] * 4,
        out_specs=[whole, pl.BlockSpec((CHUNK, width), lambda i: (i, 0))],
        out_shape=[
            jax.ShapeDtypeStruct((8, lanes), F32),
            jax.ShapeDtypeStruct((tokens, width), BF),
        ],
        cost_estimate=cost(tokens * 4 * width * 400, tokens * 10 * width),
        compiler_params=params(),
        name="mix",
    )(static, x, *parts)


def qkv_kernel(ring_ref, rows_ref, cosine_ref, sine_ref, *refs):
    out_ref, halo_ref = refs[-2:]
    pieces = refs[:-2]
    servers, _, width = rows_ref.shape
    depth = pieces[0].shape[0]
    if len(pieces) == 1:
        left = [rows_ref[server] for server in range(servers)]
    else:
        left = []
        for piece in range(len(pieces)):
            source = ring_ref[0] ^ piece
            inside = pl.multiple_of((source % (width // depth)) * depth, depth)
            left.append(rows_ref[source // (width // depth), :, pl.ds(inside, depth)])
    left = jnp.concatenate(left, axis=1)
    right = jnp.concatenate([piece[...] for piece in pieces], axis=0)
    total = contract(left, right, 1, 0)
    slot = pl.program_id(0)

    @pl.when(slot < 2)
    def _():
        cosine, sine = cosine_ref[...], sine_ref[...]
        for head in range(total.shape[1] // HEAD_DIM):
            part = total[:, head * HEAD_DIM : (head + 1) * HEAD_DIM]
            turned = part * cosine + pltpu.roll(part, HEAD_DIM // 2, 1) * sine
            out_ref[0, :, head * HEAD_DIM : (head + 1) * HEAD_DIM] = turned.astype(BF)

    @pl.when(slot == 2)
    def _():
        out_ref[0] = total.astype(BF)

    halo_ref[0] = out_ref[0, -halo_ref.shape[1] :, :]


def qkv_columns(ring, rows, pieces, cosine, sine):
    servers, tokens, width = rows.shape
    kept = min(BLOCK, tokens)
    table = pl.BlockSpec((tokens, HEAD_DIM), lambda j: (0, 0))
    return pl.pallas_call(
        qkv_kernel,
        grid=(3,),
        in_specs=[
            pl.BlockSpec(memory_space=pltpu.SMEM),
            pl.BlockSpec((servers, tokens, width), lambda j: (0, 0, 0)),
            table,
            table,
        ]
        + [pl.BlockSpec((pieces[0].shape[0], width), lambda j: (0, j))] * len(pieces),
        out_specs=[
            pl.BlockSpec((1, tokens, width), lambda j: (j, 0, 0)),
            pl.BlockSpec((1, kept, width), lambda j: (jnp.maximum(j - 1, 0), 0, 0)),
        ],
        out_shape=[
            jax.ShapeDtypeStruct((3, tokens, width), BF),
            jax.ShapeDtypeStruct((2, kept, width), BF),
        ],
        cost_estimate=cost(2 * tokens * D * 3 * width, D * 6 * width + tokens * D * 5),
        compiler_params=params(),
        name="qkv",
    )(ring, rows, cosine, sine, *pieces)


def attend_kernel(q_ref, k0, k1, k2, v0, v1, v2, qseg_ref, kseg_ref, attended_ref):
    tokens, width = q_ref.shape[1:]
    window = kseg_ref.shape[-1]
    row, col = iotas(tokens, window)
    allowed = (qseg_ref[...] == kseg_ref[0]) & (col - (window - tokens) <= row)
    bias = jnp.where(allowed, 0.0, -1e30)
    factor = 1.4426950408889634 / HEAD_DIM**0.5
    for head in range(width // HEAD_DIM):
        lanes = slice(head * HEAD_DIM, (head + 1) * HEAD_DIM)
        query = q_ref[0, :, lanes]
        scores = jnp.concatenate(
            [contract(query, k[0, :, lanes], 1, 1) for k in (k0, k1, k2)], axis=1
        )
        scores = scores + bias
        weights = jnp.exp2((scores - jnp.max(scores, axis=1, keepdims=True)) * factor)
        total = jnp.sum(weights, axis=1, keepdims=True)
        values = jnp.concatenate([v[0, :, lanes] for v in (v0, v1, v2)], axis=0)
        attended_ref[:, lanes] = (contract(weights.astype(BF), values, 1, 0) / total).astype(BF)


def attend(query, window, qseg, kseg, chunk):
    source, at = query
    width = source.shape[-1]
    block = (1, CHUNK, width)
    keys = [pl.BlockSpec(block, lambda i, s=slot, r=where: (s, r, 0)) for _, slot, where in window]
    values = [
        pl.BlockSpec(block, lambda i, s=slot + 1, r=where: (s, r, 0)) for _, slot, where in window
    ]
    arrays = [array for array, _, _ in window]
    reach = kseg.shape[-1]
    return pl.pallas_call(
        attend_kernel,
        grid=(1,),
        in_specs=[pl.BlockSpec(block, lambda i: (0, at, 0))]
        + keys
        + values
        + [
            pl.BlockSpec((CHUNK, 1), lambda i: (chunk, 0)),
            pl.BlockSpec((1, 1, reach), lambda i: (chunk, 0, 0)),
        ],
        out_specs=pl.BlockSpec((CHUNK, width), lambda i: (0, 0)),
        out_shape=jax.ShapeDtypeStruct((CHUNK, width), BF),
        cost_estimate=cost(4 * CHUNK * reach * width, CHUNK * width * 16, CHUNK * reach * 4),
        compiler_params=params(),
        name="attend",
    )(source, *arrays, *arrays, qseg, kseg)


def project_kernel(place_ref, ring_ref, own_ref, other_ref, *refs):
    pieces = refs[:-4]
    kept_ref, inner_ref, outer_ref, sums = refs[-4:]
    servers, _, width = sums.shape
    place = place_ref[0]
    even = place % 2 == 0
    own, other = own_ref[...], other_ref[...]
    both = jnp.concatenate([jnp.where(even, own, other), jnp.where(even, other, own)], axis=1)
    depth = pieces[0].shape[0]
    if len(pieces) == 1:
        for server in range(servers):
            rows = pieces[0][server * width : (server + 1) * width, :]
            sums[server] = contract(both, rows, 1, 1)
    else:
        for piece in range(len(pieces)):
            target = ring_ref[0] ^ piece
            inside = pl.multiple_of((target % (width // depth)) * depth, depth)
            sums[target // (width // depth), :, pl.ds(inside, depth)] = contract(
                both, pieces[piece][...], 1, 1
            )
    kept_ref[...] = sums[place]
    low = place < 2
    inner_ref[...] = sums[jnp.where(low, 2, 1)].astype(BF)
    outer_ref[...] = sums[jnp.where(low, 3, 0)].astype(BF)


def project(place, ring, own, other, pieces, servers):
    tokens, width = own.shape
    rows, columns = pieces[0].shape
    pair = 2 * width
    tail = pl.BlockSpec((pl.Element(rows), pl.Element(pair)), lambda i: (0, columns - pair))
    full = pl.BlockSpec((tokens, width), lambda i: (0, 0))
    return pl.pallas_call(
        project_kernel,
        grid=(1,),
        in_specs=[pl.BlockSpec(memory_space=pltpu.SMEM)] * 2 + [full] * 2 + [tail] * len(pieces),
        out_specs=[full] * 3,
        out_shape=[
            jax.ShapeDtypeStruct((tokens, width), F32),
            jax.ShapeDtypeStruct((tokens, width), BF),
            jax.ShapeDtypeStruct((tokens, width), BF),
        ],
        scratch_shapes=[pltpu.VMEM((servers, tokens, width), F32)],
        cost_estimate=cost(2 * tokens * D * pair, D * pair * 2 + tokens * width * 12),
        compiler_params=params(),
        name="project",
    )(place, ring, own, other, *pieces)


def final_kernel(
    static_ref, x_ref, first_ref, folded_ref, column_ref, own_ref, inner_ref, outer_ref, *rest
):
    new_ref = rest[-1]
    tokens, _, width = x_ref.shape
    first = first_ref[...]
    mean, inverse = centre(first)
    stream = lax.broadcasted_iota(jnp.int32, (1, 4 * tokens), 1) & 3

    def coefficient(column, projected):
        dynamic = jnp.tanh(inverse * (projected - mean * column_ref[column : column + 1, 0:1]))
        return by_stream(static_ref, column, stream) + dynamic

    def unfolded(which):
        return jnp.concatenate(
            [folded_ref[4 * which + part : 4 * which + part + 1] for part in range(4)], axis=1
        )

    projected = [first[5:6], first[6:7], first[7:8], unfolded(0), unfolded(1)]
    columns = [coefficient(1 + j, projected[j]) for j in range(5)]
    residual = jnp.concatenate(columns[:4] + columns[:4], axis=0)
    row, col = iotas(4 * SUB, 4 * SUB)
    same = (row >> 2) == (col >> 2)
    row, col = iotas(SUB, 4 * SUB)
    mine = row == (col >> 2)
    for at in range(tokens // SUB):
        lanes = slice(at * 4 * SUB, (at + 1) * 4 * SUB)
        rows = slice(at * SUB, (at + 1) * SUB)
        v = x_ref[rows].reshape(4 * SUB, width)
        matrix = jnp.where(same, jnp.tile(residual[:, lanes], (SUB // 2, 1)), 0.0)
        high, low = split(matrix, 2)
        new = contract(high, v, 1, 0) + contract(low, v, 1, 0)
        sent = inner_ref[rows, :].astype(F32) + outer_ref[rows, :].astype(F32)
        update_high, update_low = split(own_ref[rows, :] + sent, 2)
        spread_high, spread_low = split(jnp.where(mine, columns[4][:, lanes], 0.0), 2)
        new += contract(
            jnp.concatenate([spread_high, spread_high, spread_low], axis=0),
            jnp.concatenate([update_high, update_low, update_high], axis=0),
            0,
            0,
        )
        new_ref[rows] = new.astype(BF).reshape(SUB, 4, width)


def final(static, x, sums, updates, start, previous):
    tokens, width = updates[0].shape
    group = (sums.shape[1] - 128) // 5
    stream_block = pl.BlockSpec((STEP, 4, width), lambda i: (start // STEP + i, 0, 0))
    specs = [
        pl.BlockSpec(memory_space=pltpu.SMEM),
        stream_block,
        pl.BlockSpec((8, 4 * STEP), lambda i: (0, start // STEP + i)),
        pl.BlockSpec((8, STEP), lambda i: (0, 4 * group // STEP + start // STEP + i)),
        pl.BlockSpec((8, 128), lambda i: (0, 5 * group // 128)),
    ]
    specs += [pl.BlockSpec((STEP, width), lambda i: (i, 0))] * 3
    args = [static, x, sums, sums, sums, *updates]
    aliases = {}
    if previous is not None:
        specs.append(pl.BlockSpec(memory_space=pl.ANY))
        aliases = {len(args): 0}
        args.append(previous)
    return pl.pallas_call(
        final_kernel,
        grid=(tokens // STEP,),
        in_specs=specs,
        out_specs=stream_block,
        out_shape=jax.ShapeDtypeStruct(x.shape, BF),
        input_output_aliases=aliases,
        cost_estimate=cost(tokens * 4 * width * 1200, tokens * 22 * width),
        compiler_params=params(),
        name="final",
    )(*args)


def body(streams, proj_master, hc_proj, hc_static, segment_ids, block_mask):
    tokens_local, _, width = streams.shape
    group_size = lax.axis_size("mp")
    place = lax.axis_index("mp").astype(jnp.int32).reshape(1)
    ring = lax.axis_index("blk").astype(jnp.int32).reshape(1)

    proj_rows = jnp.concatenate(
        [hc_proj.T, jnp.ones((1, width), F32), jnp.zeros((1, width), F32)], axis=0
    )
    own = stats(streams, proj_rows)
    parts = list(regroup(place, proj_master, group_size))
    sums, parts = lax.optimization_barrier(([own] + from_others(own, "mp"), parts))

    def gathered(normed):
        rows = lax.all_gather(normed, "mp", axis=0, tiled=True)
        return rows.reshape(group_size, normed.shape[0], width)

    for step in range(1, group_size):
        parts[step] = lax.ppermute(
            parts[step], "mp", [(at, (at + step) % group_size) for at in range(group_size)]
        )
    sums_all, normed_late = mix(hc_static, streams, sums, CHUNK, tokens_local - CHUNK)
    _, normed_first = mix(hc_static, streams, sums, 0, CHUNK)
    parts, normed_late, normed_first = lax.optimization_barrier((parts, normed_late, normed_first))
    rows_late = gathered(normed_late)
    rows_first = gathered(normed_first)

    pieces = weight_pieces(assemble(place, parts))
    rows_late, pieces = lax.optimization_barrier((rows_late, pieces))

    halo = passed_along(segment_ids[-BLOCK:], "blk", 1)
    halo = jnp.where(lax.axis_index("blk") == 0, -1, halo)
    extended = jnp.concatenate([halo, segment_ids])
    key_at = jnp.arange(tokens_local + BLOCK, dtype=jnp.int32)[None, :]
    query_at = jnp.arange(tokens_local, dtype=jnp.int32)[:, None] + BLOCK
    earlier = (extended[None, :] == segment_ids[:, None]) & (key_at < query_at)
    positions = jnp.sum(earlier.astype(jnp.int32), axis=1)
    half = HEAD_DIM // 2
    inverse = 10000.0 ** (-(jnp.arange(half, dtype=F32) * 2.0 / HEAD_DIM))
    angles = positions.astype(F32)[:, None] * inverse[None, :]
    cosine, sine = jnp.cos(angles), jnp.sin(angles)
    cosine = jnp.concatenate([cosine, cosine], axis=1)
    sine = jnp.concatenate([-sine, sine], axis=1)
    windows = []
    for block in range(tokens_local // BLOCK):
        before = extended[block * BLOCK : (block + 1) * BLOCK]
        before = jnp.where(block_mask[block] == 1, before, -1)
        seen = jnp.concatenate([before, segment_ids[block * BLOCK : (block + 1) * BLOCK]])
        for chunk in range(BLOCK // CHUNK):
            windows.append(seen[chunk * CHUNK : chunk * CHUNK + BLOCK + CHUNK])
    key_segments = jnp.stack(windows)[:, None, :]
    query_segments = segment_ids[:, None]

    qkv_late, halo_rows = qkv_columns(ring, rows_late, pieces, cosine[CHUNK:], sine[CHUNK:])
    halo_rows = passed_along(halo_rows, "blk", 1)

    def projected(own, other):
        return project(place, ring, own, other, pieces, group_size)

    last = tokens_local // CHUNK - 1
    late_chunks = [(qkv_late, 1, at) for at in range(last)]

    def attended(chunk, window):
        source, _, at = window[-1]
        return attend((source, at), window, query_segments, key_segments, chunk)

    own = attended(last, late_chunks[-3:])
    both = (own, swapped(own, "mp", 1))
    rows_first, both = lax.optimization_barrier((rows_first, both))
    parts = {last: projected(*both)}
    qkv_first, _ = qkv_columns(ring, rows_first, pieces, cosine[:CHUNK], sine[:CHUNK])
    chunks = [(halo_rows, 0, 0), (halo_rows, 0, 1), (qkv_first, 1, 0)] + late_chunks
    for chunk in reversed(range(last)):
        own = attended(chunk, chunks[chunk : chunk + 3])
        parts[chunk] = projected(own, swapped(own, "mp", 1))

    result = None
    for chunk in reversed(range(last + 1)):
        kept, inner, outer = parts[chunk]
        outer = lax.ppermute(outer, "mp", [(1, 3), (2, 0)])
        inner = lax.ppermute(inner, "mp", [(1, 2), (2, 1)])
        updates = [kept, outer, inner]
        result = final(hc_static, streams, sums_all, updates, chunk * CHUNK, result)
    return result


def solution(mesh):
    in_specs = (
        P("blk", None, "mp"),
        P(("blk", "mp"), None, None),
        P("mp", None),
        P(),
        P("blk"),
        P("blk"),
    )
    out_specs = P("blk", None, "mp")
    return jax.shard_map(body, mesh=mesh, in_specs=in_specs, out_specs=out_specs, check_vma=False)
```

```python
import functools

import jax
import jax.numpy as jnp
from jax import lax
from jax.experimental import pallas as pl
from jax.experimental.pallas import tpu as pltpu
from jax.sharding import PartitionSpec as P

D = 2048
HEAD_DIM = 128
BLOCK = 512
CHUNK = 256
SUB = 64
STEP = 128
STREAMS = 4
EPS = 1e-05
BF = jnp.bfloat16
F32 = jnp.float32


def passed_along(value, axis, steps):
    count = lax.axis_size(axis)
    first, last = (max(0, -steps), min(count, count - steps))
    return lax.ppermute(value, axis, [(source, source + steps) for source in range(first, last)])


def from_others(value, axis):
    count = lax.axis_size(axis)
    return [
        lax.ppermute(value, axis, [(source, (source + step) % count) for source in range(count)])
        for step in range(1, count)
    ]


def cost(flops, nbytes, transcendentals=0):
    return pl.CostEstimate(flops=flops, bytes_accessed=nbytes, transcendentals=transcendentals)


def params(limit=60):
    return pltpu.CompilerParams(vmem_limit_bytes=limit << 20)


def split(value, parts):
    out = []
    for _ in range(parts):
        part = value.astype(BF)
        out.append(part)
        value = value - part.astype(F32)
    return out


def contract(a, b, a_dim, b_dim):
    return lax.dot_general(a, b, (((a_dim,), (b_dim,)), ((), ())), preferred_element_type=F32)


def iotas(rows, cols):
    return (
        lax.broadcasted_iota(jnp.int32, (rows, cols), 0),
        lax.broadcasted_iota(jnp.int32, (rows, cols), 1),
    )


def regroup_kernel(place_ref, master_ref, *parts):
    servers = len(parts)
    width = master_ref.shape[-1] // servers
    for step, part_ref in enumerate(parts):
        server = (place_ref[0] + step) % servers
        own = pl.ds(pl.multiple_of(server * width, width), width)
        pair = pl.ds(pl.multiple_of((server // 2) * 2 * width, 2 * width), 2 * width)
        for slot in range(3):
            part_ref[:, slot * width : (slot + 1) * width] = master_ref[:, slot, own].astype(BF)
        part_ref[:, 3 * width :] = master_ref[:, 3, pair].astype(BF)


def regroup(place, master, servers):
    rows, _, total = master.shape
    columns = 5 * total // servers
    return pl.pallas_call(
        regroup_kernel,
        in_specs=[pl.BlockSpec(memory_space=pltpu.SMEM), pl.BlockSpec(memory_space=pltpu.VMEM)],
        out_specs=[pl.BlockSpec(memory_space=pltpu.VMEM)] * servers,
        out_shape=[jax.ShapeDtypeStruct((rows, columns), BF)] * servers,
        cost_estimate=cost(0, rows * total * 26),
        compiler_params=params(),
        name="regroup",
    )(place, master)


def assemble_kernel(place_ref, *refs):
    out_ref = refs[-1]
    parts = refs[:-1]
    rows = parts[0].shape[0]
    for step, part_ref in enumerate(parts):
        source = (place_ref[0] + len(parts) - step) % len(parts)
        out_ref[pl.ds(pl.multiple_of(source * rows, rows), rows), :] = part_ref[...]


def assemble(place, parts):
    rows, columns = parts[0].shape
    return pl.pallas_call(
        assemble_kernel,
        in_specs=[pl.BlockSpec(memory_space=pltpu.SMEM)]
        + [pl.BlockSpec(memory_space=pltpu.VMEM)] * len(parts),
        out_specs=pl.BlockSpec(memory_space=pltpu.VMEM),
        out_shape=jax.ShapeDtypeStruct((rows * len(parts), columns), BF),
        cost_estimate=cost(0, rows * columns * len(parts) * 4),
        compiler_params=params(),
        name="assemble",
    )(place, *parts)


def swapped(value, axis, mask):
    count = lax.axis_size(axis)
    return lax.ppermute(value, axis, [(source, source ^ mask) for source in range(count)])


def weight_pieces(part):
    count = lax.axis_size("blk")
    if count & (count - 1) or part.shape[0] % HEAD_DIM or count > 8:
        return [lax.all_gather(part, "blk", axis=0, tiled=True)]
    pieces = {0: part}
    for mask in range(2, count, 2):
        if mask & (mask - 1):
            low = mask & -mask
            cut = part.shape[0] // 2
            halves = [swapped(pieces[mask ^ low][:cut], "blk", low)]
            halves.append(swapped(pieces[low][cut:], "blk", mask ^ low))
            pieces[mask] = jnp.concatenate(halves, axis=0)
        else:
            pieces[mask] = swapped(part, "blk", mask)
    for mask in range(0, count, 2):
        pieces[mask + 1] = swapped(pieces[mask], "blk", 1)
    return [pieces[mask] for mask in range(count)]


def stats_kernel(x_ref, proj_ref, out_ref):
    block, _, width = x_ref.shape
    tokens = block * pl.num_programs(0)
    base = pl.program_id(0) * (block // STEP)
    proj = proj_ref[...]
    pieces = jnp.concatenate(split(proj, 3), axis=0)
    out_ref[:, out_ref.shape[1] - 128 :] = jnp.broadcast_to(jnp.sum(proj, axis=1, keepdims=True), (8, 128))
    row, col = iotas(4 * SUB, 4 * SUB)
    same = (row >> 2) == (col >> 2)
    ring = jnp.where(same, (row - col) & 3, -1)

    @pl.loop(0, block // STEP)
    def _(local):
        step = base + local
        folded = []
        for half in range(STEP // SUB):
            lanes = pl.ds(pl.multiple_of(step * 4 * STEP, 4 * STEP) + half * 4 * SUB, 4 * SUB)
            v = x_ref[pl.ds(local * STEP + half * SUB, SUB)].reshape(4 * SUB, width)
            sums = contract(pieces, v, 1, 1)
            sums = sums[0:8] + sums[8:16] + sums[16:24]
            gram = contract(v, v, 1, 1)
            out_ref[0:1, lanes] = sums[0:1]
            out_ref[1:2, lanes] = sums[6:7]
            for shift in range(3):
                out_ref[2 + shift : 3 + shift, lanes] = jnp.sum(
                    jnp.where(ring == shift, gram, 0.0), axis=0, keepdims=True
                )
            out_ref[5:8, lanes] = sums[1:4]
            folded.append(sums[4:6])
        folded = jnp.concatenate(folded, axis=1)
        lanes = pl.ds(pl.multiple_of(4 * tokens + step * STEP, STEP), STEP)
        for part in range(4):
            for which in range(2):
                out_ref[4 * which + part : 4 * which + part + 1, lanes] = folded[
                    which : which + 1, part * STEP : (part + 1) * STEP
                ]


def stats(x, proj):
    tokens, _, width = x.shape
    lanes = 5 * tokens + 128
    return pl.pallas_call(
        stats_kernel,
        grid=(tokens // (2 * STEP),),
        in_specs=[
            pl.BlockSpec((2 * STEP, 4, width), lambda i: (i, 0, 0)),
            pl.BlockSpec((8, width), lambda i: (0, 0)),
        ],
        out_specs=pl.BlockSpec((8, lanes), lambda i: (0, 0)),
        out_shape=jax.ShapeDtypeStruct((8, lanes), F32),
        cost_estimate=cost(tokens * 4 * width * 600, tokens * 8 * width),
        compiler_params=params(),
        name="stats",
    )(x, proj)


def by_stream(static_ref, column, stream):
    value = jnp.full(stream.shape, static_ref[0, column], F32)
    for k in range(1, 4):
        value = jnp.where(stream == k, static_ref[k, column], value)
    return value


def centre(first):
    mean = first[1:2] * (1.0 / D)
    spread = first[2:3] * (1.0 / D) - mean * mean
    return mean, lax.rsqrt(spread + EPS)


def mix_kernel(offset, static_ref, x_ref, own_ref, a_ref, b_ref, c_ref, sums_ref, normed_ref):
    tokens, _, width = x_ref.shape

    @pl.when(pl.program_id(0) == 0)
    def _():
        sums_ref[...] = (own_ref[...] + a_ref[...]) + (b_ref[...] + c_ref[...])

    base = 4 * (offset + pl.program_id(0) * tokens)
    last = sums_ref.shape[1] - 128
    column = sums_ref[0:1, last : last + 1]
    stream = lax.broadcasted_iota(jnp.int32, (1, 4 * STEP), 1) & 3
    static = by_stream(static_ref, 0, stream)
    row, col = iotas(SUB, 4 * SUB)
    mine = row == (col >> 2)

    @pl.loop(0, tokens // STEP)
    def _(step):
        at = pl.multiple_of(base + step * 4 * STEP, 4 * STEP)
        first = sums_ref[:, pl.ds(at, 4 * STEP)]
        mean, inverse = centre(first)
        mix = static + jnp.tanh(inverse * (first[0:1] - mean * column))
        one = jnp.where(stream < 3, pltpu.roll(mix, 4 * STEP - 1, 1), pltpu.roll(mix, 3, 1))
        two = jnp.where(stream < 2, pltpu.roll(mix, 4 * STEP - 2, 1), pltpu.roll(mix, 2, 1))
        linear = mix * first[1:2]
        square = mix * (mix * first[2:3] + 2.0 * one * first[3:4] + two * first[4:5])
        for half in range(STEP // SUB):
            lanes = slice(half * 4 * SUB, (half + 1) * 4 * SUB)
            rows = pl.ds(step * STEP + half * SUB, SUB)
            v = x_ref[rows].reshape(4 * SUB, width)
            matrix = jnp.where(mine, mix[:, lanes], 0.0)
            mixed = contract(jnp.concatenate(split(matrix, 3), axis=0), v, 1, 0)
            mixed = mixed[0:SUB] + mixed[SUB : 2 * SUB] + mixed[2 * SUB : 3 * SUB]
            average = jnp.sum(jnp.where(mine, linear[:, lanes], 0.0), axis=1, keepdims=True)
            power = jnp.sum(jnp.where(mine, square[:, lanes], 0.0), axis=1, keepdims=True)
            average, power = average * (1.0 / D), power * (1.0 / D)
            scale = lax.rsqrt(jnp.maximum(power - average * average, 0.0) + EPS)
            normed_ref[rows, :] = ((mixed - average) * scale).astype(BF)


def mix(static, x, parts, start, tokens):
    width = x.shape[-1]
    lanes = parts[0].shape[1]
    whole = pl.BlockSpec((8, lanes), lambda i: (0, 0))
    return pl.pallas_call(
        functools.partial(mix_kernel, start),
        grid=(tokens // CHUNK,),
        in_specs=[
            pl.BlockSpec(memory_space=pltpu.SMEM),
            pl.BlockSpec((CHUNK, 4, width), lambda i: (start // CHUNK + i, 0, 0)),
        ]
        + [whole] * 4,
        out_specs=[whole, pl.BlockSpec((CHUNK, width), lambda i: (i, 0))],
        out_shape=[
            jax.ShapeDtypeStruct((8, lanes), F32),
            jax.ShapeDtypeStruct((tokens, width), BF),
        ],
        cost_estimate=cost(tokens * 4 * width * 400, tokens * 10 * width),
        compiler_params=params(),
        name="mix",
    )(static, x, *parts)


def qkv_kernel(ring_ref, rows_ref, cosine_ref, sine_ref, *refs):
    out_ref, halo_ref = refs[-2:]
    pieces = refs[:-2]
    servers, _, width = rows_ref.shape
    depth = pieces[0].shape[0]
    if len(pieces) == 1:
        left = [rows_ref[server] for server in range(servers)]
    else:
        left = []
        for piece in range(len(pieces)):
            source = ring_ref[0] ^ piece
            inside = pl.multiple_of((source % (width // depth)) * depth, depth)
            left.append(rows_ref[source // (width // depth), :, pl.ds(inside, depth)])
    left = jnp.concatenate(left, axis=1)
    right = jnp.concatenate([piece[...] for piece in pieces], axis=0)
    total = contract(left, right, 1, 0)
    slot = pl.program_id(0)

    @pl.when(slot < 2)
    def _():
        cosine, sine = cosine_ref[...], sine_ref[...]
        for head in range(total.shape[1] // HEAD_DIM):
            part = total[:, head * HEAD_DIM : (head + 1) * HEAD_DIM]
            turned = part * cosine + pltpu.roll(part, HEAD_DIM // 2, 1) * sine
            out_ref[0, :, head * HEAD_DIM : (head + 1) * HEAD_DIM] = turned.astype(BF)

    @pl.when(slot == 2)
    def _():
        out_ref[0] = total.astype(BF)

    halo_ref[0] = out_ref[0, -halo_ref.shape[1] :, :]


def qkv_columns(ring, rows, pieces, cosine, sine):
    servers, tokens, width = rows.shape
    kept = min(BLOCK, tokens)
    table = pl.BlockSpec((tokens, HEAD_DIM), lambda j: (0, 0))
    return pl.pallas_call(
        qkv_kernel,
        grid=(3,),
        in_specs=[
            pl.BlockSpec(memory_space=pltpu.SMEM),
            pl.BlockSpec((servers, tokens, width), lambda j: (0, 0, 0)),
            table,
            table,
        ]
        + [pl.BlockSpec((pieces[0].shape[0], width), lambda j: (0, j))] * len(pieces),
        out_specs=[
            pl.BlockSpec((1, tokens, width), lambda j: (j, 0, 0)),
            pl.BlockSpec((1, kept, width), lambda j: (jnp.maximum(j - 1, 0), 0, 0)),
        ],
        out_shape=[
            jax.ShapeDtypeStruct((3, tokens, width), BF),
            jax.ShapeDtypeStruct((2, kept, width), BF),
        ],
        cost_estimate=cost(2 * tokens * D * 3 * width, D * 6 * width + tokens * D * 5),
        compiler_params=params(),
        name="qkv",
    )(ring, rows, cosine, sine, *pieces)


def attend_kernel(q_ref, k0, k1, k2, v0, v1, v2, qseg_ref, kseg_ref, attended_ref):
    tokens, width = q_ref.shape[1:]
    window = kseg_ref.shape[-1]
    row, col = iotas(tokens, window)
    allowed = (qseg_ref[...] == kseg_ref[0]) & (col - (window - tokens) <= row)
    bias = jnp.where(allowed, 0.0, -1e30)
    factor = 1.4426950408889634 / HEAD_DIM**0.5
    for head in range(width // HEAD_DIM):
        lanes = slice(head * HEAD_DIM, (head + 1) * HEAD_DIM)
        query = q_ref[0, :, lanes]
        scores = jnp.concatenate(
            [contract(query, k[0, :, lanes], 1, 1) for k in (k0, k1, k2)], axis=1
        )
        scores = scores + bias
        weights = jnp.exp2((scores - jnp.max(scores, axis=1, keepdims=True)) * factor)
        total = jnp.sum(weights, axis=1, keepdims=True)
        values = jnp.concatenate([v[0, :, lanes] for v in (v0, v1, v2)], axis=0)
        attended_ref[:, lanes] = (contract(weights.astype(BF), values, 1, 0) / total).astype(BF)


def attend(query, window, qseg, kseg, chunk):
    source, at = query
    width = source.shape[-1]
    block = (1, CHUNK, width)
    keys = [pl.BlockSpec(block, lambda i, s=slot, r=where: (s, r, 0)) for _, slot, where in window]
    values = [
        pl.BlockSpec(block, lambda i, s=slot + 1, r=where: (s, r, 0)) for _, slot, where in window
    ]
    arrays = [array for array, _, _ in window]
    reach = kseg.shape[-1]
    return pl.pallas_call(
        attend_kernel,
        grid=(1,),
        in_specs=[pl.BlockSpec(block, lambda i: (0, at, 0))]
        + keys
        + values
        + [
            pl.BlockSpec((CHUNK, 1), lambda i: (chunk, 0)),
            pl.BlockSpec((1, 1, reach), lambda i: (chunk, 0, 0)),
        ],
        out_specs=pl.BlockSpec((CHUNK, width), lambda i: (0, 0)),
        out_shape=jax.ShapeDtypeStruct((CHUNK, width), BF),
        cost_estimate=cost(4 * CHUNK * reach * width, CHUNK * width * 16, CHUNK * reach * 4),
        compiler_params=params(),
        name="attend",
    )(source, *arrays, *arrays, qseg, kseg)


def project_kernel(place_ref, ring_ref, own_ref, other_ref, *refs):
    pieces = refs[:-4]
    kept_ref, inner_ref, outer_ref, sums = refs[-4:]
    servers, _, width = sums.shape
    place = place_ref[0]
    even = place % 2 == 0
    own, other = own_ref[...], other_ref[...]
    both = jnp.concatenate([jnp.where(even, own, other), jnp.where(even, other, own)], axis=1)
    depth = pieces[0].shape[0]
    if len(pieces) == 1:
        for server in range(servers):
            rows = pieces[0][server * width : (server + 1) * width, :]
            sums[server] = contract(both, rows, 1, 1)
    else:
        for piece in range(len(pieces)):
            target = ring_ref[0] ^ piece
            inside = pl.multiple_of((target % (width // depth)) * depth, depth)
            sums[target // (width // depth), :, pl.ds(inside, depth)] = contract(
                both, pieces[piece][...], 1, 1
            )
    kept_ref[...] = sums[place]
    low = place < 2
    inner_ref[...] = sums[jnp.where(low, 2, 1)].astype(BF)
    outer_ref[...] = sums[jnp.where(low, 3, 0)].astype(BF)


def project(place, ring, own, other, pieces, servers):
    tokens, width = own.shape
    rows, columns = pieces[0].shape
    pair = 2 * width
    tail = pl.BlockSpec((pl.Element(rows), pl.Element(pair)), lambda i: (0, columns - pair))
    full = pl.BlockSpec((tokens, width), lambda i: (0, 0))
    return pl.pallas_call(
        project_kernel,
        grid=(1,),
        in_specs=[pl.BlockSpec(memory_space=pltpu.SMEM)] * 2 + [full] * 2 + [tail] * len(pieces),
        out_specs=[full] * 3,
        out_shape=[
            jax.ShapeDtypeStruct((tokens, width), F32),
            jax.ShapeDtypeStruct((tokens, width), BF),
            jax.ShapeDtypeStruct((tokens, width), BF),
        ],
        scratch_shapes=[pltpu.VMEM((servers, tokens, width), F32)],
        cost_estimate=cost(2 * tokens * D * pair, D * pair * 2 + tokens * width * 12),
        compiler_params=params(),
        name="project",
    )(place, ring, own, other, *pieces)


def final_kernel(
    static_ref, x_ref, first_ref, folded_ref, column_ref, own_ref, inner_ref, outer_ref, *rest
):
    new_ref = rest[-1]
    tokens, _, width = x_ref.shape
    first = first_ref[...]
    mean, inverse = centre(first)
    stream = lax.broadcasted_iota(jnp.int32, (1, 4 * tokens), 1) & 3

    def coefficient(column, projected):
        dynamic = jnp.tanh(inverse * (projected - mean * column_ref[column : column + 1, 0:1]))
        return by_stream(static_ref, column, stream) + dynamic

    def unfolded(which):
        return jnp.concatenate(
            [folded_ref[4 * which + part : 4 * which + part + 1] for part in range(4)], axis=1
        )

    projected = [first[5:6], first[6:7], first[7:8], unfolded(0), unfolded(1)]
    columns = [coefficient(1 + j, projected[j]) for j in range(5)]
    residual = jnp.concatenate(columns[:4] + columns[:4], axis=0)
    row, col = iotas(4 * SUB, 4 * SUB)
    same = (row >> 2) == (col >> 2)
    row, col = iotas(SUB, 4 * SUB)
    mine = row == (col >> 2)
    for at in range(tokens // SUB):
        lanes = slice(at * 4 * SUB, (at + 1) * 4 * SUB)
        rows = slice(at * SUB, (at + 1) * SUB)
        v = x_ref[rows].reshape(4 * SUB, width)
        matrix = jnp.where(same, jnp.tile(residual[:, lanes], (SUB // 2, 1)), 0.0)
        high, low = split(matrix, 2)
        new = contract(high, v, 1, 0) + contract(low, v, 1, 0)
        sent = inner_ref[rows, :].astype(F32) + outer_ref[rows, :].astype(F32)
        update_high, update_low = split(own_ref[rows, :] + sent, 2)
        spread_high, spread_low = split(jnp.where(mine, columns[4][:, lanes], 0.0), 2)
        new += contract(
            jnp.concatenate([spread_high, spread_high, spread_low], axis=0),
            jnp.concatenate([update_high, update_low, update_high], axis=0),
            0,
            0,
        )
        new_ref[rows] = new.astype(BF).reshape(SUB, 4, width)


def final(static, x, sums, updates, start, previous):
    tokens, width = updates[0].shape
    group = (sums.shape[1] - 128) // 5
    stream_block = pl.BlockSpec((STEP, 4, width), lambda i: (start // STEP + i, 0, 0))
    specs = [
        pl.BlockSpec(memory_space=pltpu.SMEM),
        stream_block,
        pl.BlockSpec((8, 4 * STEP), lambda i: (0, start // STEP + i)),
        pl.BlockSpec((8, STEP), lambda i: (0, 4 * group // STEP + start // STEP + i)),
        pl.BlockSpec((8, 128), lambda i: (0, 5 * group // 128)),
    ]
    specs += [pl.BlockSpec((STEP, width), lambda i: (i, 0))] * 3
    args = [static, x, sums, sums, sums, *updates]
    aliases = {}
    if previous is not None:
        specs.append(pl.BlockSpec(memory_space=pl.ANY))
        aliases = {len(args): 0}
        args.append(previous)
    return pl.pallas_call(
        final_kernel,
        grid=(tokens // STEP,),
        in_specs=specs,
        out_specs=stream_block,
        out_shape=jax.ShapeDtypeStruct(x.shape, BF),
        input_output_aliases=aliases,
        cost_estimate=cost(tokens * 4 * width * 1200, tokens * 22 * width),
        compiler_params=params(),
        name="final",
    )(*args)


def body(streams, proj_master, hc_proj, hc_static, segment_ids, block_mask):
    tokens_local, _, width = streams.shape
    group_size = lax.axis_size("mp")
    place = lax.axis_index("mp").astype(jnp.int32).reshape(1)
    ring = lax.axis_index("blk").astype(jnp.int32).reshape(1)

    proj_rows = jnp.concatenate(
        [hc_proj.T, jnp.ones((1, width), F32), jnp.zeros((1, width), F32)], axis=0
    )
    own = stats(streams, proj_rows)
    parts = list(regroup(place, proj_master, group_size))
    sums, parts = lax.optimization_barrier(([own] + from_others(own, "mp"), parts))

    def gathered(normed):
        rows = lax.all_gather(normed, "mp", axis=0, tiled=True)
        return rows.reshape(group_size, normed.shape[0], width)

    for step in range(1, group_size):
        parts[step] = lax.ppermute(
            parts[step], "mp", [(at, (at + step) % group_size) for at in range(group_size)]
        )
    sums_all, normed_late = mix(hc_static, streams, sums, CHUNK, tokens_local - CHUNK)
    _, normed_first = mix(hc_static, streams, sums, 0, CHUNK)
    parts, normed_late, normed_first = lax.optimization_barrier((parts, normed_late, normed_first))
    rows_late = gathered(normed_late)
    rows_first = gathered(normed_first)

    pieces = weight_pieces(assemble(place, parts))
    rows_late, pieces = lax.optimization_barrier((rows_late, pieces))

    halo = passed_along(segment_ids[-BLOCK:], "blk", 1)
    halo = jnp.where(lax.axis_index("blk") == 0, -1, halo)
    extended = jnp.concatenate([halo, segment_ids])
    key_at = jnp.arange(tokens_local + BLOCK, dtype=jnp.int32)[None, :]
    query_at = jnp.arange(tokens_local, dtype=jnp.int32)[:, None] + BLOCK
    earlier = (extended[None, :] == segment_ids[:, None]) & (key_at < query_at)
    positions = jnp.sum(earlier.astype(jnp.int32), axis=1)
    half = HEAD_DIM // 2
    inverse = 10000.0 ** (-(jnp.arange(half, dtype=F32) * 2.0 / HEAD_DIM))
    angles = positions.astype(F32)[:, None] * inverse[None, :]
    cosine, sine = jnp.cos(angles), jnp.sin(angles)
    cosine = jnp.concatenate([cosine, cosine], axis=1)
    sine = jnp.concatenate([-sine, sine], axis=1)
    windows = []
    for block in range(tokens_local // BLOCK):
        before = extended[block * BLOCK : (block + 1) * BLOCK]
        before = jnp.where(block_mask[block] == 1, before, -1)
        seen = jnp.concatenate([before, segment_ids[block * BLOCK : (block + 1) * BLOCK]])
        for chunk in range(BLOCK // CHUNK):
            windows.append(seen[chunk * CHUNK : chunk * CHUNK + BLOCK + CHUNK])
    key_segments = jnp.stack(windows)[:, None, :]
    query_segments = segment_ids[:, None]

    qkv_late, halo_rows = qkv_columns(ring, rows_late, pieces, cosine[CHUNK:], sine[CHUNK:])
    halo_rows = passed_along(halo_rows, "blk", 1)

    def projected(own, other):
        return project(place, ring, own, other, pieces, group_size)

    last = tokens_local // CHUNK - 1
    late_chunks = [(qkv_late, 1, at) for at in range(last)]

    def attended(chunk, window):
        source, _, at = window[-1]
        return attend((source, at), window, query_segments, key_segments, chunk)

    own = attended(last, late_chunks[-3:])
    both = (own, swapped(own, "mp", 1))
    rows_first, both = lax.optimization_barrier((rows_first, both))
    parts = {last: projected(*both)}
    qkv_first, _ = qkv_columns(ring, rows_first, pieces, cosine[:CHUNK], sine[:CHUNK])
    chunks = [(halo_rows, 0, 0), (halo_rows, 0, 1), (qkv_first, 1, 0)] + late_chunks
    def crossed(parts):
        kept, inner, outer = parts
        outer = lax.ppermute(outer, "mp", [(1, 3), (2, 0)])
        inner = lax.ppermute(inner, "mp", [(1, 2), (2, 1)])
        return [kept, outer, inner]

    updates = {last: crossed(parts[last])}
    for chunk in reversed(range(last)):
        own = attended(chunk, chunks[chunk : chunk + 3])
        both = (own, swapped(own, "mp", 1))
        if chunk == last - 2:
            both, updates[last] = lax.optimization_barrier((both, updates[last]))
        updates[chunk] = crossed(projected(*both))

    result = None
    for chunk in reversed(range(last + 1)):
        result = final(hc_static, streams, sums_all, updates[chunk], chunk * CHUNK, result)
    return result


def solution(mesh):
    in_specs = (
        P("blk", None, "mp"),
        P(("blk", "mp"), None, None),
        P("mp", None),
        P(),
        P("blk"),
        P("blk"),
    )
    out_specs = P("blk", None, "mp")
    return jax.shard_map(body, mesh=mesh, in_specs=in_specs, out_specs=out_specs, check_vma=False)
```

```python
import functools

import jax
import jax.numpy as jnp
from jax import lax
from jax.experimental import pallas as pl
from jax.experimental.pallas import tpu as pltpu
from jax.sharding import PartitionSpec as P

D = 2048
HEAD_DIM = 128
BLOCK = 512
CHUNK = 256
SUB = 64
STEP = 128
STREAMS = 4
EPS = 1e-05
BF = jnp.bfloat16
F32 = jnp.float32


def passed_along(value, axis, steps):
    count = lax.axis_size(axis)
    first, last = (max(0, -steps), min(count, count - steps))
    return lax.ppermute(value, axis, [(source, source + steps) for source in range(first, last)])


def from_others(value, axis):
    count = lax.axis_size(axis)
    return [
        lax.ppermute(value, axis, [(source, (source + step) % count) for source in range(count)])
        for step in range(1, count)
    ]


def cost(flops, nbytes, transcendentals=0):
    return pl.CostEstimate(flops=flops, bytes_accessed=nbytes, transcendentals=transcendentals)


def params(limit=60):
    return pltpu.CompilerParams(vmem_limit_bytes=limit << 20)


def split(value, parts):
    out = []
    for _ in range(parts):
        part = value.astype(BF)
        out.append(part)
        value = value - part.astype(F32)
    return out


def contract(a, b, a_dim, b_dim):
    return lax.dot_general(a, b, (((a_dim,), (b_dim,)), ((), ())), preferred_element_type=F32)


def iotas(rows, cols):
    return (
        lax.broadcasted_iota(jnp.int32, (rows, cols), 0),
        lax.broadcasted_iota(jnp.int32, (rows, cols), 1),
    )


def regroup_kernel(place_ref, master_ref, *parts):
    servers = len(parts)
    width = master_ref.shape[-1] // servers
    for step, part_ref in enumerate(parts):
        server = (place_ref[0] + step) % servers
        own = pl.ds(pl.multiple_of(server * width, width), width)
        pair = pl.ds(pl.multiple_of((server // 2) * 2 * width, 2 * width), 2 * width)
        for slot in range(3):
            part_ref[:, slot * width : (slot + 1) * width] = master_ref[:, slot, own].astype(BF)
        part_ref[:, 3 * width :] = master_ref[:, 3, pair].astype(BF)


def regroup(place, master, servers):
    rows, _, total = master.shape
    columns = 5 * total // servers
    return pl.pallas_call(
        regroup_kernel,
        in_specs=[pl.BlockSpec(memory_space=pltpu.SMEM), pl.BlockSpec(memory_space=pltpu.VMEM)],
        out_specs=[pl.BlockSpec(memory_space=pltpu.VMEM)] * servers,
        out_shape=[jax.ShapeDtypeStruct((rows, columns), BF)] * servers,
        cost_estimate=cost(0, rows * total * 26),
        compiler_params=params(),
        name="regroup",
    )(place, master)


def assemble_kernel(place_ref, *refs):
    out_ref = refs[-1]
    parts = refs[:-1]
    rows = parts[0].shape[0]
    for step, part_ref in enumerate(parts):
        source = (place_ref[0] + len(parts) - step) % len(parts)
        out_ref[pl.ds(pl.multiple_of(source * rows, rows), rows), :] = part_ref[...]


def assemble(place, parts):
    rows, columns = parts[0].shape
    return pl.pallas_call(
        assemble_kernel,
        in_specs=[pl.BlockSpec(memory_space=pltpu.SMEM)]
        + [pl.BlockSpec(memory_space=pltpu.VMEM)] * len(parts),
        out_specs=pl.BlockSpec(memory_space=pltpu.VMEM),
        out_shape=jax.ShapeDtypeStruct((rows * len(parts), columns), BF),
        cost_estimate=cost(0, rows * columns * len(parts) * 4),
        compiler_params=params(),
        name="assemble",
    )(place, *parts)


def swapped(value, axis, mask):
    count = lax.axis_size(axis)
    return lax.ppermute(value, axis, [(source, source ^ mask) for source in range(count)])


def weight_pieces(part):
    count = lax.axis_size("blk")
    if count & (count - 1) or part.shape[0] % HEAD_DIM or count > 8:
        return [lax.all_gather(part, "blk", axis=0, tiled=True)]
    pieces = {0: part}
    for mask in range(2, count, 2):
        if mask & (mask - 1):
            low = mask & -mask
            cut = part.shape[0] // 2
            halves = [swapped(pieces[mask ^ low][:cut], "blk", low)]
            halves.append(swapped(pieces[low][cut:], "blk", mask ^ low))
            pieces[mask] = jnp.concatenate(halves, axis=0)
        else:
            pieces[mask] = swapped(part, "blk", mask)
    for mask in range(0, count, 2):
        pieces[mask + 1] = swapped(pieces[mask], "blk", 1)
    return [pieces[mask] for mask in range(count)]


def stats_kernel(x_ref, proj_ref, out_ref):
    block, _, width = x_ref.shape
    tokens = block * pl.num_programs(0)
    base = pl.program_id(0) * (block // STEP)
    proj = proj_ref[...]
    pieces = jnp.concatenate(split(proj, 3), axis=0)
    out_ref[:, out_ref.shape[1] - 128 :] = jnp.broadcast_to(jnp.sum(proj, axis=1, keepdims=True), (8, 128))
    row, col = iotas(4 * SUB, 4 * SUB)
    same = (row >> 2) == (col >> 2)
    ring = jnp.where(same, (row - col) & 3, -1)

    @pl.loop(0, block // STEP)
    def _(local):
        step = base + local
        folded = []
        for half in range(STEP // SUB):
            lanes = pl.ds(pl.multiple_of(step * 4 * STEP, 4 * STEP) + half * 4 * SUB, 4 * SUB)
            v = x_ref[pl.ds(local * STEP + half * SUB, SUB)].reshape(4 * SUB, width)
            sums = contract(pieces, v, 1, 1)
            sums = sums[0:8] + sums[8:16] + sums[16:24]
            gram = contract(v, v, 1, 1)
            out_ref[0:1, lanes] = sums[0:1]
            out_ref[1:2, lanes] = sums[6:7]
            for shift in range(3):
                out_ref[2 + shift : 3 + shift, lanes] = jnp.sum(
                    jnp.where(ring == shift, gram, 0.0), axis=0, keepdims=True
                )
            out_ref[5:8, lanes] = sums[1:4]
            folded.append(sums[4:6])
        folded = jnp.concatenate(folded, axis=1)
        lanes = pl.ds(pl.multiple_of(4 * tokens + step * STEP, STEP), STEP)
        for part in range(4):
            for which in range(2):
                out_ref[4 * which + part : 4 * which + part + 1, lanes] = folded[
                    which : which + 1, part * STEP : (part + 1) * STEP
                ]


def stats(x, proj):
    tokens, _, width = x.shape
    lanes = 5 * tokens + 128
    return pl.pallas_call(
        stats_kernel,
        grid=(tokens // (2 * STEP),),
        in_specs=[
            pl.BlockSpec((2 * STEP, 4, width), lambda i: (i, 0, 0)),
            pl.BlockSpec((8, width), lambda i: (0, 0)),
        ],
        out_specs=pl.BlockSpec((8, lanes), lambda i: (0, 0)),
        out_shape=jax.ShapeDtypeStruct((8, lanes), F32),
        cost_estimate=cost(tokens * 4 * width * 600, tokens * 8 * width),
        compiler_params=params(),
        name="stats",
    )(x, proj)


def by_stream(static_ref, column, stream):
    value = jnp.full(stream.shape, static_ref[0, column], F32)
    for k in range(1, 4):
        value = jnp.where(stream == k, static_ref[k, column], value)
    return value


def centre(first):
    mean = first[1:2] * (1.0 / D)
    spread = first[2:3] * (1.0 / D) - mean * mean
    return mean, lax.rsqrt(spread + EPS)


def mix_kernel(offset, static_ref, x_ref, own_ref, a_ref, b_ref, c_ref, sums_ref, normed_ref):
    tokens, _, width = x_ref.shape

    @pl.when(pl.program_id(0) == 0)
    def _():
        sums_ref[...] = (own_ref[...] + a_ref[...]) + (b_ref[...] + c_ref[...])

    base = 4 * (offset + pl.program_id(0) * tokens)
    last = sums_ref.shape[1] - 128
    column = sums_ref[0:1, last : last + 1]
    stream = lax.broadcasted_iota(jnp.int32, (1, 4 * STEP), 1) & 3
    static = by_stream(static_ref, 0, stream)
    row, col = iotas(SUB, 4 * SUB)
    mine = row == (col >> 2)

    @pl.loop(0, tokens // STEP)
    def _(step):
        at = pl.multiple_of(base + step * 4 * STEP, 4 * STEP)
        first = sums_ref[:, pl.ds(at, 4 * STEP)]
        mean, inverse = centre(first)
        mix = static + jnp.tanh(inverse * (first[0:1] - mean * column))
        one = jnp.where(stream < 3, pltpu.roll(mix, 4 * STEP - 1, 1), pltpu.roll(mix, 3, 1))
        two = jnp.where(stream < 2, pltpu.roll(mix, 4 * STEP - 2, 1), pltpu.roll(mix, 2, 1))
        linear = mix * first[1:2]
        square = mix * (mix * first[2:3] + 2.0 * one * first[3:4] + two * first[4:5])
        for half in range(STEP // SUB):
            lanes = slice(half * 4 * SUB, (half + 1) * 4 * SUB)
            rows = pl.ds(step * STEP + half * SUB, SUB)
            v = x_ref[rows].reshape(4 * SUB, width)
            matrix = jnp.where(mine, mix[:, lanes], 0.0)
            mixed = contract(jnp.concatenate(split(matrix, 3), axis=0), v, 1, 0)
            mixed = mixed[0:SUB] + mixed[SUB : 2 * SUB] + mixed[2 * SUB : 3 * SUB]
            average = jnp.sum(jnp.where(mine, linear[:, lanes], 0.0), axis=1, keepdims=True)
            power = jnp.sum(jnp.where(mine, square[:, lanes], 0.0), axis=1, keepdims=True)
            average, power = average * (1.0 / D), power * (1.0 / D)
            scale = lax.rsqrt(jnp.maximum(power - average * average, 0.0) + EPS)
            normed_ref[rows, :] = ((mixed - average) * scale).astype(BF)


def mix(static, x, parts, start, tokens):
    width = x.shape[-1]
    lanes = parts[0].shape[1]
    whole = pl.BlockSpec((8, lanes), lambda i: (0, 0))
    return pl.pallas_call(
        functools.partial(mix_kernel, start),
        grid=(tokens // CHUNK,),
        in_specs=[
            pl.BlockSpec(memory_space=pltpu.SMEM),
            pl.BlockSpec((CHUNK, 4, width), lambda i: (start // CHUNK + i, 0, 0)),
        ]
        + [whole] * 4,
        out_specs=[whole, pl.BlockSpec((CHUNK, width), lambda i: (i, 0))],
        out_shape=[
            jax.ShapeDtypeStruct((8, lanes), F32),
            jax.ShapeDtypeStruct((tokens, width), BF),
        ],
        cost_estimate=cost(tokens * 4 * width * 400, tokens * 10 * width),
        compiler_params=params(),
        name="mix",
    )(static, x, *parts)


def qkv_kernel(ring_ref, rows_ref, cosine_ref, sine_ref, *refs):
    out_ref, halo_ref = refs[-2:]
    pieces = refs[:-2]
    servers, _, width = rows_ref.shape
    depth = pieces[0].shape[0]
    if len(pieces) == 1:
        left = [rows_ref[server] for server in range(servers)]
    else:
        left = []
        for piece in range(len(pieces)):
            source = ring_ref[0] ^ piece
            inside = pl.multiple_of((source % (width // depth)) * depth, depth)
            left.append(rows_ref[source // (width // depth), :, pl.ds(inside, depth)])
    left = jnp.concatenate(left, axis=1)
    right = jnp.concatenate([piece[...] for piece in pieces], axis=0)
    total = contract(left, right, 1, 0)
    slot = pl.program_id(0)

    @pl.when(slot < 2)
    def _():
        cosine, sine = cosine_ref[...], sine_ref[...]
        for head in range(total.shape[1] // HEAD_DIM):
            part = total[:, head * HEAD_DIM : (head + 1) * HEAD_DIM]
            turned = part * cosine + pltpu.roll(part, HEAD_DIM // 2, 1) * sine
            out_ref[0, :, head * HEAD_DIM : (head + 1) * HEAD_DIM] = turned.astype(BF)

    @pl.when(slot == 2)
    def _():
        out_ref[0] = total.astype(BF)

    halo_ref[0] = out_ref[0, -halo_ref.shape[1] :, :]


def qkv_columns(ring, rows, pieces, cosine, sine):
    servers, tokens, width = rows.shape
    kept = min(BLOCK, tokens)
    table = pl.BlockSpec((tokens, HEAD_DIM), lambda j: (0, 0))
    return pl.pallas_call(
        qkv_kernel,
        grid=(3,),
        in_specs=[
            pl.BlockSpec(memory_space=pltpu.SMEM),
            pl.BlockSpec((servers, tokens, width), lambda j: (0, 0, 0)),
            table,
            table,
        ]
        + [pl.BlockSpec((pieces[0].shape[0], width), lambda j: (0, j))] * len(pieces),
        out_specs=[
            pl.BlockSpec((1, tokens, width), lambda j: (j, 0, 0)),
            pl.BlockSpec((1, kept, width), lambda j: (jnp.maximum(j - 1, 0), 0, 0)),
        ],
        out_shape=[
            jax.ShapeDtypeStruct((3, tokens, width), BF),
            jax.ShapeDtypeStruct((2, kept, width), BF),
        ],
        cost_estimate=cost(2 * tokens * D * 3 * width, D * 6 * width + tokens * D * 5),
        compiler_params=params(),
        name="qkv",
    )(ring, rows, cosine, sine, *pieces)


def attend_step(q_ref, k0, k1, k2, v0, v1, v2, qseg_ref, kseg_ref, attended_ref):
    tokens, width = q_ref.shape[1:]
    window = kseg_ref.shape[-1]
    row, col = iotas(tokens, window)
    allowed = (qseg_ref[...] == kseg_ref[0]) & (col - (window - tokens) <= row)
    bias = jnp.where(allowed, 0.0, -1e30)
    factor = 1.4426950408889634 / HEAD_DIM**0.5
    for head in range(width // HEAD_DIM):
        lanes = slice(head * HEAD_DIM, (head + 1) * HEAD_DIM)
        query = q_ref[0, :, lanes]
        scores = jnp.concatenate(
            [contract(query, k[0, :, lanes], 1, 1) for k in (k0, k1, k2)], axis=1
        )
        scores = scores + bias
        weights = jnp.exp2((scores - jnp.max(scores, axis=1, keepdims=True)) * factor)
        total = jnp.sum(weights, axis=1, keepdims=True)
        values = jnp.concatenate([v[0, :, lanes] for v in (v0, v1, v2)], axis=0)
        attended_ref[:, lanes] = (contract(weights.astype(BF), values, 1, 0) / total).astype(BF)


def project_step(place_ref, ring_ref, own_ref, other_ref, pieces, kept_ref, inner_ref, outer_ref, sums):
    servers, _, width = sums.shape
    half = pl.program_id(0)
    place = place_ref[0]
    left = jnp.where(place % 2 == half, own_ref[...], other_ref[...])
    depth = pieces[0].shape[0]

    def add(server, lanes, rows):
        so_far = jnp.where(half == 0, 0.0, sums[server, :, lanes])
        sums[server, :, lanes] = so_far + contract(left, rows, 1, 1)

    if len(pieces) == 1:
        for server in range(servers):
            add(server, slice(None), pieces[0][server * width : (server + 1) * width, :])
    else:
        for at, piece in enumerate(pieces):
            target = ring_ref[0] ^ at
            inside = pl.multiple_of((target % (width // depth)) * depth, depth)
            add(target // (width // depth), pl.ds(inside, depth), piece[...])

    @pl.when(half == 1)
    def _():
        kept_ref[...] = sums[place]
        low = place < 2
        inner_ref[...] = sums[jnp.where(low, 2, 1)].astype(BF)
        outer_ref[...] = sums[jnp.where(low, 3, 0)].astype(BF)


def output_kernel(attends, projects, *refs):
    refs = list(refs)
    left = [refs.pop(0) for _ in range(9 if attends else 0)]
    right = [refs.pop(0) for _ in range(4 if projects else 0)]
    sums = refs.pop() if projects else None
    updates = [refs.pop() for _ in range(3 if projects else 0)][::-1]
    if attends:
        attended_ref = refs.pop()

        @pl.when(pl.program_id(0) == 0)
        def _():
            attend_step(*left, attended_ref)

    if projects:
        project_step(*right, refs, *updates, sums)


def output_step(attends, projects):
    specs, args, outs, shapes, scratch = [], [], [], [], []
    work = 0
    smem = pl.BlockSpec(memory_space=pltpu.SMEM)
    if attends:
        chunk, window, qseg, kseg = attends
        source, _, at = window[-1]
        width = source.shape[-1]
        block = (1, CHUNK, width)
        reach = kseg.shape[-1]
        specs.append(pl.BlockSpec(block, lambda i: (0, at, 0)))
        for which in range(2):
            specs += [
                pl.BlockSpec(block, lambda i, s=slot + which, r=where: (s, r, 0))
                for _, slot, where in window
            ]
        specs += [
            pl.BlockSpec((CHUNK, 1), lambda i: (chunk, 0)),
            pl.BlockSpec((1, 1, reach), lambda i: (chunk, 0, 0)),
        ]
        args += [source] + [array for array, _, _ in window] * 2 + [qseg, kseg]
        outs.append(pl.BlockSpec((CHUNK, width), lambda i: (0, 0)))
        shapes.append(jax.ShapeDtypeStruct((CHUNK, width), BF))
        work += 4 * CHUNK * reach * width
    if projects:
        place, ring, own, other, pieces, servers = projects
        tokens, width = own.shape
        rows, columns = pieces[0].shape
        full = pl.BlockSpec((tokens, width), lambda i: (0, 0))
        tail = pl.BlockSpec((rows, width), lambda i: (0, columns // width - 2 + i))
        specs += [smem] * 2 + [full] * 2 + [tail] * len(pieces)
        args += [place, ring, own, other, *pieces]
        outs += [full] * 3
        shapes += [jax.ShapeDtypeStruct((tokens, width), kind) for kind in (F32, BF, BF)]
        scratch.append(pltpu.VMEM((servers, tokens, width), F32))
        work += 4 * tokens * D * width
    return pl.pallas_call(
        functools.partial(output_kernel, bool(attends), bool(projects)),
        grid=(2 if projects else 1,),
        in_specs=specs,
        out_specs=outs,
        out_shape=shapes,
        scratch_shapes=scratch,
        cost_estimate=cost(work, work // 512),
        compiler_params=params(),
        name="output" if attends and projects else "attend" if attends else "project",
    )(*args)


def final_kernel(
    static_ref, x_ref, first_ref, folded_ref, column_ref, own_ref, inner_ref, outer_ref, *rest
):
    new_ref = rest[-1]
    tokens, _, width = x_ref.shape
    first = first_ref[...]
    mean, inverse = centre(first)
    stream = lax.broadcasted_iota(jnp.int32, (1, 4 * tokens), 1) & 3

    def coefficient(column, projected):
        dynamic = jnp.tanh(inverse * (projected - mean * column_ref[column : column + 1, 0:1]))
        return by_stream(static_ref, column, stream) + dynamic

    def unfolded(which):
        return jnp.concatenate(
            [folded_ref[4 * which + part : 4 * which + part + 1] for part in range(4)], axis=1
        )

    projected = [first[5:6], first[6:7], first[7:8], unfolded(0), unfolded(1)]
    columns = [coefficient(1 + j, projected[j]) for j in range(5)]
    residual = jnp.concatenate(columns[:4] + columns[:4], axis=0)
    row, col = iotas(4 * SUB, 4 * SUB)
    same = (row >> 2) == (col >> 2)
    row, col = iotas(SUB, 4 * SUB)
    mine = row == (col >> 2)
    for at in range(tokens // SUB):
        lanes = slice(at * 4 * SUB, (at + 1) * 4 * SUB)
        rows = slice(at * SUB, (at + 1) * SUB)
        v = x_ref[rows].reshape(4 * SUB, width)
        matrix = jnp.where(same, jnp.tile(residual[:, lanes], (SUB // 2, 1)), 0.0)
        high, low = split(matrix, 2)
        new = contract(high, v, 1, 0) + contract(low, v, 1, 0)
        sent = inner_ref[rows, :].astype(F32) + outer_ref[rows, :].astype(F32)
        update_high, update_low = split(own_ref[rows, :] + sent, 2)
        spread_high, spread_low = split(jnp.where(mine, columns[4][:, lanes], 0.0), 2)
        new += contract(
            jnp.concatenate([spread_high, spread_high, spread_low], axis=0),
            jnp.concatenate([update_high, update_low, update_high], axis=0),
            0,
            0,
        )
        new_ref[rows] = new.astype(BF).reshape(SUB, 4, width)


def final(static, x, sums, updates, start, previous):
    tokens, width = updates[0].shape
    group = (sums.shape[1] - 128) // 5
    stream_block = pl.BlockSpec((STEP, 4, width), lambda i: (start // STEP + i, 0, 0))
    specs = [
        pl.BlockSpec(memory_space=pltpu.SMEM),
        stream_block,
        pl.BlockSpec((8, 4 * STEP), lambda i: (0, start // STEP + i)),
        pl.BlockSpec((8, STEP), lambda i: (0, 4 * group // STEP + start // STEP + i)),
        pl.BlockSpec((8, 128), lambda i: (0, 5 * group // 128)),
    ]
    specs += [pl.BlockSpec((STEP, width), lambda i: (i, 0))] * 3
    args = [static, x, sums, sums, sums, *updates]
    aliases = {}
    if previous is not None:
        specs.append(pl.BlockSpec(memory_space=pl.ANY))
        aliases = {len(args): 0}
        args.append(previous)
    return pl.pallas_call(
        final_kernel,
        grid=(tokens // STEP,),
        in_specs=specs,
        out_specs=stream_block,
        out_shape=jax.ShapeDtypeStruct(x.shape, BF),
        input_output_aliases=aliases,
        cost_estimate=cost(tokens * 4 * width * 1200, tokens * 22 * width),
        compiler_params=params(),
        name="final",
    )(*args)


def body(streams, proj_master, hc_proj, hc_static, segment_ids, block_mask):
    tokens_local, _, width = streams.shape
    group_size = lax.axis_size("mp")
    place = lax.axis_index("mp").astype(jnp.int32).reshape(1)
    ring = lax.axis_index("blk").astype(jnp.int32).reshape(1)

    proj_rows = jnp.concatenate(
        [hc_proj.T, jnp.ones((1, width), F32), jnp.zeros((1, width), F32)], axis=0
    )
    own = stats(streams, proj_rows)
    parts = list(regroup(place, proj_master, group_size))
    sums, parts = lax.optimization_barrier(([own] + from_others(own, "mp"), parts))

    def gathered(normed):
        rows = lax.all_gather(normed, "mp", axis=0, tiled=True)
        return rows.reshape(group_size, normed.shape[0], width)

    for step in range(1, group_size):
        parts[step] = lax.ppermute(
            parts[step], "mp", [(at, (at + step) % group_size) for at in range(group_size)]
        )
    sums_all, normed_late = mix(hc_static, streams, sums, CHUNK, tokens_local - CHUNK)
    _, normed_first = mix(hc_static, streams, sums, 0, CHUNK)
    parts, normed_late, normed_first = lax.optimization_barrier((parts, normed_late, normed_first))
    rows_late = gathered(normed_late)
    rows_first = gathered(normed_first)

    pieces = weight_pieces(assemble(place, parts))
    rows_late, pieces = lax.optimization_barrier((rows_late, pieces))

    halo = passed_along(segment_ids[-BLOCK:], "blk", 1)
    halo = jnp.where(lax.axis_index("blk") == 0, -1, halo)
    extended = jnp.concatenate([halo, segment_ids])
    key_at = jnp.arange(tokens_local + BLOCK, dtype=jnp.int32)[None, :]
    query_at = jnp.arange(tokens_local, dtype=jnp.int32)[:, None] + BLOCK
    earlier = (extended[None, :] == segment_ids[:, None]) & (key_at < query_at)
    positions = jnp.sum(earlier.astype(jnp.int32), axis=1)
    half = HEAD_DIM // 2
    inverse = 10000.0 ** (-(jnp.arange(half, dtype=F32) * 2.0 / HEAD_DIM))
    angles = positions.astype(F32)[:, None] * inverse[None, :]
    cosine, sine = jnp.cos(angles), jnp.sin(angles)
    cosine = jnp.concatenate([cosine, cosine], axis=1)
    sine = jnp.concatenate([-sine, sine], axis=1)
    windows = []
    for block in range(tokens_local // BLOCK):
        before = extended[block * BLOCK : (block + 1) * BLOCK]
        before = jnp.where(block_mask[block] == 1, before, -1)
        seen = jnp.concatenate([before, segment_ids[block * BLOCK : (block + 1) * BLOCK]])
        for chunk in range(BLOCK // CHUNK):
            windows.append(seen[chunk * CHUNK : chunk * CHUNK + BLOCK + CHUNK])
    key_segments = jnp.stack(windows)[:, None, :]
    query_segments = segment_ids[:, None]

    qkv_late, halo_rows = qkv_columns(ring, rows_late, pieces, cosine[CHUNK:], sine[CHUNK:])
    halo_rows = passed_along(halo_rows, "blk", 1)

    last = tokens_local // CHUNK - 1
    late_chunks = [(qkv_late, 1, at) for at in range(last)]

    def attends(chunk, window):
        return (chunk, window, query_segments, key_segments)

    def projects(own):
        return (place, ring, own, swapped(own, "mp", 1), pieces, group_size)

    waiting = []
    (own,) = output_step(attends(last, late_chunks[-3:]), None)
    both = projects(own)
    rows_first, both = lax.optimization_barrier((rows_first, both[:4]))
    waiting.append((last, (*both, pieces, group_size)))
    qkv_first, _ = qkv_columns(ring, rows_first, pieces, cosine[:CHUNK], sine[:CHUNK])
    chunks = [(halo_rows, 0, 0), (halo_rows, 0, 1), (qkv_first, 1, 0)] + late_chunks
    parts = {}
    for chunk in reversed(range(last)):
        due = waiting.pop(0) if (last - chunk) % 2 else None
        step = output_step(attends(chunk, chunks[chunk : chunk + 3]), due and due[1])
        waiting.append((chunk, projects(step[0])))
        if due:
            parts[due[0]] = step[1:]
    for chunk, due in waiting:
        parts[chunk] = output_step(None, due)

    result = None
    for chunk in reversed(range(last + 1)):
        kept, inner, outer = parts[chunk]
        outer = lax.ppermute(outer, "mp", [(1, 3), (2, 0)])
        inner = lax.ppermute(inner, "mp", [(1, 2), (2, 1)])
        updates = [kept, outer, inner]
        result = final(hc_static, streams, sums_all, updates, chunk * CHUNK, result)
    return result


def solution(mesh):
    in_specs = (
        P("blk", None, "mp"),
        P(("blk", "mp"), None, None),
        P("mp", None),
        P(),
        P("blk"),
        P("blk"),
    )
    out_specs = P("blk", None, "mp")
    return jax.shard_map(body, mesh=mesh, in_specs=in_specs, out_specs=out_specs, check_vma=False)
```

```python
import functools

import jax
import jax.numpy as jnp
from jax import lax
from jax.experimental import pallas as pl
from jax.experimental.pallas import tpu as pltpu
from jax.sharding import PartitionSpec as P

D = 2048
HEAD_DIM = 128
BLOCK = 512
CHUNK = 256
SUB = 64
STEP = 128
STREAMS = 4
EPS = 1e-05
BF = jnp.bfloat16
F32 = jnp.float32


def passed_along(value, axis, steps):
    count = lax.axis_size(axis)
    first, last = (max(0, -steps), min(count, count - steps))
    return lax.ppermute(value, axis, [(source, source + steps) for source in range(first, last)])


def from_others(value, axis):
    count = lax.axis_size(axis)
    return [
        lax.ppermute(value, axis, [(source, (source + step) % count) for source in range(count)])
        for step in range(1, count)
    ]


def cost(flops, nbytes, transcendentals=0):
    return pl.CostEstimate(flops=flops, bytes_accessed=nbytes, transcendentals=transcendentals)


def params(limit=60):
    return pltpu.CompilerParams(vmem_limit_bytes=limit << 20)


def split(value, parts):
    out = []
    for _ in range(parts):
        part = value.astype(BF)
        out.append(part)
        value = value - part.astype(F32)
    return out


def contract(a, b, a_dim, b_dim):
    return lax.dot_general(a, b, (((a_dim,), (b_dim,)), ((), ())), preferred_element_type=F32)


def iotas(rows, cols):
    return (
        lax.broadcasted_iota(jnp.int32, (rows, cols), 0),
        lax.broadcasted_iota(jnp.int32, (rows, cols), 1),
    )


def regroup_kernel(place_ref, master_ref, *parts):
    servers = len(parts)
    width = master_ref.shape[-1] // servers
    for step, part_ref in enumerate(parts):
        server = (place_ref[0] + step) % servers
        own = pl.ds(pl.multiple_of(server * width, width), width)
        pair = pl.ds(pl.multiple_of((server // 2) * 2 * width, 2 * width), 2 * width)
        for slot in range(3):
            part_ref[:, slot * width : (slot + 1) * width] = master_ref[:, slot, own].astype(BF)
        part_ref[:, 3 * width :] = master_ref[:, 3, pair].astype(BF)


def regroup(place, master, servers):
    rows, _, total = master.shape
    columns = 5 * total // servers
    return pl.pallas_call(
        regroup_kernel,
        in_specs=[pl.BlockSpec(memory_space=pltpu.SMEM), pl.BlockSpec(memory_space=pltpu.VMEM)],
        out_specs=[pl.BlockSpec(memory_space=pltpu.VMEM)] * servers,
        out_shape=[jax.ShapeDtypeStruct((rows, columns), BF)] * servers,
        cost_estimate=cost(0, rows * total * 26),
        compiler_params=params(),
        name="regroup",
    )(place, master)


def assemble_kernel(place_ref, *refs):
    out_ref = refs[-1]
    parts = refs[:-1]
    rows = parts[0].shape[0]
    for step, part_ref in enumerate(parts):
        source = (place_ref[0] + len(parts) - step) % len(parts)
        out_ref[pl.ds(pl.multiple_of(source * rows, rows), rows), :] = part_ref[...]


def assemble(place, parts):
    rows, columns = parts[0].shape
    return pl.pallas_call(
        assemble_kernel,
        in_specs=[pl.BlockSpec(memory_space=pltpu.SMEM)]
        + [pl.BlockSpec(memory_space=pltpu.VMEM)] * len(parts),
        out_specs=pl.BlockSpec(memory_space=pltpu.VMEM),
        out_shape=jax.ShapeDtypeStruct((rows * len(parts), columns), BF),
        cost_estimate=cost(0, rows * columns * len(parts) * 4),
        compiler_params=params(),
        name="assemble",
    )(place, *parts)


def swapped(value, axis, mask):
    count = lax.axis_size(axis)
    return lax.ppermute(value, axis, [(source, source ^ mask) for source in range(count)])


def weight_pieces(part):
    count = lax.axis_size("blk")
    if count & (count - 1) or part.shape[0] % HEAD_DIM or count > 8:
        return [lax.all_gather(part, "blk", axis=0, tiled=True)]
    pieces = {0: part}
    for mask in range(2, count, 2):
        if mask & (mask - 1):
            low = mask & -mask
            cut = part.shape[0] // 2
            halves = [swapped(pieces[mask ^ low][:cut], "blk", low)]
            halves.append(swapped(pieces[low][cut:], "blk", mask ^ low))
            pieces[mask] = jnp.concatenate(halves, axis=0)
        else:
            pieces[mask] = swapped(part, "blk", mask)
    for mask in range(0, count, 2):
        pieces[mask + 1] = swapped(pieces[mask], "blk", 1)
    return [pieces[mask] for mask in range(count)]


def stats_kernel(x_ref, proj_ref, out_ref):
    block, _, width = x_ref.shape
    tokens = block * pl.num_programs(0)
    base = pl.program_id(0) * (block // STEP)
    proj = proj_ref[...]
    pieces = jnp.concatenate(split(proj, 3), axis=0)
    out_ref[:, out_ref.shape[1] - 128 :] = jnp.broadcast_to(jnp.sum(proj, axis=1, keepdims=True), (8, 128))
    row, col = iotas(4 * SUB, 4 * SUB)
    same = (row >> 2) == (col >> 2)
    ring = jnp.where(same, (row - col) & 3, -1)

    @pl.loop(0, block // STEP)
    def _(local):
        step = base + local
        folded = []
        for half in range(STEP // SUB):
            lanes = pl.ds(pl.multiple_of(step * 4 * STEP, 4 * STEP) + half * 4 * SUB, 4 * SUB)
            v = x_ref[pl.ds(local * STEP + half * SUB, SUB)].reshape(4 * SUB, width)
            sums = contract(pieces, v, 1, 1)
            sums = sums[0:8] + sums[8:16] + sums[16:24]
            gram = contract(v, v, 1, 1)
            out_ref[0:1, lanes] = sums[0:1]
            out_ref[1:2, lanes] = sums[6:7]
            for shift in range(3):
                out_ref[2 + shift : 3 + shift, lanes] = jnp.sum(
                    jnp.where(ring == shift, gram, 0.0), axis=0, keepdims=True
                )
            out_ref[5:8, lanes] = sums[1:4]
            folded.append(sums[4:6])
        folded = jnp.concatenate(folded, axis=1)
        lanes = pl.ds(pl.multiple_of(4 * tokens + step * STEP, STEP), STEP)
        for part in range(4):
            for which in range(2):
                out_ref[4 * which + part : 4 * which + part + 1, lanes] = folded[
                    which : which + 1, part * STEP : (part + 1) * STEP
                ]


def stats(x, proj):
    tokens, _, width = x.shape
    lanes = 5 * tokens + 128
    return pl.pallas_call(
        stats_kernel,
        grid=(tokens // (2 * STEP),),
        in_specs=[
            pl.BlockSpec((2 * STEP, 4, width), lambda i: (i, 0, 0)),
            pl.BlockSpec((8, width), lambda i: (0, 0)),
        ],
        out_specs=pl.BlockSpec((8, lanes), lambda i: (0, 0)),
        out_shape=jax.ShapeDtypeStruct((8, lanes), F32),
        cost_estimate=cost(tokens * 4 * width * 600, tokens * 8 * width),
        compiler_params=params(),
        name="stats",
    )(x, proj)


def by_stream(static_ref, column, stream):
    value = jnp.full(stream.shape, static_ref[0, column], F32)
    for k in range(1, 4):
        value = jnp.where(stream == k, static_ref[k, column], value)
    return value


def centre(first):
    mean = first[1:2] * (1.0 / D)
    spread = first[2:3] * (1.0 / D) - mean * mean
    return mean, lax.rsqrt(spread + EPS)


def mix_kernel(offset, static_ref, x_ref, own_ref, a_ref, b_ref, c_ref, sums_ref, normed_ref):
    tokens, _, width = x_ref.shape

    @pl.when(pl.program_id(0) == 0)
    def _():
        sums_ref[...] = (own_ref[...] + a_ref[...]) + (b_ref[...] + c_ref[...])

    base = 4 * (offset + pl.program_id(0) * tokens)
    last = sums_ref.shape[1] - 128
    column = sums_ref[0:1, last : last + 1]
    stream = lax.broadcasted_iota(jnp.int32, (1, 4 * STEP), 1) & 3
    static = by_stream(static_ref, 0, stream)
    row, col = iotas(SUB, 4 * SUB)
    mine = row == (col >> 2)

    @pl.loop(0, tokens // STEP)
    def _(step):
        at = pl.multiple_of(base + step * 4 * STEP, 4 * STEP)
        first = sums_ref[:, pl.ds(at, 4 * STEP)]
        mean, inverse = centre(first)
        mix = static + jnp.tanh(inverse * (first[0:1] - mean * column))
        one = jnp.where(stream < 3, pltpu.roll(mix, 4 * STEP - 1, 1), pltpu.roll(mix, 3, 1))
        two = jnp.where(stream < 2, pltpu.roll(mix, 4 * STEP - 2, 1), pltpu.roll(mix, 2, 1))
        linear = mix * first[1:2]
        square = mix * (mix * first[2:3] + 2.0 * one * first[3:4] + two * first[4:5])
        for half in range(STEP // SUB):
            lanes = slice(half * 4 * SUB, (half + 1) * 4 * SUB)
            rows = pl.ds(step * STEP + half * SUB, SUB)
            v = x_ref[rows].reshape(4 * SUB, width)
            matrix = jnp.where(mine, mix[:, lanes], 0.0)
            mixed = contract(jnp.concatenate(split(matrix, 3), axis=0), v, 1, 0)
            mixed = mixed[0:SUB] + mixed[SUB : 2 * SUB] + mixed[2 * SUB : 3 * SUB]
            average = jnp.sum(jnp.where(mine, linear[:, lanes], 0.0), axis=1, keepdims=True)
            power = jnp.sum(jnp.where(mine, square[:, lanes], 0.0), axis=1, keepdims=True)
            average, power = average * (1.0 / D), power * (1.0 / D)
            scale = lax.rsqrt(jnp.maximum(power - average * average, 0.0) + EPS)
            normed_ref[rows, :] = ((mixed - average) * scale).astype(BF)


def mix(static, x, parts, start, tokens):
    width = x.shape[-1]
    lanes = parts[0].shape[1]
    whole = pl.BlockSpec((8, lanes), lambda i: (0, 0))
    return pl.pallas_call(
        functools.partial(mix_kernel, start),
        grid=(tokens // CHUNK,),
        in_specs=[
            pl.BlockSpec(memory_space=pltpu.SMEM),
            pl.BlockSpec((CHUNK, 4, width), lambda i: (start // CHUNK + i, 0, 0)),
        ]
        + [whole] * 4,
        out_specs=[whole, pl.BlockSpec((CHUNK, width), lambda i: (i, 0))],
        out_shape=[
            jax.ShapeDtypeStruct((8, lanes), F32),
            jax.ShapeDtypeStruct((tokens, width), BF),
        ],
        cost_estimate=cost(tokens * 4 * width * 400, tokens * 10 * width),
        compiler_params=params(),
        name="mix",
    )(static, x, *parts)


def qkv_kernel(ring_ref, rows_ref, cosine_ref, sine_ref, *refs):
    out_ref, halo_ref = refs[-2:]
    pieces = refs[:-2]
    servers, _, width = rows_ref.shape
    depth = pieces[0].shape[0]
    if len(pieces) == 1:
        left = [rows_ref[server] for server in range(servers)]
    else:
        left = []
        for piece in range(len(pieces)):
            source = ring_ref[0] ^ piece
            inside = pl.multiple_of((source % (width // depth)) * depth, depth)
            left.append(rows_ref[source // (width // depth), :, pl.ds(inside, depth)])
    left = jnp.concatenate(left, axis=1)
    right = jnp.concatenate([piece[...] for piece in pieces], axis=0)
    total = contract(left, right, 1, 0)
    slot = pl.program_id(0)

    @pl.when(slot < 2)
    def _():
        cosine, sine = cosine_ref[...], sine_ref[...]
        for head in range(total.shape[1] // HEAD_DIM):
            part = total[:, head * HEAD_DIM : (head + 1) * HEAD_DIM]
            turned = part * cosine + pltpu.roll(part, HEAD_DIM // 2, 1) * sine
            out_ref[0, :, head * HEAD_DIM : (head + 1) * HEAD_DIM] = turned.astype(BF)

    @pl.when(slot == 2)
    def _():
        out_ref[0] = total.astype(BF)

    halo_ref[0] = out_ref[0, -halo_ref.shape[1] :, :]


def qkv_columns(ring, rows, pieces, cosine, sine):
    servers, tokens, width = rows.shape
    kept = min(BLOCK, tokens)
    table = pl.BlockSpec((tokens, HEAD_DIM), lambda j: (0, 0))
    return pl.pallas_call(
        qkv_kernel,
        grid=(3,),
        in_specs=[
            pl.BlockSpec(memory_space=pltpu.SMEM),
            pl.BlockSpec((servers, tokens, width), lambda j: (0, 0, 0)),
            table,
            table,
        ]
        + [pl.BlockSpec((pieces[0].shape[0], width), lambda j: (0, j))] * len(pieces),
        out_specs=[
            pl.BlockSpec((1, tokens, width), lambda j: (j, 0, 0)),
            pl.BlockSpec((1, kept, width), lambda j: (jnp.maximum(j - 1, 0), 0, 0)),
        ],
        out_shape=[
            jax.ShapeDtypeStruct((3, tokens, width), BF),
            jax.ShapeDtypeStruct((2, kept, width), BF),
        ],
        cost_estimate=cost(2 * tokens * D * 3 * width, D * 6 * width + tokens * D * 5),
        compiler_params=params(),
        name="qkv",
    )(ring, rows, cosine, sine, *pieces)


def attend_kernel(q_ref, k0, k1, k2, v0, v1, v2, qseg_ref, kseg_ref, attended_ref):
    tokens, width = q_ref.shape[1:]
    window = kseg_ref.shape[-1]
    row, col = iotas(tokens, window)
    allowed = (qseg_ref[...] == kseg_ref[0]) & (col - (window - tokens) <= row)
    bias = jnp.where(allowed, 0.0, -1e30)
    factor = 1.4426950408889634 / HEAD_DIM**0.5
    for head in range(width // HEAD_DIM):
        lanes = slice(head * HEAD_DIM, (head + 1) * HEAD_DIM)
        query = q_ref[0, :, lanes]
        scores = jnp.concatenate(
            [contract(query, k[0, :, lanes], 1, 1) for k in (k0, k1, k2)], axis=1
        )
        scores = scores + bias
        weights = jnp.exp2((scores - jnp.max(scores, axis=1, keepdims=True)) * factor)
        total = jnp.sum(weights, axis=1, keepdims=True)
        values = jnp.concatenate([v[0, :, lanes] for v in (v0, v1, v2)], axis=0)
        attended_ref[:, lanes] = (contract(weights.astype(BF), values, 1, 0) / total).astype(BF)


def attend(query, window, qseg, kseg, chunk):
    source, at = query
    width = source.shape[-1]
    block = (1, CHUNK, width)
    keys = [pl.BlockSpec(block, lambda i, s=slot, r=where: (s, r, 0)) for _, slot, where in window]
    values = [
        pl.BlockSpec(block, lambda i, s=slot + 1, r=where: (s, r, 0)) for _, slot, where in window
    ]
    arrays = [array for array, _, _ in window]
    reach = kseg.shape[-1]
    return pl.pallas_call(
        attend_kernel,
        grid=(1,),
        in_specs=[pl.BlockSpec(block, lambda i: (0, at, 0))]
        + keys
        + values
        + [
            pl.BlockSpec((CHUNK, 1), lambda i: (chunk, 0)),
            pl.BlockSpec((1, 1, reach), lambda i: (chunk, 0, 0)),
        ],
        out_specs=pl.BlockSpec((CHUNK, width), lambda i: (0, 0)),
        out_shape=jax.ShapeDtypeStruct((CHUNK, width), BF),
        cost_estimate=cost(4 * CHUNK * reach * width, CHUNK * width * 16, CHUNK * reach * 4),
        compiler_params=params(),
        name="attend",
    )(source, *arrays, *arrays, qseg, kseg)


def project_kernel(place_ref, ring_ref, own_ref, other_ref, *refs):
    pieces = refs[:-4]
    kept_ref, inner_ref, outer_ref, sums = refs[-4:]
    servers, _, width = sums.shape
    place = place_ref[0]
    even = place % 2 == 0
    own, other = own_ref[...], other_ref[...]
    both = jnp.concatenate([jnp.where(even, own, other), jnp.where(even, other, own)], axis=1)
    depth = pieces[0].shape[0]
    if len(pieces) == 1:
        for server in range(servers):
            rows = pieces[0][server * width : (server + 1) * width, :]
            sums[server] = contract(both, rows, 1, 1)
    else:
        within = (place == 1) | (place == 2)
        for piece in range(len(pieces)):
            target = ring_ref[0] ^ piece
            server = target // (width // depth)
            inside = pl.multiple_of((target % (width // depth)) * depth, depth)

            @pl.when(jnp.where(within, server != place ^ 1, server == place))
            def _():
                sums[server, :, pl.ds(inside, depth)] = contract(both, pieces[piece][...], 1, 1)

    kept_ref[...] = sums[place]
    low = place < 2
    inner_ref[...] = sums[jnp.where(low, 2, 1)].astype(BF)
    outer_ref[...] = sums[jnp.where(low, 3, 0)].astype(BF)


def project(place, ring, own, other, pieces, servers):
    tokens, width = own.shape
    rows, columns = pieces[0].shape
    pair = 2 * width
    tail = pl.BlockSpec((pl.Element(rows), pl.Element(pair)), lambda i: (0, columns - pair))
    full = pl.BlockSpec((tokens, width), lambda i: (0, 0))
    return pl.pallas_call(
        project_kernel,
        grid=(1,),
        in_specs=[pl.BlockSpec(memory_space=pltpu.SMEM)] * 2 + [full] * 2 + [tail] * len(pieces),
        out_specs=[full] * 3,
        out_shape=[
            jax.ShapeDtypeStruct((tokens, width), F32),
            jax.ShapeDtypeStruct((tokens, width), BF),
            jax.ShapeDtypeStruct((tokens, width), BF),
        ],
        scratch_shapes=[pltpu.VMEM((servers, tokens, width), F32)],
        cost_estimate=cost(2 * tokens * D * pair, D * pair * 2 + tokens * width * 12),
        compiler_params=params(),
        name="project",
    )(place, ring, own, other, *pieces)


def final_kernel(
    static_ref, x_ref, first_ref, folded_ref, column_ref, own_ref, inner_ref, outer_ref, *rest
):
    new_ref = rest[-1]
    tokens, _, width = x_ref.shape
    first = first_ref[...]
    mean, inverse = centre(first)
    stream = lax.broadcasted_iota(jnp.int32, (1, 4 * tokens), 1) & 3

    def coefficient(column, projected):
        dynamic = jnp.tanh(inverse * (projected - mean * column_ref[column : column + 1, 0:1]))
        return by_stream(static_ref, column, stream) + dynamic

    def unfolded(which):
        return jnp.concatenate(
            [folded_ref[4 * which + part : 4 * which + part + 1] for part in range(4)], axis=1
        )

    projected = [first[5:6], first[6:7], first[7:8], unfolded(0), unfolded(1)]
    columns = [coefficient(1 + j, projected[j]) for j in range(5)]
    residual = jnp.concatenate(columns[:4] + columns[:4], axis=0)
    row, col = iotas(4 * SUB, 4 * SUB)
    same = (row >> 2) == (col >> 2)
    row, col = iotas(SUB, 4 * SUB)
    mine = row == (col >> 2)
    for at in range(tokens // SUB):
        lanes = slice(at * 4 * SUB, (at + 1) * 4 * SUB)
        rows = slice(at * SUB, (at + 1) * SUB)
        v = x_ref[rows].reshape(4 * SUB, width)
        matrix = jnp.where(same, jnp.tile(residual[:, lanes], (SUB // 2, 1)), 0.0)
        high, low = split(matrix, 2)
        new = contract(high, v, 1, 0) + contract(low, v, 1, 0)
        sent = inner_ref[rows, :].astype(F32) + outer_ref[rows, :].astype(F32)
        update_high, update_low = split(own_ref[rows, :] + sent, 2)
        spread_high, spread_low = split(jnp.where(mine, columns[4][:, lanes], 0.0), 2)
        new += contract(
            jnp.concatenate([spread_high, spread_high, spread_low], axis=0),
            jnp.concatenate([update_high, update_low, update_high], axis=0),
            0,
            0,
        )
        new_ref[rows] = new.astype(BF).reshape(SUB, 4, width)


def final(static, x, sums, updates, start, previous):
    tokens, width = updates[0].shape
    group = (sums.shape[1] - 128) // 5
    stream_block = pl.BlockSpec((STEP, 4, width), lambda i: (start // STEP + i, 0, 0))
    specs = [
        pl.BlockSpec(memory_space=pltpu.SMEM),
        stream_block,
        pl.BlockSpec((8, 4 * STEP), lambda i: (0, start // STEP + i)),
        pl.BlockSpec((8, STEP), lambda i: (0, 4 * group // STEP + start // STEP + i)),
        pl.BlockSpec((8, 128), lambda i: (0, 5 * group // 128)),
    ]
    specs += [pl.BlockSpec((STEP, width), lambda i: (i, 0))] * 3
    args = [static, x, sums, sums, sums, *updates]
    aliases = {}
    if previous is not None:
        specs.append(pl.BlockSpec(memory_space=pl.ANY))
        aliases = {len(args): 0}
        args.append(previous)
    return pl.pallas_call(
        final_kernel,
        grid=(tokens // STEP,),
        in_specs=specs,
        out_specs=stream_block,
        out_shape=jax.ShapeDtypeStruct(x.shape, BF),
        input_output_aliases=aliases,
        cost_estimate=cost(tokens * 4 * width * 1200, tokens * 22 * width),
        compiler_params=params(),
        name="final",
    )(*args)


def body(streams, proj_master, hc_proj, hc_static, segment_ids, block_mask):
    tokens_local, _, width = streams.shape
    group_size = lax.axis_size("mp")
    place = lax.axis_index("mp").astype(jnp.int32).reshape(1)
    ring = lax.axis_index("blk").astype(jnp.int32).reshape(1)

    proj_rows = jnp.concatenate(
        [hc_proj.T, jnp.ones((1, width), F32), jnp.zeros((1, width), F32)], axis=0
    )
    own = stats(streams, proj_rows)
    parts = list(regroup(place, proj_master, group_size))
    sums, parts = lax.optimization_barrier(([own] + from_others(own, "mp"), parts))

    def gathered(normed):
        rows = lax.all_gather(normed, "mp", axis=0, tiled=True)
        return rows.reshape(group_size, normed.shape[0], width)

    for step in range(1, group_size):
        parts[step] = lax.ppermute(
            parts[step], "mp", [(at, (at + step) % group_size) for at in range(group_size)]
        )
    sums_all, normed_late = mix(hc_static, streams, sums, CHUNK, tokens_local - CHUNK)
    _, normed_first = mix(hc_static, streams, sums, 0, CHUNK)
    parts, normed_late, normed_first = lax.optimization_barrier((parts, normed_late, normed_first))
    rows_late = gathered(normed_late)
    rows_first = gathered(normed_first)

    pieces = weight_pieces(assemble(place, parts))
    rows_late, pieces = lax.optimization_barrier((rows_late, pieces))

    halo = passed_along(segment_ids[-BLOCK:], "blk", 1)
    halo = jnp.where(lax.axis_index("blk") == 0, -1, halo)
    extended = jnp.concatenate([halo, segment_ids])
    key_at = jnp.arange(tokens_local + BLOCK, dtype=jnp.int32)[None, :]
    query_at = jnp.arange(tokens_local, dtype=jnp.int32)[:, None] + BLOCK
    earlier = (extended[None, :] == segment_ids[:, None]) & (key_at < query_at)
    positions = jnp.sum(earlier.astype(jnp.int32), axis=1)
    half = HEAD_DIM // 2
    inverse = 10000.0 ** (-(jnp.arange(half, dtype=F32) * 2.0 / HEAD_DIM))
    angles = positions.astype(F32)[:, None] * inverse[None, :]
    cosine, sine = jnp.cos(angles), jnp.sin(angles)
    cosine = jnp.concatenate([cosine, cosine], axis=1)
    sine = jnp.concatenate([-sine, sine], axis=1)
    windows = []
    for block in range(tokens_local // BLOCK):
        before = extended[block * BLOCK : (block + 1) * BLOCK]
        before = jnp.where(block_mask[block] == 1, before, -1)
        seen = jnp.concatenate([before, segment_ids[block * BLOCK : (block + 1) * BLOCK]])
        for chunk in range(BLOCK // CHUNK):
            windows.append(seen[chunk * CHUNK : chunk * CHUNK + BLOCK + CHUNK])
    key_segments = jnp.stack(windows)[:, None, :]
    query_segments = segment_ids[:, None]

    qkv_late, halo_rows = qkv_columns(ring, rows_late, pieces, cosine[CHUNK:], sine[CHUNK:])
    halo_rows = passed_along(halo_rows, "blk", 1)

    def projected(own, other):
        return project(place, ring, own, other, pieces, group_size)

    last = tokens_local // CHUNK - 1
    late_chunks = [(qkv_late, 1, at) for at in range(last)]

    def attended(chunk, window):
        source, _, at = window[-1]
        return attend((source, at), window, query_segments, key_segments, chunk)

    own = attended(last, late_chunks[-3:])
    both = (own, swapped(own, "mp", 1))
    rows_first, both = lax.optimization_barrier((rows_first, both))
    parts = {last: projected(*both)}
    qkv_first, _ = qkv_columns(ring, rows_first, pieces, cosine[:CHUNK], sine[:CHUNK])
    chunks = [(halo_rows, 0, 0), (halo_rows, 0, 1), (qkv_first, 1, 0)] + late_chunks
    for chunk in reversed(range(last)):
        own = attended(chunk, chunks[chunk : chunk + 3])
        parts[chunk] = projected(own, swapped(own, "mp", 1))

    result = None
    for chunk in reversed(range(last + 1)):
        kept, inner, outer = parts[chunk]
        outer = lax.ppermute(outer, "mp", [(1, 3), (2, 0)])
        inner = lax.ppermute(inner, "mp", [(1, 2), (2, 1)])
        updates = [kept, outer, inner]
        result = final(hc_static, streams, sums_all, updates, chunk * CHUNK, result)
    return result


def solution(mesh):
    in_specs = (
        P("blk", None, "mp"),
        P(("blk", "mp"), None, None),
        P("mp", None),
        P(),
        P("blk"),
        P("blk"),
    )
    out_specs = P("blk", None, "mp")
    return jax.shard_map(body, mesh=mesh, in_specs=in_specs, out_specs=out_specs, check_vma=False)
```

```python
import functools

import jax
import jax.numpy as jnp
from jax import lax
from jax.experimental import pallas as pl
from jax.experimental.pallas import tpu as pltpu
from jax.sharding import PartitionSpec as P

D = 2048
HEAD_DIM = 128
BLOCK = 512
CHUNK = 256
SUB = 64
STEP = 128
STREAMS = 4
EPS = 1e-05
BF = jnp.bfloat16
F32 = jnp.float32


def passed_along(value, axis, steps):
    count = lax.axis_size(axis)
    first, last = (max(0, -steps), min(count, count - steps))
    return lax.ppermute(value, axis, [(source, source + steps) for source in range(first, last)])


def from_others(value, axis):
    count = lax.axis_size(axis)
    return [
        lax.ppermute(value, axis, [(source, (source + step) % count) for source in range(count)])
        for step in range(1, count)
    ]


def cost(flops, nbytes, transcendentals=0):
    return pl.CostEstimate(flops=flops, bytes_accessed=nbytes, transcendentals=transcendentals)


def params(limit=28):
    return pltpu.CompilerParams(vmem_limit_bytes=limit << 20)


def split(value, parts):
    out = []
    for _ in range(parts):
        part = value.astype(BF)
        out.append(part)
        value = value - part.astype(F32)
    return out


def contract(a, b, a_dim, b_dim):
    return lax.dot_general(a, b, (((a_dim,), (b_dim,)), ((), ())), preferred_element_type=F32)


def iotas(rows, cols):
    return (
        lax.broadcasted_iota(jnp.int32, (rows, cols), 0),
        lax.broadcasted_iota(jnp.int32, (rows, cols), 1),
    )


def regroup_kernel(place_ref, master_ref, *parts):
    servers = len(parts)
    width = master_ref.shape[-1] // servers
    for step, part_ref in enumerate(parts):
        server = (place_ref[0] + step) % servers
        own = pl.ds(pl.multiple_of(server * width, width), width)
        pair = pl.ds(pl.multiple_of((server // 2) * 2 * width, 2 * width), 2 * width)
        for slot in range(3):
            part_ref[:, slot * width : (slot + 1) * width] = master_ref[:, slot, own].astype(BF)
        part_ref[:, 3 * width :] = master_ref[:, 3, pair].astype(BF)


def regroup(place, master, servers):
    rows, _, total = master.shape
    columns = 5 * total // servers
    return pl.pallas_call(
        regroup_kernel,
        in_specs=[pl.BlockSpec(memory_space=pltpu.SMEM), pl.BlockSpec(memory_space=pltpu.VMEM)],
        out_specs=[pl.BlockSpec(memory_space=pltpu.VMEM)] * servers,
        out_shape=[jax.ShapeDtypeStruct((rows, columns), BF)] * servers,
        cost_estimate=cost(0, rows * total * 26),
        compiler_params=params(),
        name="regroup",
    )(place, master)


def assemble_kernel(place_ref, *refs):
    out_ref = refs[-1]
    parts = refs[:-1]
    rows = parts[0].shape[0]
    for step, part_ref in enumerate(parts):
        source = (place_ref[0] + len(parts) - step) % len(parts)
        out_ref[pl.ds(pl.multiple_of(source * rows, rows), rows), :] = part_ref[...]


def assemble(place, parts):
    rows, columns = parts[0].shape
    return pl.pallas_call(
        assemble_kernel,
        in_specs=[pl.BlockSpec(memory_space=pltpu.SMEM)]
        + [pl.BlockSpec(memory_space=pltpu.VMEM)] * len(parts),
        out_specs=pl.BlockSpec(memory_space=pltpu.VMEM),
        out_shape=jax.ShapeDtypeStruct((rows * len(parts), columns), BF),
        cost_estimate=cost(0, rows * columns * len(parts) * 4),
        compiler_params=params(),
        name="assemble",
    )(place, *parts)


def swapped(value, axis, mask):
    count = lax.axis_size(axis)
    return lax.ppermute(value, axis, [(source, source ^ mask) for source in range(count)])


def weight_pieces(part):
    count = lax.axis_size("blk")
    if count & (count - 1) or part.shape[0] % HEAD_DIM or count > 8:
        return [lax.all_gather(part, "blk", axis=0, tiled=True)]
    pieces = {0: part}
    for mask in range(2, count, 2):
        if mask & (mask - 1):
            low = mask & -mask
            cut = part.shape[0] // 2
            halves = [swapped(pieces[mask ^ low][:cut], "blk", low)]
            halves.append(swapped(pieces[low][cut:], "blk", mask ^ low))
            pieces[mask] = jnp.concatenate(halves, axis=0)
        else:
            pieces[mask] = swapped(part, "blk", mask)
    for mask in range(0, count, 2):
        pieces[mask + 1] = swapped(pieces[mask], "blk", 1)
    return [pieces[mask] for mask in range(count)]


def stats_kernel(x_ref, proj_ref, out_ref):
    block, _, width = x_ref.shape
    tokens = block * pl.num_programs(0)
    base = pl.program_id(0) * (block // STEP)
    proj = proj_ref[...]
    pieces = jnp.concatenate(split(proj, 3), axis=0)
    out_ref[:, out_ref.shape[1] - 128 :] = jnp.broadcast_to(jnp.sum(proj, axis=1, keepdims=True), (8, 128))
    row, col = iotas(4 * SUB, 4 * SUB)
    same = (row >> 2) == (col >> 2)
    ring = jnp.where(same, (row - col) & 3, -1)

    @pl.loop(0, block // STEP)
    def _(local):
        step = base + local
        folded = []
        for half in range(STEP // SUB):
            lanes = pl.ds(pl.multiple_of(step * 4 * STEP, 4 * STEP) + half * 4 * SUB, 4 * SUB)
            v = x_ref[pl.ds(local * STEP + half * SUB, SUB)].reshape(4 * SUB, width)
            sums = contract(pieces, v, 1, 1)
            sums = sums[0:8] + sums[8:16] + sums[16:24]
            gram = contract(v, v, 1, 1)
            out_ref[0:1, lanes] = sums[0:1]
            out_ref[1:2, lanes] = sums[6:7]
            for shift in range(3):
                out_ref[2 + shift : 3 + shift, lanes] = jnp.sum(
                    jnp.where(ring == shift, gram, 0.0), axis=0, keepdims=True
                )
            out_ref[5:8, lanes] = sums[1:4]
            folded.append(sums[4:6])
        folded = jnp.concatenate(folded, axis=1)
        lanes = pl.ds(pl.multiple_of(4 * tokens + step * STEP, STEP), STEP)
        for part in range(4):
            for which in range(2):
                out_ref[4 * which + part : 4 * which + part + 1, lanes] = folded[
                    which : which + 1, part * STEP : (part + 1) * STEP
                ]


def stats(x, proj):
    tokens, _, width = x.shape
    lanes = 5 * tokens + 128
    return pl.pallas_call(
        stats_kernel,
        grid=(tokens // (2 * STEP),),
        in_specs=[
            pl.BlockSpec((2 * STEP, 4, width), lambda i: (i, 0, 0)),
            pl.BlockSpec((8, width), lambda i: (0, 0)),
        ],
        out_specs=pl.BlockSpec((8, lanes), lambda i: (0, 0)),
        out_shape=jax.ShapeDtypeStruct((8, lanes), F32),
        cost_estimate=cost(tokens * 4 * width * 600, tokens * 8 * width),
        compiler_params=params(),
        name="stats",
    )(x, proj)


def by_stream(static_ref, column, stream):
    value = jnp.full(stream.shape, static_ref[0, column], F32)
    for k in range(1, 4):
        value = jnp.where(stream == k, static_ref[k, column], value)
    return value


def centre(first):
    mean = first[1:2] * (1.0 / D)
    spread = first[2:3] * (1.0 / D) - mean * mean
    return mean, lax.rsqrt(spread + EPS)


def mix_kernel(offset, static_ref, x_ref, own_ref, a_ref, b_ref, c_ref, sums_ref, normed_ref):
    tokens, _, width = x_ref.shape

    @pl.when(pl.program_id(0) == 0)
    def _():
        sums_ref[...] = (own_ref[...] + a_ref[...]) + (b_ref[...] + c_ref[...])

    base = 4 * (offset + pl.program_id(0) * tokens)
    last = sums_ref.shape[1] - 128
    column = sums_ref[0:1, last : last + 1]
    stream = lax.broadcasted_iota(jnp.int32, (1, 4 * STEP), 1) & 3
    static = by_stream(static_ref, 0, stream)
    row, col = iotas(SUB, 4 * SUB)
    mine = row == (col >> 2)

    @pl.loop(0, tokens // STEP)
    def _(step):
        at = pl.multiple_of(base + step * 4 * STEP, 4 * STEP)
        first = sums_ref[:, pl.ds(at, 4 * STEP)]
        mean, inverse = centre(first)
        mix = static + jnp.tanh(inverse * (first[0:1] - mean * column))
        one = jnp.where(stream < 3, pltpu.roll(mix, 4 * STEP - 1, 1), pltpu.roll(mix, 3, 1))
        two = jnp.where(stream < 2, pltpu.roll(mix, 4 * STEP - 2, 1), pltpu.roll(mix, 2, 1))
        linear = mix * first[1:2]
        square = mix * (mix * first[2:3] + 2.0 * one * first[3:4] + two * first[4:5])
        for half in range(STEP // SUB):
            lanes = slice(half * 4 * SUB, (half + 1) * 4 * SUB)
            rows = pl.ds(step * STEP + half * SUB, SUB)
            v = x_ref[rows].reshape(4 * SUB, width)
            matrix = jnp.where(mine, mix[:, lanes], 0.0)
            mixed = contract(jnp.concatenate(split(matrix, 3), axis=0), v, 1, 0)
            mixed = mixed[0:SUB] + mixed[SUB : 2 * SUB] + mixed[2 * SUB : 3 * SUB]
            average = jnp.sum(jnp.where(mine, linear[:, lanes], 0.0), axis=1, keepdims=True)
            power = jnp.sum(jnp.where(mine, square[:, lanes], 0.0), axis=1, keepdims=True)
            average, power = average * (1.0 / D), power * (1.0 / D)
            scale = lax.rsqrt(jnp.maximum(power - average * average, 0.0) + EPS)
            normed_ref[rows, :] = ((mixed - average) * scale).astype(BF)


def mix(static, x, parts, start, tokens):
    width = x.shape[-1]
    lanes = parts[0].shape[1]
    whole = pl.BlockSpec((8, lanes), lambda i: (0, 0))
    return pl.pallas_call(
        functools.partial(mix_kernel, start),
        grid=(tokens // CHUNK,),
        in_specs=[
            pl.BlockSpec(memory_space=pltpu.SMEM),
            pl.BlockSpec((CHUNK, 4, width), lambda i: (start // CHUNK + i, 0, 0)),
        ]
        + [whole] * 4,
        out_specs=[whole, pl.BlockSpec((CHUNK, width), lambda i: (i, 0))],
        out_shape=[
            jax.ShapeDtypeStruct((8, lanes), F32),
            jax.ShapeDtypeStruct((tokens, width), BF),
        ],
        cost_estimate=cost(tokens * 4 * width * 400, tokens * 10 * width),
        compiler_params=params(),
        name="mix",
    )(static, x, *parts)


def qkv_kernel(ring_ref, rows_ref, cosine_ref, sine_ref, *refs):
    out_ref, halo_ref = refs[-2:]
    pieces = refs[:-2]
    servers, _, width = rows_ref.shape
    depth = pieces[0].shape[0]
    if len(pieces) == 1:
        left = [rows_ref[server] for server in range(servers)]
    else:
        left = []
        for piece in range(len(pieces)):
            source = ring_ref[0] ^ piece
            inside = pl.multiple_of((source % (width // depth)) * depth, depth)
            left.append(rows_ref[source // (width // depth), :, pl.ds(inside, depth)])
    left = jnp.concatenate(left, axis=1)
    right = jnp.concatenate([piece[...] for piece in pieces], axis=0)
    total = contract(left, right, 1, 0)
    slot = pl.program_id(0)

    @pl.when(slot < 2)
    def _():
        cosine, sine = cosine_ref[...], sine_ref[...]
        for head in range(total.shape[1] // HEAD_DIM):
            part = total[:, head * HEAD_DIM : (head + 1) * HEAD_DIM]
            turned = part * cosine + pltpu.roll(part, HEAD_DIM // 2, 1) * sine
            out_ref[0, :, head * HEAD_DIM : (head + 1) * HEAD_DIM] = turned.astype(BF)

    @pl.when(slot == 2)
    def _():
        out_ref[0] = total.astype(BF)

    halo_ref[0] = out_ref[0, -halo_ref.shape[1] :, :]


def qkv_columns(ring, rows, pieces, cosine, sine):
    servers, tokens, width = rows.shape
    kept = min(BLOCK, tokens)
    table = pl.BlockSpec((tokens, HEAD_DIM), lambda j: (0, 0))
    return pl.pallas_call(
        qkv_kernel,
        grid=(3,),
        in_specs=[
            pl.BlockSpec(memory_space=pltpu.SMEM),
            pl.BlockSpec((servers, tokens, width), lambda j: (0, 0, 0)),
            table,
            table,
        ]
        + [pl.BlockSpec((pieces[0].shape[0], width), lambda j: (0, j))] * len(pieces),
        out_specs=[
            pl.BlockSpec((1, tokens, width), lambda j: (j, 0, 0)),
            pl.BlockSpec((1, kept, width), lambda j: (jnp.maximum(j - 1, 0), 0, 0)),
        ],
        out_shape=[
            jax.ShapeDtypeStruct((3, tokens, width), BF),
            jax.ShapeDtypeStruct((2, kept, width), BF),
        ],
        cost_estimate=cost(2 * tokens * D * 3 * width, D * 6 * width + tokens * D * 5),
        compiler_params=params(),
        name="qkv",
    )(ring, rows, cosine, sine, *pieces)


def attend_kernel(q_ref, k0, k1, k2, v0, v1, v2, qseg_ref, kseg_ref, attended_ref):
    tokens, width = q_ref.shape[1:]
    window = kseg_ref.shape[-1]
    row, col = iotas(tokens, window)
    allowed = (qseg_ref[...] == kseg_ref[0]) & (col - (window - tokens) <= row)
    bias = jnp.where(allowed, 0.0, -1e30)
    factor = 1.4426950408889634 / HEAD_DIM**0.5
    for head in range(width // HEAD_DIM):
        lanes = slice(head * HEAD_DIM, (head + 1) * HEAD_DIM)
        query = q_ref[0, :, lanes]
        scores = jnp.concatenate(
            [contract(query, k[0, :, lanes], 1, 1) for k in (k0, k1, k2)], axis=1
        )
        scores = scores + bias
        weights = jnp.exp2((scores - jnp.max(scores, axis=1, keepdims=True)) * factor)
        total = jnp.sum(weights, axis=1, keepdims=True)
        values = jnp.concatenate([v[0, :, lanes] for v in (v0, v1, v2)], axis=0)
        attended_ref[:, lanes] = (contract(weights.astype(BF), values, 1, 0) / total).astype(BF)


def attend(query, window, qseg, kseg, chunk):
    source, at = query
    width = source.shape[-1]
    block = (1, CHUNK, width)
    keys = [pl.BlockSpec(block, lambda i, s=slot, r=where: (s, r, 0)) for _, slot, where in window]
    values = [
        pl.BlockSpec(block, lambda i, s=slot + 1, r=where: (s, r, 0)) for _, slot, where in window
    ]
    arrays = [array for array, _, _ in window]
    reach = kseg.shape[-1]
    return pl.pallas_call(
        attend_kernel,
        grid=(1,),
        in_specs=[pl.BlockSpec(block, lambda i: (0, at, 0))]
        + keys
        + values
        + [
            pl.BlockSpec((CHUNK, 1), lambda i: (chunk, 0)),
            pl.BlockSpec((1, 1, reach), lambda i: (chunk, 0, 0)),
        ],
        out_specs=pl.BlockSpec((CHUNK, width), lambda i: (0, 0)),
        out_shape=jax.ShapeDtypeStruct((CHUNK, width), BF),
        cost_estimate=cost(4 * CHUNK * reach * width, CHUNK * width * 16, CHUNK * reach * 4),
        compiler_params=params(),
        name="attend",
    )(source, *arrays, *arrays, qseg, kseg)


def project_kernel(place_ref, ring_ref, own_ref, other_ref, *refs):
    pieces = refs[:-4]
    kept_ref, inner_ref, outer_ref, sums = refs[-4:]
    servers, _, width = sums.shape
    place = place_ref[0]
    even = place % 2 == 0
    own, other = own_ref[...], other_ref[...]
    both = jnp.concatenate([jnp.where(even, own, other), jnp.where(even, other, own)], axis=1)
    depth = pieces[0].shape[0]
    if len(pieces) == 1:
        for server in range(servers):
            rows = pieces[0][server * width : (server + 1) * width, :]
            sums[server] = contract(both, rows, 1, 1)
    else:
        for piece in range(len(pieces)):
            target = ring_ref[0] ^ piece
            inside = pl.multiple_of((target % (width // depth)) * depth, depth)
            sums[target // (width // depth), :, pl.ds(inside, depth)] = contract(
                both, pieces[piece][...], 1, 1
            )
    kept_ref[...] = sums[place]
    low = place < 2
    inner_ref[...] = sums[jnp.where(low, 2, 1)].astype(BF)
    outer_ref[...] = sums[jnp.where(low, 3, 0)].astype(BF)


def project(place, ring, own, other, pieces, servers):
    tokens, width = own.shape
    rows, columns = pieces[0].shape
    pair = 2 * width
    tail = pl.BlockSpec((pl.Element(rows), pl.Element(pair)), lambda i: (0, columns - pair))
    full = pl.BlockSpec((tokens, width), lambda i: (0, 0))
    return pl.pallas_call(
        project_kernel,
        grid=(1,),
        in_specs=[pl.BlockSpec(memory_space=pltpu.SMEM)] * 2 + [full] * 2 + [tail] * len(pieces),
        out_specs=[full] * 3,
        out_shape=[
            jax.ShapeDtypeStruct((tokens, width), F32),
            jax.ShapeDtypeStruct((tokens, width), BF),
            jax.ShapeDtypeStruct((tokens, width), BF),
        ],
        scratch_shapes=[pltpu.VMEM((servers, tokens, width), F32)],
        cost_estimate=cost(2 * tokens * D * pair, D * pair * 2 + tokens * width * 12),
        compiler_params=params(),
        name="project",
    )(place, ring, own, other, *pieces)


def final_kernel(
    static_ref, x_ref, first_ref, folded_ref, column_ref, own_ref, inner_ref, outer_ref, *rest
):
    new_ref = rest[-1]
    tokens, _, width = x_ref.shape
    first = first_ref[...]
    mean, inverse = centre(first)
    stream = lax.broadcasted_iota(jnp.int32, (1, 4 * tokens), 1) & 3

    def coefficient(column, projected):
        dynamic = jnp.tanh(inverse * (projected - mean * column_ref[column : column + 1, 0:1]))
        return by_stream(static_ref, column, stream) + dynamic

    def unfolded(which):
        return jnp.concatenate(
            [folded_ref[4 * which + part : 4 * which + part + 1] for part in range(4)], axis=1
        )

    projected = [first[5:6], first[6:7], first[7:8], unfolded(0), unfolded(1)]
    columns = [coefficient(1 + j, projected[j]) for j in range(5)]
    residual = jnp.concatenate(columns[:4] + columns[:4], axis=0)
    row, col = iotas(4 * SUB, 4 * SUB)
    same = (row >> 2) == (col >> 2)
    row, col = iotas(SUB, 4 * SUB)
    mine = row == (col >> 2)
    for at in range(tokens // SUB):
        lanes = slice(at * 4 * SUB, (at + 1) * 4 * SUB)
        rows = slice(at * SUB, (at + 1) * SUB)
        v = x_ref[rows].reshape(4 * SUB, width)
        matrix = jnp.where(same, jnp.tile(residual[:, lanes], (SUB // 2, 1)), 0.0)
        high, low = split(matrix, 2)
        new = contract(high, v, 1, 0) + contract(low, v, 1, 0)
        sent = inner_ref[rows, :].astype(F32) + outer_ref[rows, :].astype(F32)
        update_high, update_low = split(own_ref[rows, :] + sent, 2)
        spread_high, spread_low = split(jnp.where(mine, columns[4][:, lanes], 0.0), 2)
        new += contract(
            jnp.concatenate([spread_high, spread_high, spread_low], axis=0),
            jnp.concatenate([update_high, update_low, update_high], axis=0),
            0,
            0,
        )
        new_ref[rows] = new.astype(BF).reshape(SUB, 4, width)


def final(static, x, sums, updates, start, previous):
    tokens, width = updates[0].shape
    group = (sums.shape[1] - 128) // 5
    stream_block = pl.BlockSpec((STEP, 4, width), lambda i: (start // STEP + i, 0, 0))
    specs = [
        pl.BlockSpec(memory_space=pltpu.SMEM),
        stream_block,
        pl.BlockSpec((8, 4 * STEP), lambda i: (0, start // STEP + i)),
        pl.BlockSpec((8, STEP), lambda i: (0, 4 * group // STEP + start // STEP + i)),
        pl.BlockSpec((8, 128), lambda i: (0, 5 * group // 128)),
    ]
    specs += [pl.BlockSpec((STEP, width), lambda i: (i, 0))] * 3
    args = [static, x, sums, sums, sums, *updates]
    aliases = {}
    if previous is not None:
        specs.append(pl.BlockSpec(memory_space=pl.ANY))
        aliases = {len(args): 0}
        args.append(previous)
    return pl.pallas_call(
        final_kernel,
        grid=(tokens // STEP,),
        in_specs=specs,
        out_specs=stream_block,
        out_shape=jax.ShapeDtypeStruct(x.shape, BF),
        input_output_aliases=aliases,
        cost_estimate=cost(tokens * 4 * width * 1200, tokens * 22 * width),
        compiler_params=params(),
        name="final",
    )(*args)


def body(streams, proj_master, hc_proj, hc_static, segment_ids, block_mask):
    tokens_local, _, width = streams.shape
    group_size = lax.axis_size("mp")
    place = lax.axis_index("mp").astype(jnp.int32).reshape(1)
    ring = lax.axis_index("blk").astype(jnp.int32).reshape(1)

    proj_rows = jnp.concatenate(
        [hc_proj.T, jnp.ones((1, width), F32), jnp.zeros((1, width), F32)], axis=0
    )
    own = stats(streams, proj_rows)
    parts = list(regroup(place, proj_master, group_size))
    sums, parts = lax.optimization_barrier(([own] + from_others(own, "mp"), parts))

    def gathered(normed):
        rows = lax.all_gather(normed, "mp", axis=0, tiled=True)
        return rows.reshape(group_size, normed.shape[0], width)

    for step in range(1, group_size):
        parts[step] = lax.ppermute(
            parts[step], "mp", [(at, (at + step) % group_size) for at in range(group_size)]
        )
    sums_all, normed_late = mix(hc_static, streams, sums, CHUNK, tokens_local - CHUNK)
    _, normed_first = mix(hc_static, streams, sums, 0, CHUNK)
    parts, normed_late, normed_first = lax.optimization_barrier((parts, normed_late, normed_first))
    rows_late = gathered(normed_late)
    rows_first = gathered(normed_first)

    pieces = weight_pieces(assemble(place, parts))
    rows_late, pieces = lax.optimization_barrier((rows_late, pieces))

    halo = passed_along(segment_ids[-BLOCK:], "blk", 1)
    halo = jnp.where(lax.axis_index("blk") == 0, -1, halo)
    extended = jnp.concatenate([halo, segment_ids])
    key_at = jnp.arange(tokens_local + BLOCK, dtype=jnp.int32)[None, :]
    query_at = jnp.arange(tokens_local, dtype=jnp.int32)[:, None] + BLOCK
    earlier = (extended[None, :] == segment_ids[:, None]) & (key_at < query_at)
    positions = jnp.sum(earlier.astype(jnp.int32), axis=1)
    half = HEAD_DIM // 2
    inverse = 10000.0 ** (-(jnp.arange(half, dtype=F32) * 2.0 / HEAD_DIM))
    angles = positions.astype(F32)[:, None] * inverse[None, :]
    cosine, sine = jnp.cos(angles), jnp.sin(angles)
    cosine = jnp.concatenate([cosine, cosine], axis=1)
    sine = jnp.concatenate([-sine, sine], axis=1)
    windows = []
    for block in range(tokens_local // BLOCK):
        before = extended[block * BLOCK : (block + 1) * BLOCK]
        before = jnp.where(block_mask[block] == 1, before, -1)
        seen = jnp.concatenate([before, segment_ids[block * BLOCK : (block + 1) * BLOCK]])
        for chunk in range(BLOCK // CHUNK):
            windows.append(seen[chunk * CHUNK : chunk * CHUNK + BLOCK + CHUNK])
    key_segments = jnp.stack(windows)[:, None, :]
    query_segments = segment_ids[:, None]

    qkv_late, halo_rows = qkv_columns(ring, rows_late, pieces, cosine[CHUNK:], sine[CHUNK:])
    halo_rows = passed_along(halo_rows, "blk", 1)

    def projected(own, other):
        return project(place, ring, own, other, pieces, group_size)

    last = tokens_local // CHUNK - 1
    late_chunks = [(qkv_late, 1, at) for at in range(last)]

    def attended(chunk, window):
        source, _, at = window[-1]
        return attend((source, at), window, query_segments, key_segments, chunk)

    own = attended(last, late_chunks[-3:])
    both = (own, swapped(own, "mp", 1))
    rows_first, both = lax.optimization_barrier((rows_first, both))
    parts = {last: projected(*both)}
    qkv_first, _ = qkv_columns(ring, rows_first, pieces, cosine[:CHUNK], sine[:CHUNK])
    chunks = [(halo_rows, 0, 0), (halo_rows, 0, 1), (qkv_first, 1, 0)] + late_chunks
    for chunk in reversed(range(last)):
        own = attended(chunk, chunks[chunk : chunk + 3])
        parts[chunk] = projected(own, swapped(own, "mp", 1))

    result = None
    for chunk in reversed(range(last + 1)):
        kept, inner, outer = parts[chunk]
        outer = lax.ppermute(outer, "mp", [(1, 3), (2, 0)])
        inner = lax.ppermute(inner, "mp", [(1, 2), (2, 1)])
        updates = [kept, outer, inner]
        result = final(hc_static, streams, sums_all, updates, chunk * CHUNK, result)
    return result


def solution(mesh):
    in_specs = (
        P("blk", None, "mp"),
        P(("blk", "mp"), None, None),
        P("mp", None),
        P(),
        P("blk"),
        P("blk"),
    )
    out_specs = P("blk", None, "mp")
    return jax.shard_map(body, mesh=mesh, in_specs=in_specs, out_specs=out_specs, check_vma=False)
```
